32 devices in a mesh: seq: 2 (over x), cp: 16 (over z, y, core).
Axes of the slice: x: 2, y: 2, z: 4, core: 2. Of those that a mesh axis runs over, the one named last changes fastest.
Arguments:
- layer_in: bfloat16 [1024, 4, 2048], P('cp', 'seq'), may hold values from -6 to 6
- valid_len: int32 [4], P('seq'), may hold values from 50 to 1024
- norm1_gain: bfloat16 [2048], P(('seq', 'cp')), may hold values from 0.25 to 1.75
- w_query: bfloat16 [2048, 2048], P(('seq', 'cp')), may hold values from -0.125 to 0.125
- w_key: bfloat16 [2048, 2048], P(('seq', 'cp')), may hold values from -0.125 to 0.125
- w_value: bfloat16 [2048, 2048], P(('seq', 'cp')), may hold values from -0.125 to 0.125
- w_out: bfloat16 [2048, 2048], P(('seq', 'cp')), may hold values from -3 to 3
- norm2_gain: bfloat16 [2048], P(('seq', 'cp')), may hold values from 0.25 to 1.75
- w_gate: bfloat16 [2048, 8192], P(('seq', 'cp')), may hold values from -0.125 to 0.125
- w_up: bfloat16 [2048, 8192], P(('seq', 'cp')), may hold values from -0.125 to 0.125
- w_down: bfloat16 [8192, 2048], P(('seq', 'cp')), may hold values from -0.0625 to 0.0625
- cotangent: bfloat16 [1024, 4, 2048], P('cp', 'seq'), may hold values from -6 to 6
Outputs:
- layer_out: bfloat16 [1024, 4, 2048], P('cp', 'seq')
- in_grad: float32 [1024, 4, 2048], P('cp', 'seq')
- norm1_gain_grad: float32 [2048], P(('seq', 'cp'))
- w_query_grad: float32 [2048, 2048], P(('seq', 'cp'))
- w_key_grad: float32 [2048, 2048], P(('seq', 'cp'))
- w_value_grad: float32 [2048, 2048], P(('seq', 'cp'))
- w_out_grad: float32 [2048, 2048], P(('seq', 'cp'))
- norm2_gain_grad: float32 [2048], P(('seq', 'cp'))
- w_gate_grad: float32 [2048, 8192], P(('seq', 'cp'))
- w_up_grad: float32 [2048, 8192], P(('seq', 'cp'))
- w_down_grad: float32 [8192, 2048], P(('seq', 'cp'))
The draws below stay inside these ranges and needn't reach their ends.
All inputs are finite; a program needn't handle non-finite values.
Results may differ from the reference program's by a relative error of at most 0.015.
Values may be sent and summed in bfloat16 or wider, within the bound.
A program may use at most 512 MiB of HBM per device.

```python
import math
import jax
import jax.numpy as jnp
from jax import lax

D = 2048
HEADS = 16
FF = 8192
STRIP = 32
LENGTH = 1024
SEQS_ALL = 4
N_CP = 16


def place_ends(entries, own_key, least, high):
    longest = entries.shape.index(max(entries.shape))
    spots = []
    for shift in (0, 1):
        where = [jax.random.randint(jax.random.fold_in(own_key, axis), (), 0, length) for axis, length in enumerate(entries.shape)]
        where[longest] = (where[longest] + shift) % entries.shape[longest]
        spots.append(tuple(where))
    return entries.at[spots[0]].set(least).at[spots[1]].set(high)


def block_scale(own_key, extent, split, low, high):
    def one(dim, parts):
        draws = jax.random.uniform(jax.random.fold_in(jax.random.fold_in(own_key, 6), dim), (parts,), jnp.float32, low / len(split), high / len(split))
        return jnp.repeat(jnp.exp(draws), extent[dim] // parts).reshape((-1,) + (1,) * (len(extent) - dim - 1))

    gain = one(*split[0])
    for cut in split[1:]:
        gain = gain * one(*cut)
    return gain


def normal_values(rng, extent, scale, limit, cuts=(), kind=jnp.bfloat16):
    drawn = scale * jax.random.normal(rng, extent, jnp.float32)
    if cuts:
        drawn = drawn * block_scale(rng, extent, cuts, -0.22, 0.18)
    return jnp.clip(drawn, -limit, limit).astype(kind)


def setup_inputs(seed: int = 0) -> dict:
    arg_keys = jax.random.split(jax.random.key(seed), 13)
    layer_in = normal_values(arg_keys[0], (LENGTH, SEQS_ALL, D), 1.0, 6.0, ((0, 16), (1, 2)))
    valid_len = place_ends(jax.random.randint(arg_keys[1], (SEQS_ALL,), 50, LENGTH + 1), jax.random.fold_in(arg_keys[1], 1), 50, LENGTH).astype(jnp.int32)
    norm1_gain = jnp.clip(1.0 + 0.15 * jax.random.normal(arg_keys[2], (D,), jnp.float32), 0.25, 1.75).astype(jnp.bfloat16)
    w_query = normal_values(arg_keys[3], (D, D), D ** -0.5, 0.125, ((0, 32),))
    w_key = normal_values(arg_keys[4], (D, D), D ** -0.5, 0.125, ((0, 32),))
    w_value = normal_values(arg_keys[5], (D, D), D ** -0.5, 0.125, ((0, 32),))
    w_out = normal_values(arg_keys[6], (D, D), (0.75 * LENGTH ** 0.5 * D ** -0.5), 3.0, ((0, 32),))
    norm2_gain = jnp.clip(1.0 + 0.15 * jax.random.normal(arg_keys[7], (D,), jnp.float32), 0.25, 1.75).astype(jnp.bfloat16)
    w_gate = normal_values(arg_keys[8], (D, FF), D ** -0.5, 0.125, ((0, 32),))
    w_up = normal_values(arg_keys[9], (D, FF), D ** -0.5, 0.125, ((0, 32),))
    w_down = normal_values(arg_keys[10], (FF, D), FF ** -0.5, 0.0625, ((0, 32),))
    cotangent = normal_values(arg_keys[11], (LENGTH, SEQS_ALL, D), 1.0, 6.0, ((0, 16), (1, 2)))
    return dict(layer_in=layer_in, valid_len=valid_len, norm1_gain=norm1_gain, w_query=w_query, w_key=w_key, w_value=w_value, w_out=w_out, norm2_gain=norm2_gain, w_gate=w_gate, w_up=w_up, w_down=w_down, cotangent=cotangent)


@jax.custom_vjp
def low(v):
    return lax.optimization_barrier(v.astype(jnp.bfloat16)).astype(jnp.float32)

@jax.custom_vjp
def low_back(v):
    return v

def low_keep(v):
    return (low(v), None)

def low_pass(kept, grad):
    return (grad,)

def back_keep(v):
    return (v, None)

def back_low(kept, grad):
    return (low(grad),)
low.defvjp(low_keep, low_pass)
low_back.defvjp(back_keep, back_low)
norm_eps = 1e-05
rope_base = 10000.0
highest = lax.Precision.HIGHEST

def matmul(left, right):
    return jnp.dot(left, right, precision=highest, preferred_element_type=jnp.float32)

def row_positions(indices, strip_rows, devices):
    owner_index = indices // (2 * strip_rows)
    within = indices % (2 * strip_rows)
    return jnp.where(within < strip_rows, owner_index * strip_rows + within, (2 * devices - 1 - owner_index) * strip_rows + within - strip_rows)

def rotate(values, positions, num_heads):
    count_rows, model_width = values.shape
    head_width = model_width // num_heads
    half_width = head_width // 2
    freqs_table = rope_base ** (-2.0 * jnp.arange(half_width, dtype=jnp.float32) / head_width)
    angles = positions.astype(jnp.float32)[:, None] * freqs_table[None, :]
    cosine = jnp.cos(angles)[:, None, :]
    sine_table = jnp.sin(angles)[:, None, :]
    split_heads = values.reshape(count_rows, num_heads, head_width)
    former = split_heads[:, :, :half_width]
    latter = split_heads[:, :, half_width:]
    turned = jnp.concatenate([former * cosine - latter * sine_table, latter * cosine + former * sine_table], axis=2)
    return turned.reshape(count_rows, model_width)

def norm_scale(values):
    return values * lax.rsqrt(lax.optimization_barrier(jnp.mean(values * values, axis=-1, keepdims=True)) + norm_eps)

def normed(values, gain_vector):
    return norm_scale(values) * gain_vector

def attend(q_rows, k_rows, v_rows, positions, valid_count):
    model_width = q_rows.shape[1]
    head_width = model_width // HEADS
    q_heads = q_rows.reshape(LENGTH, HEADS, head_width)
    k_heads = k_rows.reshape(LENGTH, HEADS, head_width)
    v_heads = v_rows.reshape(LENGTH, HEADS, head_width)
    block_rows = math.gcd(LENGTH, 512)
    score_scale = head_width ** (-0.5)
    score_shift = math.log(LENGTH)

    def one_block(block_index):
        first_row = block_index * block_rows
        q_block = lax.dynamic_slice_in_dim(q_heads, first_row, block_rows, 0)
        query_pos = lax.dynamic_slice_in_dim(positions, first_row, block_rows, 0)
        raw_scores = jnp.einsum('qhd,khd->hqk', q_block, k_heads, precision=highest)
        logits = low_back(raw_scores * score_scale - score_shift)
        allowed = (positions[None, :] <= query_pos[:, None]) & (positions[None, :] < valid_count)
        sig_probs = low(jax.nn.sigmoid(logits) * allowed[None, :, :].astype(jnp.float32))
        return jnp.einsum('hqk,khd->qhd', sig_probs, v_heads, precision=highest)
    outputs = lax.map(jax.checkpoint(one_block), jnp.arange(LENGTH // block_rows, dtype=jnp.int32))
    return outputs.reshape(LENGTH, model_width)

def layer(inputs, valid_count, positions, params):
    gain_one, query_weight, key_weight, value_weight, out_weight, gain_two, gate_weight, up_weight, down_weight = params
    normed_one = low(normed(inputs, gain_one))
    query = low_back(matmul(normed_one, query_weight))
    key_rows = low_back(matmul(normed_one, key_weight))
    value = low(low_back(matmul(normed_one, value_weight)))
    query_low = low(rotate(query, positions, HEADS))
    key_low = low(rotate(key_rows, positions, HEADS))
    attended = low(low_back(attend(query_low, key_low, value, positions, valid_count)))
    hidden_state = inputs + low_back(matmul(attended, out_weight))
    normed_two = low(normed(hidden_state, gain_two))
    gate_rows = low_back(matmul(normed_two, gate_weight))
    up_rows = low_back(matmul(normed_two, up_weight))
    hidden_units = low(jax.nn.silu(gate_rows) * up_rows)
    return hidden_state + matmul(hidden_units, down_weight)

def reference(layer_in, valid_len, norm1_gain, w_query, w_key, w_value, w_out, norm2_gain, w_gate, w_up, w_down, cotangent):
    positions = row_positions(jnp.arange(LENGTH, dtype=jnp.int32), STRIP, N_CP)
    params = (norm1_gain.astype(jnp.float32), w_query.astype(jnp.float32), w_key.astype(jnp.float32), w_value.astype(jnp.float32), w_out.astype(jnp.float32), norm2_gain.astype(jnp.float32), w_gate.astype(jnp.float32), w_up.astype(jnp.float32), w_down.astype(jnp.float32))
    inputs = jnp.transpose(layer_in.astype(jnp.float32), (1, 0, 2))

    def whole(seq_inputs, weights):

        def one_sequence(item):
            return layer(item[0], item[1], positions, weights)
        return lax.map(one_sequence, (seq_inputs, valid_len))
    outputs, pull_back = jax.vjp(whole, inputs, params)
    in_grad, grads = pull_back(jnp.transpose(cotangent.astype(jnp.float32), (1, 0, 2)))
    layer_out = jnp.transpose(outputs, (1, 0, 2)).astype(jnp.bfloat16)
    return (layer_out, jnp.transpose(in_grad, (1, 0, 2)), grads[0], grads[1], grads[2], grads[3], grads[4], grads[5], grads[6], grads[7], grads[8])
```

```python
import functools
import math

import jax
import jax.numpy as jnp
from jax import lax
from jax.sharding import PartitionSpec as P

HEADS = 16


norm_eps = 1e-05
rope_base = 10000.0


def row_positions(indices, strip_rows, devices):
    owner_index = indices // (2 * strip_rows)
    within = indices % (2 * strip_rows)
    return jnp.where(
        within < strip_rows,
        owner_index * strip_rows + within,
        (2 * devices - 1 - owner_index) * strip_rows + within - strip_rows,
    )


def rotate(values, positions, num_heads):
    count_rows, model_width = values.shape
    head_width = model_width // num_heads
    half_width = head_width // 2
    freqs_table = rope_base ** (-2.0 * jnp.arange(half_width, dtype=jnp.float32) / head_width)
    angles = positions.astype(jnp.float32)[:, None] * freqs_table[None, :]
    cosine = jnp.cos(angles)[:, None, :]
    sine_table = jnp.sin(angles)[:, None, :]
    split_heads = values.reshape(count_rows, num_heads, head_width)
    former = split_heads[:, :, :half_width]
    latter = split_heads[:, :, half_width:]
    turned = jnp.concatenate(
        [former * cosine - latter * sine_table, latter * cosine + former * sine_table], axis=2
    )
    return turned.reshape(count_rows, model_width)


def norm_scale(values):
    return values * lax.rsqrt(jnp.mean(values * values, axis=-1, keepdims=True) + norm_eps)


def normed(values, gain_vector):
    return norm_scale(values) * gain_vector


def swiglu(gate_rows, up_rows):
    return jax.nn.silu(gate_rows) * up_rows


def dot_right(left, right):
    return lax.dot_general(
        left, right, (((1,), (1,)), ((), ())), preferred_element_type=jnp.float32
    )


def dot_left(left, right):
    return lax.dot_general(
        left, right, (((0,), (0,)), ((), ())), preferred_element_type=jnp.float32
    )


def split_blocks(array, block_rows):
    return array.reshape((array.shape[0] // block_rows, block_rows) + array.shape[1:])


def key_mask(query_pos, key_pos, valid_count):
    causal = key_pos[None, :] <= query_pos[:, None]
    live_keys = key_pos[None, :] < valid_count[:, None]
    return (causal[None, None, :, :] & live_keys[:, None, None, :]).astype(jnp.float32)


def scores_of(queries, key_rows, query_pos, key_pos, valid_count, score_shift):
    head_width = queries.shape[3]
    raw_scores = jnp.einsum(
        "qshd,kshd->shqk", queries, key_rows, preferred_element_type=jnp.float32
    )
    return (
        raw_scores * head_width ** (-0.5) - score_shift,
        key_mask(query_pos, key_pos, valid_count),
    )


def block_grads(queries, grad_rows, key_rows, values, query_pos, key_pos, valid_count, score_shift):
    logits, mask_table = scores_of(queries, key_rows, query_pos, key_pos, valid_count, score_shift)
    sigmoid_table = jax.nn.sigmoid(logits)
    weights_low = (sigmoid_table * mask_table).astype(jnp.bfloat16)
    grad_weights = jnp.einsum(
        "qshd,kshd->shqk", grad_rows, values, preferred_element_type=jnp.float32
    )
    grad_logits = (grad_weights * mask_table * (sigmoid_table * (1.0 - sigmoid_table))).astype(
        jnp.bfloat16
    )
    return (weights_low, grad_logits)


def make_norm_fold(normalized, pieces):
    gain_part = pieces[0].astype(jnp.float32)
    scaled = (normalized * gain_part).astype(jnp.bfloat16)
    totals = tuple(
        (
            jnp.dot(scaled, weight_piece, preferred_element_type=jnp.float32)
            for weight_piece in pieces[1:]
        )
    )
    return (gain_part,) + totals


def make_row_fold(left_rows, weight_piece):
    return jnp.dot(left_rows, weight_piece, preferred_element_type=jnp.float32)


def gather_weights_step(
    layer_in,
    valid_len,
    norm1_gain,
    w_query,
    w_key,
    w_value,
    w_out,
    norm2_gain,
    w_gate,
    w_up,
    w_down,
    cotangent,
):
    local_rows, local_seqs, model_width = layer_in.shape
    num_heads = HEADS
    head_width = model_width // num_heads
    strip_rows = local_rows // 2
    cp_devices = lax.axis_size("cp")
    cp_place = lax.axis_index("cp")
    seq_length = local_rows * cp_devices
    score_shift = math.log(seq_length)
    score_scale = head_width ** (-0.5)
    token_count = local_rows * local_seqs
    local_pos = row_positions(
        cp_place * local_rows + jnp.arange(local_rows, dtype=jnp.int32), strip_rows, cp_devices
    )
    token_pos = jnp.broadcast_to(local_pos[:, None], (local_rows, local_seqs)).reshape(token_count)
    every_pos = row_positions(jnp.arange(seq_length, dtype=jnp.int32), strip_rows, cp_devices)
    block_rows = math.gcd(seq_length, 512)
    head_shape = (local_rows, local_seqs, num_heads, head_width)
    row_shape = (local_rows, local_seqs, model_width)
    zero_heads = jnp.zeros(head_shape, jnp.float32)
    inputs = layer_in.reshape(token_count, model_width).astype(jnp.float32)
    input_norm = norm_scale(inputs)
    gain_one, query, key_proj, value = make_norm_fold(
        input_norm,
        (
            lax.all_gather(norm1_gain, ("seq", "cp"), axis=0, tiled=True),
            lax.all_gather(w_query, ("seq", "cp"), axis=0, tiled=True),
            lax.all_gather(w_key, ("seq", "cp"), axis=0, tiled=True),
            lax.all_gather(w_value, ("seq", "cp"), axis=0, tiled=True),
        ),
    )
    normed_one = (input_norm * gain_one).astype(jnp.bfloat16)
    query_low = rotate(query, token_pos, num_heads).astype(jnp.bfloat16)
    key_low = rotate(key_proj, token_pos, num_heads).astype(jnp.bfloat16)
    value_low = value.astype(jnp.bfloat16)
    query_heads = query_low.reshape(head_shape)
    key_local = key_low.reshape(row_shape)
    value_local = value_low.reshape(row_shape)
    key_piece = lax.all_gather(key_local, "cp", axis=0, tiled=True)
    value_piece = lax.all_gather(value_local, "cp", axis=0, tiled=True)
    piece_rows = key_piece.shape[0]
    piece_block = math.gcd(piece_rows, 512)
    piece_pos = row_positions(jnp.arange(piece_rows, dtype=jnp.int32), strip_rows, cp_devices)

    def scan_step(partial_sum, block_items):
        key_block, value_block, block_pos = block_items
        logits, mask_table = scores_of(
            query_heads,
            key_block.reshape(piece_block, local_seqs, num_heads, head_width),
            local_pos,
            block_pos,
            valid_len,
            score_shift,
        )
        weights_low = (jax.nn.sigmoid(logits) * mask_table).astype(jnp.bfloat16)
        added = jnp.einsum(
            "shqk,kshd->qshd",
            weights_low,
            value_block.reshape(piece_block, local_seqs, num_heads, head_width),
            preferred_element_type=jnp.float32,
        )
        return (partial_sum + added, None)

    result, _ = lax.scan(
        scan_step,
        zero_heads,
        (
            split_blocks(key_piece, piece_block),
            split_blocks(value_piece, piece_block),
            split_blocks(piece_pos, piece_block),
        ),
    )
    attended_low = result.reshape(token_count, model_width).astype(jnp.bfloat16)
    attn_branch = make_row_fold(
        attended_low, lax.all_gather(w_out, ("seq", "cp"), axis=0, tiled=True)
    )
    hidden_state = inputs + attn_branch
    hidden_norm = norm_scale(hidden_state)
    gain_two, gate_rows, up_rows = make_norm_fold(
        hidden_norm,
        (
            lax.all_gather(norm2_gain, ("seq", "cp"), axis=0, tiled=True),
            lax.all_gather(w_gate, ("seq", "cp"), axis=0, tiled=True),
            lax.all_gather(w_up, ("seq", "cp"), axis=0, tiled=True),
        ),
    )
    normed_two = (hidden_norm * gain_two).astype(jnp.bfloat16)
    hidden_units = swiglu(gate_rows, up_rows).astype(jnp.bfloat16)
    ff_branch = make_row_fold(
        hidden_units, lax.all_gather(w_down, ("seq", "cp"), axis=0, tiled=True)
    )
    layer_out = (hidden_state + ff_branch).astype(jnp.bfloat16).reshape(row_shape)
    grad_out = cotangent.reshape(token_count, model_width)
    gate_all, up_all, down_all = (
        lax.all_gather(w_gate, ("seq", "cp"), axis=0, tiled=True),
        lax.all_gather(w_up, ("seq", "cp"), axis=0, tiled=True),
        lax.all_gather(w_down, ("seq", "cp"), axis=0, tiled=True),
    )
    grad_hidden = dot_right(grad_out, down_all)
    _, pull_swiglu = jax.vjp(swiglu, gate_rows, up_rows)
    grad_gate, grad_up = pull_swiglu(grad_hidden)
    grad_gate_low = grad_gate.astype(jnp.bfloat16)
    grad_up_low = grad_up.astype(jnp.bfloat16)
    grad_norm_two = dot_right(grad_gate_low, gate_all) + dot_right(grad_up_low, up_all)
    _, pull_two = jax.vjp(normed, hidden_state, gain_two)
    grad_from_two, gain_two_term = pull_two(grad_norm_two)
    ff_grads = (
        lax.psum_scatter(gain_two_term, ("seq", "cp"), scatter_dimension=0, tiled=True),
        lax.psum_scatter(
            dot_left(normed_two, grad_gate_low), ("seq", "cp"), scatter_dimension=0, tiled=True
        ),
        lax.psum_scatter(
            dot_left(normed_two, grad_up_low), ("seq", "cp"), scatter_dimension=0, tiled=True
        ),
        lax.psum_scatter(
            dot_left(hidden_units, grad_out), ("seq", "cp"), scatter_dimension=0, tiled=True
        ),
    )
    grad_state = grad_out.astype(jnp.float32) + grad_from_two
    query_all, key_all, value_all, out_all = (
        lax.all_gather(w_query, ("seq", "cp"), axis=0, tiled=True),
        lax.all_gather(w_key, ("seq", "cp"), axis=0, tiled=True),
        lax.all_gather(w_value, ("seq", "cp"), axis=0, tiled=True),
        lax.all_gather(w_out, ("seq", "cp"), axis=0, tiled=True),
    )
    grad_branch_low = grad_state.astype(jnp.bfloat16)
    grad_attended_low = dot_right(grad_branch_low, out_all).astype(jnp.bfloat16)
    grad_heads = grad_attended_low.reshape(head_shape)
    key_heads_local = key_local.reshape(head_shape)
    value_heads_local = value_local.reshape(head_shape)
    keys_every, values_every, queries_every, grads_every = (
        lax.all_gather(key_local, "cp", axis=0, tiled=True),
        lax.all_gather(value_local, "cp", axis=0, tiled=True),
        lax.all_gather(query_low.reshape(row_shape), "cp", axis=0, tiled=True),
        lax.all_gather(grad_attended_low.reshape(row_shape), "cp", axis=0, tiled=True),
    )

    def key_step(partial_sums, block_items):
        query_block, grad_block_rows, block_pos = block_items
        query_part = query_block.reshape(block_rows, local_seqs, num_heads, head_width)
        grad_part = grad_block_rows.reshape(block_rows, local_seqs, num_heads, head_width)
        weights_low, grad_logits = block_grads(
            query_part,
            grad_part,
            key_heads_local,
            value_heads_local,
            block_pos,
            local_pos,
            valid_len,
            score_shift,
        )
        key_added = jnp.einsum(
            "shqk,qshd->kshd", grad_logits, query_part, preferred_element_type=jnp.float32
        )
        value_added = jnp.einsum(
            "shqk,qshd->kshd", weights_low, grad_part, preferred_element_type=jnp.float32
        )
        return ((partial_sums[0] + key_added, partial_sums[1] + value_added), None)

    (key_sum, value_sum), _ = lax.scan(
        key_step,
        (zero_heads, zero_heads),
        (
            split_blocks(queries_every, block_rows),
            split_blocks(grads_every, block_rows),
            split_blocks(every_pos, block_rows),
        ),
    )
    grad_key_rot = key_sum.reshape(token_count, model_width) * score_scale
    grad_value_sum = value_sum.reshape(token_count, model_width)

    def query_step(partial_sum, block_items):
        key_block, value_block, block_pos = block_items
        key_heads = key_block.reshape(block_rows, local_seqs, num_heads, head_width)
        _, grad_logits = block_grads(
            query_heads,
            grad_heads,
            key_heads,
            value_block.reshape(block_rows, local_seqs, num_heads, head_width),
            local_pos,
            block_pos,
            valid_len,
            score_shift,
        )
        added = jnp.einsum(
            "shqk,kshd->qshd", grad_logits, key_heads, preferred_element_type=jnp.float32
        )
        return (partial_sum + added, None)

    query_sum, _ = lax.scan(
        query_step,
        zero_heads,
        (
            split_blocks(keys_every, block_rows),
            split_blocks(values_every, block_rows),
            split_blocks(every_pos, block_rows),
        ),
    )
    grad_query_rot = query_sum.reshape(token_count, model_width) * score_scale
    grad_query_low = rotate(grad_query_rot, -token_pos, num_heads).astype(jnp.bfloat16)
    grad_key_low = rotate(grad_key_rot, -token_pos, num_heads).astype(jnp.bfloat16)
    grad_value_low = grad_value_sum.astype(jnp.bfloat16)
    grad_norm_one = (
        dot_right(grad_query_low, query_all)
        + dot_right(grad_key_low, key_all)
        + dot_right(grad_value_low, value_all)
    )
    _, pull_one = jax.vjp(normed, inputs, gain_one)
    grad_from_one, gain_one_term = pull_one(grad_norm_one)
    in_grad = (grad_state + grad_from_one).reshape(row_shape)
    attn_grads = (
        lax.psum_scatter(gain_one_term, ("seq", "cp"), scatter_dimension=0, tiled=True),
        lax.psum_scatter(
            dot_left(normed_one, grad_query_low), ("seq", "cp"), scatter_dimension=0, tiled=True
        ),
        lax.psum_scatter(
            dot_left(normed_one, grad_key_low), ("seq", "cp"), scatter_dimension=0, tiled=True
        ),
        lax.psum_scatter(
            dot_left(normed_one, grad_value_low), ("seq", "cp"), scatter_dimension=0, tiled=True
        ),
        lax.psum_scatter(
            dot_left(attended_low, grad_branch_low), ("seq", "cp"), scatter_dimension=0, tiled=True
        ),
    )
    return (
        layer_out,
        in_grad,
        attn_grads[0],
        attn_grads[1],
        attn_grads[2],
        attn_grads[3],
        attn_grads[4],
        ff_grads[0],
        ff_grads[1],
        ff_grads[2],
        ff_grads[3],
    )


def exchange_pair(values, axis, flip):
    size = lax.axis_size(axis)
    return lax.ppermute(values, axis, [(place, place ^ flip) for place in range(size)])


def take_columns(shard, blocks):
    rows = shard.shape[0]
    moved = lax.all_to_all(blocks, "cp", split_axis=2, concat_axis=0, tiled=True)
    width = moved.shape[1] * moved.shape[3]
    half = moved.reshape(moved.shape[0], width)
    return lax.all_gather(half, "seq", axis=0, tiled=True)


def give_rows(grad, halves):
    cp_devices = lax.axis_size("cp")
    half = lax.psum_scatter(grad, "seq", scatter_dimension=0, tiled=True)
    rows = half.shape[0] // cp_devices
    width = half.shape[1] // halves
    blocks = half.reshape(half.shape[0], halves, 1, width)
    moved = lax.all_to_all(blocks, "cp", split_axis=0, concat_axis=2, tiled=True)
    return moved


def norm_back(values, gain_part, grads):
    width = values.shape[-1]
    scale = lax.rsqrt(jnp.mean(values * values, axis=-1, keepdims=True) + norm_eps)
    weighted = grads * gain_part
    inner = jnp.mean(values * weighted, axis=-1, keepdims=True)
    return (
        scale * weighted - values * (scale * scale * scale * inner),
        jnp.sum(values * scale * grads, axis=0),
    )


def move_tokens_step(
    layer_in,
    valid_len,
    norm1_gain,
    w_query,
    w_key,
    w_value,
    w_out,
    norm2_gain,
    w_gate,
    w_up,
    w_down,
    cotangent,
):
    local_rows, local_seqs, model_width = layer_in.shape
    num_heads = HEADS
    head_width = model_width // num_heads
    strip_rows = local_rows // 2
    cp_devices = lax.axis_size("cp")
    seq_devices = lax.axis_size("seq")
    cp_place = lax.axis_index("cp")
    seq_length = local_rows * cp_devices
    score_shift = math.log(seq_length)
    score_scale = head_width ** (-0.5)
    local_tokens = local_rows * local_seqs
    group_tokens = seq_length * local_seqs
    low = jnp.bfloat16

    def gather_tokens(values):
        return lax.all_gather(values, "cp", axis=0, tiled=True)

    def scatter_tokens(values):
        return lax.psum_scatter(
            values.astype(low), "cp", scatter_dimension=0, tiled=True
        ).astype(jnp.float32)

    def head_columns(shard):
        rows = shard.shape[0]
        blocks = shard.reshape(rows, 2, num_heads // 2, head_width).transpose(0, 2, 1, 3)
        return take_columns(shard, blocks.reshape(rows, 1, num_heads, head_width))

    def unit_columns(shard):
        rows = shard.shape[0]
        return take_columns(
            shard, shard.reshape(rows, seq_devices, cp_devices, shard.shape[1] // (seq_devices * cp_devices))
        )

    gains = lax.all_gather(
        jnp.stack([norm1_gain, norm2_gain]), ("seq", "cp"), axis=1, tiled=True
    ).astype(jnp.float32)
    gain_one, gain_two = gains[0], gains[1]
    query_w, key_w, value_w = head_columns(w_query), head_columns(w_key), head_columns(w_value)
    gate_w, up_w = unit_columns(w_gate), unit_columns(w_up)
    down_w = lax.all_gather(w_down, "seq", axis=0, tiled=True)
    out_pair = lax.all_gather(w_out[None], "seq", axis=0, tiled=True)
    odd = cp_place % 2
    out_other = exchange_pair(jnp.where(odd == 0, out_pair[1], out_pair[0]), "cp", 1)
    out_own = jnp.where(odd == 0, out_pair[0], out_pair[1])
    out_w = jnp.where(
        odd == 0,
        jnp.concatenate([out_own, out_other], 0),
        jnp.concatenate([out_other, out_own], 0),
    )

    positions = row_positions(jnp.arange(seq_length, dtype=jnp.int32), strip_rows, cp_devices)
    token_pos = jnp.broadcast_to(positions[:, None], (seq_length, local_seqs)).reshape(group_tokens)
    inputs = layer_in.reshape(local_tokens, model_width).astype(jnp.float32)
    grad_local = cotangent.reshape(local_tokens, model_width)
    normed_one = gather_tokens(normed(inputs, gain_one).astype(low))
    grad_all = gather_tokens(grad_local)

    dot = functools.partial(jnp.dot, preferred_element_type=jnp.float32)
    query_low = rotate(dot(normed_one, query_w), token_pos, 1).astype(low)
    key_low = rotate(dot(normed_one, key_w), token_pos, 1).astype(low)
    value_low = dot(normed_one, value_w).astype(low)
    row_shape = (seq_length, local_seqs, head_width)
    query_rows, key_rows, value_rows = (
        query_low.reshape(row_shape),
        key_low.reshape(row_shape),
        value_low.reshape(row_shape),
    )
    mask = (
        (positions[None, :] <= positions[:, None])[None]
        & (positions[None, :] < valid_len[:, None])[:, None, :]
    ).astype(jnp.float32)

    def pairs(left, right):
        return jnp.einsum("qsd,ksd->sqk", left, right, preferred_element_type=jnp.float32)

    sig = jax.nn.sigmoid(pairs(query_rows, key_rows) * score_scale - score_shift)
    weights_low = (sig * mask).astype(low)
    attended = jnp.einsum(
        "sqk,ksd->qsd", weights_low, value_rows, preferred_element_type=jnp.float32
    ).astype(low).reshape(group_tokens, head_width)
    hidden_state = inputs + scatter_tokens(dot(attended, out_w))
    normed_two = gather_tokens(normed(hidden_state, gain_two).astype(low))
    gate_rows = dot(normed_two, gate_w)
    up_rows = dot(normed_two, up_w)
    hidden_units = swiglu(gate_rows, up_rows).astype(low)
    layer_out = (hidden_state + scatter_tokens(dot(hidden_units, down_w))).astype(low)

    grad_hidden = dot_right(grad_all, down_w)
    _, pull_swiglu = jax.vjp(swiglu, gate_rows, up_rows)
    grad_gate, grad_up = pull_swiglu(grad_hidden)
    grad_gate, grad_up = grad_gate.astype(low), grad_up.astype(low)
    grad_norm_two = scatter_tokens(dot_right(grad_gate, gate_w) + dot_right(grad_up, up_w))
    from_two, gain_two_term = norm_back(hidden_state, gain_two, grad_norm_two)
    grad_state = grad_local.astype(jnp.float32) + from_two
    branch_all = gather_tokens(grad_state.astype(low))
    grad_rows = dot_right(branch_all, out_w).astype(low).reshape(row_shape)
    grad_logits = (pairs(grad_rows, value_rows) * mask * (sig * (1.0 - sig))).astype(low)
    grad_value = jnp.einsum(
        "sqk,qsd->ksd", weights_low, grad_rows, preferred_element_type=jnp.float32
    ).astype(low).reshape(group_tokens, head_width)
    grad_query = (
        jnp.einsum("sqk,ksd->qsd", grad_logits, key_rows, preferred_element_type=jnp.float32)
        * score_scale
    ).reshape(group_tokens, head_width)
    grad_key = (
        jnp.einsum("sqk,qsd->ksd", grad_logits, query_rows, preferred_element_type=jnp.float32)
        * score_scale
    ).reshape(group_tokens, head_width)
    grad_query = rotate(grad_query, -token_pos, 1).astype(low)
    grad_key = rotate(grad_key, -token_pos, 1).astype(low)
    grad_norm_one = scatter_tokens(
        dot_right(grad_query, query_w) + dot_right(grad_key, key_w) + dot_right(grad_value, value_w)
    )
    from_one, gain_one_term = norm_back(inputs, gain_one, grad_norm_one)
    in_grad = grad_state + from_one

    def head_rows(grad):
        moved = give_rows(grad.astype(low), 1)
        rows = moved.shape[0]
        return (
            moved.reshape(rows, num_heads // 2, 2, head_width)
            .transpose(0, 2, 1, 3)
            .reshape(rows, model_width)
            .astype(jnp.float32)
        )

    def unit_rows(grad):
        moved = give_rows(grad.astype(low), seq_devices)
        return moved.reshape(moved.shape[0], -1).astype(jnp.float32)

    out_grad = dot_left(attended, branch_all).astype(low)
    out_grad = out_grad.reshape(2, head_width // 2, model_width)
    sent = exchange_pair(jnp.where(odd == 0, out_grad[1], out_grad[0]), "cp", 1)
    kept = jnp.where(odd == 0, out_grad[0], out_grad[1])
    out_grad = jnp.concatenate(
        [jnp.where(odd == 0, kept, sent), jnp.where(odd == 0, sent, kept)], 0
    )
    out_grad = lax.psum_scatter(out_grad, "seq", scatter_dimension=0, tiled=True)
    down_grad = lax.psum_scatter(
        dot_left(hidden_units, grad_all).astype(low), "seq", scatter_dimension=0, tiled=True
    )
    gain_terms = lax.psum_scatter(
        jnp.stack([gain_one_term, gain_two_term]), ("seq", "cp"), scatter_dimension=1, tiled=True
    )
    row_out = (local_rows, local_seqs, model_width)
    return (
        layer_out.reshape(row_out),
        in_grad.reshape(row_out),
        gain_terms[0],
        head_rows(dot_left(normed_one, grad_query)),
        head_rows(dot_left(normed_one, grad_key)),
        head_rows(dot_left(normed_one, grad_value)),
        out_grad.astype(jnp.float32),
        gain_terms[1],
        unit_rows(dot_left(normed_two, grad_gate)),
        unit_rows(dot_left(normed_two, grad_up)),
        down_grad.astype(jnp.float32),
    )


def solution(mesh):
    on_device = (
        move_tokens_step if mesh.shape["cp"] == HEADS and mesh.shape["seq"] == 2 else gather_weights_step
    )
    placed = (
        P("cp", "seq", None),
        P("seq"),
        P(("seq", "cp")),
        P(("seq", "cp"), None),
        P(("seq", "cp"), None),
        P(("seq", "cp"), None),
        P(("seq", "cp"), None),
        P(("seq", "cp")),
        P(("seq", "cp"), None),
        P(("seq", "cp"), None),
        P(("seq", "cp"), None),
        P("cp", "seq", None),
    )
    return jax.shard_map(
        on_device,
        mesh=mesh,
        in_specs=placed,
        out_specs=(
            P("cp", "seq", None),
            P("cp", "seq", None),
            P(("seq", "cp")),
            P(("seq", "cp"), None),
            P(("seq", "cp"), None),
            P(("seq", "cp"), None),
            P(("seq", "cp"), None),
            P(("seq", "cp")),
            P(("seq", "cp"), None),
            P(("seq", "cp"), None),
            P(("seq", "cp"), None),
        ),
        check_vma=False,
    )
```

```python
import functools
import math

import jax
import jax.numpy as jnp
from jax import lax
from jax.experimental import pallas as pl
from jax.experimental.pallas import tpu as pltpu
from jax.sharding import PartitionSpec as P

HEADS = 16


norm_eps = 1e-05
rope_base = 10000.0


def row_positions(indices, strip_rows, devices):
    owner_index = indices // (2 * strip_rows)
    within = indices % (2 * strip_rows)
    return jnp.where(
        within < strip_rows,
        owner_index * strip_rows + within,
        (2 * devices - 1 - owner_index) * strip_rows + within - strip_rows,
    )


def rotate(values, positions, num_heads):
    count_rows, model_width = values.shape
    head_width = model_width // num_heads
    half_width = head_width // 2
    freqs_table = rope_base ** (-2.0 * jnp.arange(half_width, dtype=jnp.float32) / head_width)
    angles = positions.astype(jnp.float32)[:, None] * freqs_table[None, :]
    cosine = jnp.cos(angles)[:, None, :]
    sine_table = jnp.sin(angles)[:, None, :]
    split_heads = values.reshape(count_rows, num_heads, head_width)
    former = split_heads[:, :, :half_width]
    latter = split_heads[:, :, half_width:]
    turned = jnp.concatenate(
        [former * cosine - latter * sine_table, latter * cosine + former * sine_table], axis=2
    )
    return turned.reshape(count_rows, model_width)


def norm_scale(values):
    return values * lax.rsqrt(jnp.mean(values * values, axis=-1, keepdims=True) + norm_eps)


def normed(values, gain_vector):
    return norm_scale(values) * gain_vector


def swiglu(gate_rows, up_rows):
    return jax.nn.silu(gate_rows) * up_rows


def dot_right(left, right):
    return lax.dot_general(
        left, right, (((1,), (1,)), ((), ())), preferred_element_type=jnp.float32
    )


def dot_left(left, right):
    return lax.dot_general(
        left, right, (((0,), (0,)), ((), ())), preferred_element_type=jnp.float32
    )


def split_blocks(array, block_rows):
    return array.reshape((array.shape[0] // block_rows, block_rows) + array.shape[1:])


def key_mask(query_pos, key_pos, valid_count):
    causal = key_pos[None, :] <= query_pos[:, None]
    live_keys = key_pos[None, :] < valid_count[:, None]
    return (causal[None, None, :, :] & live_keys[:, None, None, :]).astype(jnp.float32)


def scores_of(queries, key_rows, query_pos, key_pos, valid_count, score_shift):
    head_width = queries.shape[3]
    raw_scores = jnp.einsum(
        "qshd,kshd->shqk", queries, key_rows, preferred_element_type=jnp.float32
    )
    return (
        raw_scores * head_width ** (-0.5) - score_shift,
        key_mask(query_pos, key_pos, valid_count),
    )


def block_grads(queries, grad_rows, key_rows, values, query_pos, key_pos, valid_count, score_shift):
    logits, mask_table = scores_of(queries, key_rows, query_pos, key_pos, valid_count, score_shift)
    sigmoid_table = jax.nn.sigmoid(logits)
    weights_low = (sigmoid_table * mask_table).astype(jnp.bfloat16)
    grad_weights = jnp.einsum(
        "qshd,kshd->shqk", grad_rows, values, preferred_element_type=jnp.float32
    )
    grad_logits = (grad_weights * mask_table * (sigmoid_table * (1.0 - sigmoid_table))).astype(
        jnp.bfloat16
    )
    return (weights_low, grad_logits)


def make_norm_fold(normalized, pieces):
    gain_part = pieces[0].astype(jnp.float32)
    scaled = (normalized * gain_part).astype(jnp.bfloat16)
    totals = tuple(
        (
            jnp.dot(scaled, weight_piece, preferred_element_type=jnp.float32)
            for weight_piece in pieces[1:]
        )
    )
    return (gain_part,) + totals


def make_row_fold(left_rows, weight_piece):
    return jnp.dot(left_rows, weight_piece, preferred_element_type=jnp.float32)


def gather_weights_step(
    layer_in,
    valid_len,
    norm1_gain,
    w_query,
    w_key,
    w_value,
    w_out,
    norm2_gain,
    w_gate,
    w_up,
    w_down,
    cotangent,
):
    local_rows, local_seqs, model_width = layer_in.shape
    num_heads = HEADS
    head_width = model_width // num_heads
    strip_rows = local_rows // 2
    cp_devices = lax.axis_size("cp")
    cp_place = lax.axis_index("cp")
    seq_length = local_rows * cp_devices
    score_shift = math.log(seq_length)
    score_scale = head_width ** (-0.5)
    token_count = local_rows * local_seqs
    local_pos = row_positions(
        cp_place * local_rows + jnp.arange(local_rows, dtype=jnp.int32), strip_rows, cp_devices
    )
    token_pos = jnp.broadcast_to(local_pos[:, None], (local_rows, local_seqs)).reshape(token_count)
    every_pos = row_positions(jnp.arange(seq_length, dtype=jnp.int32), strip_rows, cp_devices)
    block_rows = math.gcd(seq_length, 512)
    head_shape = (local_rows, local_seqs, num_heads, head_width)
    row_shape = (local_rows, local_seqs, model_width)
    zero_heads = jnp.zeros(head_shape, jnp.float32)
    inputs = layer_in.reshape(token_count, model_width).astype(jnp.float32)
    input_norm = norm_scale(inputs)
    gain_one, query, key_proj, value = make_norm_fold(
        input_norm,
        (
            lax.all_gather(norm1_gain, ("seq", "cp"), axis=0, tiled=True),
            lax.all_gather(w_query, ("seq", "cp"), axis=0, tiled=True),
            lax.all_gather(w_key, ("seq", "cp"), axis=0, tiled=True),
            lax.all_gather(w_value, ("seq", "cp"), axis=0, tiled=True),
        ),
    )
    normed_one = (input_norm * gain_one).astype(jnp.bfloat16)
    query_low = rotate(query, token_pos, num_heads).astype(jnp.bfloat16)
    key_low = rotate(key_proj, token_pos, num_heads).astype(jnp.bfloat16)
    value_low = value.astype(jnp.bfloat16)
    query_heads = query_low.reshape(head_shape)
    key_local = key_low.reshape(row_shape)
    value_local = value_low.reshape(row_shape)
    key_piece = lax.all_gather(key_local, "cp", axis=0, tiled=True)
    value_piece = lax.all_gather(value_local, "cp", axis=0, tiled=True)
    piece_rows = key_piece.shape[0]
    piece_block = math.gcd(piece_rows, 512)
    piece_pos = row_positions(jnp.arange(piece_rows, dtype=jnp.int32), strip_rows, cp_devices)

    def scan_step(partial_sum, block_items):
        key_block, value_block, block_pos = block_items
        logits, mask_table = scores_of(
            query_heads,
            key_block.reshape(piece_block, local_seqs, num_heads, head_width),
            local_pos,
            block_pos,
            valid_len,
            score_shift,
        )
        weights_low = (jax.nn.sigmoid(logits) * mask_table).astype(jnp.bfloat16)
        added = jnp.einsum(
            "shqk,kshd->qshd",
            weights_low,
            value_block.reshape(piece_block, local_seqs, num_heads, head_width),
            preferred_element_type=jnp.float32,
        )
        return (partial_sum + added, None)

    result, _ = lax.scan(
        scan_step,
        zero_heads,
        (
            split_blocks(key_piece, piece_block),
            split_blocks(value_piece, piece_block),
            split_blocks(piece_pos, piece_block),
        ),
    )
    attended_low = result.reshape(token_count, model_width).astype(jnp.bfloat16)
    attn_branch = make_row_fold(
        attended_low, lax.all_gather(w_out, ("seq", "cp"), axis=0, tiled=True)
    )
    hidden_state = inputs + attn_branch
    hidden_norm = norm_scale(hidden_state)
    gain_two, gate_rows, up_rows = make_norm_fold(
        hidden_norm,
        (
            lax.all_gather(norm2_gain, ("seq", "cp"), axis=0, tiled=True),
            lax.all_gather(w_gate, ("seq", "cp"), axis=0, tiled=True),
            lax.all_gather(w_up, ("seq", "cp"), axis=0, tiled=True),
        ),
    )
    normed_two = (hidden_norm * gain_two).astype(jnp.bfloat16)
    hidden_units = swiglu(gate_rows, up_rows).astype(jnp.bfloat16)
    ff_branch = make_row_fold(
        hidden_units, lax.all_gather(w_down, ("seq", "cp"), axis=0, tiled=True)
    )
    layer_out = (hidden_state + ff_branch).astype(jnp.bfloat16).reshape(row_shape)
    grad_out = cotangent.reshape(token_count, model_width)
    gate_all, up_all, down_all = (
        lax.all_gather(w_gate, ("seq", "cp"), axis=0, tiled=True),
        lax.all_gather(w_up, ("seq", "cp"), axis=0, tiled=True),
        lax.all_gather(w_down, ("seq", "cp"), axis=0, tiled=True),
    )
    grad_hidden = dot_right(grad_out, down_all)
    _, pull_swiglu = jax.vjp(swiglu, gate_rows, up_rows)
    grad_gate, grad_up = pull_swiglu(grad_hidden)
    grad_gate_low = grad_gate.astype(jnp.bfloat16)
    grad_up_low = grad_up.astype(jnp.bfloat16)
    grad_norm_two = dot_right(grad_gate_low, gate_all) + dot_right(grad_up_low, up_all)
    _, pull_two = jax.vjp(normed, hidden_state, gain_two)
    grad_from_two, gain_two_term = pull_two(grad_norm_two)
    ff_grads = (
        lax.psum_scatter(gain_two_term, ("seq", "cp"), scatter_dimension=0, tiled=True),
        lax.psum_scatter(
            dot_left(normed_two, grad_gate_low), ("seq", "cp"), scatter_dimension=0, tiled=True
        ),
        lax.psum_scatter(
            dot_left(normed_two, grad_up_low), ("seq", "cp"), scatter_dimension=0, tiled=True
        ),
        lax.psum_scatter(
            dot_left(hidden_units, grad_out), ("seq", "cp"), scatter_dimension=0, tiled=True
        ),
    )
    grad_state = grad_out.astype(jnp.float32) + grad_from_two
    query_all, key_all, value_all, out_all = (
        lax.all_gather(w_query, ("seq", "cp"), axis=0, tiled=True),
        lax.all_gather(w_key, ("seq", "cp"), axis=0, tiled=True),
        lax.all_gather(w_value, ("seq", "cp"), axis=0, tiled=True),
        lax.all_gather(w_out, ("seq", "cp"), axis=0, tiled=True),
    )
    grad_branch_low = grad_state.astype(jnp.bfloat16)
    grad_attended_low = dot_right(grad_branch_low, out_all).astype(jnp.bfloat16)
    grad_heads = grad_attended_low.reshape(head_shape)
    key_heads_local = key_local.reshape(head_shape)
    value_heads_local = value_local.reshape(head_shape)
    keys_every, values_every, queries_every, grads_every = (
        lax.all_gather(key_local, "cp", axis=0, tiled=True),
        lax.all_gather(value_local, "cp", axis=0, tiled=True),
        lax.all_gather(query_low.reshape(row_shape), "cp", axis=0, tiled=True),
        lax.all_gather(grad_attended_low.reshape(row_shape), "cp", axis=0, tiled=True),
    )

    def key_step(partial_sums, block_items):
        query_block, grad_block_rows, block_pos = block_items
        query_part = query_block.reshape(block_rows, local_seqs, num_heads, head_width)
        grad_part = grad_block_rows.reshape(block_rows, local_seqs, num_heads, head_width)
        weights_low, grad_logits = block_grads(
            query_part,
            grad_part,
            key_heads_local,
            value_heads_local,
            block_pos,
            local_pos,
            valid_len,
            score_shift,
        )
        key_added = jnp.einsum(
            "shqk,qshd->kshd", grad_logits, query_part, preferred_element_type=jnp.float32
        )
        value_added = jnp.einsum(
            "shqk,qshd->kshd", weights_low, grad_part, preferred_element_type=jnp.float32
        )
        return ((partial_sums[0] + key_added, partial_sums[1] + value_added), None)

    (key_sum, value_sum), _ = lax.scan(
        key_step,
        (zero_heads, zero_heads),
        (
            split_blocks(queries_every, block_rows),
            split_blocks(grads_every, block_rows),
            split_blocks(every_pos, block_rows),
        ),
    )
    grad_key_rot = key_sum.reshape(token_count, model_width) * score_scale
    grad_value_sum = value_sum.reshape(token_count, model_width)

    def query_step(partial_sum, block_items):
        key_block, value_block, block_pos = block_items
        key_heads = key_block.reshape(block_rows, local_seqs, num_heads, head_width)
        _, grad_logits = block_grads(
            query_heads,
            grad_heads,
            key_heads,
            value_block.reshape(block_rows, local_seqs, num_heads, head_width),
            local_pos,
            block_pos,
            valid_len,
            score_shift,
        )
        added = jnp.einsum(
            "shqk,kshd->qshd", grad_logits, key_heads, preferred_element_type=jnp.float32
        )
        return (partial_sum + added, None)

    query_sum, _ = lax.scan(
        query_step,
        zero_heads,
        (
            split_blocks(keys_every, block_rows),
            split_blocks(values_every, block_rows),
            split_blocks(every_pos, block_rows),
        ),
    )
    grad_query_rot = query_sum.reshape(token_count, model_width) * score_scale
    grad_query_low = rotate(grad_query_rot, -token_pos, num_heads).astype(jnp.bfloat16)
    grad_key_low = rotate(grad_key_rot, -token_pos, num_heads).astype(jnp.bfloat16)
    grad_value_low = grad_value_sum.astype(jnp.bfloat16)
    grad_norm_one = (
        dot_right(grad_query_low, query_all)
        + dot_right(grad_key_low, key_all)
        + dot_right(grad_value_low, value_all)
    )
    _, pull_one = jax.vjp(normed, inputs, gain_one)
    grad_from_one, gain_one_term = pull_one(grad_norm_one)
    in_grad = (grad_state + grad_from_one).reshape(row_shape)
    attn_grads = (
        lax.psum_scatter(gain_one_term, ("seq", "cp"), scatter_dimension=0, tiled=True),
        lax.psum_scatter(
            dot_left(normed_one, grad_query_low), ("seq", "cp"), scatter_dimension=0, tiled=True
        ),
        lax.psum_scatter(
            dot_left(normed_one, grad_key_low), ("seq", "cp"), scatter_dimension=0, tiled=True
        ),
        lax.psum_scatter(
            dot_left(normed_one, grad_value_low), ("seq", "cp"), scatter_dimension=0, tiled=True
        ),
        lax.psum_scatter(
            dot_left(attended_low, grad_branch_low), ("seq", "cp"), scatter_dimension=0, tiled=True
        ),
    )
    return (
        layer_out,
        in_grad,
        attn_grads[0],
        attn_grads[1],
        attn_grads[2],
        attn_grads[3],
        attn_grads[4],
        ff_grads[0],
        ff_grads[1],
        ff_grads[2],
        ff_grads[3],
    )


MESH = pl.DeviceIdType.MESH


class Place:
    def __init__(self):
        self.s = lax.axis_index("seq")
        self.c = lax.axis_index("cp")
        self.z = self.c // 4
        self.y = (self.c // 2) % 2
        self.k = self.c % 2

    def at(self, z, y, k):
        return z * 4 + y * 2 + k

    def device(self, place):
        return (self.s, place)


def pick(z, table):
    value = jnp.int32(table[0])
    for index in range(1, 4):
        value = jnp.where(z == index, jnp.int32(table[index]), value)
    return value


NEAREST = ((1, 0, 1, 2), (2, 2, 3, 1), (3, 3, 0, 0))
FARTHEST = ((3, 3, 0, 0), (2, 2, 3, 1), (1, 0, 1, 2))


def remote(source, target, send, recv, device):
    return pltpu.make_async_remote_copy(
        src_ref=source, dst_ref=target, send_sem=send, recv_sem=recv,
        device_id=device, device_id_type=MESH,
    )


def greet(me, x_too=False):
    barrier = pltpu.get_barrier_semaphore()

    def hail(device):
        pl.semaphore_signal(barrier, inc=1, device_id=device, device_id_type=MESH)

    hail((me.s, me.at(me.z, 1 - me.y, me.k)))
    hail((me.s, me.at(me.z, me.y, 1 - me.k)))

    @pl.when(me.z < 3)
    def _():
        hail((me.s, me.at(me.z + 1, me.y, me.k)))

    @pl.when(me.z > 0)
    def _():
        hail((me.s, me.at(me.z - 1, me.y, me.k)))

    ends = (me.z == 0).astype(jnp.int32) + (me.z == 3).astype(jnp.int32)
    if x_too:
        hail((1 - me.s, me.c))
    pl.semaphore_wait(barrier, 4 - ends + (1 if x_too else 0))


class Gather:
    sems = (5, 4, 8, 16)

    def __init__(self, me, held, z_sem, y_sem, k_sem, recv):
        self.me, self.held = me, held
        self.z_sem, self.y_sem, self.k_sem, self.recv = z_sem, y_sem, k_sem, recv

    def copy(self, place, sem, device):
        block = self.held.at[place]
        return remote(block, block, sem, self.recv.at[place], device)

    def arrived(self, place):
        me = self.me
        self.copy(place, self.k_sem.at[0], me.device(me.c)).wait_recv()

    def up(self, place, index):
        me = self.me
        return self.copy(place, self.z_sem.at[index], me.device(jnp.minimum(me.c + 4, 12 + me.c % 4)))

    def down(self, place, index):
        me = self.me
        return self.copy(place, self.z_sem.at[index], me.device(jnp.maximum(me.c - 4, me.c % 4)))

    def across(self, place, index):
        me = self.me
        return self.copy(place, self.y_sem.at[index], me.device(me.at(me.z, 1 - me.y, me.k)))

    def partner(self, place, index):
        me = self.me
        return self.copy(place, self.k_sem.at[index], me.device(me.at(me.z, me.y, 1 - me.k)))

    def line(self, index):
        return self.me.z if index == 0 else pick(self.me.z, NEAREST[index - 1])

    def send_line(self, index, wait=False):
        me, z = self.me, self.line(index)
        place = me.at(z, me.y, me.k)

        def go(copy):
            copy.wait_send() if wait else copy.start()

        if index == 0:
            @pl.when(me.z < 3)
            def _():
                go(self.up(place, 0))

            @pl.when(me.z > 0)
            def _():
                go(self.down(place, 4))
        else:
            @pl.when((z < me.z) & (me.z < 3))
            def _():
                go(self.up(place, index))

            @pl.when((z > me.z) & (me.z > 0))
            def _():
                go(self.down(place, index))
        go(self.across(place, index))
        go(self.partner(place, index))

    def run(self, consume):
        me = self.me
        self.send_line(0)
        consume(me.c)
        other = me.at(me.z, me.y, 1 - me.k)
        self.arrived(other)
        consume(other)
        for index in range(4):
            if index < 3:
                near = me.at(self.line(index + 1), me.y, me.k)
                self.arrived(near)
                self.send_line(index + 1)
            far = me.at(self.line(index), 1 - me.y, me.k)
            self.arrived(far)
            self.partner(far, 4 + index).start()
            if index < 3:
                consume(near)
            consume(far)
            if index < 3:
                near = me.at(self.line(index + 1), me.y, 1 - me.k)
                self.arrived(near)
                consume(near)
            far = me.at(self.line(index), 1 - me.y, 1 - me.k)
            self.arrived(far)
            consume(far)

    def finish(self):
        me = self.me
        for index in range(4):
            self.send_line(index, wait=True)
            far = me.at(self.line(index), 1 - me.y, me.k)
            self.partner(far, 4 + index).wait_send()


class Scatter:
    sems = (8, 8, 4, 4, 3, 3, 3)

    def __init__(self, me, k_out, k_in, y_out, y_in, z_out, z_in, ks, kr, ys, yr, zs, zl, zr):
        self.me = me
        self.k_out, self.k_in, self.y_out, self.y_in = k_out, k_in, y_out, y_in
        self.z_out, self.z_in = z_out, z_in
        self.ks, self.kr, self.ys, self.yr, self.zs, self.zl, self.zr = ks, kr, ys, yr, zs, zl, zr

    def partner(self, slot):
        me = self.me
        return remote(self.k_out.at[slot], self.k_in.at[slot], self.ks.at[slot], self.kr.at[slot],
                      me.device(me.at(me.z, me.y, 1 - me.k)))

    def across(self, z, index):
        me = self.me
        return remote(self.y_out.at[index], self.y_in.at[z], self.ys.at[index], self.yr.at[z],
                      me.device(me.at(me.z, 1 - me.y, me.k)))

    def up(self, z, index):
        me = self.me
        return remote(self.z_out.at[index], self.z_in.at[z], self.zs.at[index], self.zl.at[z],
                      me.device(jnp.minimum(me.c + 4, 12 + me.c % 4)))

    def down(self, z, index):
        me = self.me
        return remote(self.z_out.at[index], self.z_in.at[4 + z], self.zs.at[index], self.zr.at[z],
                      me.device(jnp.maximum(me.c - 4, me.c % 4)))

    def line(self, index):
        return self.me.z if index == 3 else pick(self.me.z, FARTHEST[index])

    def fill(self, produce, place, target, *added):
        part = 512

        @pl.loop(0, target.shape[-1] // part)
        def _(index):
            columns = pl.ds(pl.multiple_of(index * part, part), part)
            value = produce(place, columns)
            for block in added:
                value = value + block[:, columns].astype(jnp.float32)
            target[:, columns] = value.astype(target.dtype)

    def run(self, prepare, produce, finish):
        me = self.me
        f32 = jnp.float32
        for index in range(4):
            z = self.line(index)
            if prepare is not None:
                prepare(me.at(z, 1 - me.y, 1 - me.k))
            self.fill(produce, me.at(z, 1 - me.y, 1 - me.k), self.k_out.at[index])
            self.partner(index).start()
            if prepare is not None:
                prepare(me.at(z, 1 - me.y, me.k))
            self.partner(index).wait_recv()
            self.fill(produce, me.at(z, 1 - me.y, me.k), self.y_out.at[index], self.k_in.at[index])
            self.across(z, index).start()
        for index in range(4):
            z = self.line(index)
            slot = 4 + index
            if prepare is not None:
                prepare(me.at(z, me.y, 1 - me.k))
            self.fill(produce, me.at(z, me.y, 1 - me.k), self.k_out.at[slot])
            self.partner(slot).start()
        for index in range(4):
            z = self.line(index)
            slot = 4 + index
            if prepare is not None:
                prepare(me.at(z, me.y, me.k))
            self.partner(slot).wait_recv()
            self.across(z, index).wait_recv()
            self.fill(produce, me.at(z, me.y, me.k), self.total, self.k_in.at[slot], self.y_in.at[z])
            if index < 3:

                @pl.when((z > me.z) & (me.z > 0))
                def _():
                    self.up(z, index).wait_recv()
                    self.total[...] += self.z_in[z].astype(f32)

                @pl.when((z < me.z) & (me.z < 3))
                def _():
                    self.down(z, index).wait_recv()
                    self.total[...] += self.z_in[4 + z].astype(f32)

                self.z_out[index] = self.total[...].astype(jnp.bfloat16)

                @pl.when(z > me.z)
                def _():
                    self.up(z, index).start()

                @pl.when(z < me.z)
                def _():
                    self.down(z, index).start()
            else:

                @pl.when(me.z > 0)
                def _():
                    self.up(z, 0).wait_recv()
                    self.total[...] += self.z_in[z].astype(f32)

                @pl.when(me.z < 3)
                def _():
                    self.down(z, 0).wait_recv()
                    self.total[...] += self.z_in[4 + z].astype(f32)

                finish(self.total)

    def drain(self):
        me = self.me
        for slot in range(8):
            self.partner(slot).wait_send()
        for index in range(4):
            self.across(self.line(index), index).wait_send()
        for index in range(3):
            z = self.line(index)

            @pl.when(z > me.z)
            def _():
                self.up(z, index).wait_send()

            @pl.when(z < me.z)
            def _():
                self.down(z, index).wait_send()


DMA = pltpu.SemaphoreType.DMA
LOW = jnp.bfloat16
F32 = jnp.float32
ANYWHERE = pl.BlockSpec(memory_space=pl.ANY)
IN_VMEM = pl.BlockSpec(memory_space=pltpu.VMEM)
IN_SMEM = pl.BlockSpec(memory_space=pltpu.SMEM)


def params(collective_id):
    return pltpu.CompilerParams(
        collective_id=collective_id, has_side_effects=True, vmem_limit_bytes=60 << 20
    )


def greet_plane(me):
    barrier = pltpu.get_barrier_semaphore()
    for step in range(1, 16):
        place = (me.c + step) % 16
        pl.semaphore_signal(barrier, inc=1, device_id=(me.s, place), device_id_type=MESH)
    pl.semaphore_signal(barrier, inc=1, device_id=(1 - me.s, me.c), device_id_type=MESH)
    pl.semaphore_wait(barrier, 16)


def turn(me, step):
    dz, dy, dk = step // 4, (step // 2) % 2, step % 2
    to = me.at((me.z + dz) % 4, (me.y + dy) % 2, (me.k + dk) % 2)
    source = me.at((me.z + 4 - dz) % 4, (me.y + dy) % 2, (me.k + dk) % 2)
    return to, source


def spread_kernel(unit, grad, qkv, gate_up, down, units, grads, qkv_all, gate_up_all, down_all, *sems):
    (uz, uy, uk, ur, gz, gy, gk, gr, qs, qr, qxs, qxr, ps, pr, pxs, pxr, ds, dr, local) = sems
    me = Place()
    own = [
        pltpu.make_async_copy(unit, units.at[me.c], local.at[0]),
        pltpu.make_async_copy(grad, grads.at[me.c], local.at[1]),
        pltpu.make_async_copy(qkv.at[me.c], qkv_all.at[me.s, me.c], local.at[2]),
        pltpu.make_async_copy(gate_up.at[me.c], gate_up_all.at[me.s, me.c], local.at[3]),
        pltpu.make_async_copy(down, down_all.at[me.s], local.at[4]),
    ]
    for copy in own:
        copy.start()
    greet_plane(me)
    for copy in own:
        copy.wait()
    over = (1 - me.s, me.c)
    gathers = [Gather(me, units, uz, uy, uk, ur), Gather(me, grads, gz, gy, gk, gr)]
    moves = [
        (qkv, qkv_all, qs, qr, qxs, qxr),
        (gate_up, gate_up_all, ps, pr, pxs, pxr),
    ]
    down_copy = remote(down, down_all.at[me.s], ds, dr, over)

    def send(move, step):
        to, _ = turn(me, step)
        mine, everyone, s_sem, r_sem, _, _ = move
        return remote(mine.at[to], everyone.at[me.s, me.c], s_sem.at[step], r_sem.at[me.c], (me.s, to))

    def forward(move, source):
        _, everyone, _, _, s_sem, r_sem = move
        block = everyone.at[me.s, source]
        return remote(block, block, s_sem.at[source], r_sem.at[source], over)

    for gather in gathers:
        gather.send_line(0)
    for move in moves:
        for step in range(1, 16):
            send(move, step).start()
        forward(move, me.c).start()
    down_copy.start()

    def pass_on(step):
        _, source = turn(me, step)
        for move in moves:
            _, everyone, s_sem, r_sem, _, _ = move
            remote(move[0].at[0], everyone.at[me.s, source], s_sem.at[step], r_sem.at[source], over).wait_recv()
            forward(move, source).start()

    steps = iter(range(1, 16))
    for gather in gathers:
        gather.arrived(me.at(me.z, me.y, 1 - me.k))
    for index in range(4):
        for gather in gathers:
            if index < 3:
                near = me.at(gather.line(index + 1), me.y, me.k)
                gather.arrived(near)
                gather.send_line(index + 1)
            far = me.at(gather.line(index), 1 - me.y, me.k)
            gather.arrived(far)
            gather.partner(far, 4 + index).start()
        for _ in range(4):
            step = next(steps, None)
            if step is not None:
                pass_on(step)
    for gather in gathers:
        for index in range(4):
            if index < 3:
                gather.arrived(me.at(gather.line(index + 1), me.y, 1 - me.k))
            gather.arrived(me.at(gather.line(index), 1 - me.y, 1 - me.k))
        gather.finish()
    for move in moves:
        for step in range(1, 16):
            send(move, step).wait_send()
        for source in range(16):
            copy = forward(move, source)
            copy.wait_send()
            copy.wait_recv()
    down_copy.wait()


def spread(unit, grad, qkv, gate_up, down):
    def shape(lead, array, tail):
        return jax.ShapeDtypeStruct(lead + array.shape[tail:], array.dtype)

    sems = [DMA((n,)) for n in Gather.sems * 2] + [DMA((16,))] * 8 + [DMA, DMA, DMA((5,))]
    return pl.pallas_call(
        spread_kernel,
        out_shape=[
            shape((16,), unit, 0),
            shape((16,), grad, 0),
            shape((2, 16), qkv, 1),
            shape((2, 16), gate_up, 1),
            shape((2,), down, 0),
        ],
        in_specs=[ANYWHERE] * 5,
        out_specs=[ANYWHERE] * 5,
        scratch_shapes=sems,
        compiler_params=params(0),
    )(unit, grad, qkv, gate_up, down)


SCATTER_SEMS = [DMA((n,)) for n in (8, 8, 4, 4, 3, 4, 4)]


def scatter_scratch(rows, width):
    return [pltpu.VMEM((n, rows, width), LOW) for n in (8, 8, 4, 4, 3, 8)] + SCATTER_SEMS + [
        pltpu.VMEM((rows, width), F32)
    ]


def row_place(place, row, strip):
    return jnp.where(row < strip, place * strip + row, (31 - place) * strip + row - strip)


def key_places(strip):
    index = lax.broadcasted_iota(jnp.int32, (1, 32 * strip), 1)
    return row_place(index // (2 * strip), index % (2 * strip), strip)


def query_places(place, strip):
    index = lax.broadcasted_iota(jnp.int32, (2 * strip, 1), 0)
    return row_place(place, index, strip)


def attend_kernel(shift, valid, query, key, value, out_w, total_out, attended, *scratch):
    me = Place()
    greet(me)
    scatter = Scatter(me, *scratch[:13])
    scatter.total = scratch[13]
    rows, width = query.shape[2], query.shape[3]
    strip = rows // 2
    length = rows * 16
    scale = width ** (-0.5)

    def prepare(place):
        where = query_places(place, strip)
        keys_at = key_places(strip)
        for seq in range(2):
            keys = key[:, seq].reshape(length, width)
            values = value[:, seq].reshape(length, width)
            logits = dot_right(query[place, seq], keys) * scale - shift
            live = (keys_at <= where) & (keys_at < valid[seq])
            weights = jnp.where(live, jax.nn.sigmoid(logits), 0.0).astype(LOW)
            attended[place, pl.ds(seq * rows, rows)] = jnp.dot(
                weights, values, preferred_element_type=F32
            ).astype(LOW)

    def produce(place, columns):
        return jnp.dot(attended[place], out_w[:, columns], preferred_element_type=F32)

    def finish(total):
        total_out[...] = total[...]

    scatter.run(prepare, produce, finish)
    scatter.drain()


def attend(shift, valid, query, key, value, out_w):
    rows, width = query.shape[2:]
    tokens, model = 2 * rows, out_w.shape[1]
    return pl.pallas_call(
        functools.partial(attend_kernel, shift),
        out_shape=[
            jax.ShapeDtypeStruct((tokens, model), F32),
            jax.ShapeDtypeStruct((16, tokens, width), LOW),
        ],
        in_specs=[IN_SMEM] + [IN_VMEM] * 4,
        out_specs=[IN_VMEM] * 2,
        scratch_shapes=scatter_scratch(tokens, model),
        compiler_params=params(1),
    )(valid, query, key, value, out_w)


def mlp_kernel(unit, grads, gate_up, down, total_out, units, hidden, grad_gate_up, grads_here, *scratch):
    me = Place()
    gather = Gather(me, units, *scratch[14:18])
    local = scratch[-1]
    bring = pltpu.make_async_copy(grads, grads_here, local.at[0])
    own = pltpu.make_async_copy(unit, units.at[me.c], local.at[1])
    bring.start()
    own.start()
    greet(me)
    own.wait()
    hold = {"first": True}
    width = down.shape[0]

    def consume(place):
        if hold["first"]:
            bring.wait()
            hold["first"] = False
        part = 256

        @pl.loop(0, width // part)
        def _(index):
            gate_at = pl.ds(pl.multiple_of(index * part, part), part)
            up_at = pl.ds(pl.multiple_of(width + index * part, part), part)
            rows = units[place]
            gate = jnp.dot(rows, gate_up[:, gate_at], preferred_element_type=F32)
            up = jnp.dot(rows, gate_up[:, up_at], preferred_element_type=F32)
            grad = dot_right(grads_here[place], down[gate_at, :])
            sig = jax.nn.sigmoid(gate)
            silu = gate * sig
            hidden[place, :, gate_at] = (silu * up).astype(LOW)
            grad_gate_up[place, :, gate_at] = (grad * up * (sig * (1.0 + gate * (1.0 - sig)))).astype(LOW)
            grad_gate_up[place, :, up_at] = (grad * silu).astype(LOW)

    gather.run(consume)
    scatter = Scatter(me, *scratch[:13])
    scatter.total = scratch[13]

    def produce(place, columns):
        return dot_right(grad_gate_up[place], gate_up[columns, :])

    def finish(total):
        total_out[...] = total[...]

    scatter.run(None, produce, finish)
    scatter.drain()
    gather.finish()


def mlp(unit, grads, gate_up, down):
    tokens, model = unit.shape
    width = down.shape[0]
    return pl.pallas_call(
        mlp_kernel,
        out_shape=[
            jax.ShapeDtypeStruct((tokens, model), F32),
            jax.ShapeDtypeStruct((16, tokens, model), LOW),
            jax.ShapeDtypeStruct((16, tokens, width), LOW),
            jax.ShapeDtypeStruct((16, tokens, 2 * width), LOW),
        ],
        in_specs=[ANYWHERE] * 2 + [IN_VMEM] * 2,
        out_specs=[IN_VMEM] * 4,
        scratch_shapes=[pltpu.VMEM((16, tokens, model), LOW)]
        + scatter_scratch(tokens, model)
        + [DMA((n,)) for n in Gather.sems]
        + [DMA((2,))],
        compiler_params=params(2),
    )(unit, grads, gate_up, down)


def rows_out_kernel(hidden, down, total_out, *scratch):
    me = Place()
    greet(me)
    scatter = Scatter(me, *scratch[:13])
    scatter.total = scratch[13]

    def produce(place, columns):
        return jnp.dot(hidden[place], down[:, columns], preferred_element_type=F32)

    def finish(total):
        total_out[...] = total[...]

    scatter.run(None, produce, finish)
    scatter.drain()


def rows_out(hidden, down):
    tokens, model = hidden.shape[1], down.shape[1]
    return pl.pallas_call(
        rows_out_kernel,
        out_shape=jax.ShapeDtypeStruct((tokens, model), F32),
        in_specs=[IN_VMEM] * 2,
        out_specs=IN_VMEM,
        scratch_shapes=scatter_scratch(tokens, model),
        compiler_params=params(3),
    )(hidden, down)


def attend_back_kernel(
    shift, valid, branch, query, key, value, out_w, qkv_w, cosine, sine, total_out, branches, grad_qkv,
    key_sum, value_sum, *scratch
):
    me = Place()
    gather = Gather(me, branches, *scratch[14:18])
    own = pltpu.make_async_copy(branch, branches.at[me.c], scratch[-1])
    own.start()
    greet(me)
    own.wait()
    rows, width = query.shape[2], query.shape[3]
    strip = rows // 2
    length = rows * 16
    scale = width ** (-0.5)
    key_sum[...] = jnp.zeros_like(key_sum)
    value_sum[...] = jnp.zeros_like(value_sum)

    def unturn(values, place):
        swapped = pltpu.roll(values, width // 2, axis=1)
        return values * cosine[place] + swapped * sine[place]

    def consume(place):
        where = query_places(place, strip)
        keys_at = key_places(strip)
        for seq in range(2):
            here = pl.ds(seq * rows, rows)
            grad = dot_right(branches[place, here], out_w[...]).astype(LOW)
            keys = key[:, seq].reshape(length, width)
            values = value[:, seq].reshape(length, width)
            queries = query[place, seq]
            logits = dot_right(queries, keys) * scale - shift
            live = (keys_at <= where) & (keys_at < valid[seq])
            sig = jnp.where(live, jax.nn.sigmoid(logits), 0.0)
            weights = sig.astype(LOW)
            grad_logits = (dot_right(grad, values) * (sig * (1.0 - sig))).astype(LOW)
            turned = jnp.dot(grad_logits, keys, preferred_element_type=F32) * scale
            swapped = pltpu.roll(turned, width // 2, axis=1)
            grad_qkv[place, here, 0:width] = (
                turned * cosine[place] + swapped * sine[place]
            ).astype(LOW)
            key_sum[seq] += dot_left(grad_logits, queries)
            value_sum[seq] += dot_left(weights, grad)

    gather.run(consume)
    for seq in range(2):

        @pl.loop(0, 16)
        def _(place):
            at = pl.ds(pl.multiple_of(place * rows, rows), rows)
            here = pl.ds(seq * rows, rows)
            turned = key_sum[seq, at] * scale
            swapped = pltpu.roll(turned, width // 2, axis=1)
            grad_qkv[place, here, width : 2 * width] = (
                turned * cosine[place] + swapped * sine[place]
            ).astype(LOW)
            grad_qkv[place, here, 2 * width :] = value_sum[seq, at].astype(LOW)

    scatter = Scatter(me, *scratch[:13])
    scatter.total = scratch[13]

    def produce(place, columns):
        return dot_right(grad_qkv[place], qkv_w[columns, :])

    def finish(total):
        total_out[...] = total[...]

    scatter.run(None, produce, finish)
    scatter.drain()
    gather.finish()


def attend_back(shift, valid, branch, query, key, value, out_w, qkv_w, cosine, sine):
    tokens, model = branch.shape
    rows, width = query.shape[2:]
    return pl.pallas_call(
        functools.partial(attend_back_kernel, shift),
        out_shape=[
            jax.ShapeDtypeStruct((tokens, model), F32),
            jax.ShapeDtypeStruct((16, tokens, model), LOW),
            jax.ShapeDtypeStruct((16, tokens, 3 * width), LOW),
        ],
        in_specs=[IN_SMEM, ANYWHERE] + [IN_VMEM] * 7,
        out_specs=[IN_VMEM] * 3,
        scratch_shapes=[pltpu.VMEM((2, 16 * rows, width), F32)] * 2
        + scatter_scratch(tokens, model)
        + [DMA((n,)) for n in Gather.sems]
        + [DMA],
        compiler_params=params(4),
    )(valid, branch, query, key, value, out_w, qkv_w, cosine, sine)


def return_kernel(qkv, gate_up, down, out_pair, qkv_back, gate_up_back, down_back, out_back, *scratch):
    (qx, qsum, px, psum, dx, ox, qxs, qxr, qs, qr, pxs, pxr, ps, pr, ds, dr, os, ow) = scratch
    me = Place()
    greet_plane(me)
    over = (1 - me.s, me.c)
    moves = [
        (qkv, qx, qsum, qkv_back, qxs, qxr, qs, qr),
        (gate_up, px, psum, gate_up_back, pxs, pxr, ps, pr),
    ]
    down_copy = remote(down.at[1 - me.s], dx, ds, dr, over)
    out_copy = remote(out_pair.at[1 - me.s], ox, os, ow, over)

    def cross(move, place):
        return remote(move[0].at[1 - me.s, place], move[1].at[place], move[4].at[place], move[5].at[place], over)

    def send(move, step):
        to, _ = turn(me, step)
        return remote(move[2].at[to], move[3].at[me.c], move[6].at[step], move[7].at[me.c], (me.s, to))

    for step in range(1, 16):
        for move in moves:
            cross(move, turn(me, step)[0]).start()
    for move in moves:
        cross(move, me.c).start()
    out_copy.start()
    down_copy.start()
    for step in range(1, 16):
        to, _ = turn(me, step)
        for move in moves:
            cross(move, to).wait_recv()
            move[2][to] = (move[0][me.s, to].astype(F32) + move[1][to].astype(F32)).astype(LOW)
            send(move, step).start()
    for move in moves:
        cross(move, me.c).wait_recv()
        move[3][me.c] = (move[0][me.s, me.c].astype(F32) + move[1][me.c].astype(F32)).astype(LOW)
    out_copy.wait_recv()
    out_back[...] = out_pair[me.s].astype(F32) + ox[...].astype(F32)
    down_copy.wait_recv()
    down_back[...] = down[me.s].astype(F32) + dx[...].astype(F32)
    for move in moves:
        for step in range(1, 16):
            to, source = turn(me, step)
            remote(move[2].at[0], move[3].at[source], move[6].at[step], move[7].at[source], over).wait_recv()
            send(move, step).wait_send()
            cross(move, to).wait_send()
        cross(move, me.c).wait_send()
    out_copy.wait_send()
    down_copy.wait_send()


def give_back(qkv, gate_up, down, out_pair):
    def like(array, lead, tail, kind=LOW):
        return lead + array.shape[tail:]

    blocks = [pltpu.VMEM(array.shape[1:], LOW) for array in (qkv, qkv, gate_up, gate_up, down, out_pair)]
    return pl.pallas_call(
        return_kernel,
        out_shape=[
            jax.ShapeDtypeStruct(qkv.shape[1:], LOW),
            jax.ShapeDtypeStruct(gate_up.shape[1:], LOW),
            jax.ShapeDtypeStruct(down.shape[1:], F32),
            jax.ShapeDtypeStruct(out_pair.shape[1:], F32),
        ],
        in_specs=[IN_VMEM] * 4,
        out_specs=[IN_VMEM] * 4,
        scratch_shapes=blocks + [DMA((16,))] * 8 + [DMA] * 4,
        compiler_params=params(5),
    )(qkv, gate_up, down, out_pair)


def exchange_pair(values, axis, flip):
    size = lax.axis_size(axis)
    return lax.ppermute(values, axis, [(place, place ^ flip) for place in range(size)])


def norm_back(values, scale, weighted):
    inner = jnp.mean(values * weighted, axis=-1, keepdims=True)
    return scale * weighted - values * (scale * scale * scale * inner)


def scale_of(values):
    return lax.rsqrt(jnp.mean(values * values, axis=-1, keepdims=True) + norm_eps)


def move_tokens_step(
    layer_in,
    valid_len,
    norm1_gain,
    w_query,
    w_key,
    w_value,
    w_out,
    norm2_gain,
    w_gate,
    w_up,
    w_down,
    cotangent,
):
    local_rows, local_seqs, model = layer_in.shape
    strip = local_rows // 2
    width = model // HEADS
    cp_devices = 16
    tokens = local_rows * local_seqs
    every = cp_devices * tokens
    shift = math.log(cp_devices * local_rows)
    weight_rows = w_gate.shape[0]
    gain_one = norm1_gain.astype(F32)[:, None]
    gain_two = norm2_gain.astype(F32)[:, None]

    def by_seq(values):
        return values.transpose(1, 0, 2).reshape(tokens, model)

    def by_row(values):
        return values.reshape(local_seqs, local_rows, model).transpose(1, 0, 2)

    def head_blocks(weight):
        scaled = (weight.astype(F32) * gain_one).astype(LOW)
        blocks = scaled.reshape(weight_rows, 2, HEADS // 2, width).transpose(2, 1, 0, 3)
        return blocks.reshape(HEADS, weight_rows, width)

    def unit_blocks(weight):
        scaled = (weight.astype(F32) * gain_two).astype(LOW)
        blocks = scaled.reshape(weight_rows, 2, cp_devices, -1).transpose(2, 0, 1, 3)
        return blocks.reshape(cp_devices, weight_rows, -1)

    qkv_blocks = jnp.concatenate([head_blocks(w) for w in (w_query, w_key, w_value)], axis=2)
    gate_up_blocks = jnp.concatenate([unit_blocks(w) for w in (w_gate, w_up)], axis=2)
    out_pair = lax.all_gather(w_out[None], "seq", axis=0, tiled=True)
    odd = lax.axis_index("cp") % 2
    out_other = exchange_pair(jnp.where(odd == 0, out_pair[1], out_pair[0]), "cp", 1)
    out_own = jnp.where(odd == 0, out_pair[0], out_pair[1])
    out_w = jnp.where(
        odd == 0,
        jnp.concatenate([out_own, out_other], 0),
        jnp.concatenate([out_other, out_own], 0),
    )

    inputs = by_seq(layer_in).astype(F32)
    grad_local = by_seq(cotangent)
    scale_one = scale_of(inputs)
    units, grads, qkv_w, gate_up_w, down_w = spread(
        (inputs * scale_one).astype(LOW), grad_local, qkv_blocks, gate_up_blocks, w_down
    )
    qkv_w = qkv_w.reshape(model, 3 * width)
    gate_up_w = gate_up_w.reshape(model, -1)
    down_w = down_w.reshape(-1, model)

    freqs = rope_base ** (-2.0 * jnp.arange(width // 2, dtype=F32) / width)
    place_pos = row_positions(
        jnp.arange(cp_devices * local_rows, dtype=jnp.int32), strip, cp_devices
    ).reshape(cp_devices, local_rows)
    angles = place_pos.astype(F32)[:, :, None] * freqs
    cosine, sine = jnp.cos(angles), jnp.sin(angles)
    cosine = jnp.concatenate([cosine, cosine], axis=2)
    back_sine = jnp.concatenate([sine, -sine], axis=2)

    qkv = jnp.dot(units.reshape(every, model), qkv_w, preferred_element_type=F32)
    qkv = qkv.reshape(cp_devices, local_seqs, local_rows, 3 * width)

    def turned(values):
        halves = jnp.roll(values, width // 2, axis=3)
        return (values * cosine[:, None] - halves * back_sine[:, None]).astype(LOW)

    query = turned(qkv[..., :width])
    key = turned(qkv[..., width : 2 * width])
    value = qkv[..., 2 * width :].astype(LOW)
    branch, attended = attend(shift, valid_len, query, key, value, out_w)
    hidden_state = inputs + branch
    scale_two = scale_of(hidden_state)
    weighted_two, units_two, hidden, grad_gate_up = mlp(
        (hidden_state * scale_two).astype(LOW), grads, gate_up_w, down_w
    )
    grad_state = grad_local.astype(F32) + norm_back(hidden_state, scale_two, weighted_two)
    layer_out = (hidden_state + rows_out(hidden, down_w)).astype(LOW)
    weighted_one, branches, grad_qkv = attend_back(
        shift, valid_len, grad_state.astype(LOW), query, key, value, out_w, qkv_w, cosine, back_sine
    )
    in_grad = grad_state + norm_back(inputs, scale_one, weighted_one)

    def gradient(left, right):
        return dot_left(left.reshape(every, -1), right.reshape(every, -1)).astype(LOW)

    out_grad = gradient(attended, branches).reshape(2, width // 2, model)
    sent = exchange_pair(jnp.where(odd == 0, out_grad[1], out_grad[0]), "cp", 1)
    kept = jnp.where(odd == 0, out_grad[0], out_grad[1])
    out_grad = jnp.where(odd == 0, jnp.stack([kept, sent]), jnp.stack([sent, kept]))
    qkv_back, gate_up_back, down_back, out_back = give_back(
        gradient(units, grad_qkv).reshape(2, cp_devices, weight_rows, -1),
        gradient(units_two, grad_gate_up).reshape(2, cp_devices, weight_rows, -1),
        gradient(hidden, grads).reshape(2, -1, model),
        out_grad,
    )

    def head_rows(index):
        blocks = qkv_back[:, :, index * width : (index + 1) * width].astype(F32)
        blocks = blocks.reshape(HEADS // 2, 2, weight_rows, width).transpose(2, 1, 0, 3)
        return blocks.reshape(weight_rows, model)

    def unit_rows(index):
        half = gate_up_back.shape[2] // 2
        blocks = gate_up_back[:, :, index * half : (index + 1) * half].astype(F32)
        blocks = blocks.reshape(cp_devices, weight_rows, 2, -1).transpose(1, 2, 0, 3)
        return blocks.reshape(weight_rows, -1)

    def gain_grad(weights, grads):
        return sum(jnp.sum(w.astype(F32) * g, axis=1) for w, g in zip(weights, grads))

    heads = [head_rows(index) for index in range(3)]
    unit_grads = [unit_rows(index) for index in range(2)]
    return (
        by_row(layer_out),
        by_row(in_grad),
        gain_grad((w_query, w_key, w_value), heads),
        heads[0] * gain_one,
        heads[1] * gain_one,
        heads[2] * gain_one,
        out_back,
        gain_grad((w_gate, w_up), unit_grads),
        unit_grads[0] * gain_two,
        unit_grads[1] * gain_two,
        down_back,
    )


def solution(mesh):
    fits = mesh.shape["cp"] == HEADS and mesh.shape["seq"] == 2
    on_device = move_tokens_step if fits else gather_weights_step
    placed = (
        P("cp", "seq", None),
        P("seq"),
        P(("seq", "cp")),
        P(("seq", "cp"), None),
        P(("seq", "cp"), None),
        P(("seq", "cp"), None),
        P(("seq", "cp"), None),
        P(("seq", "cp")),
        P(("seq", "cp"), None),
        P(("seq", "cp"), None),
        P(("seq", "cp"), None),
        P("cp", "seq", None),
    )
    return jax.shard_map(
        on_device,
        mesh=mesh,
        in_specs=placed,
        out_specs=(
            P("cp", "seq", None),
            P("cp", "seq", None),
            P(("seq", "cp")),
            P(("seq", "cp"), None),
            P(("seq", "cp"), None),
            P(("seq", "cp"), None),
            P(("seq", "cp"), None),
            P(("seq", "cp")),
            P(("seq", "cp"), None),
            P(("seq", "cp"), None),
            P(("seq", "cp"), None),
        ),
        check_vma=False,
    )
```

```python
import functools
import math

import jax
import jax.numpy as jnp
from jax import lax
from jax.experimental import pallas as pl
from jax.experimental.pallas import tpu as pltpu
from jax.sharding import PartitionSpec as P

HEADS = 16


norm_eps = 1e-05
rope_base = 10000.0


def row_positions(indices, strip_rows, devices):
    owner_index = indices // (2 * strip_rows)
    within = indices % (2 * strip_rows)
    return jnp.where(
        within < strip_rows,
        owner_index * strip_rows + within,
        (2 * devices - 1 - owner_index) * strip_rows + within - strip_rows,
    )


def rotate(values, positions, num_heads):
    count_rows, model_width = values.shape
    head_width = model_width // num_heads
    half_width = head_width // 2
    freqs_table = rope_base ** (-2.0 * jnp.arange(half_width, dtype=jnp.float32) / head_width)
    angles = positions.astype(jnp.float32)[:, None] * freqs_table[None, :]
    cosine = jnp.cos(angles)[:, None, :]
    sine_table = jnp.sin(angles)[:, None, :]
    split_heads = values.reshape(count_rows, num_heads, head_width)
    former = split_heads[:, :, :half_width]
    latter = split_heads[:, :, half_width:]
    turned = jnp.concatenate(
        [former * cosine - latter * sine_table, latter * cosine + former * sine_table], axis=2
    )
    return turned.reshape(count_rows, model_width)


def norm_scale(values):
    return values * lax.rsqrt(jnp.mean(values * values, axis=-1, keepdims=True) + norm_eps)


def normed(values, gain_vector):
    return norm_scale(values) * gain_vector


def swiglu(gate_rows, up_rows):
    return jax.nn.silu(gate_rows) * up_rows


def dot_right(left, right):
    return lax.dot_general(
        left, right, (((1,), (1,)), ((), ())), preferred_element_type=jnp.float32
    )


def dot_left(left, right):
    return lax.dot_general(
        left, right, (((0,), (0,)), ((), ())), preferred_element_type=jnp.float32
    )


def split_blocks(array, block_rows):
    return array.reshape((array.shape[0] // block_rows, block_rows) + array.shape[1:])


def key_mask(query_pos, key_pos, valid_count):
    causal = key_pos[None, :] <= query_pos[:, None]
    live_keys = key_pos[None, :] < valid_count[:, None]
    return (causal[None, None, :, :] & live_keys[:, None, None, :]).astype(jnp.float32)


def scores_of(queries, key_rows, query_pos, key_pos, valid_count, score_shift):
    head_width = queries.shape[3]
    raw_scores = jnp.einsum(
        "qshd,kshd->shqk", queries, key_rows, preferred_element_type=jnp.float32
    )
    return (
        raw_scores * head_width ** (-0.5) - score_shift,
        key_mask(query_pos, key_pos, valid_count),
    )


def block_grads(queries, grad_rows, key_rows, values, query_pos, key_pos, valid_count, score_shift):
    logits, mask_table = scores_of(queries, key_rows, query_pos, key_pos, valid_count, score_shift)
    sigmoid_table = jax.nn.sigmoid(logits)
    weights_low = (sigmoid_table * mask_table).astype(jnp.bfloat16)
    grad_weights = jnp.einsum(
        "qshd,kshd->shqk", grad_rows, values, preferred_element_type=jnp.float32
    )
    grad_logits = (grad_weights * mask_table * (sigmoid_table * (1.0 - sigmoid_table))).astype(
        jnp.bfloat16
    )
    return (weights_low, grad_logits)


def make_norm_fold(normalized, pieces):
    gain_part = pieces[0].astype(jnp.float32)
    scaled = (normalized * gain_part).astype(jnp.bfloat16)
    totals = tuple(
        (
            jnp.dot(scaled, weight_piece, preferred_element_type=jnp.float32)
            for weight_piece in pieces[1:]
        )
    )
    return (gain_part,) + totals


def make_row_fold(left_rows, weight_piece):
    return jnp.dot(left_rows, weight_piece, preferred_element_type=jnp.float32)


def gather_weights_step(
    layer_in,
    valid_len,
    norm1_gain,
    w_query,
    w_key,
    w_value,
    w_out,
    norm2_gain,
    w_gate,
    w_up,
    w_down,
    cotangent,
):
    local_rows, local_seqs, model_width = layer_in.shape
    num_heads = HEADS
    head_width = model_width // num_heads
    strip_rows = local_rows // 2
    cp_devices = lax.axis_size("cp")
    cp_place = lax.axis_index("cp")
    seq_length = local_rows * cp_devices
    score_shift = math.log(seq_length)
    score_scale = head_width ** (-0.5)
    token_count = local_rows * local_seqs
    local_pos = row_positions(
        cp_place * local_rows + jnp.arange(local_rows, dtype=jnp.int32), strip_rows, cp_devices
    )
    token_pos = jnp.broadcast_to(local_pos[:, None], (local_rows, local_seqs)).reshape(token_count)
    every_pos = row_positions(jnp.arange(seq_length, dtype=jnp.int32), strip_rows, cp_devices)
    block_rows = math.gcd(seq_length, 512)
    head_shape = (local_rows, local_seqs, num_heads, head_width)
    row_shape = (local_rows, local_seqs, model_width)
    zero_heads = jnp.zeros(head_shape, jnp.float32)
    inputs = layer_in.reshape(token_count, model_width).astype(jnp.float32)
    input_norm = norm_scale(inputs)
    gain_one, query, key_proj, value = make_norm_fold(
        input_norm,
        (
            lax.all_gather(norm1_gain, ("seq", "cp"), axis=0, tiled=True),
            lax.all_gather(w_query, ("seq", "cp"), axis=0, tiled=True),
            lax.all_gather(w_key, ("seq", "cp"), axis=0, tiled=True),
            lax.all_gather(w_value, ("seq", "cp"), axis=0, tiled=True),
        ),
    )
    normed_one = (input_norm * gain_one).astype(jnp.bfloat16)
    query_low = rotate(query, token_pos, num_heads).astype(jnp.bfloat16)
    key_low = rotate(key_proj, token_pos, num_heads).astype(jnp.bfloat16)
    value_low = value.astype(jnp.bfloat16)
    query_heads = query_low.reshape(head_shape)
    key_local = key_low.reshape(row_shape)
    value_local = value_low.reshape(row_shape)
    key_piece = lax.all_gather(key_local, "cp", axis=0, tiled=True)
    value_piece = lax.all_gather(value_local, "cp", axis=0, tiled=True)
    piece_rows = key_piece.shape[0]
    piece_block = math.gcd(piece_rows, 512)
    piece_pos = row_positions(jnp.arange(piece_rows, dtype=jnp.int32), strip_rows, cp_devices)

    def scan_step(partial_sum, block_items):
        key_block, value_block, block_pos = block_items
        logits, mask_table = scores_of(
            query_heads,
            key_block.reshape(piece_block, local_seqs, num_heads, head_width),
            local_pos,
            block_pos,
            valid_len,
            score_shift,
        )
        weights_low = (jax.nn.sigmoid(logits) * mask_table).astype(jnp.bfloat16)
        added = jnp.einsum(
            "shqk,kshd->qshd",
            weights_low,
            value_block.reshape(piece_block, local_seqs, num_heads, head_width),
            preferred_element_type=jnp.float32,
        )
        return (partial_sum + added, None)

    result, _ = lax.scan(
        scan_step,
        zero_heads,
        (
            split_blocks(key_piece, piece_block),
            split_blocks(value_piece, piece_block),
            split_blocks(piece_pos, piece_block),
        ),
    )
    attended_low = result.reshape(token_count, model_width).astype(jnp.bfloat16)
    attn_branch = make_row_fold(
        attended_low, lax.all_gather(w_out, ("seq", "cp"), axis=0, tiled=True)
    )
    hidden_state = inputs + attn_branch
    hidden_norm = norm_scale(hidden_state)
    gain_two, gate_rows, up_rows = make_norm_fold(
        hidden_norm,
        (
            lax.all_gather(norm2_gain, ("seq", "cp"), axis=0, tiled=True),
            lax.all_gather(w_gate, ("seq", "cp"), axis=0, tiled=True),
            lax.all_gather(w_up, ("seq", "cp"), axis=0, tiled=True),
        ),
    )
    normed_two = (hidden_norm * gain_two).astype(jnp.bfloat16)
    hidden_units = swiglu(gate_rows, up_rows).astype(jnp.bfloat16)
    ff_branch = make_row_fold(
        hidden_units, lax.all_gather(w_down, ("seq", "cp"), axis=0, tiled=True)
    )
    layer_out = (hidden_state + ff_branch).astype(jnp.bfloat16).reshape(row_shape)
    grad_out = cotangent.reshape(token_count, model_width)
    gate_all, up_all, down_all = (
        lax.all_gather(w_gate, ("seq", "cp"), axis=0, tiled=True),
        lax.all_gather(w_up, ("seq", "cp"), axis=0, tiled=True),
        lax.all_gather(w_down, ("seq", "cp"), axis=0, tiled=True),
    )
    grad_hidden = dot_right(grad_out, down_all)
    _, pull_swiglu = jax.vjp(swiglu, gate_rows, up_rows)
    grad_gate, grad_up = pull_swiglu(grad_hidden)
    grad_gate_low = grad_gate.astype(jnp.bfloat16)
    grad_up_low = grad_up.astype(jnp.bfloat16)
    grad_norm_two = dot_right(grad_gate_low, gate_all) + dot_right(grad_up_low, up_all)
    _, pull_two = jax.vjp(normed, hidden_state, gain_two)
    grad_from_two, gain_two_term = pull_two(grad_norm_two)
    ff_grads = (
        lax.psum_scatter(gain_two_term, ("seq", "cp"), scatter_dimension=0, tiled=True),
        lax.psum_scatter(
            dot_left(normed_two, grad_gate_low), ("seq", "cp"), scatter_dimension=0, tiled=True
        ),
        lax.psum_scatter(
            dot_left(normed_two, grad_up_low), ("seq", "cp"), scatter_dimension=0, tiled=True
        ),
        lax.psum_scatter(
            dot_left(hidden_units, grad_out), ("seq", "cp"), scatter_dimension=0, tiled=True
        ),
    )
    grad_state = grad_out.astype(jnp.float32) + grad_from_two
    query_all, key_all, value_all, out_all = (
        lax.all_gather(w_query, ("seq", "cp"), axis=0, tiled=True),
        lax.all_gather(w_key, ("seq", "cp"), axis=0, tiled=True),
        lax.all_gather(w_value, ("seq", "cp"), axis=0, tiled=True),
        lax.all_gather(w_out, ("seq", "cp"), axis=0, tiled=True),
    )
    grad_branch_low = grad_state.astype(jnp.bfloat16)
    grad_attended_low = dot_right(grad_branch_low, out_all).astype(jnp.bfloat16)
    grad_heads = grad_attended_low.reshape(head_shape)
    key_heads_local = key_local.reshape(head_shape)
    value_heads_local = value_local.reshape(head_shape)
    keys_every, values_every, queries_every, grads_every = (
        lax.all_gather(key_local, "cp", axis=0, tiled=True),
        lax.all_gather(value_local, "cp", axis=0, tiled=True),
        lax.all_gather(query_low.reshape(row_shape), "cp", axis=0, tiled=True),
        lax.all_gather(grad_attended_low.reshape(row_shape), "cp", axis=0, tiled=True),
    )

    def key_step(partial_sums, block_items):
        query_block, grad_block_rows, block_pos = block_items
        query_part = query_block.reshape(block_rows, local_seqs, num_heads, head_width)
        grad_part = grad_block_rows.reshape(block_rows, local_seqs, num_heads, head_width)
        weights_low, grad_logits = block_grads(
            query_part,
            grad_part,
            key_heads_local,
            value_heads_local,
            block_pos,
            local_pos,
            valid_len,
            score_shift,
        )
        key_added = jnp.einsum(
            "shqk,qshd->kshd", grad_logits, query_part, preferred_element_type=jnp.float32
        )
        value_added = jnp.einsum(
            "shqk,qshd->kshd", weights_low, grad_part, preferred_element_type=jnp.float32
        )
        return ((partial_sums[0] + key_added, partial_sums[1] + value_added), None)

    (key_sum, value_sum), _ = lax.scan(
        key_step,
        (zero_heads, zero_heads),
        (
            split_blocks(queries_every, block_rows),
            split_blocks(grads_every, block_rows),
            split_blocks(every_pos, block_rows),
        ),
    )
    grad_key_rot = key_sum.reshape(token_count, model_width) * score_scale
    grad_value_sum = value_sum.reshape(token_count, model_width)

    def query_step(partial_sum, block_items):
        key_block, value_block, block_pos = block_items
        key_heads = key_block.reshape(block_rows, local_seqs, num_heads, head_width)
        _, grad_logits = block_grads(
            query_heads,
            grad_heads,
            key_heads,
            value_block.reshape(block_rows, local_seqs, num_heads, head_width),
            local_pos,
            block_pos,
            valid_len,
            score_shift,
        )
        added = jnp.einsum(
            "shqk,kshd->qshd", grad_logits, key_heads, preferred_element_type=jnp.float32
        )
        return (partial_sum + added, None)

    query_sum, _ = lax.scan(
        query_step,
        zero_heads,
        (
            split_blocks(keys_every, block_rows),
            split_blocks(values_every, block_rows),
            split_blocks(every_pos, block_rows),
        ),
    )
    grad_query_rot = query_sum.reshape(token_count, model_width) * score_scale
    grad_query_low = rotate(grad_query_rot, -token_pos, num_heads).astype(jnp.bfloat16)
    grad_key_low = rotate(grad_key_rot, -token_pos, num_heads).astype(jnp.bfloat16)
    grad_value_low = grad_value_sum.astype(jnp.bfloat16)
    grad_norm_one = (
        dot_right(grad_query_low, query_all)
        + dot_right(grad_key_low, key_all)
        + dot_right(grad_value_low, value_all)
    )
    _, pull_one = jax.vjp(normed, inputs, gain_one)
    grad_from_one, gain_one_term = pull_one(grad_norm_one)
    in_grad = (grad_state + grad_from_one).reshape(row_shape)
    attn_grads = (
        lax.psum_scatter(gain_one_term, ("seq", "cp"), scatter_dimension=0, tiled=True),
        lax.psum_scatter(
            dot_left(normed_one, grad_query_low), ("seq", "cp"), scatter_dimension=0, tiled=True
        ),
        lax.psum_scatter(
            dot_left(normed_one, grad_key_low), ("seq", "cp"), scatter_dimension=0, tiled=True
        ),
        lax.psum_scatter(
            dot_left(normed_one, grad_value_low), ("seq", "cp"), scatter_dimension=0, tiled=True
        ),
        lax.psum_scatter(
            dot_left(attended_low, grad_branch_low), ("seq", "cp"), scatter_dimension=0, tiled=True
        ),
    )
    return (
        layer_out,
        in_grad,
        attn_grads[0],
        attn_grads[1],
        attn_grads[2],
        attn_grads[3],
        attn_grads[4],
        ff_grads[0],
        ff_grads[1],
        ff_grads[2],
        ff_grads[3],
    )


MESH = pl.DeviceIdType.MESH
DMA = pltpu.SemaphoreType.DMA
LOW = jnp.bfloat16
F32 = jnp.float32
ANYWHERE = pl.BlockSpec(memory_space=pl.ANY)
IN_VMEM = pl.BlockSpec(memory_space=pltpu.VMEM)
IN_SMEM = pl.BlockSpec(memory_space=pltpu.SMEM)


class Place:
    def __init__(self):
        self.s = lax.axis_index("seq")
        self.c = lax.axis_index("cp")
        self.z = self.c // 4
        self.y = (self.c // 2) % 2
        self.k = self.c % 2

    def at(self, z, y, k):
        return z * 4 + y * 2 + k

    def device(self, place):
        return (self.s, place)


def pick(z, table):
    value = jnp.int32(table[0])
    for index in range(1, 4):
        value = jnp.where(z == index, jnp.int32(table[index]), value)
    return value


NEAREST = ((1, 0, 1, 2), (2, 2, 3, 1), (3, 3, 0, 0))
FARTHEST = ((3, 3, 0, 0), (2, 2, 3, 1), (1, 0, 1, 2))


def remote(source, target, send, recv, device):
    return pltpu.make_async_remote_copy(
        src_ref=source,
        dst_ref=target,
        send_sem=send,
        recv_sem=recv,
        device_id=device,
        device_id_type=MESH,
    )


def hail(device):
    pl.semaphore_signal(
        pltpu.get_barrier_semaphore(), inc=1, device_id=device, device_id_type=MESH
    )


def greet(me, over_seq=False):
    hail((me.s, me.at(me.z, 1 - me.y, me.k)))
    hail((me.s, me.at(me.z, me.y, 1 - me.k)))

    @pl.when(me.z < 3)
    def _():
        hail((me.s, me.at(me.z + 1, me.y, me.k)))

    @pl.when(me.z > 0)
    def _():
        hail((me.s, me.at(me.z - 1, me.y, me.k)))

    ends = (me.z == 0).astype(jnp.int32) + (me.z == 3).astype(jnp.int32)
    if over_seq:
        hail((1 - me.s, me.c))
    pl.semaphore_wait(pltpu.get_barrier_semaphore(), 4 - ends + (1 if over_seq else 0))


def greet_plane(me):
    for step in range(1, 16):
        hail((me.s, (me.c + step) % 16))
    hail((1 - me.s, me.c))
    hail((1 - me.s, me.at(me.z, me.y, 1 - me.k)))
    pl.semaphore_wait(pltpu.get_barrier_semaphore(), 17)


class Gather:
    def __init__(self, me, views, z_sem, y_sem, k_sem, recv):
        self.me, self.views = me, views
        self.z_sem, self.y_sem, self.k_sem, self.recv = z_sem, y_sem, k_sem, recv

    @staticmethod
    def sems(pieces):
        return [DMA((pieces * n,)) for n in (5, 4, 8, 16)]

    def copy(self, piece, place, sem, device):
        block = self.views[piece](place)
        return remote(block, block, sem, self.recv.at[piece * 16 + place], device)

    def arrived(self, piece, place):
        self.copy(piece, place, self.k_sem.at[0], self.me.device(self.me.c)).wait_recv()

    def line(self, index):
        return self.me.z if index == 0 else pick(self.me.z, NEAREST[index - 1])

    def along(self, piece, place, index, up):
        me = self.me
        target = jnp.minimum(me.c + 4, 12 + me.c % 4) if up else jnp.maximum(me.c - 4, me.c % 4)
        return self.copy(piece, place, self.z_sem.at[piece * 5 + index], me.device(target))

    def across(self, piece, place, index):
        me = self.me
        target = me.at(me.z, 1 - me.y, me.k)
        return self.copy(piece, place, self.y_sem.at[piece * 4 + index], me.device(target))

    def partner(self, piece, place, index):
        me = self.me
        target = me.at(me.z, me.y, 1 - me.k)
        return self.copy(piece, place, self.k_sem.at[piece * 8 + index], me.device(target))

    def send_line(self, piece, index, go=lambda copy: copy.start()):
        me, z = self.me, self.line(index)
        place = me.at(z, me.y, me.k)
        if index == 0:
            go(self.across(piece, place, index))

            @pl.when(me.z < 3)
            def _():
                go(self.along(piece, place, 0, True))

            @pl.when(me.z > 0)
            def _():
                go(self.along(piece, place, 4, False))
        else:

            @pl.when((z < me.z) & (me.z < 3))
            def _():
                go(self.along(piece, place, index, True))

            @pl.when((z > me.z) & (me.z > 0))
            def _():
                go(self.along(piece, place, index, False))

            go(self.across(piece, place, index))
        go(self.partner(piece, place, index))

    def begin(self):
        for piece in range(len(self.views)):
            self.send_line(piece, 0)

    def near(self, piece, index):
        self.arrived(piece, self.me.at(self.line(index), self.me.y, self.me.k))
        self.send_line(piece, index)

    def round(self, index):
        me = self.me
        for piece in range(len(self.views)):
            if index < 3:
                self.near(piece, index + 1)
            far = me.at(self.line(index), 1 - me.y, me.k)
            self.arrived(piece, far)
            self.partner(piece, far, 4 + index).start()

    def settle(self, z, y):
        for piece in range(len(self.views)):
            self.arrived(piece, self.me.at(z, y, 1 - self.me.k))

    def run(self, consume):
        me = self.me
        self.begin()
        waiting = [(me.z, me.y)]
        for index in range(4):
            self.round(index)
            ready, waiting = waiting, []
            if index < 3:
                waiting.append((self.line(index + 1), me.y))
            waiting.append((self.line(index), 1 - me.y))
            for z, y in ready:
                self.settle(z, y)
                consume(z * 2 + y)
        for z, y in waiting:
            self.settle(z, y)
            consume(z * 2 + y)

    def finish(self):
        me = self.me
        for piece in range(len(self.views)):
            for index in range(4):
                self.send_line(piece, index, lambda copy: copy.wait_send())
                far = me.at(self.line(index), 1 - me.y, me.k)
                self.partner(piece, far, 4 + index).wait_send()


class Scatter:
    pieces = 2

    def __init__(self, me, scratch):
        self.me = me
        (self.k_out, self.k_in, self.y_out, self.y_in, self.z_out, self.z_in, self.mine, self.kept) = scratch[:8]
        (self.ks, self.kr, self.ys, self.yr, self.zs, self.zl, self.zr) = scratch[8:15]

    count = 15

    @classmethod
    def scratch(cls, rows, width):
        n = cls.pieces
        part = width // n
        low = [pltpu.VMEM((n * count, rows, part), LOW) for count in (8, 8, 4, 4, 3, 8)]
        full = [pltpu.VMEM((n * count, rows, part), F32) for count in (1, 4)]
        return low + full + [DMA((n * count,)) for count in (8, 8, 4, 4, 3, 4, 4)]

    def partner(self, slot):
        me = self.me
        target = me.device(me.at(me.z, me.y, 1 - me.k))
        return remote(self.k_out.at[slot], self.k_in.at[slot], self.ks.at[slot], self.kr.at[slot], target)

    def across(self, z, index, piece):
        me, n = self.me, self.pieces
        out, land = index * n + piece, z * n + piece
        target = me.device(me.at(me.z, 1 - me.y, me.k))
        return remote(self.y_out.at[out], self.y_in.at[land], self.ys.at[out], self.yr.at[land], target)

    def along(self, z, index, piece, up):
        me, n = self.me, self.pieces
        out, land = index * n + piece, z * n + piece
        target = jnp.minimum(me.c + 4, 12 + me.c % 4) if up else jnp.maximum(me.c - 4, me.c % 4)
        into = self.z_in.at[land if up else 4 * n + land]
        sem = (self.zl if up else self.zr).at[land]
        return remote(self.z_out.at[out], into, self.zs.at[out], sem, me.device(target))

    def line(self, index):
        return self.me.z if index == 3 else pick(self.me.z, FARTHEST[index])

    def emit(self, produce, z, y, piece, slot, keep):
        part = 512
        rows, width = keep.shape

        @pl.loop(0, width // part)
        def _(index):
            here = pl.ds(pl.multiple_of(index * part, part), part)
            start = pl.multiple_of(piece * width + index * part, part)
            value = produce(self.me.at(z, y, 0), pl.ds(start, part))
            self.k_out[slot, :, here] = value[:rows].astype(LOW)
            keep[:, here] = value[rows:]

        self.partner(slot).start()

    def add(self, target, base, *blocks):
        part = 512

        @pl.loop(0, target.shape[-1] // part)
        def _(index):
            here = pl.ds(pl.multiple_of(index * part, part), part)
            value = base[:, here]
            for block in blocks:
                value = value + block[:, here].astype(F32)
            target[:, here] = value.astype(target.dtype)

    def run(self, prepare, produce, finish, between=lambda: None):
        me, n = self.me, self.pieces
        steps = [(index, piece) for index in range(4) for piece in range(n)]
        for number in range(len(steps) + 1):
            if number < len(steps):
                index, piece = steps[number]
                z = self.line(index)
                if prepare is not None and piece == 0:
                    prepare(z * 2 + 1 - me.y)
                self.emit(produce, z, 1 - me.y, piece, number, self.mine.at[number % 2])
            if number > 0:
                index, piece = steps[number - 1]
                self.partner(number - 1).wait_recv()
                self.add(self.y_out.at[number - 1], self.mine.at[(number - 1) % 2], self.k_in.at[number - 1])
                self.across(self.line(index), index, piece).start()
        for number, (index, piece) in enumerate(steps):
            z = self.line(index)
            if prepare is not None and piece == 0:
                prepare(z * 2 + me.y)
            self.emit(produce, z, me.y, piece, 4 * n + number, self.kept.at[number])
        between()
        for number, (index, piece) in enumerate(steps):
            z = self.line(index)
            slot, land = 4 * n + number, z * n + piece
            kept = self.kept.at[number]
            self.partner(slot).wait_recv()
            self.across(z, index, piece).wait_recv()
            self.add(kept, kept, self.k_in.at[slot], self.y_in.at[land])
            if index < 3:
                from_below, from_above = (z > me.z) & (me.z > 0), (z < me.z) & (me.z < 3)
            else:
                from_below, from_above = me.z > 0, me.z < 3

            @pl.when(from_below)
            def _():
                self.along(z, 0, piece, True).wait_recv()
                self.add(kept, kept, self.z_in.at[land])

            @pl.when(from_above)
            def _():
                self.along(z, 0, piece, False).wait_recv()
                self.add(kept, kept, self.z_in.at[4 * n + land])

            if index < 3:
                self.add(self.z_out.at[number], kept)

                @pl.when(z > me.z)
                def _():
                    self.along(z, index, piece, True).start()

                @pl.when(z < me.z)
                def _():
                    self.along(z, index, piece, False).start()
            else:
                finish(piece, kept)

    def drain(self):
        me, n = self.me, self.pieces
        for slot in range(8 * n):
            self.partner(slot).wait_send()
        for index in range(4):
            z = self.line(index)
            for piece in range(n):
                self.across(z, index, piece).wait_send()
                if index < 3:

                    @pl.when(z > me.z)
                    def _():
                        self.along(z, index, piece, True).wait_send()

                    @pl.when(z < me.z)
                    def _():
                        self.along(z, index, piece, False).wait_send()


def write_total(total_out):
    def finish(piece, kept):
        width = kept.shape[-1]
        total_out[:, piece * width : (piece + 1) * width] = kept[...]

    return finish


def own_last(me, block, first):
    return jnp.concatenate([block[first + 1 - me.k], block[first + me.k]], axis=0)


def params(collective_id):
    return pltpu.CompilerParams(
        collective_id=collective_id, has_side_effects=True, vmem_limit_bytes=60 << 20
    )


def turn(me, step):
    dz, dy, dk = step // 4, (step // 2) % 2, step % 2
    to = me.at((me.z + dz) % 4, (me.y + dy) % 2, (me.k + dk) % 2)
    source = me.at((me.z + 4 - dz) % 4, (me.y + dy) % 2, (me.k + dk) % 2)
    return to, source


def halves(array, rows):
    return [
        lambda place, seq=seq: array.at[place, pl.ds(seq * rows, rows)] for seq in range(2)
    ]


def spread_kernel(
    unit, grad, qkv, gate_up, out_w, down, cosine, sine,
    units, grads, query, key, value, qkv_full, gate_up_half, out_all, down_other, *scratch
):
    gather_sems = scratch[:4]
    (qs, qr, qxs, qxr, ps, pr, os, ox, orecv, local, dsem, leave, units_here, grads_here, qkv_all) = scratch[4:]
    me = Place()
    own = [
        pltpu.make_async_copy(unit, units_here.at[me.c], local.at[0]),
        pltpu.make_async_copy(grad, grads_here.at[me.c], local.at[1]),
        pltpu.make_async_copy(qkv.at[me.c], qkv_all.at[me.s, me.c], local.at[2]),
        pltpu.make_async_copy(gate_up.at[me.c], gate_up_half.at[me.c], local.at[3]),
    ]
    for copy in own:
        copy.start()
    greet_plane(me)
    over = (1 - me.s, me.c)
    tokens = unit.shape[0]
    rows = tokens // 2
    gather = Gather(me, halves(units_here, rows) + halves(grads_here, rows), *gather_sems)
    down_copy = remote(down, down_other, dsem.at[0], dsem.at[1], over)

    def send_qkv(step):
        to, _ = turn(me, step)
        return remote(qkv.at[to], qkv_all.at[me.s, me.c], qs.at[step], qr.at[me.c], (me.s, to))

    def send_gate_up(step):
        to, _ = turn(me, step)
        return remote(gate_up.at[to], gate_up_half.at[me.c], ps.at[step], pr.at[me.c], (me.s, to))

    def forward(source):
        block = qkv_all.at[me.s, source]
        return remote(block, block, qxs.at[source], qxr.at[source], over)

    holder = me.at(me.z, me.y, me.s)
    out_local = pltpu.make_async_copy(out_w, out_all.at[me.k], local.at[4])
    out_near = remote(out_w, out_all.at[me.k], os.at[0], orecv.at[me.k], (me.s, me.at(me.z, me.y, 1 - me.k)))
    out_far = remote(out_w, out_all.at[me.k], ox, orecv.at[me.k], (1 - me.s, holder))

    for copy in own[:2]:
        copy.wait()
    gather.begin()
    for step in range(1, 16):
        send_qkv(step).start()
    own[2].wait()
    forward(me.c).start()
    out_far.start()

    @pl.when(holder == me.c)
    def _():
        out_local.start()

    @pl.when(holder != me.c)
    def _():
        out_near.start()

    down_copy.start()
    width = query.shape[3]
    leaving = []

    def write_out(z, y):
        pair = z * 2 + y
        both = pl.ds(2 * pair, 2)
        number = len(leaving)
        for index, (here, there) in enumerate(((units_here, units), (grads_here, grads))):
            copy = pltpu.make_async_copy(here.at[both], there.at[both], leave.at[2 * number + index])
            copy.start()
            leaving.append(copy)

    def turned(values, both):
        swapped = pltpu.roll(values, width // 2, axis=1)
        place_cos = cosine[both].reshape(2 * rows, width)
        place_sin = sine[both].reshape(2 * rows, width)
        return (values * place_cos - swapped * place_sin).astype(LOW).reshape(2, rows, width)

    def project(z, y):
        both = pl.ds(2 * (z * 2 + y), 2)
        model = unit.shape[1]
        weights = qkv_all[...].reshape(model, 3 * width)
        for seq in range(2):
            block = units_here[both, seq * rows : (seq + 1) * rows].reshape(2 * rows, model)
            result = jnp.dot(block, weights, preferred_element_type=F32)
            query[both, seq] = turned(result[:, :width], both)
            key[both, seq] = turned(result[:, width : 2 * width], both)
            value[both, seq] = result[:, 2 * width :].astype(LOW).reshape(2, rows, width)

    steps = list(range(1, 16))
    waiting, ready = [(me.z, me.y)], []
    for index in range(4):
        for step in steps[4 * index : 4 * index + 4]:
            send_gate_up(step).start()
        gather.round(index)
        for z, y in waiting:
            gather.settle(z, y)
            write_out(z, y)
        ready += waiting
        waiting = [(gather.line(index), 1 - me.y)]
        if index < 3:
            waiting.append((gather.line(index + 1), me.y))
        if index == 1:
            for step in steps:
                _, source = turn(me, step)
                remote(qkv.at[0], qkv_all.at[me.s, source], qs.at[step], qr.at[source], over).wait_recv()
                forward(source).start()
        if index == 2:
            for source in range(16):
                forward(source).wait_send()
                forward(source).wait_recv()
            leave_qkv = pltpu.make_async_copy(qkv_all, qkv_full, local.at[5])
            leave_qkv.start()
        if index >= 2:
            for z, y in ready:
                project(z, y)
            ready = []
    for z, y in waiting:
        gather.settle(z, y)
        write_out(z, y)
        project(z, y)
    gather.finish()
    own[3].wait()
    leave_qkv.wait()
    for copy in leaving:
        copy.wait()
    for step in steps:
        _, source = turn(me, step)
        send_qkv(step).wait_send()
        send_gate_up(step).wait_send()
        remote(gate_up.at[0], gate_up_half.at[source], ps.at[step], pr.at[source], over).wait_recv()
    out_far.wait_send()
    down_copy.wait()

    @pl.when(holder == me.c)
    def _():
        out_local.wait()
        remote(out_w, out_all.at[1 - me.k], ox, orecv.at[1 - me.k], over).wait_recv()

    @pl.when(holder != me.c)
    def _():
        out_near.wait_send()
        for half in range(2):
            remote(out_w, out_all.at[half], ox, orecv.at[half], over).wait_recv()


def spread(unit, grad, qkv, gate_up, out_w, down, cosine, sine):
    def shape(lead, array, tail):
        return jax.ShapeDtypeStruct(lead + array.shape[tail:], array.dtype)

    tokens, model = unit.shape
    heads = jax.ShapeDtypeStruct((16, 2, tokens // 2, qkv.shape[2] // 3), LOW)
    return pl.pallas_call(
        spread_kernel,
        out_shape=[
            shape((16,), unit, 0),
            shape((16,), grad, 0),
            heads,
            heads,
            heads,
            shape((2, 16), qkv, 1),
            shape((16,), gate_up, 1),
            shape((2,), out_w, 0),
            shape((), down, 0),
        ],
        in_specs=[ANYWHERE] * 6 + [IN_VMEM] * 2,
        out_specs=[ANYWHERE] * 2 + [IN_VMEM] * 3 + [ANYWHERE] * 4,
        scratch_shapes=Gather.sems(4)
        + [DMA((16,))] * 6
        + [DMA((1,)), DMA, DMA((2,)), DMA((6,)), DMA((2,)), DMA((32,))]
        + [pltpu.VMEM((16, tokens, model), LOW)] * 2
        + [pltpu.VMEM((2, 16) + qkv.shape[1:], LOW)],
        compiler_params=params(0),
    )(unit, grad, qkv, gate_up, out_w, down, cosine, sine)


def row_place(place, row, strip):
    return jnp.where(row < strip, place * strip + row, (31 - place) * strip + row - strip)


def key_places(strip):
    index = lax.broadcasted_iota(jnp.int32, (1, 32 * strip), 1)
    return row_place(index // (2 * strip), index % (2 * strip), strip)


def query_places(pair, strip):
    index = lax.broadcasted_iota(jnp.int32, (4 * strip, 1), 0)
    return row_place(2 * pair + index // (2 * strip), index % (2 * strip), strip)


def of_pair(block, pair, seq):
    rows, width = block.shape[2:]
    return block[pl.ds(2 * pair, 2), seq].reshape(2 * rows, width)


def attend_kernel(
    shift, valid, query, key, value, out_w, gate_up, total_out, attended, gate_up_other, *scratch
):
    me = Place()
    greet(me, over_seq=True)
    over = (1 - me.s, me.c)
    sems = scratch[Scatter.count]
    swaps = [
        remote(gate_up, gate_up_other, sems.at[0], sems.at[1], over),
    ]
    for copy in swaps:
        copy.start()
    scatter = Scatter(me, scratch)
    rows, width = query.shape[2], query.shape[3]
    strip = rows // 2
    length = rows * 16
    scale = width ** (-0.5)

    def prepare(pair):
        where = query_places(pair, strip)
        keys_at = key_places(strip)
        for seq in range(2):
            keys = key[:, seq].reshape(length, width)
            values = value[:, seq].reshape(length, width)
            logits = dot_right(of_pair(query, pair, seq), keys) * scale - shift
            live = (keys_at <= where) & (keys_at < valid[seq])
            weights = jnp.where(live, jax.nn.sigmoid(logits), 0.0).astype(LOW)
            attended[pl.ds(2 * pair, 2), pl.ds(seq * rows, rows)] = (
                jnp.dot(weights, values, preferred_element_type=F32).astype(LOW).reshape(2, rows, width)
            )

    def produce(first, columns):
        return jnp.dot(own_last(me, attended, first), out_w[:, columns], preferred_element_type=F32)

    scatter.run(prepare, produce, write_total(total_out))
    scatter.drain()
    for copy in swaps:
        copy.wait()


def attend(shift, valid, query, key, value, out_w, gate_up):
    rows, width = query.shape[2:]
    tokens, model = 2 * rows, out_w.shape[1]
    return pl.pallas_call(
        functools.partial(attend_kernel, shift),
        out_shape=[
            jax.ShapeDtypeStruct((tokens, model), F32),
            jax.ShapeDtypeStruct((16, tokens, width), LOW),
            jax.ShapeDtypeStruct(gate_up.shape, LOW),
        ],
        in_specs=[IN_SMEM] + [IN_VMEM] * 4 + [ANYWHERE],
        out_specs=[IN_VMEM] * 2 + [ANYWHERE],
        scratch_shapes=Scatter.scratch(tokens, model) + [DMA((2,))],
        compiler_params=params(1),
    )(valid, query, key, value, out_w, gate_up)


def mlp_kernel(
    unit, grads, gate_up_own, gate_up_other, down_own, down_other,
    total_out, units, hidden, grad_gate_up, down_full, *scratch
):
    me = Place()
    tokens, model = unit.shape
    width = hidden.shape[2]
    gate_up_full, grads_here, local = scratch[-3:]
    gather = Gather(me, halves(units, tokens // 2), *scratch[Scatter.count : Scatter.count + 4])
    own = pltpu.make_async_copy(unit, units.at[me.c], local.at[0])
    brought = [
        pltpu.make_async_copy(gate_up_own, gate_up_full.at[me.s], local.at[1]),
        pltpu.make_async_copy(gate_up_other, gate_up_full.at[1 - me.s], local.at[2]),
        pltpu.make_async_copy(down_own, down_full.at[me.s], local.at[3]),
        pltpu.make_async_copy(down_other, down_full.at[1 - me.s], local.at[4]),
        pltpu.make_async_copy(grads, grads_here, local.at[5]),
    ]
    own.start()
    for copy in brought:
        copy.start()
    greet(me)
    own.wait()
    rows_of = gate_up_full.shape[1] * gate_up_full.shape[2]
    units_of = down_full.shape[1]
    first = [True]

    def consume(pair):
        if first[0]:
            for copy in brought:
                copy.wait()
            first[0] = False
        both = pl.ds(2 * pair, 2)

        def dot_rows(rows, columns):
            return jnp.dot(
                rows,
                gate_up_full[:, :, :, columns].reshape(2 * rows_of, units_of),
                preferred_element_type=F32,
            )

        @pl.loop(0, 2)
        def _(half):
            gate_at = pl.ds(pl.multiple_of(half * units_of, units_of), units_of)
            up_at = pl.ds(pl.multiple_of(width + half * units_of, units_of), units_of)
            rows = units[both].reshape(2 * tokens, model)
            gate = dot_rows(rows, gate_at)
            up = dot_rows(rows, up_at)
            grad = dot_right(grads_here[both].reshape(2 * tokens, model), down_full[half])
            sig = jax.nn.sigmoid(gate)
            silu = gate * sig

            def store(target, columns, value):
                target[both, :, columns] = value.astype(LOW).reshape(2, tokens, units_of)

            store(hidden, gate_at, silu * up)
            store(grad_gate_up, gate_at, grad * up * (sig * (1.0 + gate * (1.0 - sig))))
            store(grad_gate_up, up_at, grad * silu)

    gather.run(consume)
    scatter = Scatter(me, scratch)
    block_rows = gate_up_full.shape[2]

    def produce(first, columns):
        start, size = columns.start, columns.size
        blocks = size // block_rows
        block = start // block_rows
        weights = gate_up_full[block // 16, pl.ds(block % 16, blocks)].reshape(size, 2 * width)
        return dot_right(own_last(me, grad_gate_up, first), weights)

    scatter.run(None, produce, write_total(total_out))
    scatter.drain()
    gather.finish()


def mlp(unit, grads, gate_up_own, gate_up_other, down_own, down_other):
    tokens, model = unit.shape
    width = 2 * down_own.shape[0]
    return pl.pallas_call(
        mlp_kernel,
        out_shape=[
            jax.ShapeDtypeStruct((tokens, model), F32),
            jax.ShapeDtypeStruct((16, tokens, model), LOW),
            jax.ShapeDtypeStruct((16, tokens, width), LOW),
            jax.ShapeDtypeStruct((16, tokens, 2 * width), LOW),
            jax.ShapeDtypeStruct((2,) + down_own.shape, LOW),
        ],
        in_specs=[ANYWHERE] * 6,
        out_specs=[IN_VMEM] * 5,
        scratch_shapes=Scatter.scratch(tokens, model)
        + Gather.sems(2)
        + [pltpu.VMEM((2,) + gate_up_own.shape, LOW), pltpu.VMEM((16, tokens, model), LOW), DMA((6,))],
        compiler_params=params(2),
    )(unit, grads, gate_up_own, gate_up_other, down_own, down_other)


def attend_back_kernel(
    shift, valid, branch, query, key, value, out_w, qkv_w, cosine, sine, gate_up, down,
    total_out, branches, grad_qkv, gate_up_other, down_other, key_sum, value_sum, *scratch
):
    me = Place()
    tokens = branch.shape[0]
    gather = Gather(me, halves(branches, tokens // 2), *scratch[Scatter.count : Scatter.count + 4])
    sems, local = scratch[-2:]
    own = pltpu.make_async_copy(branch, branches.at[me.c], local)
    own.start()
    greet(me, over_seq=True)
    own.wait()
    over = (1 - me.s, me.c)
    swaps = [
        remote(gate_up.at[1 - me.s], gate_up_other, sems.at[0], sems.at[1], over),
        remote(down.at[1 - me.s], down_other, sems.at[2], sems.at[3], over),
    ]
    for copy in swaps:
        copy.start()
    rows, width = query.shape[2], query.shape[3]
    strip = rows // 2
    length = rows * 16
    scale = width ** (-0.5)
    key_sum[...] = jnp.zeros_like(key_sum)
    value_sum[...] = jnp.zeros_like(value_sum)

    def turn_back(values, places):
        swapped = pltpu.roll(values, width // 2, axis=1)
        turned = values * cosine[places].reshape(2 * rows, width)
        return (turned + swapped * sine[places].reshape(2 * rows, width)).astype(LOW).reshape(2, rows, width)

    def consume(pair):
        where = query_places(pair, strip)
        keys_at = key_places(strip)
        both = pl.ds(2 * pair, 2)
        for seq in range(2):
            here = pl.ds(seq * rows, rows)
            grad = dot_right(branches[both, here].reshape(2 * rows, -1), out_w[...]).astype(LOW)
            keys = key[:, seq].reshape(length, width)
            values = value[:, seq].reshape(length, width)
            queries = of_pair(query, pair, seq)
            logits = dot_right(queries, keys) * scale - shift
            live = (keys_at <= where) & (keys_at < valid[seq])
            sig = jnp.where(live, jax.nn.sigmoid(logits), 0.0)
            weights = sig.astype(LOW)
            grad_logits = (dot_right(grad, values) * (sig * (1.0 - sig))).astype(LOW)
            grad_query = jnp.dot(grad_logits, keys, preferred_element_type=F32) * scale
            grad_qkv[both, here, 0:width] = turn_back(grad_query, both)
            key_sum[seq] += dot_left(grad_logits, queries)
            value_sum[seq] += dot_left(weights, grad)

    gather.run(consume)
    for seq in range(2):

        @pl.loop(0, 8)
        def _(pair):
            at = pl.ds(pl.multiple_of(pair * 2 * rows, 2 * rows), 2 * rows)
            here = pl.ds(seq * rows, rows)
            both = pl.ds(2 * pair, 2)
            grad_qkv[both, here, width : 2 * width] = turn_back(key_sum[seq, at] * scale, both)
            grad_qkv[both, here, 2 * width :] = value_sum[seq, at].astype(LOW).reshape(2, rows, width)

    scatter = Scatter(me, scratch)

    def produce(first, columns):
        return dot_right(own_last(me, grad_qkv, first), qkv_w[columns, :])

    scatter.run(None, produce, write_total(total_out))
    scatter.drain()
    gather.finish()
    for copy in swaps:
        copy.wait()


def attend_back(shift, valid, branch, query, key, value, out_w, qkv_w, cosine, sine, gate_up, down):
    tokens, model = branch.shape
    rows, width = query.shape[2:]
    return pl.pallas_call(
        functools.partial(attend_back_kernel, shift),
        out_shape=[
            jax.ShapeDtypeStruct((tokens, model), F32),
            jax.ShapeDtypeStruct((16, tokens, model), LOW),
            jax.ShapeDtypeStruct((16, tokens, 3 * width), LOW),
            jax.ShapeDtypeStruct(gate_up.shape[1:], LOW),
            jax.ShapeDtypeStruct(down.shape[1:], LOW),
        ],
        in_specs=[IN_SMEM, ANYWHERE] + [IN_VMEM] * 7 + [ANYWHERE] * 2,
        out_specs=[IN_VMEM] * 3 + [ANYWHERE] * 2,
        scratch_shapes=[pltpu.VMEM((2, 16 * rows, width), F32)] * 2
        + Scatter.scratch(tokens, model)
        + Gather.sems(2)
        + [DMA((4,)), DMA],
        compiler_params=params(4),
    )(valid, branch, query, key, value, out_w, qkv_w, cosine, sine, gate_up, down)


def return_kernel(
    hidden, down_w, qkv, gate_up, gate_up_other, out_pair,
    total_out, qkv_back, gate_up_back, out_back, *scratch
):
    (qx, qsum, qxs, qxr, qs, qr, psum, ps, pr, oland, os, orecv) = scratch[Scatter.count :]
    me = Place()
    greet_plane(me)
    over = (1 - me.s, me.c)

    def cross(place):
        return remote(qkv.at[1 - me.s, place], qx.at[place], qxs.at[place], qxr.at[place], over)

    def send(sums, back, s_sem, r_sem, step):
        to, _ = turn(me, step)
        return remote(sums.at[to], back.at[me.c], s_sem.at[step], r_sem.at[me.c], (me.s, to))

    for step in range(1, 16):
        cross(turn(me, step)[0]).start()
    cross(me.c).start()
    holder = me.at(me.z, me.y, me.s)

    def out_send(target_core, same):
        target = (me.s if same else 1 - me.s, me.at(me.z, me.y, target_core))
        slot = 0 if same else 1
        return remote(out_pair.at[target_core], oland.at[me.s], os.at[slot], orecv.at[me.s], target)

    inside = me.k == me.s

    @pl.when(inside)
    def _():
        out_send(1 - me.k, True).start()

    @pl.when(jnp.logical_not(inside))
    def _():
        out_send(me.k, False).start()
        remote(
            out_pair.at[1 - me.k], oland.at[me.s], os.at[0], orecv.at[me.s],
            (1 - me.s, me.at(me.z, me.y, 1 - me.k)),
        ).start()

    def summed(place):
        return (gate_up[me.s, place].astype(F32) + gate_up_other[place].astype(F32)).astype(LOW)

    gate_up_back[me.c] = summed(me.c)

    @pl.loop(0, 16)
    def _(place):
        psum[place] = summed(place)

    for step in range(1, 16):
        send(psum, gate_up_back, ps, pr, step).start()

    def between():
        for step in range(1, 16):
            to, _ = turn(me, step)
            cross(to).wait_recv()
            qsum[to] = (qkv[me.s, to].astype(F32) + qx[to].astype(F32)).astype(LOW)
            send(qsum, qkv_back, qs, qr, step).start()
        cross(me.c).wait_recv()
        qkv_back[me.c] = (qkv[me.s, me.c].astype(F32) + qx[me.c].astype(F32)).astype(LOW)

    scatter = Scatter(me, scratch)

    def produce(first, columns):
        return jnp.dot(own_last(me, hidden, first), down_w[:, columns], preferred_element_type=F32)

    scatter.run(None, produce, write_total(total_out), between)
    scatter.drain()
    for step in range(1, 16):
        to, source = turn(me, step)
        for sums, back, s_sem, r_sem in ((qsum, qkv_back, qs, qr), (psum, gate_up_back, ps, pr)):
            remote(sums.at[0], back.at[source], s_sem.at[step], r_sem.at[source], over).wait_recv()
            send(sums, back, s_sem, r_sem, step).wait_send()
        cross(to).wait_send()
    cross(me.c).wait_send()

    @pl.when(inside)
    def _():
        out_send(1 - me.k, True).wait_send()
        remote(out_pair.at[0], oland.at[1 - me.s], os.at[0], orecv.at[1 - me.s], over).wait_recv()
        out_back[...] = out_pair[me.k].astype(F32) + oland[1 - me.s].astype(F32)

    @pl.when(jnp.logical_not(inside))
    def _():
        out_send(me.k, False).wait_send()
        out_send(1 - me.k, True).wait_send()
        for half in range(2):
            remote(out_pair.at[0], oland.at[half], os.at[0], orecv.at[half], over).wait_recv()
        out_back[...] = oland[0].astype(F32) + oland[1].astype(F32)


def give_back(hidden, down_w, qkv, gate_up, gate_up_other, out_pair):
    tokens, model = hidden.shape[1], down_w.shape[1]
    block = lambda array: pltpu.VMEM(array.shape[1:], LOW)
    return pl.pallas_call(
        return_kernel,
        out_shape=[
            jax.ShapeDtypeStruct((tokens, model), F32),
            jax.ShapeDtypeStruct(qkv.shape[1:], LOW),
            jax.ShapeDtypeStruct(gate_up.shape[1:], LOW),
            jax.ShapeDtypeStruct(out_pair.shape[1:], F32),
        ],
        in_specs=[IN_VMEM] * 6,
        out_specs=[IN_VMEM] * 4,
        scratch_shapes=Scatter.scratch(tokens, model)
        + [block(qkv), block(qkv)]
        + [DMA((16,))] * 4
        + [block(gate_up)]
        + [DMA((16,))] * 2
        + [pltpu.VMEM(out_pair.shape, LOW), DMA((2,)), DMA((2,))],
        compiler_params=params(5),
    )(hidden, down_w, qkv, gate_up, gate_up_other, out_pair)


def norm_back(values, scale, weighted):
    inner = jnp.mean(values * weighted, axis=-1, keepdims=True)
    return scale * weighted - values * (scale * scale * scale * inner)


def scale_of(values):
    return lax.rsqrt(jnp.mean(values * values, axis=-1, keepdims=True) + norm_eps)


def move_tokens_step(
    layer_in,
    valid_len,
    norm1_gain,
    w_query,
    w_key,
    w_value,
    w_out,
    norm2_gain,
    w_gate,
    w_up,
    w_down,
    cotangent,
):
    local_rows, local_seqs, model = layer_in.shape
    strip = local_rows // 2
    width = model // HEADS
    cp_devices = 16
    tokens = local_rows * local_seqs
    every = cp_devices * tokens
    shift = math.log(cp_devices * local_rows)
    weight_rows = w_gate.shape[0]
    gain_one = norm1_gain.astype(F32)[:, None]
    gain_two = norm2_gain.astype(F32)[:, None]

    def by_seq(values):
        return values.transpose(1, 0, 2).reshape(tokens, model)

    def by_row(values):
        return values.reshape(local_seqs, local_rows, model).transpose(1, 0, 2)

    def head_blocks(weight):
        scaled = (weight.astype(F32) * gain_one).astype(LOW)
        blocks = scaled.reshape(weight_rows, 2, HEADS // 2, width).transpose(2, 1, 0, 3)
        return blocks.reshape(HEADS, weight_rows, width)

    def unit_blocks(weight):
        scaled = (weight.astype(F32) * gain_two).astype(LOW)
        blocks = scaled.reshape(weight_rows, 2, cp_devices, -1).transpose(2, 0, 1, 3)
        return blocks.reshape(cp_devices, weight_rows, -1)

    qkv_blocks = jnp.concatenate([head_blocks(w) for w in (w_query, w_key, w_value)], axis=2)
    gate_up_blocks = jnp.concatenate([unit_blocks(w) for w in (w_gate, w_up)], axis=2)
    inputs = by_seq(layer_in).astype(F32)
    grad_local = by_seq(cotangent)
    scale_one = scale_of(inputs)
    freqs = rope_base ** (-2.0 * jnp.arange(width // 2, dtype=F32) / width)
    place_pos = row_positions(
        jnp.arange(cp_devices * local_rows, dtype=jnp.int32), strip, cp_devices
    ).reshape(cp_devices, local_rows)
    angles = place_pos.astype(F32)[:, :, None] * freqs
    cosine, sine = jnp.cos(angles), jnp.sin(angles)
    cosine = jnp.concatenate([cosine, cosine], axis=2)
    back_sine = jnp.concatenate([sine, -sine], axis=2)

    units, grads, query, key, value, qkv_w, gate_up_own, head_out, down_other = spread(
        (inputs * scale_one).astype(LOW), grad_local, qkv_blocks, gate_up_blocks, w_out, w_down,
        cosine, back_sine,
    )
    qkv_w = qkv_w.reshape(model, 3 * width)
    head_out = head_out.reshape(width, model)
    branch, attended, gate_up_other = attend(shift, valid_len, query, key, value, head_out, gate_up_own)
    hidden_state = inputs + branch
    scale_two = scale_of(hidden_state)
    weighted_two, units_two, hidden, grad_gate_up, down_full = mlp(
        (hidden_state * scale_two).astype(LOW), grads, gate_up_own, gate_up_other, w_down, down_other
    )

    def gradient(left, right):
        return dot_left(left.reshape(every, -1), right.reshape(every, -1)).astype(LOW)

    grad_state = grad_local.astype(F32) + norm_back(hidden_state, scale_two, weighted_two)
    gate_up_grad = gradient(units_two, grad_gate_up).reshape(2, cp_devices, weight_rows, -1)
    down_grad = gradient(hidden, grads).reshape(2, -1, model)
    weighted_one, branches, grad_qkv, gate_up_grad_other, down_grad_other = attend_back(
        shift, valid_len, grad_state.astype(LOW), query, key, value, head_out, qkv_w, cosine, back_sine,
        gate_up_grad, down_grad,
    )
    in_grad = grad_state + norm_back(inputs, scale_one, weighted_one)

    seq_place = lax.axis_index("seq")
    down_back = lax.dynamic_index_in_dim(down_grad, seq_place, 0, False).astype(F32) + down_grad_other.astype(F32)
    ff_branch, qkv_back, gate_up_back, out_back = give_back(
        hidden,
        down_full.reshape(-1, model),
        gradient(units, grad_qkv).reshape(2, cp_devices, weight_rows, -1),
        gate_up_grad,
        gate_up_grad_other,
        gradient(attended, branches).reshape(2, width // 2, model),
    )
    layer_out = (hidden_state + ff_branch).astype(LOW)

    def head_rows(index):
        blocks = qkv_back[:, :, index * width : (index + 1) * width].astype(F32)
        blocks = blocks.reshape(HEADS // 2, 2, weight_rows, width).transpose(2, 1, 0, 3)
        return blocks.reshape(weight_rows, model)

    def unit_rows(index):
        half = gate_up_back.shape[2] // 2
        blocks = gate_up_back[:, :, index * half : (index + 1) * half].astype(F32)
        blocks = blocks.reshape(cp_devices, weight_rows, 2, -1).transpose(1, 2, 0, 3)
        return blocks.reshape(weight_rows, -1)

    def gain_grad(weights, grads):
        return sum(jnp.sum(w.astype(F32) * g, axis=1) for w, g in zip(weights, grads))

    heads = [head_rows(index) for index in range(3)]
    unit_grads = [unit_rows(index) for index in range(2)]
    return (
        by_row(layer_out),
        by_row(in_grad),
        gain_grad((w_query, w_key, w_value), heads),
        heads[0] * gain_one,
        heads[1] * gain_one,
        heads[2] * gain_one,
        out_back,
        gain_grad((w_gate, w_up), unit_grads),
        unit_grads[0] * gain_two,
        unit_grads[1] * gain_two,
        down_back,
    )


def solution(mesh):
    fits = mesh.shape["cp"] == HEADS and mesh.shape["seq"] == 2
    on_device = move_tokens_step if fits else gather_weights_step
    placed = (
        P("cp", "seq", None),
        P("seq"),
        P(("seq", "cp")),
        P(("seq", "cp"), None),
        P(("seq", "cp"), None),
        P(("seq", "cp"), None),
        P(("seq", "cp"), None),
        P(("seq", "cp")),
        P(("seq", "cp"), None),
        P(("seq", "cp"), None),
        P(("seq", "cp"), None),
        P("cp", "seq", None),
    )
    return jax.shard_map(
        on_device,
        mesh=mesh,
        in_specs=placed,
        out_specs=(
            P("cp", "seq", None),
            P("cp", "seq", None),
            P(("seq", "cp")),
            P(("seq", "cp"), None),
            P(("seq", "cp"), None),
            P(("seq", "cp"), None),
            P(("seq", "cp"), None),
            P(("seq", "cp")),
            P(("seq", "cp"), None),
            P(("seq", "cp"), None),
            P(("seq", "cp"), None),
        ),
        check_vma=False,
    )
```

```python
import functools
import math

import jax
import jax.numpy as jnp
from jax import lax
from jax.experimental import pallas as pl
from jax.experimental.pallas import tpu as pltpu
from jax.sharding import PartitionSpec as P

HEADS = 16


norm_eps = 1e-05
rope_base = 10000.0


def row_positions(indices, strip_rows, devices):
    owner_index = indices // (2 * strip_rows)
    within = indices % (2 * strip_rows)
    return jnp.where(
        within < strip_rows,
        owner_index * strip_rows + within,
        (2 * devices - 1 - owner_index) * strip_rows + within - strip_rows,
    )


def rotate(values, positions, num_heads):
    count_rows, model_width = values.shape
    head_width = model_width // num_heads
    half_width = head_width // 2
    freqs_table = rope_base ** (-2.0 * jnp.arange(half_width, dtype=jnp.float32) / head_width)
    angles = positions.astype(jnp.float32)[:, None] * freqs_table[None, :]
    cosine = jnp.cos(angles)[:, None, :]
    sine_table = jnp.sin(angles)[:, None, :]
    split_heads = values.reshape(count_rows, num_heads, head_width)
    former = split_heads[:, :, :half_width]
    latter = split_heads[:, :, half_width:]
    turned = jnp.concatenate(
        [former * cosine - latter * sine_table, latter * cosine + former * sine_table], axis=2
    )
    return turned.reshape(count_rows, model_width)


def norm_scale(values):
    return values * lax.rsqrt(jnp.mean(values * values, axis=-1, keepdims=True) + norm_eps)


def normed(values, gain_vector):
    return norm_scale(values) * gain_vector


def swiglu(gate_rows, up_rows):
    return jax.nn.silu(gate_rows) * up_rows


def dot_right(left, right):
    return lax.dot_general(
        left, right, (((1,), (1,)), ((), ())), preferred_element_type=jnp.float32
    )


def dot_left(left, right):
    return lax.dot_general(
        left, right, (((0,), (0,)), ((), ())), preferred_element_type=jnp.float32
    )


def split_blocks(array, block_rows):
    return array.reshape((array.shape[0] // block_rows, block_rows) + array.shape[1:])


def key_mask(query_pos, key_pos, valid_count):
    causal = key_pos[None, :] <= query_pos[:, None]
    live_keys = key_pos[None, :] < valid_count[:, None]
    return (causal[None, None, :, :] & live_keys[:, None, None, :]).astype(jnp.float32)


def scores_of(queries, key_rows, query_pos, key_pos, valid_count, score_shift):
    head_width = queries.shape[3]
    raw_scores = jnp.einsum(
        "qshd,kshd->shqk", queries, key_rows, preferred_element_type=jnp.float32
    )
    return (
        raw_scores * head_width ** (-0.5) - score_shift,
        key_mask(query_pos, key_pos, valid_count),
    )


def block_grads(queries, grad_rows, key_rows, values, query_pos, key_pos, valid_count, score_shift):
    logits, mask_table = scores_of(queries, key_rows, query_pos, key_pos, valid_count, score_shift)
    sigmoid_table = jax.nn.sigmoid(logits)
    weights_low = (sigmoid_table * mask_table).astype(jnp.bfloat16)
    grad_weights = jnp.einsum(
        "qshd,kshd->shqk", grad_rows, values, preferred_element_type=jnp.float32
    )
    grad_logits = (grad_weights * mask_table * (sigmoid_table * (1.0 - sigmoid_table))).astype(
        jnp.bfloat16
    )
    return (weights_low, grad_logits)


def make_norm_fold(normalized, pieces):
    gain_part = pieces[0].astype(jnp.float32)
    scaled = (normalized * gain_part).astype(jnp.bfloat16)
    totals = tuple(
        (
            jnp.dot(scaled, weight_piece, preferred_element_type=jnp.float32)
            for weight_piece in pieces[1:]
        )
    )
    return (gain_part,) + totals


def make_row_fold(left_rows, weight_piece):
    return jnp.dot(left_rows, weight_piece, preferred_element_type=jnp.float32)


def gather_weights_step(
    layer_in,
    valid_len,
    norm1_gain,
    w_query,
    w_key,
    w_value,
    w_out,
    norm2_gain,
    w_gate,
    w_up,
    w_down,
    cotangent,
):
    local_rows, local_seqs, model_width = layer_in.shape
    num_heads = HEADS
    head_width = model_width // num_heads
    strip_rows = local_rows // 2
    cp_devices = lax.axis_size("cp")
    cp_place = lax.axis_index("cp")
    seq_length = local_rows * cp_devices
    score_shift = math.log(seq_length)
    score_scale = head_width ** (-0.5)
    token_count = local_rows * local_seqs
    local_pos = row_positions(
        cp_place * local_rows + jnp.arange(local_rows, dtype=jnp.int32), strip_rows, cp_devices
    )
    token_pos = jnp.broadcast_to(local_pos[:, None], (local_rows, local_seqs)).reshape(token_count)
    every_pos = row_positions(jnp.arange(seq_length, dtype=jnp.int32), strip_rows, cp_devices)
    block_rows = math.gcd(seq_length, 512)
    head_shape = (local_rows, local_seqs, num_heads, head_width)
    row_shape = (local_rows, local_seqs, model_width)
    zero_heads = jnp.zeros(head_shape, jnp.float32)
    inputs = layer_in.reshape(token_count, model_width).astype(jnp.float32)
    input_norm = norm_scale(inputs)
    gain_one, query, key_proj, value = make_norm_fold(
        input_norm,
        (
            lax.all_gather(norm1_gain, ("seq", "cp"), axis=0, tiled=True),
            lax.all_gather(w_query, ("seq", "cp"), axis=0, tiled=True),
            lax.all_gather(w_key, ("seq", "cp"), axis=0, tiled=True),
            lax.all_gather(w_value, ("seq", "cp"), axis=0, tiled=True),
        ),
    )
    normed_one = (input_norm * gain_one).astype(jnp.bfloat16)
    query_low = rotate(query, token_pos, num_heads).astype(jnp.bfloat16)
    key_low = rotate(key_proj, token_pos, num_heads).astype(jnp.bfloat16)
    value_low = value.astype(jnp.bfloat16)
    query_heads = query_low.reshape(head_shape)
    key_local = key_low.reshape(row_shape)
    value_local = value_low.reshape(row_shape)
    key_piece = lax.all_gather(key_local, "cp", axis=0, tiled=True)
    value_piece = lax.all_gather(value_local, "cp", axis=0, tiled=True)
    piece_rows = key_piece.shape[0]
    piece_block = math.gcd(piece_rows, 512)
    piece_pos = row_positions(jnp.arange(piece_rows, dtype=jnp.int32), strip_rows, cp_devices)

    def scan_step(partial_sum, block_items):
        key_block, value_block, block_pos = block_items
        logits, mask_table = scores_of(
            query_heads,
            key_block.reshape(piece_block, local_seqs, num_heads, head_width),
            local_pos,
            block_pos,
            valid_len,
            score_shift,
        )
        weights_low = (jax.nn.sigmoid(logits) * mask_table).astype(jnp.bfloat16)
        added = jnp.einsum(
            "shqk,kshd->qshd",
            weights_low,
            value_block.reshape(piece_block, local_seqs, num_heads, head_width),
            preferred_element_type=jnp.float32,
        )
        return (partial_sum + added, None)

    result, _ = lax.scan(
        scan_step,
        zero_heads,
        (
            split_blocks(key_piece, piece_block),
            split_blocks(value_piece, piece_block),
            split_blocks(piece_pos, piece_block),
        ),
    )
    attended_low = result.reshape(token_count, model_width).astype(jnp.bfloat16)
    attn_branch = make_row_fold(
        attended_low, lax.all_gather(w_out, ("seq", "cp"), axis=0, tiled=True)
    )
    hidden_state = inputs + attn_branch
    hidden_norm = norm_scale(hidden_state)
    gain_two, gate_rows, up_rows = make_norm_fold(
        hidden_norm,
        (
            lax.all_gather(norm2_gain, ("seq", "cp"), axis=0, tiled=True),
            lax.all_gather(w_gate, ("seq", "cp"), axis=0, tiled=True),
            lax.all_gather(w_up, ("seq", "cp"), axis=0, tiled=True),
        ),
    )
    normed_two = (hidden_norm * gain_two).astype(jnp.bfloat16)
    hidden_units = swiglu(gate_rows, up_rows).astype(jnp.bfloat16)
    ff_branch = make_row_fold(
        hidden_units, lax.all_gather(w_down, ("seq", "cp"), axis=0, tiled=True)
    )
    layer_out = (hidden_state + ff_branch).astype(jnp.bfloat16).reshape(row_shape)
    grad_out = cotangent.reshape(token_count, model_width)
    gate_all, up_all, down_all = (
        lax.all_gather(w_gate, ("seq", "cp"), axis=0, tiled=True),
        lax.all_gather(w_up, ("seq", "cp"), axis=0, tiled=True),
        lax.all_gather(w_down, ("seq", "cp"), axis=0, tiled=True),
    )
    grad_hidden = dot_right(grad_out, down_all)
    _, pull_swiglu = jax.vjp(swiglu, gate_rows, up_rows)
    grad_gate, grad_up = pull_swiglu(grad_hidden)
    grad_gate_low = grad_gate.astype(jnp.bfloat16)
    grad_up_low = grad_up.astype(jnp.bfloat16)
    grad_norm_two = dot_right(grad_gate_low, gate_all) + dot_right(grad_up_low, up_all)
    _, pull_two = jax.vjp(normed, hidden_state, gain_two)
    grad_from_two, gain_two_term = pull_two(grad_norm_two)
    ff_grads = (
        lax.psum_scatter(gain_two_term, ("seq", "cp"), scatter_dimension=0, tiled=True),
        lax.psum_scatter(
            dot_left(normed_two, grad_gate_low), ("seq", "cp"), scatter_dimension=0, tiled=True
        ),
        lax.psum_scatter(
            dot_left(normed_two, grad_up_low), ("seq", "cp"), scatter_dimension=0, tiled=True
        ),
        lax.psum_scatter(
            dot_left(hidden_units, grad_out), ("seq", "cp"), scatter_dimension=0, tiled=True
        ),
    )
    grad_state = grad_out.astype(jnp.float32) + grad_from_two
    query_all, key_all, value_all, out_all = (
        lax.all_gather(w_query, ("seq", "cp"), axis=0, tiled=True),
        lax.all_gather(w_key, ("seq", "cp"), axis=0, tiled=True),
        lax.all_gather(w_value, ("seq", "cp"), axis=0, tiled=True),
        lax.all_gather(w_out, ("seq", "cp"), axis=0, tiled=True),
    )
    grad_branch_low = grad_state.astype(jnp.bfloat16)
    grad_attended_low = dot_right(grad_branch_low, out_all).astype(jnp.bfloat16)
    grad_heads = grad_attended_low.reshape(head_shape)
    key_heads_local = key_local.reshape(head_shape)
    value_heads_local = value_local.reshape(head_shape)
    keys_every, values_every, queries_every, grads_every = (
        lax.all_gather(key_local, "cp", axis=0, tiled=True),
        lax.all_gather(value_local, "cp", axis=0, tiled=True),
        lax.all_gather(query_low.reshape(row_shape), "cp", axis=0, tiled=True),
        lax.all_gather(grad_attended_low.reshape(row_shape), "cp", axis=0, tiled=True),
    )

    def key_step(partial_sums, block_items):
        query_block, grad_block_rows, block_pos = block_items
        query_part = query_block.reshape(block_rows, local_seqs, num_heads, head_width)
        grad_part = grad_block_rows.reshape(block_rows, local_seqs, num_heads, head_width)
        weights_low, grad_logits = block_grads(
            query_part,
            grad_part,
            key_heads_local,
            value_heads_local,
            block_pos,
            local_pos,
            valid_len,
            score_shift,
        )
        key_added = jnp.einsum(
            "shqk,qshd->kshd", grad_logits, query_part, preferred_element_type=jnp.float32
        )
        value_added = jnp.einsum(
            "shqk,qshd->kshd", weights_low, grad_part, preferred_element_type=jnp.float32
        )
        return ((partial_sums[0] + key_added, partial_sums[1] + value_added), None)

    (key_sum, value_sum), _ = lax.scan(
        key_step,
        (zero_heads, zero_heads),
        (
            split_blocks(queries_every, block_rows),
            split_blocks(grads_every, block_rows),
            split_blocks(every_pos, block_rows),
        ),
    )
    grad_key_rot = key_sum.reshape(token_count, model_width) * score_scale
    grad_value_sum = value_sum.reshape(token_count, model_width)

    def query_step(partial_sum, block_items):
        key_block, value_block, block_pos = block_items
        key_heads = key_block.reshape(block_rows, local_seqs, num_heads, head_width)
        _, grad_logits = block_grads(
            query_heads,
            grad_heads,
            key_heads,
            value_block.reshape(block_rows, local_seqs, num_heads, head_width),
            local_pos,
            block_pos,
            valid_len,
            score_shift,
        )
        added = jnp.einsum(
            "shqk,kshd->qshd", grad_logits, key_heads, preferred_element_type=jnp.float32
        )
        return (partial_sum + added, None)

    query_sum, _ = lax.scan(
        query_step,
        zero_heads,
        (
            split_blocks(keys_every, block_rows),
            split_blocks(values_every, block_rows),
            split_blocks(every_pos, block_rows),
        ),
    )
    grad_query_rot = query_sum.reshape(token_count, model_width) * score_scale
    grad_query_low = rotate(grad_query_rot, -token_pos, num_heads).astype(jnp.bfloat16)
    grad_key_low = rotate(grad_key_rot, -token_pos, num_heads).astype(jnp.bfloat16)
    grad_value_low = grad_value_sum.astype(jnp.bfloat16)
    grad_norm_one = (
        dot_right(grad_query_low, query_all)
        + dot_right(grad_key_low, key_all)
        + dot_right(grad_value_low, value_all)
    )
    _, pull_one = jax.vjp(normed, inputs, gain_one)
    grad_from_one, gain_one_term = pull_one(grad_norm_one)
    in_grad = (grad_state + grad_from_one).reshape(row_shape)
    attn_grads = (
        lax.psum_scatter(gain_one_term, ("seq", "cp"), scatter_dimension=0, tiled=True),
        lax.psum_scatter(
            dot_left(normed_one, grad_query_low), ("seq", "cp"), scatter_dimension=0, tiled=True
        ),
        lax.psum_scatter(
            dot_left(normed_one, grad_key_low), ("seq", "cp"), scatter_dimension=0, tiled=True
        ),
        lax.psum_scatter(
            dot_left(normed_one, grad_value_low), ("seq", "cp"), scatter_dimension=0, tiled=True
        ),
        lax.psum_scatter(
            dot_left(attended_low, grad_branch_low), ("seq", "cp"), scatter_dimension=0, tiled=True
        ),
    )
    return (
        layer_out,
        in_grad,
        attn_grads[0],
        attn_grads[1],
        attn_grads[2],
        attn_grads[3],
        attn_grads[4],
        ff_grads[0],
        ff_grads[1],
        ff_grads[2],
        ff_grads[3],
    )


MESH = pl.DeviceIdType.MESH
DMA = pltpu.SemaphoreType.DMA
LOW = jnp.bfloat16
F32 = jnp.float32
ANYWHERE = pl.BlockSpec(memory_space=pl.ANY)
IN_VMEM = pl.BlockSpec(memory_space=pltpu.VMEM)
IN_SMEM = pl.BlockSpec(memory_space=pltpu.SMEM)


class Place:
    def __init__(self):
        self.s = lax.axis_index("seq")
        self.c = lax.axis_index("cp")
        self.z = self.c // 4
        self.y = (self.c // 2) % 2
        self.k = self.c % 2

    def at(self, z, y, k):
        return z * 4 + y * 2 + k

    def device(self, place):
        return (self.s, place)


def pick(z, table):
    value = jnp.int32(table[0])
    for index in range(1, 4):
        value = jnp.where(z == index, jnp.int32(table[index]), value)
    return value


NEAREST = ((1, 0, 1, 2), (2, 2, 3, 1), (3, 3, 0, 0))
FARTHEST = ((3, 3, 0, 0), (2, 2, 3, 1), (1, 0, 1, 2))


def remote(source, target, send, recv, device):
    return pltpu.make_async_remote_copy(
        src_ref=source,
        dst_ref=target,
        send_sem=send,
        recv_sem=recv,
        device_id=device,
        device_id_type=MESH,
    )


def hail(device):
    pl.semaphore_signal(
        pltpu.get_barrier_semaphore(), inc=1, device_id=device, device_id_type=MESH
    )


def greet(me, over_seq=False):
    hail((me.s, me.at(me.z, 1 - me.y, me.k)))
    hail((me.s, me.at(me.z, me.y, 1 - me.k)))

    @pl.when(me.z < 3)
    def _():
        hail((me.s, me.at(me.z + 1, me.y, me.k)))

    @pl.when(me.z > 0)
    def _():
        hail((me.s, me.at(me.z - 1, me.y, me.k)))

    ends = (me.z == 0).astype(jnp.int32) + (me.z == 3).astype(jnp.int32)
    if over_seq:
        hail((1 - me.s, me.c))
    pl.semaphore_wait(pltpu.get_barrier_semaphore(), 4 - ends + (1 if over_seq else 0))


def greet_plane(me):
    for step in range(1, 16):
        hail((me.s, (me.c + step) % 16))
    hail((1 - me.s, me.c))
    hail((1 - me.s, me.at(me.z, me.y, 1 - me.k)))
    pl.semaphore_wait(pltpu.get_barrier_semaphore(), 17)


class Gather:
    def __init__(self, me, views, early, z_sem, far_sem, y_sem, k_sem, recv):
        self.me, self.views, self.early = me, views, early
        self.z_sem, self.far_sem, self.y_sem, self.k_sem, self.recv = z_sem, far_sem, y_sem, k_sem, recv

    count = 5

    @staticmethod
    def sems(pieces):
        return [DMA((pieces * n,)) for n in (5, 5, 4, 8, 16)]

    def copy(self, piece, place, sem, device):
        block = self.views[piece](place)
        return remote(block, block, sem, self.recv.at[piece * 16 + place], device)

    def arrived(self, piece, place):
        self.copy(piece, place, self.k_sem.at[0], self.me.device(self.me.c)).wait_recv()

    def line(self, index):
        return self.me.z if index == 0 else pick(self.me.z, NEAREST[index - 1])

    def along(self, piece, place, index, up, sems):
        me = self.me
        target = jnp.minimum(me.c + 4, 12 + me.c % 4) if up else jnp.maximum(me.c - 4, me.c % 4)
        return self.copy(piece, place, sems.at[piece * 5 + index], me.device(target))

    def across(self, piece, place, index):
        me = self.me
        target = me.at(me.z, 1 - me.y, me.k)
        return self.copy(piece, place, self.y_sem.at[piece * 4 + index], me.device(target))

    def partner(self, piece, place, index):
        me = self.me
        target = me.at(me.z, me.y, 1 - me.k)
        return self.copy(piece, place, self.k_sem.at[piece * 8 + index], me.device(target))

    def spread_along(self, piece, place, index, sems, go):
        me, z = self.me, self.line(index)
        if index == 0:

            @pl.when(me.z < 3)
            def _():
                go(self.along(piece, place, 0, True, sems))

            @pl.when(me.z > 0)
            def _():
                go(self.along(piece, place, 4, False, sems))
        else:

            @pl.when((z < me.z) & (me.z < 3))
            def _():
                go(self.along(piece, place, index, True, sems))

            @pl.when((z > me.z) & (me.z > 0))
            def _():
                go(self.along(piece, place, index, False, sems))

    def send_near(self, piece, index, go=lambda copy: copy.start()):
        me = self.me
        place = me.at(self.line(index), me.y, me.k)
        if index == 0 or not self.early[piece]:
            go(self.across(piece, place, index))
        self.spread_along(piece, place, index, self.z_sem, go)
        go(self.partner(piece, place, index))

    def send_far(self, piece, index, go=lambda copy: copy.start()):
        me = self.me
        place = me.at(self.line(index), 1 - me.y, me.k)
        if self.early[piece]:
            self.spread_along(piece, place, index, self.far_sem, go)
        go(self.partner(piece, place, 4 + index))

    def begin(self):
        for piece in range(len(self.views)):
            self.send_near(piece, 0)

    def round(self, index):
        me = self.me
        for piece in range(len(self.views)):
            if index < 3:
                self.arrived(piece, me.at(self.line(index + 1), me.y, me.k))
                self.send_near(piece, index + 1)
            self.arrived(piece, me.at(self.line(index), 1 - me.y, me.k))
            self.send_far(piece, index)

    def settle(self, z, y):
        for piece in range(len(self.views)):
            self.arrived(piece, self.me.at(z, y, 1 - self.me.k))

    def run(self, consume):
        me = self.me
        self.begin()
        waiting = [(me.z, me.y)]
        for index in range(4):
            self.round(index)
            ready, waiting = waiting, []
            if index < 3:
                waiting.append((self.line(index + 1), me.y))
            waiting.append((self.line(index), 1 - me.y))
            for z, y in ready:
                self.settle(z, y)
                consume(z * 2 + y)
        for z, y in waiting:
            self.settle(z, y)
            consume(z * 2 + y)

    def finish(self):
        for piece in range(len(self.views)):
            for index in range(4):
                self.send_near(piece, index, lambda copy: copy.wait_send())
                self.send_far(piece, index, lambda copy: copy.wait_send())


class Scatter:
    pieces = 2

    def __init__(self, me, scratch):
        self.me = me
        (self.k_out, self.k_in, self.y_out, self.y_in, self.z_out, self.z_in, self.mine, self.kept) = scratch[:8]
        (self.ks, self.kr, self.ys, self.yr, self.zs, self.zl, self.zr) = scratch[8:15]

    count = 15

    @classmethod
    def scratch(cls, rows, width):
        n = cls.pieces
        part = width // n
        low = [pltpu.VMEM((n * count, rows, part), LOW) for count in (8, 8, 4, 4, 3, 8)]
        full = [pltpu.VMEM((n * count, rows, part), F32) for count in (1, 4)]
        return low + full + [DMA((n * count,)) for count in (8, 8, 4, 4, 3, 4, 4)]

    def partner(self, slot):
        me = self.me
        target = me.device(me.at(me.z, me.y, 1 - me.k))
        return remote(self.k_out.at[slot], self.k_in.at[slot], self.ks.at[slot], self.kr.at[slot], target)

    def across(self, z, index, piece):
        me, n = self.me, self.pieces
        out, land = index * n + piece, z * n + piece
        target = me.device(me.at(me.z, 1 - me.y, me.k))
        return remote(self.y_out.at[out], self.y_in.at[land], self.ys.at[out], self.yr.at[land], target)

    def along(self, z, index, piece, up):
        me, n = self.me, self.pieces
        out, land = index * n + piece, z * n + piece
        target = jnp.minimum(me.c + 4, 12 + me.c % 4) if up else jnp.maximum(me.c - 4, me.c % 4)
        into = self.z_in.at[land if up else 4 * n + land]
        sem = (self.zl if up else self.zr).at[land]
        return remote(self.z_out.at[out], into, self.zs.at[out], sem, me.device(target))

    def line(self, index):
        return self.me.z if index == 3 else pick(self.me.z, FARTHEST[index])

    def emit(self, produce, z, y, piece, slot, keep):
        part = 512
        rows, width = keep.shape

        @pl.loop(0, width // part)
        def _(index):
            here = pl.ds(pl.multiple_of(index * part, part), part)
            start = pl.multiple_of(piece * width + index * part, part)
            value = produce(self.me.at(z, y, 0), pl.ds(start, part))
            self.k_out[slot, :, here] = value[:rows].astype(LOW)
            keep[:, here] = value[rows:]

        self.partner(slot).start()

    def add(self, target, base, *blocks):
        part = 512

        @pl.loop(0, target.shape[-1] // part)
        def _(index):
            here = pl.ds(pl.multiple_of(index * part, part), part)
            value = base[:, here]
            for block in blocks:
                value = value + block[:, here].astype(F32)
            target[:, here] = value.astype(target.dtype)

    def run(self, prepare, produce, finish, fillers=()):
        me, n = self.me, self.pieces
        fillers = list(fillers)
        steps = [(index, piece) for index in range(4) for piece in range(n)]
        for number in range(len(steps) + 1):
            if number < len(steps):
                index, piece = steps[number]
                z = self.line(index)
                if prepare is not None and piece == 0:
                    prepare(z * 2 + 1 - me.y)
                self.emit(produce, z, 1 - me.y, piece, number, self.mine.at[number % 2])
            if number > 0:
                index, piece = steps[number - 1]
                self.partner(number - 1).wait_recv()
                self.add(self.y_out.at[number - 1], self.mine.at[(number - 1) % 2], self.k_in.at[number - 1])
                self.across(self.line(index), index, piece).start()

        def own(number):
            index, piece = steps[number]
            z = self.line(index)
            if prepare is not None and piece == 0:
                prepare(z * 2 + me.y)
            self.emit(produce, z, me.y, piece, 4 * n + number, self.kept.at[number])

        ahead = n
        for number in range(ahead):
            own(number)
        for number in range(len(steps)):
            if number + ahead < len(steps):
                own(number + ahead)
            for _ in range(-(-len(fillers) // (len(steps) - number))):
                fillers.pop(0)()
            self.collect(number, *steps[number], finish)

    def collect(self, number, index, piece, finish):
        me, n = self.me, self.pieces
        z = self.line(index)
        slot, land = 4 * n + number, z * n + piece
        kept = self.kept.at[number]
        self.partner(slot).wait_recv()
        self.across(z, index, piece).wait_recv()
        self.add(kept, kept, self.k_in.at[slot], self.y_in.at[land])
        if index < 3:
            from_below, from_above = (z > me.z) & (me.z > 0), (z < me.z) & (me.z < 3)
        else:
            from_below, from_above = me.z > 0, me.z < 3

        @pl.when(from_below)
        def _():
            self.along(z, 0, piece, True).wait_recv()
            self.add(kept, kept, self.z_in.at[land])

        @pl.when(from_above)
        def _():
            self.along(z, 0, piece, False).wait_recv()
            self.add(kept, kept, self.z_in.at[4 * n + land])

        if index < 3:
            self.add(self.z_out.at[number], kept)

            @pl.when(z > me.z)
            def _():
                self.along(z, index, piece, True).start()

            @pl.when(z < me.z)
            def _():
                self.along(z, index, piece, False).start()
        else:
            finish(piece, kept)

    def drain(self):
        me, n = self.me, self.pieces
        for slot in range(8 * n):
            self.partner(slot).wait_send()
        for index in range(4):
            z = self.line(index)
            for piece in range(n):
                self.across(z, index, piece).wait_send()
                if index < 3:

                    @pl.when(z > me.z)
                    def _():
                        self.along(z, index, piece, True).wait_send()

                    @pl.when(z < me.z)
                    def _():
                        self.along(z, index, piece, False).wait_send()


def write_total(total_out):
    def finish(piece, kept):
        width = kept.shape[-1]
        total_out[:, piece * width : (piece + 1) * width] = kept[...]

    return finish


def leave(stage, parts, sems):
    copies = []

    def run(number, work, place):
        if number >= 2:
            copies[number - 2].wait()
        slot = stage.at[number % 2]
        work(slot)
        copies.append(pltpu.make_async_copy(slot, place, sems.at[number]))
        copies[number].start()

    def end():
        for copy in copies[-2:]:
            copy.wait()

    return [functools.partial(run, number, *part) for number, part in enumerate(parts)], end


def own_last(me, block, first):
    return jnp.concatenate([block[first + 1 - me.k], block[first + me.k]], axis=0)


def params(collective_id):
    return pltpu.CompilerParams(
        collective_id=collective_id, has_side_effects=True, vmem_limit_bytes=60 << 20
    )


def turn(me, step):
    dz, dy, dk = step // 4, (step // 2) % 2, step % 2
    to = me.at((me.z + dz) % 4, (me.y + dy) % 2, (me.k + dk) % 2)
    source = me.at((me.z + 4 - dz) % 4, (me.y + dy) % 2, (me.k + dk) % 2)
    return to, source


def cuts(rows):
    return ((0, rows // 2), (rows // 2, rows * 7 // 8 - rows // 2), (rows * 7 // 8, rows // 8))


EARLY = [False, False, True]


def pieces_of(array):
    return [
        lambda place, start=start, size=size: array.at[place, pl.ds(start, size)]
        for start, size in cuts(array.shape[1])
    ]


def spread_kernel(
    unit, grad, w_query, w_key, w_value, w_gate, w_up, gain_one, gain_two, out_w, down, cosine, sine,
    units, grads, query, key, value, qkv_full, gate_up_half, out_all, down_other, *scratch
):
    gather_sems = scratch[: Gather.count]
    (qs, qr, qxs, qxr, ps, pr, os, ox, orecv, local, dsem, leave, units_here, grads_here, qkv_all, qkv, gate_up) = scratch[Gather.count :]
    me = Place()
    own = [
        pltpu.make_async_copy(unit, units_here.at[me.c], local.at[0]),
        pltpu.make_async_copy(grad, grads_here.at[me.c], local.at[1]),
        pltpu.make_async_copy(qkv.at[me.c], qkv_all.at[me.s, me.c], local.at[2]),
        pltpu.make_async_copy(gate_up.at[me.c], gate_up_half.at[me.c], local.at[3]),
    ]
    own[0].start()
    own[1].start()
    greet_plane(me)
    over = (1 - me.s, me.c)
    tokens = unit.shape[0]
    rows = tokens // 2
    gather = Gather(me, pieces_of(units_here) + pieces_of(grads_here), [False] * 6, *gather_sems)
    down_copy = remote(down, down_other, dsem.at[0], dsem.at[1], over)

    def send_qkv(step):
        to, _ = turn(me, step)
        return remote(qkv.at[to], qkv_all.at[me.s, me.c], qs.at[step], qr.at[me.c], (me.s, to))

    def send_gate_up(step):
        to, _ = turn(me, step)
        return remote(gate_up.at[to], gate_up_half.at[me.c], ps.at[step], pr.at[me.c], (me.s, to))

    def forward(source):
        block = qkv_all.at[me.s, source]
        return remote(block, block, qxs.at[source], qxr.at[source], over)

    holder = me.at(me.z, me.y, me.s)
    out_local = pltpu.make_async_copy(out_w, out_all.at[me.k], local.at[4])
    out_near = remote(out_w, out_all.at[me.k], os.at[0], orecv.at[me.k], (me.s, me.at(me.z, me.y, 1 - me.k)))
    out_far = remote(out_w, out_all.at[me.k], ox, orecv.at[me.k], (1 - me.s, holder))

    for copy in own[:2]:
        copy.wait()
    gather.begin()
    width = query.shape[3]
    weight_rows = w_query.shape[0]
    one = jnp.broadcast_to(gain_one[...], (weight_rows, width))
    for place in range(16):
        head = place // 2 + 8 * (place % 2)
        for index, weight in enumerate((w_query, w_key, w_value)):
            block = weight[:, head * width : (head + 1) * width].astype(F32) * one
            qkv[place, :, index * width : (index + 1) * width] = block.astype(LOW)
    own[2].start()
    for step in range(1, 16):
        send_qkv(step).start()
    units_of = gate_up.shape[2] // 4
    two = jnp.broadcast_to(gain_two[...], (weight_rows, units_of))
    for place in range(16):
        for index, weight in enumerate((w_gate, w_up)):
            for half in range(2):
                start = (half * 16 + place) * units_of
                block = weight[:, start : start + units_of].astype(F32) * two
                start = (2 * index + half) * units_of
                gate_up[place, :, start : start + units_of] = block.astype(LOW)
    own[3].start()
    own[2].wait()
    forward(me.c).start()
    out_far.start()

    @pl.when(holder == me.c)
    def _():
        out_local.start()

    @pl.when(holder != me.c)
    def _():
        out_near.start()

    down_copy.start()
    leaving = []

    def write_out(z, y):
        pair = z * 2 + y
        both = pl.ds(2 * pair, 2)
        number = len(leaving)
        for index, (here, there) in enumerate(((units_here, units), (grads_here, grads))):
            copy = pltpu.make_async_copy(here.at[both], there.at[both], leave.at[2 * number + index])
            copy.start()
            leaving.append(copy)

    def turned(values, both):
        swapped = pltpu.roll(values, width // 2, axis=1)
        place_cos = cosine[both].reshape(2 * rows, width)
        place_sin = sine[both].reshape(2 * rows, width)
        return (values * place_cos - swapped * place_sin).astype(LOW).reshape(2, rows, width)

    def project(z, y):
        both = pl.ds(2 * (z * 2 + y), 2)
        model = unit.shape[1]
        weights = qkv_all[...].reshape(model, 3 * width)
        for seq in range(2):
            block = units_here[both, seq * rows : (seq + 1) * rows].reshape(2 * rows, model)
            result = jnp.dot(block, weights, preferred_element_type=F32)
            query[both, seq] = turned(result[:, :width], both)
            key[both, seq] = turned(result[:, width : 2 * width], both)
            value[both, seq] = result[:, 2 * width :].astype(LOW).reshape(2, rows, width)

    steps = list(range(1, 16))
    waiting, ready = [(me.z, me.y)], []
    for index in range(4):
        for step in steps[4 * index : 4 * index + 4]:
            send_gate_up(step).start()
        gather.round(index)
        for z, y in waiting:
            gather.settle(z, y)
            write_out(z, y)
        ready += waiting
        waiting = [(gather.line(index), 1 - me.y)]
        if index < 3:
            waiting.append((gather.line(index + 1), me.y))
        if index == 1:
            for step in steps:
                _, source = turn(me, step)
                remote(qkv.at[0], qkv_all.at[me.s, source], qs.at[step], qr.at[source], over).wait_recv()
                forward(source).start()
        if index == 2:
            for source in range(16):
                forward(source).wait_send()
                forward(source).wait_recv()
            leave_qkv = pltpu.make_async_copy(qkv_all, qkv_full, local.at[5])
            leave_qkv.start()
        if index >= 2:
            for z, y in ready:
                project(z, y)
            ready = []
    for z, y in waiting:
        gather.settle(z, y)
        write_out(z, y)
        project(z, y)
    gather.finish()
    own[3].wait()
    leave_qkv.wait()
    for copy in leaving:
        copy.wait()
    for step in steps:
        _, source = turn(me, step)
        send_qkv(step).wait_send()
        send_gate_up(step).wait_send()
        remote(gate_up.at[0], gate_up_half.at[source], ps.at[step], pr.at[source], over).wait_recv()
    out_far.wait_send()
    down_copy.wait()

    @pl.when(holder == me.c)
    def _():
        out_local.wait()
        remote(out_w, out_all.at[1 - me.k], ox, orecv.at[1 - me.k], over).wait_recv()

    @pl.when(holder != me.c)
    def _():
        out_near.wait_send()
        for half in range(2):
            remote(out_w, out_all.at[half], ox, orecv.at[half], over).wait_recv()


def spread(unit, grad, w_query, w_key, w_value, w_gate, w_up, gain_one, gain_two, out_w, down, cosine, sine):
    def shape(lead, array):
        return jax.ShapeDtypeStruct(lead + array.shape, array.dtype)

    tokens, model = unit.shape
    width = model // 16
    weight_rows = w_query.shape[0]
    qkv = (weight_rows, 3 * width)
    gate_up = (weight_rows, 2 * w_gate.shape[1] // 16)
    heads = jax.ShapeDtypeStruct((16, 2, tokens // 2, width), LOW)
    return pl.pallas_call(
        spread_kernel,
        out_shape=[
            shape((16,), unit),
            shape((16,), grad),
            heads,
            heads,
            heads,
            jax.ShapeDtypeStruct((2, 16) + qkv, LOW),
            jax.ShapeDtypeStruct((16,) + gate_up, LOW),
            shape((2,), out_w),
            shape((), down),
        ],
        in_specs=[ANYWHERE] * 2 + [IN_VMEM] * 7 + [ANYWHERE] * 2 + [IN_VMEM] * 2,
        out_specs=[ANYWHERE] * 2 + [IN_VMEM] * 3 + [ANYWHERE] * 4,
        scratch_shapes=Gather.sems(6)
        + [DMA((16,))] * 6
        + [DMA((1,)), DMA, DMA((2,)), DMA((6,)), DMA((2,)), DMA((32,))]
        + [pltpu.VMEM((16, tokens, model), LOW)] * 2
        + [pltpu.VMEM((2, 16) + qkv, LOW), pltpu.VMEM((16,) + qkv, LOW), pltpu.VMEM((16,) + gate_up, LOW)],
        compiler_params=params(0),
    )(unit, grad, w_query, w_key, w_value, w_gate, w_up, gain_one, gain_two, out_w, down, cosine, sine)


def row_place(place, row, strip):
    return jnp.where(row < strip, place * strip + row, (31 - place) * strip + row - strip)


def key_places(strip):
    index = lax.broadcasted_iota(jnp.int32, (1, 32 * strip), 1)
    return row_place(index // (2 * strip), index % (2 * strip), strip)


def query_places(pair, strip):
    index = lax.broadcasted_iota(jnp.int32, (4 * strip, 1), 0)
    return row_place(2 * pair + index // (2 * strip), index % (2 * strip), strip)


def of_pair(block, pair, seq):
    rows, width = block.shape[2:]
    return block[pl.ds(2 * pair, 2), seq].reshape(2 * rows, width)


def attend_kernel(
    shift, valid, query, key, value, out_w, gate_up, total_out, attended, gate_up_other, *scratch
):
    me = Place()
    greet(me, over_seq=True)
    over = (1 - me.s, me.c)
    sems = scratch[Scatter.count]
    swaps = [
        remote(gate_up, gate_up_other, sems.at[0], sems.at[1], over),
    ]
    for copy in swaps:
        copy.start()
    scatter = Scatter(me, scratch)
    rows, width = query.shape[2], query.shape[3]
    strip = rows // 2
    length = rows * 16
    scale = width ** (-0.5)

    def prepare(pair):
        where = query_places(pair, strip)
        keys_at = key_places(strip)
        for seq in range(2):
            keys = key[:, seq].reshape(length, width)
            values = value[:, seq].reshape(length, width)
            logits = dot_right(of_pair(query, pair, seq), keys) * scale - shift
            live = (keys_at <= where) & (keys_at < valid[seq])
            weights = jnp.where(live, jax.nn.sigmoid(logits), 0.0).astype(LOW)
            attended[pl.ds(2 * pair, 2), pl.ds(seq * rows, rows)] = (
                jnp.dot(weights, values, preferred_element_type=F32).astype(LOW).reshape(2, rows, width)
            )

    def produce(first, columns):
        return jnp.dot(own_last(me, attended, first), out_w[:, columns], preferred_element_type=F32)

    scatter.run(prepare, produce, write_total(total_out))
    scatter.drain()
    for copy in swaps:
        copy.wait()


def attend(shift, valid, query, key, value, out_w, gate_up):
    rows, width = query.shape[2:]
    tokens, model = 2 * rows, out_w.shape[1]
    return pl.pallas_call(
        functools.partial(attend_kernel, shift),
        out_shape=[
            jax.ShapeDtypeStruct((tokens, model), F32),
            jax.ShapeDtypeStruct((16, tokens, width), LOW),
            jax.ShapeDtypeStruct(gate_up.shape, LOW),
        ],
        in_specs=[IN_SMEM] + [IN_VMEM] * 4 + [ANYWHERE],
        out_specs=[IN_VMEM] * 2 + [ANYWHERE],
        scratch_shapes=Scatter.scratch(tokens, model) + [DMA((2,))],
        compiler_params=params(1),
    )(valid, query, key, value, out_w, gate_up)


def mlp_kernel(
    unit, grads, gate_up_own, gate_up_other, down_own, down_other,
    total_out, hidden, down_full, gate_up_grad, down_grad, *scratch
):
    me = Place()
    tokens, model = unit.shape
    width = hidden.shape[2]
    units, grad_gate_up, gate_up_full, grads_here, stage, leaving, local = scratch[-7:]
    gather = Gather(me, pieces_of(units), EARLY, *scratch[Scatter.count : Scatter.count + Gather.count])
    own = pltpu.make_async_copy(unit, units.at[me.c], local.at[0])
    brought = [
        pltpu.make_async_copy(gate_up_own, gate_up_full.at[me.s], local.at[1]),
        pltpu.make_async_copy(gate_up_other, gate_up_full.at[1 - me.s], local.at[2]),
        pltpu.make_async_copy(down_own, down_full.at[me.s], local.at[3]),
        pltpu.make_async_copy(down_other, down_full.at[1 - me.s], local.at[4]),
        pltpu.make_async_copy(grads, grads_here, local.at[5]),
    ]
    own.start()
    for copy in brought:
        copy.start()
    greet(me)
    own.wait()
    rows_of = gate_up_full.shape[1] * gate_up_full.shape[2]
    units_of = down_full.shape[1]
    first = [True]

    def consume(pair):
        if first[0]:
            for copy in brought:
                copy.wait()
            first[0] = False
        both = pl.ds(2 * pair, 2)

        def dot_rows(rows, columns):
            return jnp.dot(
                rows,
                gate_up_full[:, :, :, columns].reshape(2 * rows_of, units_of),
                preferred_element_type=F32,
            )

        @pl.loop(0, 2)
        def _(half):
            gate_at = pl.ds(pl.multiple_of(half * units_of, units_of), units_of)
            up_at = pl.ds(pl.multiple_of(width + half * units_of, units_of), units_of)
            rows = units[both].reshape(2 * tokens, model)
            gate = dot_rows(rows, gate_at)
            up = dot_rows(rows, up_at)
            grad = dot_right(grads_here[both].reshape(2 * tokens, model), down_full[half])
            sig = jax.nn.sigmoid(gate)
            silu = gate * sig

            def store(target, columns, value):
                target[both, :, columns] = value.astype(LOW).reshape(2, tokens, units_of)

            store(hidden, gate_at, silu * up)
            store(grad_gate_up, gate_at, grad * up * (sig * (1.0 + gate * (1.0 - sig))))
            store(grad_gate_up, up_at, grad * silu)

    gather.run(consume)
    scatter = Scatter(me, scratch)
    block_rows = gate_up_full.shape[2]

    def produce(first, columns):
        start, size = columns.start, columns.size
        blocks = size // block_rows
        block = start // block_rows
        weights = gate_up_full[block // 16, pl.ds(block % 16, blocks)].reshape(size, 2 * width)
        return dot_right(own_last(me, grad_gate_up, first), weights)

    every = 16 * tokens
    part = model // 8
    depth = width // 4

    def gate_up_part(number):
        def work(slot):
            left = units[:, :, number * part : (number + 1) * part].reshape(every, part)
            slot[...] = dot_left(left, grad_gate_up[...].reshape(every, 2 * width)).astype(LOW)

        return work, gate_up_grad.at[pl.ds(number * part, part)]

    def down_part(number):
        def work(slot):
            left = hidden[:, :, number * depth : (number + 1) * depth].reshape(every, depth)
            for half in range(2):
                right = grads_here[:, :, half * 2 * width : (half + 1) * 2 * width].reshape(every, 2 * width)
                slot[pl.ds(half * depth, depth)] = dot_left(left, right).astype(LOW)

        return work, down_grad.at[number]

    fillers, end = leave(
        stage, [gate_up_part(n) for n in range(8)] + [down_part(n) for n in range(4)], leaving
    )
    scatter.run(None, produce, write_total(total_out), fillers)
    end()
    scatter.drain()
    gather.finish()


def mlp(unit, grads, gate_up_own, gate_up_other, down_own, down_other):
    tokens, model = unit.shape
    width = 2 * down_own.shape[0]
    return pl.pallas_call(
        mlp_kernel,
        out_shape=[
            jax.ShapeDtypeStruct((tokens, model), F32),
            jax.ShapeDtypeStruct((16, tokens, width), LOW),
            jax.ShapeDtypeStruct((2,) + down_own.shape, LOW),
            jax.ShapeDtypeStruct((model, 2 * width), LOW),
            jax.ShapeDtypeStruct((4, width // 2, 2 * width), LOW),
        ],
        in_specs=[ANYWHERE] * 6,
        out_specs=[IN_VMEM] * 3 + [ANYWHERE] * 2,
        scratch_shapes=Scatter.scratch(tokens, model)
        + Gather.sems(3)
        + [
            pltpu.VMEM((16, tokens, model), LOW),
            pltpu.VMEM((16, tokens, 2 * width), LOW),
            pltpu.VMEM((2,) + gate_up_own.shape, LOW),
            pltpu.VMEM((16, tokens, model), LOW),
            pltpu.VMEM((2, model // 8, 2 * width), LOW),
            DMA((12,)),
            DMA((6,)),
        ],
        compiler_params=params(2),
    )(unit, grads, gate_up_own, gate_up_other, down_own, down_other)


def attend_back_kernel(
    shift, valid, branch, units, query, key, value, out_w, qkv_w, attended, cosine, sine, gate_up, down,
    total_out, qkv_grad, out_grad, gate_up_other, down_other,
    key_sum, value_sum, branches, grad_qkv, units_here, *scratch
):
    me = Place()
    tokens, model = branch.shape
    gather = Gather(me, pieces_of(branches), EARLY, *scratch[Scatter.count : Scatter.count + Gather.count])
    sems, local = scratch[-2:]
    own = pltpu.make_async_copy(branch, branches.at[me.c], local.at[0])
    own.start()
    bring = pltpu.make_async_copy(units, units_here, local.at[1])
    bring.start()
    greet(me, over_seq=True)
    own.wait()
    over = (1 - me.s, me.c)
    swaps = [
        remote(gate_up.at[1 - me.s], gate_up_other, sems.at[0], sems.at[1], over),
        remote(down.at[1 - me.s], down_other, sems.at[2], sems.at[3], over),
    ]
    for copy in swaps:
        copy.start()
    rows, width = query.shape[2], query.shape[3]
    strip = rows // 2
    length = rows * 16
    scale = width ** (-0.5)
    key_sum[...] = jnp.zeros_like(key_sum)
    value_sum[...] = jnp.zeros_like(value_sum)

    def turn_back(values, places):
        swapped = pltpu.roll(values, width // 2, axis=1)
        turned = values * cosine[places].reshape(2 * rows, width)
        return (turned + swapped * sine[places].reshape(2 * rows, width)).astype(LOW).reshape(2, rows, width)

    def consume(pair):
        where = query_places(pair, strip)
        keys_at = key_places(strip)
        both = pl.ds(2 * pair, 2)
        for seq in range(2):
            here = pl.ds(seq * rows, rows)
            grad = dot_right(branches[both, here].reshape(2 * rows, -1), out_w[...]).astype(LOW)
            keys = key[:, seq].reshape(length, width)
            values = value[:, seq].reshape(length, width)
            queries = of_pair(query, pair, seq)
            logits = dot_right(queries, keys) * scale - shift
            live = (keys_at <= where) & (keys_at < valid[seq])
            sig = jnp.where(live, jax.nn.sigmoid(logits), 0.0)
            weights = sig.astype(LOW)
            grad_logits = (dot_right(grad, values) * (sig * (1.0 - sig))).astype(LOW)
            grad_query = jnp.dot(grad_logits, keys, preferred_element_type=F32) * scale
            grad_qkv[both, here, 0:width] = turn_back(grad_query, both)
            key_sum[seq] += dot_left(grad_logits, queries)
            value_sum[seq] += dot_left(weights, grad)

    gather.run(consume)
    for seq in range(2):

        @pl.loop(0, 8)
        def _(pair):
            at = pl.ds(pl.multiple_of(pair * 2 * rows, 2 * rows), 2 * rows)
            here = pl.ds(seq * rows, rows)
            both = pl.ds(2 * pair, 2)
            grad_qkv[both, here, width : 2 * width] = turn_back(key_sum[seq, at] * scale, both)
            grad_qkv[both, here, 2 * width :] = value_sum[seq, at].astype(LOW).reshape(2, rows, width)

    scatter = Scatter(me, scratch)

    def produce(first, columns):
        return dot_right(own_last(me, grad_qkv, first), qkv_w[columns, :])

    every = 16 * tokens
    bring.wait()

    def qkv_part(number, part=model // 8):
        at = slice(number * part, (number + 1) * part)
        left = units_here[:, :, at].reshape(every, part)
        qkv_grad[at, :] = dot_left(left, grad_qkv[...].reshape(every, 3 * width)).astype(LOW)

    def out_part(number, part=model // 4):
        at = slice(number * part, (number + 1) * part)
        left = attended[...].reshape(every, width)
        out_grad[:, at] = dot_left(left, branches[:, :, at].reshape(every, part)).astype(LOW)

    fillers = [functools.partial(out_part, n) for n in range(4)]
    fillers += [functools.partial(qkv_part, n) for n in range(8)]
    scatter.run(None, produce, write_total(total_out), fillers)
    scatter.drain()
    gather.finish()
    for copy in swaps:
        copy.wait()


def attend_back(
    shift, valid, branch, units, query, key, value, out_w, qkv_w, attended, cosine, sine, gate_up, down
):
    tokens, model = branch.shape
    rows, width = query.shape[2:]
    return pl.pallas_call(
        functools.partial(attend_back_kernel, shift),
        out_shape=[
            jax.ShapeDtypeStruct((tokens, model), F32),
            jax.ShapeDtypeStruct((model, 3 * width), LOW),
            jax.ShapeDtypeStruct((width, model), LOW),
            jax.ShapeDtypeStruct(gate_up.shape[1:], LOW),
            jax.ShapeDtypeStruct(down.shape[1:], LOW),
        ],
        in_specs=[IN_SMEM] + [ANYWHERE] * 2 + [IN_VMEM] * 8 + [ANYWHERE] * 2,
        out_specs=[IN_VMEM] * 3 + [ANYWHERE] * 2,
        scratch_shapes=[pltpu.VMEM((2, 16 * rows, width), F32)] * 2
        + [
            pltpu.VMEM((16, tokens, model), LOW),
            pltpu.VMEM((16, tokens, 3 * width), LOW),
            pltpu.VMEM((16, tokens, model), LOW),
        ]
        + Scatter.scratch(tokens, model)
        + Gather.sems(3)
        + [DMA((4,)), DMA((2,))],
        compiler_params=params(4),
    )(valid, branch, units, query, key, value, out_w, qkv_w, attended, cosine, sine, gate_up, down)


def return_kernel(
    hidden, down_w, qkv, gate_up, gate_up_other, out_pair,
    total_out, qkv_back, gate_up_back, out_back, *scratch
):
    (qx, qsum, qxs, qxr, qs, qr, psum, ps, pr, oland, os, orecv) = scratch[Scatter.count :]
    me = Place()
    greet_plane(me)
    over = (1 - me.s, me.c)

    def cross(place):
        return remote(qkv.at[1 - me.s, place], qx.at[place], qxs.at[place], qxr.at[place], over)

    def send(sums, back, s_sem, r_sem, step):
        to, _ = turn(me, step)
        return remote(sums.at[to], back.at[me.c], s_sem.at[step], r_sem.at[me.c], (me.s, to))

    for step in range(1, 16):
        cross(turn(me, step)[0]).start()
    cross(me.c).start()
    holder = me.at(me.z, me.y, me.s)

    def out_send(target_core, same):
        target = (me.s if same else 1 - me.s, me.at(me.z, me.y, target_core))
        slot = 0 if same else 1
        return remote(out_pair.at[target_core], oland.at[me.s], os.at[slot], orecv.at[me.s], target)

    inside = me.k == me.s

    @pl.when(inside)
    def _():
        out_send(1 - me.k, True).start()

    @pl.when(jnp.logical_not(inside))
    def _():
        out_send(me.k, False).start()
        remote(
            out_pair.at[1 - me.k], oland.at[me.s], os.at[0], orecv.at[me.s],
            (1 - me.s, me.at(me.z, me.y, 1 - me.k)),
        ).start()

    def summed(place):
        return (gate_up[me.s, place].astype(F32) + gate_up_other[place].astype(F32)).astype(LOW)

    gate_up_back[me.c] = summed(me.c)

    @pl.loop(0, 16)
    def _(place):
        psum[place] = summed(place)

    for step in range(1, 16):
        send(psum, gate_up_back, ps, pr, step).start()

    def between():
        for step in range(1, 16):
            to, _ = turn(me, step)
            cross(to).wait_recv()
            qsum[to] = (qkv[me.s, to].astype(F32) + qx[to].astype(F32)).astype(LOW)
            send(qsum, qkv_back, qs, qr, step).start()
        cross(me.c).wait_recv()
        qkv_back[me.c] = (qkv[me.s, me.c].astype(F32) + qx[me.c].astype(F32)).astype(LOW)

    scatter = Scatter(me, scratch)

    def produce(first, columns):
        return jnp.dot(own_last(me, hidden, first), down_w[:, columns], preferred_element_type=F32)

    scatter.run(None, produce, write_total(total_out), [between])
    scatter.drain()
    for step in range(1, 16):
        to, source = turn(me, step)
        for sums, back, s_sem, r_sem in ((qsum, qkv_back, qs, qr), (psum, gate_up_back, ps, pr)):
            remote(sums.at[0], back.at[source], s_sem.at[step], r_sem.at[source], over).wait_recv()
            send(sums, back, s_sem, r_sem, step).wait_send()
        cross(to).wait_send()
    cross(me.c).wait_send()

    @pl.when(inside)
    def _():
        out_send(1 - me.k, True).wait_send()
        remote(out_pair.at[0], oland.at[1 - me.s], os.at[0], orecv.at[1 - me.s], over).wait_recv()
        out_back[...] = out_pair[me.k].astype(F32) + oland[1 - me.s].astype(F32)

    @pl.when(jnp.logical_not(inside))
    def _():
        out_send(me.k, False).wait_send()
        out_send(1 - me.k, True).wait_send()
        for half in range(2):
            remote(out_pair.at[0], oland.at[half], os.at[0], orecv.at[half], over).wait_recv()
        out_back[...] = oland[0].astype(F32) + oland[1].astype(F32)


def give_back(hidden, down_w, qkv, gate_up, gate_up_other, out_pair):
    tokens, model = hidden.shape[1], down_w.shape[1]
    block = lambda array: pltpu.VMEM(array.shape[1:], LOW)
    return pl.pallas_call(
        return_kernel,
        out_shape=[
            jax.ShapeDtypeStruct((tokens, model), F32),
            jax.ShapeDtypeStruct(qkv.shape[1:], LOW),
            jax.ShapeDtypeStruct(gate_up.shape[1:], LOW),
            jax.ShapeDtypeStruct(out_pair.shape[1:], F32),
        ],
        in_specs=[IN_VMEM] * 6,
        out_specs=[IN_VMEM] * 4,
        scratch_shapes=Scatter.scratch(tokens, model)
        + [block(qkv), block(qkv)]
        + [DMA((16,))] * 4
        + [block(gate_up)]
        + [DMA((16,))] * 2
        + [pltpu.VMEM(out_pair.shape, LOW), DMA((2,)), DMA((2,))],
        compiler_params=params(5),
    )(hidden, down_w, qkv, gate_up, gate_up_other, out_pair)


def assemble_kernel(
    qkv_back, gate_up_back, down_own, down_other, w_query, w_key, w_value, w_gate, w_up, gain_one, gain_two,
    query_grad, key_grad, value_grad, gate_grad, up_grad, down_grad, gain_one_grad, gain_two_grad
):
    width = qkv_back.shape[2] // 3
    rows = qkv_back.shape[1]
    one = jnp.broadcast_to(gain_one[...], (rows, width))
    total = jnp.zeros((rows, width), F32)
    for place in range(16):
        at = slice((place // 2 + 8 * (place % 2)) * width, (place // 2 + 8 * (place % 2) + 1) * width)
        for index, (weight, target) in enumerate(
            ((w_query, query_grad), (w_key, key_grad), (w_value, value_grad))
        ):
            block = qkv_back[place, :, index * width : (index + 1) * width].astype(F32)
            target[:, at] = block * one
            total += block * weight[:, at].astype(F32)
    gain_one_grad[...] = jnp.broadcast_to(jnp.sum(total, axis=1, keepdims=True), gain_one_grad.shape)
    width = gate_up_back.shape[2] // 4
    two = jnp.broadcast_to(gain_two[...], (rows, width))
    total = jnp.zeros((rows, width), F32)
    for place in range(16):
        for half in range(2):
            at = slice((half * 16 + place) * width, (half * 16 + place + 1) * width)
            for index, (weight, target) in enumerate(((w_gate, gate_grad), (w_up, up_grad))):
                start = (2 * index + half) * width
                block = gate_up_back[place, :, start : start + width].astype(F32)
                target[:, at] = block * two
                total += block * weight[:, at].astype(F32)
    gain_two_grad[...] = jnp.broadcast_to(jnp.sum(total, axis=1, keepdims=True), gain_two_grad.shape)
    parts, double, part = down_own.shape
    depth = double // 2
    for number in range(parts):
        for half in range(2):
            at = slice(half * depth, (half + 1) * depth)
            down_grad[number * depth : (number + 1) * depth, half * part : (half + 1) * part] = (
                down_own[number, at].astype(F32) + down_other[number, at].astype(F32)
            )


def assemble(qkv_back, gate_up_back, down_own, down_other, w_query, w_key, w_value, w_gate, w_up, gain_one, gain_two):
    rows, model = w_query.shape
    narrow = jax.ShapeDtypeStruct((rows, model), F32)
    wide = jax.ShapeDtypeStruct(w_gate.shape, F32)
    gain = jax.ShapeDtypeStruct((rows, 128), F32)
    parts, double, part = down_own.shape
    down = jax.ShapeDtypeStruct((parts * double // 2, 2 * part), F32)
    return pl.pallas_call(
        assemble_kernel,
        out_shape=[narrow] * 3 + [wide] * 2 + [down] + [gain] * 2,
        in_specs=[IN_VMEM] * 11,
        out_specs=[IN_VMEM] * 8,
        compiler_params=pltpu.CompilerParams(vmem_limit_bytes=48 << 20),
    )(qkv_back, gate_up_back, down_own, down_other, w_query, w_key, w_value, w_gate, w_up, gain_one, gain_two)


def norm_back(values, scale, weighted):
    inner = jnp.mean(values * weighted, axis=-1, keepdims=True)
    return scale * weighted - values * (scale * scale * scale * inner)


def scale_of(values):
    return lax.rsqrt(jnp.mean(values * values, axis=-1, keepdims=True) + norm_eps)


def move_tokens_step(
    layer_in,
    valid_len,
    norm1_gain,
    w_query,
    w_key,
    w_value,
    w_out,
    norm2_gain,
    w_gate,
    w_up,
    w_down,
    cotangent,
):
    local_rows, local_seqs, model = layer_in.shape
    strip = local_rows // 2
    width = model // HEADS
    cp_devices = 16
    tokens = local_rows * local_seqs
    shift = math.log(cp_devices * local_rows)
    weight_rows = w_gate.shape[0]
    gain_one = norm1_gain.astype(F32)[:, None]
    gain_two = norm2_gain.astype(F32)[:, None]

    def by_seq(values):
        return values.transpose(1, 0, 2).reshape(tokens, model)

    def by_row(values):
        return values.reshape(local_seqs, local_rows, model).transpose(1, 0, 2)

    inputs = by_seq(layer_in).astype(F32)
    grad_local = by_seq(cotangent)
    scale_one = scale_of(inputs)
    freqs = rope_base ** (-2.0 * jnp.arange(width // 2, dtype=F32) / width)
    place_pos = row_positions(
        jnp.arange(cp_devices * local_rows, dtype=jnp.int32), strip, cp_devices
    ).reshape(cp_devices, local_rows)
    angles = place_pos.astype(F32)[:, :, None] * freqs
    cosine, sine = jnp.cos(angles), jnp.sin(angles)
    cosine = jnp.concatenate([cosine, cosine], axis=2)
    back_sine = jnp.concatenate([sine, -sine], axis=2)

    units, grads, query, key, value, qkv_w, gate_up_own, head_out, down_other = spread(
        (inputs * scale_one).astype(LOW), grad_local, w_query, w_key, w_value, w_gate, w_up,
        gain_one, gain_two, w_out, w_down, cosine, back_sine,
    )
    qkv_w = qkv_w.reshape(model, 3 * width)
    head_out = head_out.reshape(width, model)
    branch, attended, gate_up_other = attend(shift, valid_len, query, key, value, head_out, gate_up_own)
    hidden_state = inputs + branch
    scale_two = scale_of(hidden_state)
    weighted_two, hidden, down_full, gate_up_grad, down_grad = mlp(
        (hidden_state * scale_two).astype(LOW), grads, gate_up_own, gate_up_other, w_down, down_other
    )
    grad_state = grad_local.astype(F32) + norm_back(hidden_state, scale_two, weighted_two)
    gate_up_grad = gate_up_grad.reshape(2, cp_devices, weight_rows, -1)
    down_grad = down_grad.reshape((2, 2) + down_grad.shape[1:])
    weighted_one, qkv_grad, out_grad, gate_up_grad_other, down_grad_other = attend_back(
        shift, valid_len, grad_state.astype(LOW), units, query, key, value, head_out, qkv_w, attended,
        cosine, back_sine, gate_up_grad, down_grad,
    )
    in_grad = grad_state + norm_back(inputs, scale_one, weighted_one)
    ff_branch, qkv_back, gate_up_back, out_back = give_back(
        hidden,
        down_full.reshape(-1, model),
        qkv_grad.reshape(2, cp_devices, weight_rows, -1),
        gate_up_grad,
        gate_up_grad_other,
        out_grad.reshape(2, width // 2, model),
    )
    layer_out = (hidden_state + ff_branch).astype(LOW)
    down_own = lax.dynamic_index_in_dim(down_grad, lax.axis_index("seq"), 0, False)
    query_grad, key_grad, value_grad, gate_grad, up_grad, down_back, gain_one_grad, gain_two_grad = assemble(
        qkv_back, gate_up_back, down_own, down_grad_other, w_query, w_key, w_value, w_gate, w_up, gain_one, gain_two
    )
    return (
        by_row(layer_out),
        by_row(in_grad),
        gain_one_grad[:, 0],
        query_grad,
        key_grad,
        value_grad,
        out_back,
        gain_two_grad[:, 0],
        gate_grad,
        up_grad,
        down_back,
    )


def solution(mesh):
    fits = mesh.shape["cp"] == HEADS and mesh.shape["seq"] == 2
    on_device = move_tokens_step if fits else gather_weights_step
    placed = (
        P("cp", "seq", None),
        P("seq"),
        P(("seq", "cp")),
        P(("seq", "cp"), None),
        P(("seq", "cp"), None),
        P(("seq", "cp"), None),
        P(("seq", "cp"), None),
        P(("seq", "cp")),
        P(("seq", "cp"), None),
        P(("seq", "cp"), None),
        P(("seq", "cp"), None),
        P("cp", "seq", None),
    )
    return jax.shard_map(
        on_device,
        mesh=mesh,
        in_specs=placed,
        out_specs=(
            P("cp", "seq", None),
            P("cp", "seq", None),
            P(("seq", "cp")),
            P(("seq", "cp"), None),
            P(("seq", "cp"), None),
            P(("seq", "cp"), None),
            P(("seq", "cp"), None),
            P(("seq", "cp")),
            P(("seq", "cp"), None),
            P(("seq", "cp"), None),
            P(("seq", "cp"), None),
        ),
        check_vma=False,
    )
```

```python
import functools
import math

import jax
import jax.numpy as jnp
from jax import lax
from jax.experimental import pallas as pl
from jax.experimental.pallas import tpu as pltpu
from jax.sharding import PartitionSpec as P

HEADS = 16


norm_eps = 1e-05
rope_base = 10000.0


def row_positions(indices, strip_rows, devices):
    owner_index = indices // (2 * strip_rows)
    within = indices % (2 * strip_rows)
    return jnp.where(
        within < strip_rows,
        owner_index * strip_rows + within,
        (2 * devices - 1 - owner_index) * strip_rows + within - strip_rows,
    )


def rotate(values, positions, num_heads):
    count_rows, model_width = values.shape
    head_width = model_width // num_heads
    half_width = head_width // 2
    freqs_table = rope_base ** (-2.0 * jnp.arange(half_width, dtype=jnp.float32) / head_width)
    angles = positions.astype(jnp.float32)[:, None] * freqs_table[None, :]
    cosine = jnp.cos(angles)[:, None, :]
    sine_table = jnp.sin(angles)[:, None, :]
    split_heads = values.reshape(count_rows, num_heads, head_width)
    former = split_heads[:, :, :half_width]
    latter = split_heads[:, :, half_width:]
    turned = jnp.concatenate(
        [former * cosine - latter * sine_table, latter * cosine + former * sine_table], axis=2
    )
    return turned.reshape(count_rows, model_width)


def norm_scale(values):
    return values * lax.rsqrt(jnp.mean(values * values, axis=-1, keepdims=True) + norm_eps)


def normed(values, gain_vector):
    return norm_scale(values) * gain_vector


def swiglu(gate_rows, up_rows):
    return jax.nn.silu(gate_rows) * up_rows


def dot_right(left, right):
    return lax.dot_general(
        left, right, (((1,), (1,)), ((), ())), preferred_element_type=jnp.float32
    )


def dot_left(left, right):
    return lax.dot_general(
        left, right, (((0,), (0,)), ((), ())), preferred_element_type=jnp.float32
    )


def split_blocks(array, block_rows):
    return array.reshape((array.shape[0] // block_rows, block_rows) + array.shape[1:])


def key_mask(query_pos, key_pos, valid_count):
    causal = key_pos[None, :] <= query_pos[:, None]
    live_keys = key_pos[None, :] < valid_count[:, None]
    return (causal[None, None, :, :] & live_keys[:, None, None, :]).astype(jnp.float32)


def scores_of(queries, key_rows, query_pos, key_pos, valid_count, score_shift):
    head_width = queries.shape[3]
    raw_scores = jnp.einsum(
        "qshd,kshd->shqk", queries, key_rows, preferred_element_type=jnp.float32
    )
    return (
        raw_scores * head_width ** (-0.5) - score_shift,
        key_mask(query_pos, key_pos, valid_count),
    )


def block_grads(queries, grad_rows, key_rows, values, query_pos, key_pos, valid_count, score_shift):
    logits, mask_table = scores_of(queries, key_rows, query_pos, key_pos, valid_count, score_shift)
    sigmoid_table = jax.nn.sigmoid(logits)
    weights_low = (sigmoid_table * mask_table).astype(jnp.bfloat16)
    grad_weights = jnp.einsum(
        "qshd,kshd->shqk", grad_rows, values, preferred_element_type=jnp.float32
    )
    grad_logits = (grad_weights * mask_table * (sigmoid_table * (1.0 - sigmoid_table))).astype(
        jnp.bfloat16
    )
    return (weights_low, grad_logits)


def make_norm_fold(normalized, pieces):
    gain_part = pieces[0].astype(jnp.float32)
    scaled = (normalized * gain_part).astype(jnp.bfloat16)
    totals = tuple(
        (
            jnp.dot(scaled, weight_piece, preferred_element_type=jnp.float32)
            for weight_piece in pieces[1:]
        )
    )
    return (gain_part,) + totals


def make_row_fold(left_rows, weight_piece):
    return jnp.dot(left_rows, weight_piece, preferred_element_type=jnp.float32)


def gather_weights_step(
    layer_in,
    valid_len,
    norm1_gain,
    w_query,
    w_key,
    w_value,
    w_out,
    norm2_gain,
    w_gate,
    w_up,
    w_down,
    cotangent,
):
    local_rows, local_seqs, model_width = layer_in.shape
    num_heads = HEADS
    head_width = model_width // num_heads
    strip_rows = local_rows // 2
    cp_devices = lax.axis_size("cp")
    cp_place = lax.axis_index("cp")
    seq_length = local_rows * cp_devices
    score_shift = math.log(seq_length)
    score_scale = head_width ** (-0.5)
    token_count = local_rows * local_seqs
    local_pos = row_positions(
        cp_place * local_rows + jnp.arange(local_rows, dtype=jnp.int32), strip_rows, cp_devices
    )
    token_pos = jnp.broadcast_to(local_pos[:, None], (local_rows, local_seqs)).reshape(token_count)
    every_pos = row_positions(jnp.arange(seq_length, dtype=jnp.int32), strip_rows, cp_devices)
    block_rows = math.gcd(seq_length, 512)
    head_shape = (local_rows, local_seqs, num_heads, head_width)
    row_shape = (local_rows, local_seqs, model_width)
    zero_heads = jnp.zeros(head_shape, jnp.float32)
    inputs = layer_in.reshape(token_count, model_width).astype(jnp.float32)
    input_norm = norm_scale(inputs)
    gain_one, query, key_proj, value = make_norm_fold(
        input_norm,
        (
            lax.all_gather(norm1_gain, ("seq", "cp"), axis=0, tiled=True),
            lax.all_gather(w_query, ("seq", "cp"), axis=0, tiled=True),
            lax.all_gather(w_key, ("seq", "cp"), axis=0, tiled=True),
            lax.all_gather(w_value, ("seq", "cp"), axis=0, tiled=True),
        ),
    )
    normed_one = (input_norm * gain_one).astype(jnp.bfloat16)
    query_low = rotate(query, token_pos, num_heads).astype(jnp.bfloat16)
    key_low = rotate(key_proj, token_pos, num_heads).astype(jnp.bfloat16)
    value_low = value.astype(jnp.bfloat16)
    query_heads = query_low.reshape(head_shape)
    key_local = key_low.reshape(row_shape)
    value_local = value_low.reshape(row_shape)
    key_piece = lax.all_gather(key_local, "cp", axis=0, tiled=True)
    value_piece = lax.all_gather(value_local, "cp", axis=0, tiled=True)
    piece_rows = key_piece.shape[0]
    piece_block = math.gcd(piece_rows, 512)
    piece_pos = row_positions(jnp.arange(piece_rows, dtype=jnp.int32), strip_rows, cp_devices)

    def scan_step(partial_sum, block_items):
        key_block, value_block, block_pos = block_items
        logits, mask_table = scores_of(
            query_heads,
            key_block.reshape(piece_block, local_seqs, num_heads, head_width),
            local_pos,
            block_pos,
            valid_len,
            score_shift,
        )
        weights_low = (jax.nn.sigmoid(logits) * mask_table).astype(jnp.bfloat16)
        added = jnp.einsum(
            "shqk,kshd->qshd",
            weights_low,
            value_block.reshape(piece_block, local_seqs, num_heads, head_width),
            preferred_element_type=jnp.float32,
        )
        return (partial_sum + added, None)

    result, _ = lax.scan(
        scan_step,
        zero_heads,
        (
            split_blocks(key_piece, piece_block),
            split_blocks(value_piece, piece_block),
            split_blocks(piece_pos, piece_block),
        ),
    )
    attended_low = result.reshape(token_count, model_width).astype(jnp.bfloat16)
    attn_branch = make_row_fold(
        attended_low, lax.all_gather(w_out, ("seq", "cp"), axis=0, tiled=True)
    )
    hidden_state = inputs + attn_branch
    hidden_norm = norm_scale(hidden_state)
    gain_two, gate_rows, up_rows = make_norm_fold(
        hidden_norm,
        (
            lax.all_gather(norm2_gain, ("seq", "cp"), axis=0, tiled=True),
            lax.all_gather(w_gate, ("seq", "cp"), axis=0, tiled=True),
            lax.all_gather(w_up, ("seq", "cp"), axis=0, tiled=True),
        ),
    )
    normed_two = (hidden_norm * gain_two).astype(jnp.bfloat16)
    hidden_units = swiglu(gate_rows, up_rows).astype(jnp.bfloat16)
    ff_branch = make_row_fold(
        hidden_units, lax.all_gather(w_down, ("seq", "cp"), axis=0, tiled=True)
    )
    layer_out = (hidden_state + ff_branch).astype(jnp.bfloat16).reshape(row_shape)
    grad_out = cotangent.reshape(token_count, model_width)
    gate_all, up_all, down_all = (
        lax.all_gather(w_gate, ("seq", "cp"), axis=0, tiled=True),
        lax.all_gather(w_up, ("seq", "cp"), axis=0, tiled=True),
        lax.all_gather(w_down, ("seq", "cp"), axis=0, tiled=True),
    )
    grad_hidden = dot_right(grad_out, down_all)
    _, pull_swiglu = jax.vjp(swiglu, gate_rows, up_rows)
    grad_gate, grad_up = pull_swiglu(grad_hidden)
    grad_gate_low = grad_gate.astype(jnp.bfloat16)
    grad_up_low = grad_up.astype(jnp.bfloat16)
    grad_norm_two = dot_right(grad_gate_low, gate_all) + dot_right(grad_up_low, up_all)
    _, pull_two = jax.vjp(normed, hidden_state, gain_two)
    grad_from_two, gain_two_term = pull_two(grad_norm_two)
    ff_grads = (
        lax.psum_scatter(gain_two_term, ("seq", "cp"), scatter_dimension=0, tiled=True),
        lax.psum_scatter(
            dot_left(normed_two, grad_gate_low), ("seq", "cp"), scatter_dimension=0, tiled=True
        ),
        lax.psum_scatter(
            dot_left(normed_two, grad_up_low), ("seq", "cp"), scatter_dimension=0, tiled=True
        ),
        lax.psum_scatter(
            dot_left(hidden_units, grad_out), ("seq", "cp"), scatter_dimension=0, tiled=True
        ),
    )
    grad_state = grad_out.astype(jnp.float32) + grad_from_two
    query_all, key_all, value_all, out_all = (
        lax.all_gather(w_query, ("seq", "cp"), axis=0, tiled=True),
        lax.all_gather(w_key, ("seq", "cp"), axis=0, tiled=True),
        lax.all_gather(w_value, ("seq", "cp"), axis=0, tiled=True),
        lax.all_gather(w_out, ("seq", "cp"), axis=0, tiled=True),
    )
    grad_branch_low = grad_state.astype(jnp.bfloat16)
    grad_attended_low = dot_right(grad_branch_low, out_all).astype(jnp.bfloat16)
    grad_heads = grad_attended_low.reshape(head_shape)
    key_heads_local = key_local.reshape(head_shape)
    value_heads_local = value_local.reshape(head_shape)
    keys_every, values_every, queries_every, grads_every = (
        lax.all_gather(key_local, "cp", axis=0, tiled=True),
        lax.all_gather(value_local, "cp", axis=0, tiled=True),
        lax.all_gather(query_low.reshape(row_shape), "cp", axis=0, tiled=True),
        lax.all_gather(grad_attended_low.reshape(row_shape), "cp", axis=0, tiled=True),
    )

    def key_step(partial_sums, block_items):
        query_block, grad_block_rows, block_pos = block_items
        query_part = query_block.reshape(block_rows, local_seqs, num_heads, head_width)
        grad_part = grad_block_rows.reshape(block_rows, local_seqs, num_heads, head_width)
        weights_low, grad_logits = block_grads(
            query_part,
            grad_part,
            key_heads_local,
            value_heads_local,
            block_pos,
            local_pos,
            valid_len,
            score_shift,
        )
        key_added = jnp.einsum(
            "shqk,qshd->kshd", grad_logits, query_part, preferred_element_type=jnp.float32
        )
        value_added = jnp.einsum(
            "shqk,qshd->kshd", weights_low, grad_part, preferred_element_type=jnp.float32
        )
        return ((partial_sums[0] + key_added, partial_sums[1] + value_added), None)

    (key_sum, value_sum), _ = lax.scan(
        key_step,
        (zero_heads, zero_heads),
        (
            split_blocks(queries_every, block_rows),
            split_blocks(grads_every, block_rows),
            split_blocks(every_pos, block_rows),
        ),
    )
    grad_key_rot = key_sum.reshape(token_count, model_width) * score_scale
    grad_value_sum = value_sum.reshape(token_count, model_width)

    def query_step(partial_sum, block_items):
        key_block, value_block, block_pos = block_items
        key_heads = key_block.reshape(block_rows, local_seqs, num_heads, head_width)
        _, grad_logits = block_grads(
            query_heads,
            grad_heads,
            key_heads,
            value_block.reshape(block_rows, local_seqs, num_heads, head_width),
            local_pos,
            block_pos,
            valid_len,
            score_shift,
        )
        added = jnp.einsum(
            "shqk,kshd->qshd", grad_logits, key_heads, preferred_element_type=jnp.float32
        )
        return (partial_sum + added, None)

    query_sum, _ = lax.scan(
        query_step,
        zero_heads,
        (
            split_blocks(keys_every, block_rows),
            split_blocks(values_every, block_rows),
            split_blocks(every_pos, block_rows),
        ),
    )
    grad_query_rot = query_sum.reshape(token_count, model_width) * score_scale
    grad_query_low = rotate(grad_query_rot, -token_pos, num_heads).astype(jnp.bfloat16)
    grad_key_low = rotate(grad_key_rot, -token_pos, num_heads).astype(jnp.bfloat16)
    grad_value_low = grad_value_sum.astype(jnp.bfloat16)
    grad_norm_one = (
        dot_right(grad_query_low, query_all)
        + dot_right(grad_key_low, key_all)
        + dot_right(grad_value_low, value_all)
    )
    _, pull_one = jax.vjp(normed, inputs, gain_one)
    grad_from_one, gain_one_term = pull_one(grad_norm_one)
    in_grad = (grad_state + grad_from_one).reshape(row_shape)
    attn_grads = (
        lax.psum_scatter(gain_one_term, ("seq", "cp"), scatter_dimension=0, tiled=True),
        lax.psum_scatter(
            dot_left(normed_one, grad_query_low), ("seq", "cp"), scatter_dimension=0, tiled=True
        ),
        lax.psum_scatter(
            dot_left(normed_one, grad_key_low), ("seq", "cp"), scatter_dimension=0, tiled=True
        ),
        lax.psum_scatter(
            dot_left(normed_one, grad_value_low), ("seq", "cp"), scatter_dimension=0, tiled=True
        ),
        lax.psum_scatter(
            dot_left(attended_low, grad_branch_low), ("seq", "cp"), scatter_dimension=0, tiled=True
        ),
    )
    return (
        layer_out,
        in_grad,
        attn_grads[0],
        attn_grads[1],
        attn_grads[2],
        attn_grads[3],
        attn_grads[4],
        ff_grads[0],
        ff_grads[1],
        ff_grads[2],
        ff_grads[3],
    )


MESH = pl.DeviceIdType.MESH
DMA = pltpu.SemaphoreType.DMA
LOW = jnp.bfloat16
F32 = jnp.float32
ANYWHERE = pl.BlockSpec(memory_space=pl.ANY)
IN_VMEM = pl.BlockSpec(memory_space=pltpu.VMEM)
IN_SMEM = pl.BlockSpec(memory_space=pltpu.SMEM)


class Place:
    def __init__(self):
        self.s = lax.axis_index("seq")
        self.c = lax.axis_index("cp")
        self.z = self.c // 4
        self.y = (self.c // 2) % 2
        self.k = self.c % 2

    def at(self, z, y, k):
        return z * 4 + y * 2 + k

    def device(self, place):
        return (self.s, place)


def pick(z, table):
    value = jnp.int32(table[0])
    for index in range(1, 4):
        value = jnp.where(z == index, jnp.int32(table[index]), value)
    return value


NEAREST = ((1, 0, 1, 2), (2, 2, 3, 1), (3, 3, 0, 0))
FARTHEST = ((3, 3, 0, 0), (2, 2, 3, 1), (1, 0, 1, 2))


def remote(source, target, send, recv, device):
    return pltpu.make_async_remote_copy(
        src_ref=source,
        dst_ref=target,
        send_sem=send,
        recv_sem=recv,
        device_id=device,
        device_id_type=MESH,
    )


def hail(device):
    pl.semaphore_signal(
        pltpu.get_barrier_semaphore(), inc=1, device_id=device, device_id_type=MESH
    )


def greet(me, over_seq=False):
    hail((me.s, me.at(me.z, 1 - me.y, me.k)))
    hail((me.s, me.at(me.z, me.y, 1 - me.k)))

    @pl.when(me.z < 3)
    def _():
        hail((me.s, me.at(me.z + 1, me.y, me.k)))

    @pl.when(me.z > 0)
    def _():
        hail((me.s, me.at(me.z - 1, me.y, me.k)))

    ends = (me.z == 0).astype(jnp.int32) + (me.z == 3).astype(jnp.int32)
    if over_seq:
        hail((1 - me.s, me.c))
    return lambda: pl.semaphore_wait(
        pltpu.get_barrier_semaphore(), 4 - ends + (1 if over_seq else 0)
    )


def greet_plane(me):
    for step in range(1, 16):
        hail((me.s, (me.c + step) % 16))
    hail((1 - me.s, me.c))
    hail((1 - me.s, me.at(me.z, me.y, 1 - me.k)))
    return lambda: pl.semaphore_wait(pltpu.get_barrier_semaphore(), 17)


class Gather:
    def __init__(self, me, views, early, z_sem, far_sem, y_sem, k_sem, recv):
        self.me, self.views, self.early = me, views, early
        self.z_sem, self.far_sem, self.y_sem, self.k_sem, self.recv = z_sem, far_sem, y_sem, k_sem, recv

    count = 5

    @staticmethod
    def sems(pieces):
        return [DMA((pieces * n,)) for n in (5, 5, 4, 8, 16)]

    def copy(self, piece, place, sem, device):
        block = self.views[piece](place)
        return remote(block, block, sem, self.recv.at[piece * 16 + place], device)

    def arrived(self, piece, place):
        self.copy(piece, place, self.k_sem.at[0], self.me.device(self.me.c)).wait_recv()

    def line(self, index):
        return self.me.z if index == 0 else pick(self.me.z, NEAREST[index - 1])

    def along(self, piece, place, index, up, sems):
        me = self.me
        target = jnp.minimum(me.c + 4, 12 + me.c % 4) if up else jnp.maximum(me.c - 4, me.c % 4)
        return self.copy(piece, place, sems.at[piece * 5 + index], me.device(target))

    def across(self, piece, place, index):
        me = self.me
        target = me.at(me.z, 1 - me.y, me.k)
        return self.copy(piece, place, self.y_sem.at[piece * 4 + index], me.device(target))

    def partner(self, piece, place, index):
        me = self.me
        target = me.at(me.z, me.y, 1 - me.k)
        return self.copy(piece, place, self.k_sem.at[piece * 8 + index], me.device(target))

    def spread_along(self, piece, place, index, sems, go):
        me, z = self.me, self.line(index)
        if index == 0:

            @pl.when(me.z < 3)
            def _():
                go(self.along(piece, place, 0, True, sems))

            @pl.when(me.z > 0)
            def _():
                go(self.along(piece, place, 4, False, sems))
        else:

            @pl.when((z < me.z) & (me.z < 3))
            def _():
                go(self.along(piece, place, index, True, sems))

            @pl.when((z > me.z) & (me.z > 0))
            def _():
                go(self.along(piece, place, index, False, sems))

    def send_near(self, piece, index, go=lambda copy: copy.start()):
        me = self.me
        place = me.at(self.line(index), me.y, me.k)
        if index == 0 or not self.early[piece]:
            go(self.across(piece, place, index))
        self.spread_along(piece, place, index, self.z_sem, go)
        go(self.partner(piece, place, index))

    def send_far(self, piece, index, go=lambda copy: copy.start()):
        me = self.me
        place = me.at(self.line(index), 1 - me.y, me.k)
        if self.early[piece]:
            self.spread_along(piece, place, index, self.far_sem, go)
        go(self.partner(piece, place, 4 + index))

    def begin(self):
        for piece in range(len(self.views)):
            self.send_near(piece, 0)

    def round(self, index):
        me = self.me
        for piece in range(len(self.views)):
            if index < 3:
                self.arrived(piece, me.at(self.line(index + 1), me.y, me.k))
                self.send_near(piece, index + 1)
            self.arrived(piece, me.at(self.line(index), 1 - me.y, me.k))
            self.send_far(piece, index)

    def settle(self, z, y):
        for piece in range(len(self.views)):
            self.arrived(piece, self.me.at(z, y, 1 - self.me.k))

    def run(self, consume):
        me = self.me
        self.begin()
        waiting = [(me.z, me.y)]
        for index in range(4):
            self.round(index)
            ready, waiting = waiting, []
            if index < 3:
                waiting.append((self.line(index + 1), me.y))
            waiting.append((self.line(index), 1 - me.y))
            for z, y in ready:
                self.settle(z, y)
                consume(z * 2 + y)
        for z, y in waiting:
            self.settle(z, y)
            consume(z * 2 + y)

    def finish(self):
        for piece in range(len(self.views)):
            for index in range(4):
                self.send_near(piece, index, lambda copy: copy.wait_send())
                self.send_far(piece, index, lambda copy: copy.wait_send())


class Scatter:
    pieces = 2

    def __init__(self, me, scratch):
        self.me = me
        (self.k_out, self.k_in, self.y_out, self.y_in, self.z_out, self.z_in, self.mine, self.kept) = scratch[:8]
        (self.ks, self.kr, self.ys, self.yr, self.zs, self.zl, self.zr) = scratch[8:15]

    count = 15

    @classmethod
    def scratch(cls, rows, width):
        n = cls.pieces
        part = width // n
        low = [pltpu.VMEM((n * count, rows, part), LOW) for count in (8, 8, 4, 4, 3, 5)]
        full = [pltpu.VMEM((n * count, rows, part), F32) for count in (1, 4)]
        return low + full + [DMA((n * count,)) for count in (8, 8, 4, 4, 3, 4, 4)]

    def partner(self, slot):
        me = self.me
        target = me.device(me.at(me.z, me.y, 1 - me.k))
        return remote(self.k_out.at[slot], self.k_in.at[slot], self.ks.at[slot], self.kr.at[slot], target)

    def across(self, z, index, piece):
        me, n = self.me, self.pieces
        out, land = index * n + piece, z * n + piece
        target = me.device(me.at(me.z, 1 - me.y, me.k))
        return remote(self.y_out.at[out], self.y_in.at[land], self.ys.at[out], self.yr.at[land], target)

    def along(self, z, index, piece, up):
        me, n = self.me, self.pieces
        out, land = index * n + piece, z * n + piece
        target = jnp.minimum(me.c + 4, 12 + me.c % 4) if up else jnp.maximum(me.c - 4, me.c % 4)
        into = self.z_in.at[land if up else jnp.where(z == me.z - 1, 4, z) * n + piece]
        sem = (self.zl if up else self.zr).at[land]
        return remote(self.z_out.at[out], into, self.zs.at[out], sem, me.device(target))

    def line(self, index):
        return self.me.z if index == 3 else pick(self.me.z, FARTHEST[index])

    def emit(self, produce, z, y, piece, slot, keep):
        part = 512
        rows, width = keep.shape

        @pl.loop(0, width // part)
        def _(index):
            here = pl.ds(pl.multiple_of(index * part, part), part)
            start = pl.multiple_of(piece * width + index * part, part)
            value = produce(self.me.at(z, y, 0), pl.ds(start, part))
            self.k_out[slot, :, here] = value[:rows].astype(LOW)
            keep[:, here] = value[rows:]

    def add(self, target, base, *blocks):
        part = 512

        @pl.loop(0, target.shape[-1] // part)
        def _(index):
            here = pl.ds(pl.multiple_of(index * part, part), part)
            value = base[:, here]
            for block in blocks:
                value = value + block[:, here].astype(F32)
            target[:, here] = value.astype(target.dtype)

    def run(self, prepare, produce, finish, fillers=(), ready=lambda: None, after=lambda: None):
        me, n = self.me, self.pieces
        fillers = list(fillers)
        steps = [(index, piece) for index in range(4) for piece in range(n)]
        for number in range(len(steps) + 1):
            if number < len(steps):
                index, piece = steps[number]
                z = self.line(index)
                if prepare is not None and piece == 0:
                    prepare(z * 2 + 1 - me.y)
                self.emit(produce, z, 1 - me.y, piece, number, self.mine.at[number % 2])
                if number == 0:
                    ready()
                self.partner(number).start()
            if number > 0:
                index, piece = steps[number - 1]
                self.partner(number - 1).wait_recv()
                self.add(self.y_out.at[number - 1], self.mine.at[(number - 1) % 2], self.k_in.at[number - 1])
                self.across(self.line(index), index, piece).start()

        after()

        def own(number):
            index, piece = steps[number]
            z = self.line(index)
            if prepare is not None and piece == 0:
                prepare(z * 2 + me.y)
            self.emit(produce, z, me.y, piece, 4 * n + number, self.kept.at[number])
            self.partner(4 * n + number).start()

        ahead = n
        for number in range(ahead):
            own(number)
        for number in range(len(steps)):
            if number + ahead < len(steps):
                own(number + ahead)
            if prepare is None or number + ahead >= len(steps) - n:
                for _ in range(-(-len(fillers) // (len(steps) - number))):
                    fillers.pop(0)()
            self.collect(number, *steps[number], finish)

    def collect(self, number, index, piece, finish):
        me, n = self.me, self.pieces
        z = self.line(index)
        slot, land = 4 * n + number, z * n + piece
        kept = self.kept.at[number]
        self.partner(slot).wait_recv()
        self.across(z, index, piece).wait_recv()
        self.add(kept, kept, self.k_in.at[slot], self.y_in.at[land])
        if index < 3:
            from_below, from_above = (z > me.z) & (me.z > 0), (z < me.z) & (me.z < 3)
        else:
            from_below, from_above = me.z > 0, me.z < 3

        @pl.when(from_below)
        def _():
            self.along(z, 0, piece, True).wait_recv()
            self.add(kept, kept, self.z_in.at[land])

        @pl.when(from_above)
        def _():
            self.along(z, 0, piece, False).wait_recv()
            self.add(kept, kept, self.z_in.at[4 * n + piece if index == 3 else land])

        if index < 3:
            self.add(self.z_out.at[number], kept)

            @pl.when(z > me.z)
            def _():
                self.along(z, index, piece, True).start()

            @pl.when(z < me.z)
            def _():
                self.along(z, index, piece, False).start()
        else:
            finish(piece, kept)

    def drain(self):
        me, n = self.me, self.pieces
        for slot in range(8 * n):
            self.partner(slot).wait_send()
        for index in range(4):
            z = self.line(index)
            for piece in range(n):
                self.across(z, index, piece).wait_send()
                if index < 3:

                    @pl.when(z > me.z)
                    def _():
                        self.along(z, index, piece, True).wait_send()

                    @pl.when(z < me.z)
                    def _():
                        self.along(z, index, piece, False).wait_send()


def write_total(total_out):
    def finish(piece, kept):
        width = kept.shape[-1]
        total_out[:, piece * width : (piece + 1) * width] = kept[...]

    return finish


def leave(stage, parts, sems):
    copies = []

    def run(number, work, place):
        if number >= 2:
            copies[number - 2].wait()
        slot = stage.at[number % 2]
        work(slot)
        copies.append(pltpu.make_async_copy(slot, place, sems.at[number]))
        copies[number].start()

    def end():
        for copy in copies[-2:]:
            copy.wait()

    return [functools.partial(run, number, *part) for number, part in enumerate(parts)], end


def own_last(me, block, first):
    return jnp.concatenate([block[first + 1 - me.k], block[first + me.k]], axis=0)


def params(collective_id):
    return pltpu.CompilerParams(
        collective_id=collective_id, has_side_effects=True, vmem_limit_bytes=60 << 20
    )


def turn(me, step):
    dz, dy, dk = step // 4, (step // 2) % 2, step % 2
    to = me.at((me.z + dz) % 4, (me.y + dy) % 2, (me.k + dk) % 2)
    source = me.at((me.z + 4 - dz) % 4, (me.y + dy) % 2, (me.k + dk) % 2)
    return to, source


def cuts(rows):
    return ((0, rows // 2), (rows // 2, rows * 7 // 8 - rows // 2), (rows * 7 // 8, rows // 8))


EARLY = [False, False, True]


def pieces_of(array):
    return [
        lambda place, start=start, size=size: array.at[place, pl.ds(start, size)]
        for start, size in cuts(array.shape[1])
    ]


def scale_of(values):
    return lax.rsqrt(jnp.mean(values * values, axis=-1, keepdims=True) + norm_eps)


def norm_back(values, scale, weighted):
    inner = jnp.mean(values * weighted, axis=-1, keepdims=True)
    return scale * weighted - values * (scale * scale * scale * inner)


def by_rows(total, work, rows=32):
    @pl.loop(0, total // rows)
    def _(index):
        work(pl.ds(pl.multiple_of(index * rows, rows), rows))


def down_rows(row, width):
    full = jnp.broadcast_to(row[...].astype(F32), (width, row.shape[1]))
    return jnp.transpose(full)


def spread_kernel(
    unit, grad, w_query, w_key, w_value, w_gate, w_up, gain_one, gain_two, out_w, down,
    units, grads, query, key, value, cosine, sine, qkv_full, gate_up_half, out_all, down_other, *scratch
):
    gather_sems = scratch[: Gather.count]
    (qs, qr, qxs, qxr, ps, pr, os, ox, orecv, local, dsem, leave, units_here, grads_here, qkv_all, qkv, gate_up) = scratch[Gather.count :]
    me = Place()
    own = [
        pltpu.make_async_copy(grad, grads_here.at[me.c], local.at[1]),
        pltpu.make_async_copy(qkv.at[me.c], qkv_all.at[me.s, me.c], local.at[2]),
        pltpu.make_async_copy(gate_up.at[me.c], gate_up_half.at[me.c], local.at[3]),
    ]
    own[0].start()
    ready = greet_plane(me)
    over = (1 - me.s, me.c)
    tokens = unit.shape[0]

    def to_unit(at):
        values = unit[at, :].astype(F32)
        units_here[me.c, at] = (values * scale_of(values)).astype(LOW)

    by_rows(tokens, to_unit)
    ready()
    rows = tokens // 2
    gather = Gather(me, pieces_of(units_here) + pieces_of(grads_here), [False] * 6, *gather_sems)
    down_copy = remote(down, down_other, dsem.at[0], dsem.at[1], over)

    def send_qkv(step):
        to, _ = turn(me, step)
        return remote(qkv.at[to], qkv_all.at[me.s, me.c], qs.at[step], qr.at[me.c], (me.s, to))

    def send_gate_up(step):
        to, _ = turn(me, step)
        return remote(gate_up.at[to], gate_up_half.at[me.c], ps.at[step], pr.at[me.c], (me.s, to))

    def forward(source):
        block = qkv_all.at[me.s, source]
        return remote(block, block, qxs.at[source], qxr.at[source], over)

    holder = me.at(me.z, me.y, me.s)
    out_local = pltpu.make_async_copy(out_w, out_all.at[me.k], local.at[4])
    out_near = remote(out_w, out_all.at[me.k], os.at[0], orecv.at[me.k], (me.s, me.at(me.z, me.y, 1 - me.k)))
    out_far = remote(out_w, out_all.at[me.k], ox, orecv.at[me.k], (1 - me.s, holder))

    own[0].wait()
    gather.begin()
    width = query.shape[3]
    weight_rows = w_query.shape[0]
    one = down_rows(gain_one, width)
    for place in range(16):
        head = place // 2 + 8 * (place % 2)
        for index, weight in enumerate((w_query, w_key, w_value)):
            block = weight[:, head * width : (head + 1) * width].astype(F32) * one
            qkv[place, :, index * width : (index + 1) * width] = block.astype(LOW)
    own[1].start()
    for step in range(1, 16):
        send_qkv(step).start()
    units_of = gate_up.shape[2] // 4
    two = down_rows(gain_two, units_of)
    for place in range(16):
        for index, weight in enumerate((w_gate, w_up)):
            for half in range(2):
                start = (half * 16 + place) * units_of
                block = weight[:, start : start + units_of].astype(F32) * two
                start = (2 * index + half) * units_of
                gate_up[place, :, start : start + units_of] = block.astype(LOW)
    own[2].start()
    own[1].wait()
    forward(me.c).start()
    out_far.start()

    @pl.when(holder == me.c)
    def _():
        out_local.start()

    @pl.when(holder != me.c)
    def _():
        out_near.start()

    down_copy.start()
    leaving = []

    half_width = width // 2
    lane = lax.broadcasted_iota(jnp.int32, (rows, width), 1)
    row = lax.broadcasted_iota(jnp.int32, (rows, width), 0)
    freqs = jnp.exp((lane % half_width).astype(F32) * (-2.0 * math.log(rope_base) / width))
    sign = jnp.where(lane < half_width, 1.0, -1.0)

    @pl.loop(0, 16)
    def _(place):
        angles = row_place(place, row, rows // 2).astype(F32) * freqs
        cosine[place] = jnp.cos(angles)
        sine[place] = jnp.sin(angles) * sign

    def write_out(z, y):
        pair = z * 2 + y
        both = pl.ds(2 * pair, 2)
        number = len(leaving)
        for index, (here, there) in enumerate(((units_here, units), (grads_here, grads))):
            copy = pltpu.make_async_copy(here.at[both], there.at[both], leave.at[2 * number + index])
            copy.start()
            leaving.append(copy)

    def turned(values, both):
        swapped = pltpu.roll(values, width // 2, axis=1)
        place_cos = cosine[both].reshape(2 * rows, width)
        place_sin = sine[both].reshape(2 * rows, width)
        return (values * place_cos - swapped * place_sin).astype(LOW).reshape(2, rows, width)

    def project(z, y):
        both = pl.ds(2 * (z * 2 + y), 2)
        model = unit.shape[1]
        weights = qkv_all[...].reshape(model, 3 * width)
        for seq in range(2):
            block = units_here[both, seq * rows : (seq + 1) * rows].reshape(2 * rows, model)
            result = jnp.dot(block, weights, preferred_element_type=F32)
            query[both, seq] = turned(result[:, :width], both)
            key[both, seq] = turned(result[:, width : 2 * width], both)
            value[both, seq] = result[:, 2 * width :].astype(LOW).reshape(2, rows, width)

    steps = list(range(1, 16))
    waiting, ready = [(me.z, me.y)], []
    for index in range(4):
        for step in steps[4 * index : 4 * index + 4]:
            send_gate_up(step).start()
        gather.round(index)
        for z, y in waiting:
            gather.settle(z, y)
            write_out(z, y)
        ready += waiting
        waiting = [(gather.line(index), 1 - me.y)]
        if index < 3:
            waiting.append((gather.line(index + 1), me.y))
        if index == 1:
            for step in steps:
                _, source = turn(me, step)
                remote(qkv.at[0], qkv_all.at[me.s, source], qs.at[step], qr.at[source], over).wait_recv()
                forward(source).start()
        if index == 2:
            for source in range(16):
                forward(source).wait_send()
                forward(source).wait_recv()
            leave_qkv = pltpu.make_async_copy(qkv_all, qkv_full, local.at[5])
            leave_qkv.start()
        if index >= 2:
            for z, y in ready:
                project(z, y)
            ready = []
    for z, y in waiting:
        gather.settle(z, y)
        write_out(z, y)
        project(z, y)
    gather.finish()
    own[2].wait()
    leave_qkv.wait()
    for copy in leaving:
        copy.wait()
    for step in steps:
        _, source = turn(me, step)
        send_qkv(step).wait_send()
        send_gate_up(step).wait_send()
        remote(gate_up.at[0], gate_up_half.at[source], ps.at[step], pr.at[source], over).wait_recv()
    out_far.wait_send()
    down_copy.wait()

    @pl.when(holder == me.c)
    def _():
        out_local.wait()
        remote(out_w, out_all.at[1 - me.k], ox, orecv.at[1 - me.k], over).wait_recv()

    @pl.when(holder != me.c)
    def _():
        out_near.wait_send()
        for half in range(2):
            remote(out_w, out_all.at[half], ox, orecv.at[half], over).wait_recv()


def spread(unit, grad, w_query, w_key, w_value, w_gate, w_up, gain_one, gain_two, out_w, down):
    def shape(lead, array):
        return jax.ShapeDtypeStruct(lead + array.shape, array.dtype)

    tokens, model = unit.shape
    width = model // 16
    weight_rows = w_query.shape[0]
    qkv = (weight_rows, 3 * width)
    gate_up = (weight_rows, 2 * w_gate.shape[1] // 16)
    heads = jax.ShapeDtypeStruct((16, 2, tokens // 2, width), LOW)
    table = jax.ShapeDtypeStruct((16, tokens // 2, width), F32)
    return pl.pallas_call(
        spread_kernel,
        out_shape=[
            shape((16,), unit),
            shape((16,), grad),
            heads,
            heads,
            heads,
            table,
            table,
            jax.ShapeDtypeStruct((2, 16) + qkv, LOW),
            jax.ShapeDtypeStruct((16,) + gate_up, LOW),
            shape((2,), out_w),
            shape((), down),
        ],
        in_specs=[IN_VMEM, ANYWHERE] + [IN_VMEM] * 7 + [ANYWHERE] * 2,
        out_specs=[ANYWHERE] * 2 + [IN_VMEM] * 5 + [ANYWHERE] * 4,
        scratch_shapes=Gather.sems(6)
        + [DMA((16,))] * 6
        + [DMA((1,)), DMA, DMA((2,)), DMA((6,)), DMA((2,)), DMA((32,))]
        + [pltpu.VMEM((16, tokens, model), LOW)] * 2
        + [pltpu.VMEM((2, 16) + qkv, LOW), pltpu.VMEM((16,) + qkv, LOW), pltpu.VMEM((16,) + gate_up, LOW)],
        compiler_params=params(0),
    )(unit, grad, w_query, w_key, w_value, w_gate, w_up, gain_one, gain_two, out_w, down)


def row_place(place, row, strip):
    return jnp.where(row < strip, place * strip + row, (31 - place) * strip + row - strip)


def key_places(strip):
    index = lax.broadcasted_iota(jnp.int32, (1, 32 * strip), 1)
    return row_place(index // (2 * strip), index % (2 * strip), strip)


def query_places(pair, strip):
    index = lax.broadcasted_iota(jnp.int32, (4 * strip, 1), 0)
    return row_place(2 * pair + index // (2 * strip), index % (2 * strip), strip)


def of_pair(block, pair, seq):
    rows, width = block.shape[2:]
    return block[pl.ds(2 * pair, 2), seq].reshape(2 * rows, width)


def forward_kernel(
    shift, valid, query, key, value, out_w, token_far, grad_far, grads, gate_up, down_own, down_other,
    grad_state, branch, hidden_own_far, attended_far, hidden_far, down_far, gate_up_grad, *scratch
):
    me = Place()
    hidden_own, attended, hidden, down_full, token, grad_own, side = scratch[-15:-8]
    tokens, model = token.shape
    width = hidden.shape[2]
    gather_sems = scratch[Scatter.count : Scatter.count + Gather.count]
    units, grad_gate_up, gate_up_full, grads_here, stage, leaving, local, swap_sems = scratch[-8:]
    scatter = Scatter(me, scratch)
    brought = [
        pltpu.make_async_copy(gate_up, gate_up_full.at[me.s], local.at[0]),
        pltpu.make_async_copy(down_own, down_full.at[me.s], local.at[1]),
        pltpu.make_async_copy(down_other, down_full.at[1 - me.s], local.at[2]),
        pltpu.make_async_copy(grads, grads_here, local.at[3]),
    ]
    near = [
        pltpu.make_async_copy(token_far, token, side.at[0]),
        pltpu.make_async_copy(grad_far, grad_own, side.at[1]),
    ]
    away = [
        pltpu.make_async_copy(attended, attended_far, side.at[2]),
        pltpu.make_async_copy(hidden_own, hidden_own_far, side.at[3]),
        pltpu.make_async_copy(hidden, hidden_far, side.at[4]),
        pltpu.make_async_copy(down_full, down_far, side.at[5]),
    ]
    ready = greet(me, over_seq=True)
    swap = remote(gate_up, gate_up_full.at[me.s], swap_sems.at[0], swap_sems.at[1], (1 - me.s, me.c))
    rows, depth = query.shape[2], query.shape[3]
    strip = rows // 2
    length = rows * 16
    scale = depth ** (-0.5)

    def attention(pair):
        where = query_places(pair, strip)
        keys_at = key_places(strip)
        for seq in range(2):
            keys = key[:, seq].reshape(length, depth)
            values = value[:, seq].reshape(length, depth)
            logits = dot_right(of_pair(query, pair, seq), keys) * scale - shift
            live = (keys_at <= where) & (keys_at < valid[seq])
            weights = jnp.where(live, jax.nn.sigmoid(logits), 0.0).astype(LOW)
            attended[pl.ds(2 * pair, 2), pl.ds(seq * rows, rows)] = (
                jnp.dot(weights, values, preferred_element_type=F32).astype(LOW).reshape(2, rows, depth)
            )

    def out_terms(first, columns):
        return jnp.dot(own_last(me, attended, first), out_w[:, columns], preferred_element_type=F32)

    def met():
        ready()
        swap.start()
        for copy in near + brought:
            copy.start()

    scatter.run(attention, out_terms, write_total(hidden_own), ready=met)
    scatter.drain()
    for copy in near:
        copy.wait()

    def to_unit(at):
        values = hidden_own[at, :] + token[at, :].astype(F32)
        hidden_own[at, :] = values
        units[me.c, at] = (values * scale_of(values)).astype(LOW)

    by_rows(tokens, to_unit)
    gather = Gather(me, pieces_of(units), EARLY, *gather_sems)
    rows_of = gate_up_full.shape[1] * gate_up_full.shape[2]
    units_of = down_full.shape[1]
    first = [True]

    def consume(pair):
        if first[0]:
            for copy in brought:
                copy.wait()
            swap.wait()
            first[0] = False
        both = pl.ds(2 * pair, 2)

        def dot_rows(rows, columns):
            return jnp.dot(
                rows,
                gate_up_full[:, :, :, columns].reshape(2 * rows_of, units_of),
                preferred_element_type=F32,
            )

        @pl.loop(0, 2)
        def _(half):
            gate_at = pl.ds(pl.multiple_of(half * units_of, units_of), units_of)
            up_at = pl.ds(pl.multiple_of(width + half * units_of, units_of), units_of)
            rows = units[both].reshape(2 * tokens, model)
            gate = dot_rows(rows, gate_at)
            up = dot_rows(rows, up_at)
            grad = dot_right(grads_here[both].reshape(2 * tokens, model), down_full[half])
            sig = jax.nn.sigmoid(gate)
            silu = gate * sig

            def store(target, columns, value):
                target[both, :, columns] = value.astype(LOW).reshape(2, tokens, units_of)

            store(hidden, gate_at, silu * up)
            store(grad_gate_up, gate_at, grad * up * (sig * (1.0 + gate * (1.0 - sig))))
            store(grad_gate_up, up_at, grad * silu)

    gather.run(consume)
    for copy in away:
        copy.start()
    block_rows = gate_up_full.shape[2]

    def unit_terms(first, columns):
        start, size = columns.start, columns.size
        blocks = size // block_rows
        block = start // block_rows
        weights = gate_up_full[block // 16, pl.ds(block % 16, blocks)].reshape(size, 2 * width)
        return dot_right(own_last(me, grad_gate_up, first), weights)

    every = 16 * tokens
    part = model // 8

    def gate_up_part(number):
        def work(slot):
            left = units[:, :, number * part : (number + 1) * part].reshape(every, part)
            slot[...] = dot_left(left, grad_gate_up[...].reshape(every, 2 * width)).astype(LOW)

        return work, gate_up_grad.at[pl.ds(number * part, part)]

    fillers, end = leave(stage, [gate_up_part(n) for n in range(8)], leaving)
    scatter.run(None, unit_terms, write_total(grad_state), fillers)

    def to_state(at):
        values = hidden_own[at, :]
        back = norm_back(values, scale_of(values), grad_state[at, :])
        state = grad_own[at, :].astype(F32) + back
        grad_state[at, :] = state
        branch[at, :] = state.astype(LOW)

    by_rows(tokens, to_state)
    end()
    for copy in away:
        copy.wait()
    scatter.drain()
    gather.finish()


def forward(shift, valid, query, key, value, out_w, token, grad_own, grads, gate_up, down_own, down_other):
    tokens, model = token.shape
    width = 2 * down_own.shape[0]
    full = jax.ShapeDtypeStruct((tokens, model), F32)
    return pl.pallas_call(
        functools.partial(forward_kernel, shift),
        out_shape=[
            full,
            jax.ShapeDtypeStruct((tokens, model), LOW),
            full,
            jax.ShapeDtypeStruct((16, tokens, query.shape[3]), LOW),
            jax.ShapeDtypeStruct((16, tokens, width), LOW),
            jax.ShapeDtypeStruct((2,) + down_own.shape, LOW),
            jax.ShapeDtypeStruct((model, 2 * width), LOW),
        ],
        in_specs=[IN_SMEM] + [IN_VMEM] * 4 + [ANYWHERE] * 6,
        out_specs=[IN_VMEM] * 2 + [ANYWHERE] * 5,
        scratch_shapes=Scatter.scratch(tokens, model)
        + Gather.sems(3)
        + [
            pltpu.VMEM((tokens, model), F32),
            pltpu.VMEM((16, tokens, query.shape[3]), LOW),
            pltpu.VMEM((16, tokens, width), LOW),
            pltpu.VMEM((2,) + down_own.shape, LOW),
            pltpu.VMEM((tokens, model), LOW),
            pltpu.VMEM((tokens, model), LOW),
            DMA((6,)),
        ]
        + [
            pltpu.VMEM((16, tokens, model), LOW),
            pltpu.VMEM((16, tokens, 2 * width), LOW),
            pltpu.VMEM((2,) + gate_up.shape, LOW),
            pltpu.VMEM((16, tokens, model), LOW),
            pltpu.VMEM((2, model // 8, 2 * width), LOW),
            DMA((8,)),
            DMA((4,)),
            DMA((2,)),
        ],
        compiler_params=params(1),
    )(valid, query, key, value, out_w, token, grad_own, grads, gate_up, down_own, down_other)


def attend_back_kernel(
    shift, valid, branch, units, gate_up, *rest
):
    far, rest = rest[:10], rest[10:]
    total_out, qkv_grad, out_grad, gate_up_other = rest[:4]
    key_sum, value_sum, branches, grad_qkv, units_here = rest[4:9]
    side, near, scratch = rest[9], rest[10:20], rest[20:]
    query, key, value, out_w, cosine, sine, qkv_w, attended, token, grad_state = near
    near_copies = [pltpu.make_async_copy(a, b, side.at[n]) for n, (a, b) in enumerate(zip(far, near))]
    me = Place()
    tokens, model = branch.shape
    gather = Gather(me, pieces_of(branches), EARLY, *scratch[Scatter.count : Scatter.count + Gather.count])
    sems, local = scratch[-2:]
    own = pltpu.make_async_copy(branch, branches.at[me.c], local.at[0])
    own.start()
    bring = pltpu.make_async_copy(units, units_here, local.at[1])
    ready = greet(me, over_seq=True)
    for copy in near_copies:
        copy.start()
    bring.start()
    own.wait()
    ready()
    over = (1 - me.s, me.c)
    swaps = [
        remote(gate_up.at[1 - me.s], gate_up_other, sems.at[0], sems.at[1], over),
    ]
    for copy in swaps:
        copy.start()
    rows, width = query.shape[2:]
    strip = rows // 2
    length = rows * 16
    scale = width ** (-0.5)
    key_sum[...] = jnp.zeros_like(key_sum)
    value_sum[...] = jnp.zeros_like(value_sum)

    def turn_back(values, places):
        swapped = pltpu.roll(values, width // 2, axis=1)
        turned = values * cosine[places].reshape(2 * rows, width)
        return (turned + swapped * sine[places].reshape(2 * rows, width)).astype(LOW).reshape(2, rows, width)

    first = [True]

    def consume(pair):
        if first[0]:
            for copy in near_copies[:6]:
                copy.wait()
            first[0] = False
        where = query_places(pair, strip)
        keys_at = key_places(strip)
        both = pl.ds(2 * pair, 2)
        for seq in range(2):
            here = pl.ds(seq * rows, rows)
            grad = dot_right(branches[both, here].reshape(2 * rows, -1), out_w[...]).astype(LOW)
            keys = key[:, seq].reshape(length, width)
            values = value[:, seq].reshape(length, width)
            queries = of_pair(query, pair, seq)
            logits = dot_right(queries, keys) * scale - shift
            live = (keys_at <= where) & (keys_at < valid[seq])
            sig = jnp.where(live, jax.nn.sigmoid(logits), 0.0)
            weights = sig.astype(LOW)
            grad_logits = (dot_right(grad, values) * (sig * (1.0 - sig))).astype(LOW)
            grad_query = jnp.dot(grad_logits, keys, preferred_element_type=F32) * scale
            grad_qkv[both, here, 0:width] = turn_back(grad_query, both)
            key_sum[seq] += dot_left(grad_logits, queries)
            value_sum[seq] += dot_left(weights, grad)

    gather.run(consume)

    def prepare(pair):
        both = pl.ds(2 * pair, 2)
        at = pl.ds(pl.multiple_of(pair * 2 * rows, 2 * rows), 2 * rows)
        for seq in range(2):
            here = pl.ds(seq * rows, rows)
            grad_qkv[both, here, width : 2 * width] = turn_back(key_sum[seq, at] * scale, both)
            grad_qkv[both, here, 2 * width :] = value_sum[seq, at].astype(LOW).reshape(2, rows, width)

    scatter = Scatter(me, scratch)

    def produce(first, columns):
        return dot_right(own_last(me, grad_qkv, first), qkv_w[columns, :])

    every = 16 * tokens
    for copy in near_copies[6:] + [bring]:
        copy.wait()

    def qkv_part(number, part=model // 8):
        at = slice(number * part, (number + 1) * part)
        left = units_here[:, :, at].reshape(every, part)
        qkv_grad[at, :] = dot_left(left, grad_qkv[...].reshape(every, 3 * width)).astype(LOW)

    def out_part(number, part=model // 4):
        at = slice(number * part, (number + 1) * part)
        left = attended[...].reshape(every, width)
        out_grad[:, at] = dot_left(left, branches[:, :, at].reshape(every, part)).astype(LOW)

    fillers = [functools.partial(out_part, n) for n in range(4)]
    fillers += [functools.partial(qkv_part, n) for n in range(8)]
    scatter.run(prepare, produce, write_total(total_out), fillers)

    def to_input(at):
        values = token[at, :].astype(F32)
        total_out[at, :] = grad_state[at, :] + norm_back(values, scale_of(values), total_out[at, :])

    by_rows(tokens, to_input)
    scatter.drain()
    gather.finish()
    for copy in swaps:
        copy.wait()


def attend_back(
    shift, valid, branch, units, query, key, value, out_w, qkv_w, attended, cosine, sine, gate_up, token, grad_state
):
    tokens, model = branch.shape
    rows, width = query.shape[2:]
    near = (query, key, value, out_w, cosine, sine, qkv_w, attended, token, grad_state)
    return pl.pallas_call(
        functools.partial(attend_back_kernel, shift),
        out_shape=[
            jax.ShapeDtypeStruct((tokens, model), F32),
            jax.ShapeDtypeStruct((model, 3 * width), LOW),
            jax.ShapeDtypeStruct((width, model), LOW),
            jax.ShapeDtypeStruct(gate_up.shape[1:], LOW),
        ],
        in_specs=[IN_SMEM] + [ANYWHERE] * 13,
        out_specs=[IN_VMEM] * 3 + [ANYWHERE],
        scratch_shapes=[pltpu.VMEM((2, 16 * rows, width), F32)] * 2
        + [
            pltpu.VMEM((16, tokens, model), LOW),
            pltpu.VMEM((16, tokens, 3 * width), LOW),
            pltpu.VMEM((16, tokens, model), LOW),
        ]
        + [DMA((10,))]
        + [pltpu.VMEM(array.shape, array.dtype) for array in near]
        + Scatter.scratch(tokens, model)
        + Gather.sems(3)
        + [DMA((4,)), DMA((2,))],
        compiler_params=params(4),
    )(valid, branch, units, gate_up, *near)


def return_kernel(
    hidden_far, down_far, qkv_far, gate_up_far, gate_up_other, out_far, hidden_own_far, grads_far,
    total_out, qkv_back, gate_up_back, out_back, down_grad, down_other, *scratch
):
    (qx, qsum, qxs, qxr, qs, qr, psum, ps, pr, oland, os, orecv, hidden, down_w, px, sums, qkv, out_pair, hidden_own, grads, local, across) = scratch[
        Scatter.count :
    ]
    me = Place()
    ready = greet_plane(me)
    bring = [
        pltpu.make_async_copy(hidden_far, hidden, local.at[0]),
        pltpu.make_async_copy(down_far, down_w, local.at[1]),
        pltpu.make_async_copy(gate_up_far.at[me.s], psum, local.at[2]),
        pltpu.make_async_copy(gate_up_other, px, local.at[3]),
        pltpu.make_async_copy(qkv_far, qkv, local.at[4]),
        pltpu.make_async_copy(out_far, out_pair, local.at[5]),
        pltpu.make_async_copy(hidden_own_far, hidden_own, local.at[6]),
        pltpu.make_async_copy(grads_far, grads, local.at[7]),
    ]
    for copy in bring:
        copy.start()
    over = (1 - me.s, me.c)

    def cross(place):
        return remote(qkv.at[1 - me.s, place], qx.at[place], qxs.at[place], qxr.at[place], over)

    def send(sums, back, s_sem, r_sem, step):
        to, _ = turn(me, step)
        return remote(sums.at[to], back.at[me.c], s_sem.at[step], r_sem.at[me.c], (me.s, to))

    holder = me.at(me.z, me.y, me.s)

    def out_send(target_core, same):
        target = (me.s if same else 1 - me.s, me.at(me.z, me.y, target_core))
        slot = 0 if same else 1
        return remote(out_pair.at[target_core], oland.at[me.s], os.at[slot], orecv.at[me.s], target)

    inside = me.k == me.s

    def met():
        ready()
        for step in range(1, 16):
            send(psum, gate_up_back, ps, pr, step).start()
        for copy in bring[4:]:
            copy.wait()
        for step in range(1, 16):
            cross(turn(me, step)[0]).start()
        cross(me.c).start()

        @pl.when(inside)
        def _():
            out_send(1 - me.k, True).start()

        @pl.when(jnp.logical_not(inside))
        def _():
            out_send(me.k, False).start()
            remote(
                out_pair.at[1 - me.k], oland.at[me.s], os.at[0], orecv.at[me.s],
                (1 - me.s, me.at(me.z, me.y, 1 - me.k)),
            ).start()

    def between():
        for step in range(1, 16):
            to, _ = turn(me, step)
            cross(to).wait_recv()
            qsum[to] = (qkv[me.s, to].astype(F32) + qx[to].astype(F32)).astype(LOW)
            send(qsum, qkv_back, qs, qr, step).start()
        cross(me.c).wait_recv()
        qkv_back[me.c] = (qkv[me.s, me.c].astype(F32) + qx[me.c].astype(F32)).astype(LOW)

    scatter = Scatter(me, scratch)

    def produce(first, columns):
        return jnp.dot(own_last(me, hidden, first), down_w[:, columns], preferred_element_type=F32)

    for copy in bring[:4]:
        copy.wait()

    @pl.loop(0, 16)
    def _(place):
        psum[place] = (psum[place].astype(F32) + px[place].astype(F32)).astype(LOW)

    gate_up_back[me.c] = psum[me.c]
    down_swap = remote(down_grad.at[1 - me.s], down_other, across.at[0], across.at[1], over)
    parts, double, part = down_other.shape
    every = hidden.shape[0] * hidden.shape[1]

    def down_part(half, number):
        seq = 1 - me.s if half == 0 else me.s
        thin = double // 2
        start = pl.multiple_of((seq * parts + number) * thin, thin)
        left = hidden[:, :, pl.ds(start, thin)].reshape(every, thin)
        for side in range(2):
            right = grads[:, :, side * part : (side + 1) * part].reshape(every, part)
            down_grad[seq, number, pl.ds(side * thin, thin)] = dot_left(left, right).astype(LOW)
        if half == 0 and number == parts - 1:
            down_swap.start()

    fillers = [between] + [functools.partial(down_part, half, n) for half in range(2) for n in range(parts)]
    scatter.run(None, produce, write_total(sums), fillers, met)
    down_swap.wait()

    def to_out(at):
        total_out[at, :] = (sums[at, :] + hidden_own[at, :]).astype(LOW)

    by_rows(total_out.shape[0], to_out)
    scatter.drain()
    for step in range(1, 16):
        to, source = turn(me, step)
        for sums, back, s_sem, r_sem in ((qsum, qkv_back, qs, qr), (psum, gate_up_back, ps, pr)):
            remote(sums.at[0], back.at[source], s_sem.at[step], r_sem.at[source], over).wait_recv()
            send(sums, back, s_sem, r_sem, step).wait_send()
        cross(to).wait_send()
    cross(me.c).wait_send()

    @pl.when(inside)
    def _():
        out_send(1 - me.k, True).wait_send()
        remote(out_pair.at[0], oland.at[1 - me.s], os.at[0], orecv.at[1 - me.s], over).wait_recv()
        out_back[...] = out_pair[me.k].astype(F32) + oland[1 - me.s].astype(F32)

    @pl.when(jnp.logical_not(inside))
    def _():
        out_send(me.k, False).wait_send()
        out_send(1 - me.k, True).wait_send()
        for half in range(2):
            remote(out_pair.at[0], oland.at[half], os.at[0], orecv.at[half], over).wait_recv()
        out_back[...] = oland[0].astype(F32) + oland[1].astype(F32)


def give_back(hidden, down_w, qkv, gate_up, gate_up_other, out_pair, hidden_own, grads):
    tokens, model = hidden.shape[1], down_w.shape[1]
    down_half = (2, hidden.shape[2] // 2, model // 2)
    block = lambda array: pltpu.VMEM(array.shape[1:], LOW)
    return pl.pallas_call(
        return_kernel,
        out_shape=[
            jax.ShapeDtypeStruct((tokens, model), LOW),
            jax.ShapeDtypeStruct(qkv.shape[1:], LOW),
            jax.ShapeDtypeStruct(gate_up.shape[1:], LOW),
            jax.ShapeDtypeStruct(out_pair.shape[1:], F32),
            jax.ShapeDtypeStruct((2,) + down_half, LOW),
            jax.ShapeDtypeStruct(down_half, LOW),
        ],
        in_specs=[ANYWHERE] * 8,
        out_specs=[IN_VMEM] * 6,
        scratch_shapes=Scatter.scratch(tokens, model)
        + [block(qkv), block(qkv)]
        + [DMA((16,))] * 4
        + [block(gate_up)]
        + [DMA((16,))] * 2
        + [pltpu.VMEM(out_pair.shape, LOW), DMA((2,)), DMA((2,))]
        + [pltpu.VMEM(hidden.shape, LOW), pltpu.VMEM(down_w.shape, LOW), block(gate_up)]
        + [pltpu.VMEM((tokens, model), F32), pltpu.VMEM(qkv.shape, LOW), pltpu.VMEM(out_pair.shape, LOW)]
        + [pltpu.VMEM((tokens, model), F32), pltpu.VMEM(grads.shape, LOW), DMA((8,)), DMA((2,))],
        compiler_params=params(5),
    )(hidden, down_w, qkv, gate_up, gate_up_other, out_pair, hidden_own, grads)


def assemble_kernel(
    gain_one, gain_two, qkv_far, w_query_far, w_key_far, w_value_far, gate_up_far, w_gate_far, w_up_far,
    down_far, down_other_far,
    query_grad, key_grad, value_grad, gate_grad, up_grad, down_grad, gain_one_grad, gain_two_grad, *near
):
    qkv_back, w_query, w_key, w_value, gate_up_back, w_gate, w_up, down_own, down_other, sems = near
    far = (qkv_far, w_query_far, w_key_far, w_value_far, gate_up_far, w_gate_far, w_up_far)
    far += (down_far.at[lax.axis_index("seq")], down_other_far)
    copies = [pltpu.make_async_copy(a, b, sems.at[n]) for n, (a, b) in enumerate(zip(far, near))]
    for copy in copies:
        copy.start()

    def lanes(total):
        return jnp.sum(jnp.transpose(total), axis=0, keepdims=True)

    width = qkv_back.shape[2] // 3
    rows = qkv_back.shape[1]
    one = down_rows(gain_one, width)
    total = jnp.zeros((rows, width), F32)
    for copy in copies[:4]:
        copy.wait()
    for place in range(16):
        at = slice((place // 2 + 8 * (place % 2)) * width, (place // 2 + 8 * (place % 2) + 1) * width)
        for index, (weight, target) in enumerate(
            ((w_query, query_grad), (w_key, key_grad), (w_value, value_grad))
        ):
            block = qkv_back[place, :, index * width : (index + 1) * width].astype(F32)
            target[:, at] = block * one
            total += block * weight[:, at].astype(F32)
    gain_one_grad[...] = lanes(total)
    width = gate_up_back.shape[2] // 4
    two = down_rows(gain_two, width)
    total = jnp.zeros((rows, width), F32)
    for copy in copies[4:7]:
        copy.wait()
    for place in range(16):
        for half in range(2):
            at = slice((half * 16 + place) * width, (half * 16 + place + 1) * width)
            for index, (weight, target) in enumerate(((w_gate, gate_grad), (w_up, up_grad))):
                start = (2 * index + half) * width
                block = gate_up_back[place, :, start : start + width].astype(F32)
                target[:, at] = block * two
                total += block * weight[:, at].astype(F32)
    gain_two_grad[...] = lanes(total)
    for copy in copies[7:]:
        copy.wait()
    parts, double, part = down_own.shape
    depth = double // 2
    for number in range(parts):
        for half in range(2):
            at = slice(half * depth, (half + 1) * depth)
            down_grad[number * depth : (number + 1) * depth, half * part : (half + 1) * part] = (
                down_own[number, at].astype(F32) + down_other[number, at].astype(F32)
            )


def assemble(gain_one, gain_two, qkv_back, w_query, w_key, w_value, gate_up_back, w_gate, w_up, down, down_other):
    rows, model = w_query.shape
    narrow = jax.ShapeDtypeStruct((rows, model), F32)
    wide = jax.ShapeDtypeStruct(w_gate.shape, F32)
    gain = jax.ShapeDtypeStruct((1, rows), F32)
    parts, double, part = down_other.shape
    near = (qkv_back, w_query, w_key, w_value, gate_up_back, w_gate, w_up, down_other, down_other)
    return pl.pallas_call(
        assemble_kernel,
        out_shape=[narrow] * 3
        + [wide] * 2
        + [jax.ShapeDtypeStruct((parts * double // 2, 2 * part), F32)]
        + [gain] * 2,
        in_specs=[IN_VMEM] * 2 + [ANYWHERE] * 9,
        out_specs=[IN_VMEM] * 8,
        scratch_shapes=[pltpu.VMEM(array.shape, LOW) for array in near] + [DMA((9,))],
        compiler_params=pltpu.CompilerParams(vmem_limit_bytes=60 << 20),
    )(gain_one, gain_two, qkv_back, w_query, w_key, w_value, gate_up_back, w_gate, w_up, down, down_other)


def move_tokens_step(
    layer_in,
    valid_len,
    norm1_gain,
    w_query,
    w_key,
    w_value,
    w_out,
    norm2_gain,
    w_gate,
    w_up,
    w_down,
    cotangent,
):
    local_rows, local_seqs, model = layer_in.shape
    strip = local_rows // 2
    width = model // HEADS
    cp_devices = 16
    tokens = local_rows * local_seqs
    shift = math.log(cp_devices * local_rows)
    weight_rows = w_gate.shape[0]
    gain_one, gain_two = norm1_gain[None], norm2_gain[None]

    def by_seq(values):
        return values.transpose(1, 0, 2).reshape(tokens, model)

    def by_row(values):
        return values.reshape(local_seqs, local_rows, model).transpose(1, 0, 2)

    token_local = by_seq(layer_in)
    grad_local = by_seq(cotangent)

    units, grads, query, key, value, cosine, back_sine, qkv_w, gate_up_own, head_out, down_other = spread(
        token_local, grad_local, w_query, w_key, w_value, w_gate, w_up,
        gain_one, gain_two, w_out, w_down,
    )
    qkv_w = qkv_w.reshape(model, 3 * width)
    head_out = head_out.reshape(width, model)
    grad_state, branch, hidden_state, attended, hidden, down_full, gate_up_grad = forward(
        shift, valid_len, query, key, value, head_out, token_local, grad_local, grads, gate_up_own, w_down, down_other
    )
    gate_up_grad = gate_up_grad.reshape(2, cp_devices, weight_rows, -1)
    in_grad, qkv_grad, out_grad, gate_up_grad_other = attend_back(
        shift, valid_len, branch, units, query, key, value, head_out, qkv_w, attended,
        cosine, back_sine, gate_up_grad, token_local, grad_state,
    )
    layer_out, qkv_back, gate_up_back, out_back, down_grad, down_grad_other = give_back(
        hidden,
        down_full.reshape(-1, model),
        qkv_grad.reshape(2, cp_devices, weight_rows, -1),
        gate_up_grad,
        gate_up_grad_other,
        out_grad.reshape(2, width // 2, model),
        hidden_state,
        grads,
    )
    query_grad, key_grad, value_grad, gate_grad, up_grad, down_back, gain_one_grad, gain_two_grad = assemble(
        gain_one, gain_two, qkv_back, w_query, w_key, w_value, gate_up_back, w_gate, w_up, down_grad, down_grad_other
    )
    return (
        by_row(layer_out),
        by_row(in_grad),
        gain_one_grad[0],
        query_grad,
        key_grad,
        value_grad,
        out_back,
        gain_two_grad[0],
        gate_grad,
        up_grad,
        down_back,
    )


def solution(mesh):
    fits = mesh.shape["cp"] == HEADS and mesh.shape["seq"] == 2
    on_device = move_tokens_step if fits else gather_weights_step
    placed = (
        P("cp", "seq", None),
        P("seq"),
        P(("seq", "cp")),
        P(("seq", "cp"), None),
        P(("seq", "cp"), None),
        P(("seq", "cp"), None),
        P(("seq", "cp"), None),
        P(("seq", "cp")),
        P(("seq", "cp"), None),
        P(("seq", "cp"), None),
        P(("seq", "cp"), None),
        P("cp", "seq", None),
    )
    return jax.shard_map(
        on_device,
        mesh=mesh,
        in_specs=placed,
        out_specs=(
            P("cp", "seq", None),
            P("cp", "seq", None),
            P(("seq", "cp")),
            P(("seq", "cp"), None),
            P(("seq", "cp"), None),
            P(("seq", "cp"), None),
            P(("seq", "cp"), None),
            P(("seq", "cp")),
            P(("seq", "cp"), None),
            P(("seq", "cp"), None),
            P(("seq", "cp"), None),
        ),
        check_vma=False,
    )
```

```python
import functools
import math

import jax
import jax.numpy as jnp
from jax import lax
from jax.experimental import pallas as pl
from jax.experimental.pallas import tpu as pltpu
from jax.sharding import PartitionSpec as P

HEADS = 16


norm_eps = 1e-05
rope_base = 10000.0


def row_positions(indices, strip_rows, devices):
    owner_index = indices // (2 * strip_rows)
    within = indices % (2 * strip_rows)
    return jnp.where(
        within < strip_rows,
        owner_index * strip_rows + within,
        (2 * devices - 1 - owner_index) * strip_rows + within - strip_rows,
    )


def rotate(values, positions, num_heads):
    count_rows, model_width = values.shape
    head_width = model_width // num_heads
    half_width = head_width // 2
    freqs_table = rope_base ** (-2.0 * jnp.arange(half_width, dtype=jnp.float32) / head_width)
    angles = positions.astype(jnp.float32)[:, None] * freqs_table[None, :]
    cosine = jnp.cos(angles)[:, None, :]
    sine_table = jnp.sin(angles)[:, None, :]
    split_heads = values.reshape(count_rows, num_heads, head_width)
    former = split_heads[:, :, :half_width]
    latter = split_heads[:, :, half_width:]
    turned = jnp.concatenate(
        [former * cosine - latter * sine_table, latter * cosine + former * sine_table], axis=2
    )
    return turned.reshape(count_rows, model_width)


def norm_scale(values):
    return values * lax.rsqrt(jnp.mean(values * values, axis=-1, keepdims=True) + norm_eps)


def normed(values, gain_vector):
    return norm_scale(values) * gain_vector


def swiglu(gate_rows, up_rows):
    return jax.nn.silu(gate_rows) * up_rows


def dot_right(left, right):
    return lax.dot_general(
        left, right, (((1,), (1,)), ((), ())), preferred_element_type=jnp.float32
    )


def dot_left(left, right):
    return lax.dot_general(
        left, right, (((0,), (0,)), ((), ())), preferred_element_type=jnp.float32
    )


def split_blocks(array, block_rows):
    return array.reshape((array.shape[0] // block_rows, block_rows) + array.shape[1:])


def key_mask(query_pos, key_pos, valid_count):
    causal = key_pos[None, :] <= query_pos[:, None]
    live_keys = key_pos[None, :] < valid_count[:, None]
    return (causal[None, None, :, :] & live_keys[:, None, None, :]).astype(jnp.float32)


def scores_of(queries, key_rows, query_pos, key_pos, valid_count, score_shift):
    head_width = queries.shape[3]
    raw_scores = jnp.einsum(
        "qshd,kshd->shqk", queries, key_rows, preferred_element_type=jnp.float32
    )
    return (
        raw_scores * head_width ** (-0.5) - score_shift,
        key_mask(query_pos, key_pos, valid_count),
    )


def block_grads(queries, grad_rows, key_rows, values, query_pos, key_pos, valid_count, score_shift):
    logits, mask_table = scores_of(queries, key_rows, query_pos, key_pos, valid_count, score_shift)
    sigmoid_table = jax.nn.sigmoid(logits)
    weights_low = (sigmoid_table * mask_table).astype(jnp.bfloat16)
    grad_weights = jnp.einsum(
        "qshd,kshd->shqk", grad_rows, values, preferred_element_type=jnp.float32
    )
    grad_logits = (grad_weights * mask_table * (sigmoid_table * (1.0 - sigmoid_table))).astype(
        jnp.bfloat16
    )
    return (weights_low, grad_logits)


def make_norm_fold(normalized, pieces):
    gain_part = pieces[0].astype(jnp.float32)
    scaled = (normalized * gain_part).astype(jnp.bfloat16)
    totals = tuple(
        (
            jnp.dot(scaled, weight_piece, preferred_element_type=jnp.float32)
            for weight_piece in pieces[1:]
        )
    )
    return (gain_part,) + totals


def make_row_fold(left_rows, weight_piece):
    return jnp.dot(left_rows, weight_piece, preferred_element_type=jnp.float32)


def gather_weights_step(
    layer_in,
    valid_len,
    norm1_gain,
    w_query,
    w_key,
    w_value,
    w_out,
    norm2_gain,
    w_gate,
    w_up,
    w_down,
    cotangent,
):
    local_rows, local_seqs, model_width = layer_in.shape
    num_heads = HEADS
    head_width = model_width // num_heads
    strip_rows = local_rows // 2
    cp_devices = lax.axis_size("cp")
    cp_place = lax.axis_index("cp")
    seq_length = local_rows * cp_devices
    score_shift = math.log(seq_length)
    score_scale = head_width ** (-0.5)
    token_count = local_rows * local_seqs
    local_pos = row_positions(
        cp_place * local_rows + jnp.arange(local_rows, dtype=jnp.int32), strip_rows, cp_devices
    )
    token_pos = jnp.broadcast_to(local_pos[:, None], (local_rows, local_seqs)).reshape(token_count)
    every_pos = row_positions(jnp.arange(seq_length, dtype=jnp.int32), strip_rows, cp_devices)
    block_rows = math.gcd(seq_length, 512)
    head_shape = (local_rows, local_seqs, num_heads, head_width)
    row_shape = (local_rows, local_seqs, model_width)
    zero_heads = jnp.zeros(head_shape, jnp.float32)
    inputs = layer_in.reshape(token_count, model_width).astype(jnp.float32)
    input_norm = norm_scale(inputs)
    gain_one, query, key_proj, value = make_norm_fold(
        input_norm,
        (
            lax.all_gather(norm1_gain, ("seq", "cp"), axis=0, tiled=True),
            lax.all_gather(w_query, ("seq", "cp"), axis=0, tiled=True),
            lax.all_gather(w_key, ("seq", "cp"), axis=0, tiled=True),
            lax.all_gather(w_value, ("seq", "cp"), axis=0, tiled=True),
        ),
    )
    normed_one = (input_norm * gain_one).astype(jnp.bfloat16)
    query_low = rotate(query, token_pos, num_heads).astype(jnp.bfloat16)
    key_low = rotate(key_proj, token_pos, num_heads).astype(jnp.bfloat16)
    value_low = value.astype(jnp.bfloat16)
    query_heads = query_low.reshape(head_shape)
    key_local = key_low.reshape(row_shape)
    value_local = value_low.reshape(row_shape)
    key_piece = lax.all_gather(key_local, "cp", axis=0, tiled=True)
    value_piece = lax.all_gather(value_local, "cp", axis=0, tiled=True)
    piece_rows = key_piece.shape[0]
    piece_block = math.gcd(piece_rows, 512)
    piece_pos = row_positions(jnp.arange(piece_rows, dtype=jnp.int32), strip_rows, cp_devices)

    def scan_step(partial_sum, block_items):
        key_block, value_block, block_pos = block_items
        logits, mask_table = scores_of(
            query_heads,
            key_block.reshape(piece_block, local_seqs, num_heads, head_width),
            local_pos,
            block_pos,
            valid_len,
            score_shift,
        )
        weights_low = (jax.nn.sigmoid(logits) * mask_table).astype(jnp.bfloat16)
        added = jnp.einsum(
            "shqk,kshd->qshd",
            weights_low,
            value_block.reshape(piece_block, local_seqs, num_heads, head_width),
            preferred_element_type=jnp.float32,
        )
        return (partial_sum + added, None)

    result, _ = lax.scan(
        scan_step,
        zero_heads,
        (
            split_blocks(key_piece, piece_block),
            split_blocks(value_piece, piece_block),
            split_blocks(piece_pos, piece_block),
        ),
    )
    attended_low = result.reshape(token_count, model_width).astype(jnp.bfloat16)
    attn_branch = make_row_fold(
        attended_low, lax.all_gather(w_out, ("seq", "cp"), axis=0, tiled=True)
    )
    hidden_state = inputs + attn_branch
    hidden_norm = norm_scale(hidden_state)
    gain_two, gate_rows, up_rows = make_norm_fold(
        hidden_norm,
        (
            lax.all_gather(norm2_gain, ("seq", "cp"), axis=0, tiled=True),
            lax.all_gather(w_gate, ("seq", "cp"), axis=0, tiled=True),
            lax.all_gather(w_up, ("seq", "cp"), axis=0, tiled=True),
        ),
    )
    normed_two = (hidden_norm * gain_two).astype(jnp.bfloat16)
    hidden_units = swiglu(gate_rows, up_rows).astype(jnp.bfloat16)
    ff_branch = make_row_fold(
        hidden_units, lax.all_gather(w_down, ("seq", "cp"), axis=0, tiled=True)
    )
    layer_out = (hidden_state + ff_branch).astype(jnp.bfloat16).reshape(row_shape)
    grad_out = cotangent.reshape(token_count, model_width)
    gate_all, up_all, down_all = (
        lax.all_gather(w_gate, ("seq", "cp"), axis=0, tiled=True),
        lax.all_gather(w_up, ("seq", "cp"), axis=0, tiled=True),
        lax.all_gather(w_down, ("seq", "cp"), axis=0, tiled=True),
    )
    grad_hidden = dot_right(grad_out, down_all)
    _, pull_swiglu = jax.vjp(swiglu, gate_rows, up_rows)
    grad_gate, grad_up = pull_swiglu(grad_hidden)
    grad_gate_low = grad_gate.astype(jnp.bfloat16)
    grad_up_low = grad_up.astype(jnp.bfloat16)
    grad_norm_two = dot_right(grad_gate_low, gate_all) + dot_right(grad_up_low, up_all)
    _, pull_two = jax.vjp(normed, hidden_state, gain_two)
    grad_from_two, gain_two_term = pull_two(grad_norm_two)
    ff_grads = (
        lax.psum_scatter(gain_two_term, ("seq", "cp"), scatter_dimension=0, tiled=True),
        lax.psum_scatter(
            dot_left(normed_two, grad_gate_low), ("seq", "cp"), scatter_dimension=0, tiled=True
        ),
        lax.psum_scatter(
            dot_left(normed_two, grad_up_low), ("seq", "cp"), scatter_dimension=0, tiled=True
        ),
        lax.psum_scatter(
            dot_left(hidden_units, grad_out), ("seq", "cp"), scatter_dimension=0, tiled=True
        ),
    )
    grad_state = grad_out.astype(jnp.float32) + grad_from_two
    query_all, key_all, value_all, out_all = (
        lax.all_gather(w_query, ("seq", "cp"), axis=0, tiled=True),
        lax.all_gather(w_key, ("seq", "cp"), axis=0, tiled=True),
        lax.all_gather(w_value, ("seq", "cp"), axis=0, tiled=True),
        lax.all_gather(w_out, ("seq", "cp"), axis=0, tiled=True),
    )
    grad_branch_low = grad_state.astype(jnp.bfloat16)
    grad_attended_low = dot_right(grad_branch_low, out_all).astype(jnp.bfloat16)
    grad_heads = grad_attended_low.reshape(head_shape)
    key_heads_local = key_local.reshape(head_shape)
    value_heads_local = value_local.reshape(head_shape)
    keys_every, values_every, queries_every, grads_every = (
        lax.all_gather(key_local, "cp", axis=0, tiled=True),
        lax.all_gather(value_local, "cp", axis=0, tiled=True),
        lax.all_gather(query_low.reshape(row_shape), "cp", axis=0, tiled=True),
        lax.all_gather(grad_attended_low.reshape(row_shape), "cp", axis=0, tiled=True),
    )

    def key_step(partial_sums, block_items):
        query_block, grad_block_rows, block_pos = block_items
        query_part = query_block.reshape(block_rows, local_seqs, num_heads, head_width)
        grad_part = grad_block_rows.reshape(block_rows, local_seqs, num_heads, head_width)
        weights_low, grad_logits = block_grads(
            query_part,
            grad_part,
            key_heads_local,
            value_heads_local,
            block_pos,
            local_pos,
            valid_len,
            score_shift,
        )
        key_added = jnp.einsum(
            "shqk,qshd->kshd", grad_logits, query_part, preferred_element_type=jnp.float32
        )
        value_added = jnp.einsum(
            "shqk,qshd->kshd", weights_low, grad_part, preferred_element_type=jnp.float32
        )
        return ((partial_sums[0] + key_added, partial_sums[1] + value_added), None)

    (key_sum, value_sum), _ = lax.scan(
        key_step,
        (zero_heads, zero_heads),
        (
            split_blocks(queries_every, block_rows),
            split_blocks(grads_every, block_rows),
            split_blocks(every_pos, block_rows),
        ),
    )
    grad_key_rot = key_sum.reshape(token_count, model_width) * score_scale
    grad_value_sum = value_sum.reshape(token_count, model_width)

    def query_step(partial_sum, block_items):
        key_block, value_block, block_pos = block_items
        key_heads = key_block.reshape(block_rows, local_seqs, num_heads, head_width)
        _, grad_logits = block_grads(
            query_heads,
            grad_heads,
            key_heads,
            value_block.reshape(block_rows, local_seqs, num_heads, head_width),
            local_pos,
            block_pos,
            valid_len,
            score_shift,
        )
        added = jnp.einsum(
            "shqk,kshd->qshd", grad_logits, key_heads, preferred_element_type=jnp.float32
        )
        return (partial_sum + added, None)

    query_sum, _ = lax.scan(
        query_step,
        zero_heads,
        (
            split_blocks(keys_every, block_rows),
            split_blocks(values_every, block_rows),
            split_blocks(every_pos, block_rows),
        ),
    )
    grad_query_rot = query_sum.reshape(token_count, model_width) * score_scale
    grad_query_low = rotate(grad_query_rot, -token_pos, num_heads).astype(jnp.bfloat16)
    grad_key_low = rotate(grad_key_rot, -token_pos, num_heads).astype(jnp.bfloat16)
    grad_value_low = grad_value_sum.astype(jnp.bfloat16)
    grad_norm_one = (
        dot_right(grad_query_low, query_all)
        + dot_right(grad_key_low, key_all)
        + dot_right(grad_value_low, value_all)
    )
    _, pull_one = jax.vjp(normed, inputs, gain_one)
    grad_from_one, gain_one_term = pull_one(grad_norm_one)
    in_grad = (grad_state + grad_from_one).reshape(row_shape)
    attn_grads = (
        lax.psum_scatter(gain_one_term, ("seq", "cp"), scatter_dimension=0, tiled=True),
        lax.psum_scatter(
            dot_left(normed_one, grad_query_low), ("seq", "cp"), scatter_dimension=0, tiled=True
        ),
        lax.psum_scatter(
            dot_left(normed_one, grad_key_low), ("seq", "cp"), scatter_dimension=0, tiled=True
        ),
        lax.psum_scatter(
            dot_left(normed_one, grad_value_low), ("seq", "cp"), scatter_dimension=0, tiled=True
        ),
        lax.psum_scatter(
            dot_left(attended_low, grad_branch_low), ("seq", "cp"), scatter_dimension=0, tiled=True
        ),
    )
    return (
        layer_out,
        in_grad,
        attn_grads[0],
        attn_grads[1],
        attn_grads[2],
        attn_grads[3],
        attn_grads[4],
        ff_grads[0],
        ff_grads[1],
        ff_grads[2],
        ff_grads[3],
    )


MESH = pl.DeviceIdType.MESH
DMA = pltpu.SemaphoreType.DMA
LOW = jnp.bfloat16
F32 = jnp.float32
ANYWHERE = pl.BlockSpec(memory_space=pl.ANY)
IN_VMEM = pl.BlockSpec(memory_space=pltpu.VMEM)
IN_SMEM = pl.BlockSpec(memory_space=pltpu.SMEM)


class Place:
    def __init__(self):
        self.s = lax.axis_index("seq")
        self.c = lax.axis_index("cp")
        self.z = self.c // 4
        self.y = (self.c // 2) % 2
        self.k = self.c % 2

    def at(self, z, y, k):
        return z * 4 + y * 2 + k

    def device(self, place):
        return (self.s, place)


def pick(z, table):
    value = jnp.int32(table[0])
    for index in range(1, 4):
        value = jnp.where(z == index, jnp.int32(table[index]), value)
    return value


NEAREST = ((1, 0, 1, 2), (2, 2, 3, 1), (3, 3, 0, 0))
FARTHEST = ((3, 3, 0, 0), (2, 2, 3, 1), (1, 0, 1, 2))


def remote(source, target, send, recv, device):
    return pltpu.make_async_remote_copy(
        src_ref=source,
        dst_ref=target,
        send_sem=send,
        recv_sem=recv,
        device_id=device,
        device_id_type=MESH,
    )


def hail(device):
    pl.semaphore_signal(
        pltpu.get_barrier_semaphore(), inc=1, device_id=device, device_id_type=MESH
    )


def greet(me, over_seq=False):
    hail((me.s, me.at(me.z, 1 - me.y, me.k)))
    hail((me.s, me.at(me.z, me.y, 1 - me.k)))

    @pl.when(me.z < 3)
    def _():
        hail((me.s, me.at(me.z + 1, me.y, me.k)))

    @pl.when(me.z > 0)
    def _():
        hail((me.s, me.at(me.z - 1, me.y, me.k)))

    ends = (me.z == 0).astype(jnp.int32) + (me.z == 3).astype(jnp.int32)
    if over_seq:
        hail((1 - me.s, me.c))
    return lambda: pl.semaphore_wait(
        pltpu.get_barrier_semaphore(), 4 - ends + (1 if over_seq else 0)
    )


def greet_plane(me):
    for step in range(1, 16):
        hail((me.s, (me.c + step) % 16))
    hail((1 - me.s, me.c))
    hail((1 - me.s, me.at(me.z, me.y, 1 - me.k)))
    return lambda: pl.semaphore_wait(pltpu.get_barrier_semaphore(), 17)


class Gather:
    def __init__(self, me, views, early, z_sem, far_sem, y_sem, k_sem, recv):
        self.me, self.views, self.early = me, views, early
        self.z_sem, self.far_sem, self.y_sem, self.k_sem, self.recv = z_sem, far_sem, y_sem, k_sem, recv

    count = 5

    @staticmethod
    def sems(pieces):
        return [DMA((pieces * n,)) for n in (5, 5, 4, 8, 16)]

    def copy(self, piece, place, sem, device):
        block = self.views[piece](place)
        return remote(block, block, sem, self.recv.at[piece * 16 + place], device)

    def arrived(self, piece, place):
        self.copy(piece, place, self.k_sem.at[0], self.me.device(self.me.c)).wait_recv()

    def line(self, index):
        return self.me.z if index == 0 else pick(self.me.z, NEAREST[index - 1])

    def along(self, piece, place, index, up, sems):
        me = self.me
        target = jnp.minimum(me.c + 4, 12 + me.c % 4) if up else jnp.maximum(me.c - 4, me.c % 4)
        return self.copy(piece, place, sems.at[piece * 5 + index], me.device(target))

    def across(self, piece, place, index):
        me = self.me
        target = me.at(me.z, 1 - me.y, me.k)
        return self.copy(piece, place, self.y_sem.at[piece * 4 + index], me.device(target))

    def partner(self, piece, place, index):
        me = self.me
        target = me.at(me.z, me.y, 1 - me.k)
        return self.copy(piece, place, self.k_sem.at[piece * 8 + index], me.device(target))

    def spread_along(self, piece, place, index, sems, go):
        me, z = self.me, self.line(index)
        if index == 0:

            @pl.when(me.z < 3)
            def _():
                go(self.along(piece, place, 0, True, sems))

            @pl.when(me.z > 0)
            def _():
                go(self.along(piece, place, 4, False, sems))
        else:

            @pl.when((z < me.z) & (me.z < 3))
            def _():
                go(self.along(piece, place, index, True, sems))

            @pl.when((z > me.z) & (me.z > 0))
            def _():
                go(self.along(piece, place, index, False, sems))

    def send_near(self, piece, index, go=lambda copy: copy.start()):
        me = self.me
        place = me.at(self.line(index), me.y, me.k)
        if index == 0 or not self.early[piece]:
            go(self.across(piece, place, index))
        self.spread_along(piece, place, index, self.z_sem, go)
        go(self.partner(piece, place, index))

    def send_far(self, piece, index, go=lambda copy: copy.start()):
        me = self.me
        place = me.at(self.line(index), 1 - me.y, me.k)
        if self.early[piece]:
            self.spread_along(piece, place, index, self.far_sem, go)
        go(self.partner(piece, place, 4 + index))

    def begin(self):
        for piece in range(len(self.views)):
            self.send_near(piece, 0)

    def round(self, index):
        me = self.me
        for piece in range(len(self.views)):
            if index < 3:
                self.arrived(piece, me.at(self.line(index + 1), me.y, me.k))
                self.send_near(piece, index + 1)
            self.arrived(piece, me.at(self.line(index), 1 - me.y, me.k))
            self.send_far(piece, index)

    def settle(self, z, y):
        for piece in range(len(self.views)):
            self.arrived(piece, self.me.at(z, y, 1 - self.me.k))

    def run(self, consume):
        me = self.me
        self.begin()
        waiting = [(me.z, me.y)]
        for index in range(4):
            self.round(index)
            ready, waiting = waiting, []
            if index < 3:
                waiting.append((self.line(index + 1), me.y))
            waiting.append((self.line(index), 1 - me.y))
            for z, y in ready:
                self.settle(z, y)
                consume(z * 2 + y)
        for z, y in waiting:
            self.settle(z, y)
            consume(z * 2 + y)

    def finish(self):
        for piece in range(len(self.views)):
            for index in range(4):
                self.send_near(piece, index, lambda copy: copy.wait_send())
                self.send_far(piece, index, lambda copy: copy.wait_send())


class Scatter:
    pieces = 2

    def __init__(self, me, scratch):
        self.me = me
        (self.k_out, self.k_in, self.y_out, self.y_in, self.z_out, self.z_in, self.mine, self.kept) = scratch[:8]
        (self.ks, self.kr, self.ys, self.yr, self.zs, self.zl, self.zr) = scratch[8:15]

    count = 15

    @classmethod
    def scratch(cls, rows, width):
        n = cls.pieces
        part = width // n
        low = [pltpu.VMEM((n * count, rows, part), LOW) for count in (8, 8, 4, 4, 3, 5)]
        full = [pltpu.VMEM((n * count, rows, part), F32) for count in (1, 4)]
        return low + full + [DMA((n * count,)) for count in (8, 8, 4, 4, 3, 4, 4)]

    def partner(self, slot):
        me = self.me
        target = me.device(me.at(me.z, me.y, 1 - me.k))
        return remote(self.k_out.at[slot], self.k_in.at[slot], self.ks.at[slot], self.kr.at[slot], target)

    def across(self, z, index, piece):
        me, n = self.me, self.pieces
        out, land = index * n + piece, z * n + piece
        target = me.device(me.at(me.z, 1 - me.y, me.k))
        return remote(self.y_out.at[out], self.y_in.at[land], self.ys.at[out], self.yr.at[land], target)

    def along(self, z, index, piece, up):
        me, n = self.me, self.pieces
        out, land = index * n + piece, z * n + piece
        target = jnp.minimum(me.c + 4, 12 + me.c % 4) if up else jnp.maximum(me.c - 4, me.c % 4)
        into = self.z_in.at[land if up else jnp.where(z == me.z - 1, 4, z) * n + piece]
        sem = (self.zl if up else self.zr).at[land]
        return remote(self.z_out.at[out], into, self.zs.at[out], sem, me.device(target))

    def line(self, index):
        return self.me.z if index == 3 else pick(self.me.z, FARTHEST[index])

    def emit(self, produce, z, y, piece, slot, keep):
        part = 512
        rows, width = keep.shape

        @pl.loop(0, width // part)
        def _(index):
            here = pl.ds(pl.multiple_of(index * part, part), part)
            start = pl.multiple_of(piece * width + index * part, part)
            value = produce(self.me.at(z, y, 0), pl.ds(start, part))
            self.k_out[slot, :, here] = value[:rows].astype(LOW)
            keep[:, here] = value[rows:]

    def add(self, target, base, *blocks):
        part = 512

        @pl.loop(0, target.shape[-1] // part)
        def _(index):
            here = pl.ds(pl.multiple_of(index * part, part), part)
            value = base[:, here]
            for block in blocks:
                value = value + block[:, here].astype(F32)
            target[:, here] = value.astype(target.dtype)

    def run(self, prepare, produce, finish, fillers=(), ready=lambda: None, after=lambda: None):
        me, n = self.me, self.pieces
        fillers = list(fillers)
        steps = [(index, piece) for index in range(4) for piece in range(n)]
        for number in range(len(steps) + 1):
            if number < len(steps):
                index, piece = steps[number]
                z = self.line(index)
                if prepare is not None and piece == 0:
                    prepare(z * 2 + 1 - me.y)
                self.emit(produce, z, 1 - me.y, piece, number, self.mine.at[number % 2])
                if number == 0:
                    ready()
                self.partner(number).start()
            if number > 0:
                index, piece = steps[number - 1]
                self.partner(number - 1).wait_recv()
                self.add(self.y_out.at[number - 1], self.mine.at[(number - 1) % 2], self.k_in.at[number - 1])
                self.across(self.line(index), index, piece).start()

        after()

        def own(number):
            index, piece = steps[number]
            z = self.line(index)
            if prepare is not None and piece == 0:
                prepare(z * 2 + me.y)
            self.emit(produce, z, me.y, piece, 4 * n + number, self.kept.at[number])
            self.partner(4 * n + number).start()

        ahead = n
        for number in range(ahead):
            own(number)
        for number in range(len(steps)):
            if number + ahead < len(steps):
                own(number + ahead)
            if prepare is None or number + ahead >= len(steps) - n:
                for _ in range(-(-len(fillers) // (len(steps) - number))):
                    fillers.pop(0)()
            self.collect(number, *steps[number], finish)

    def collect(self, number, index, piece, finish):
        me, n = self.me, self.pieces
        z = self.line(index)
        slot, land = 4 * n + number, z * n + piece
        kept = self.kept.at[number]
        self.partner(slot).wait_recv()
        self.across(z, index, piece).wait_recv()
        self.add(kept, kept, self.k_in.at[slot], self.y_in.at[land])
        if index < 3:
            from_below, from_above = (z > me.z) & (me.z > 0), (z < me.z) & (me.z < 3)
        else:
            from_below, from_above = me.z > 0, me.z < 3

        @pl.when(from_below)
        def _():
            self.along(z, 0, piece, True).wait_recv()
            self.add(kept, kept, self.z_in.at[land])

        @pl.when(from_above)
        def _():
            self.along(z, 0, piece, False).wait_recv()
            self.add(kept, kept, self.z_in.at[4 * n + piece if index == 3 else land])

        if index < 3:
            self.add(self.z_out.at[number], kept)

            @pl.when(z > me.z)
            def _():
                self.along(z, index, piece, True).start()

            @pl.when(z < me.z)
            def _():
                self.along(z, index, piece, False).start()
        else:
            finish(piece, kept)

    def drain(self):
        me, n = self.me, self.pieces
        for slot in range(8 * n):
            self.partner(slot).wait_send()
        for index in range(4):
            z = self.line(index)
            for piece in range(n):
                self.across(z, index, piece).wait_send()
                if index < 3:

                    @pl.when(z > me.z)
                    def _():
                        self.along(z, index, piece, True).wait_send()

                    @pl.when(z < me.z)
                    def _():
                        self.along(z, index, piece, False).wait_send()


def write_total(total_out):
    def finish(piece, kept):
        width = kept.shape[-1]
        total_out[:, piece * width : (piece + 1) * width] = kept[...]

    return finish


def leave(stage, parts, sems):
    copies = []

    def run(number, work, place):
        if number >= 2:
            copies[number - 2].wait()
        slot = stage.at[number % 2]
        work(slot)
        copies.append(pltpu.make_async_copy(slot, place, sems.at[number]))
        copies[number].start()

    def end():
        for copy in copies[-2:]:
            copy.wait()

    return [functools.partial(run, number, *part) for number, part in enumerate(parts)], end


def own_last(me, block, first):
    return jnp.concatenate([block[first + 1 - me.k], block[first + me.k]], axis=0)


def params(collective_id):
    return pltpu.CompilerParams(
        collective_id=collective_id, has_side_effects=True, vmem_limit_bytes=60 << 20
    )


def turn(me, step):
    dz, dy, dk = step // 4, (step // 2) % 2, step % 2
    to = me.at((me.z + dz) % 4, (me.y + dy) % 2, (me.k + dk) % 2)
    source = me.at((me.z + 4 - dz) % 4, (me.y + dy) % 2, (me.k + dk) % 2)
    return to, source


def cuts(rows):
    return ((0, rows // 2), (rows // 2, rows * 7 // 8 - rows // 2), (rows * 7 // 8, rows // 8))


EARLY = [False, False, True]


def pieces_of(array):
    return [
        lambda place, start=start, size=size: array.at[place, pl.ds(start, size)]
        for start, size in cuts(array.shape[1])
    ]


def scale_of(values):
    return lax.rsqrt(jnp.mean(values * values, axis=-1, keepdims=True) + norm_eps)


def norm_back(values, scale, weighted):
    inner = jnp.mean(values * weighted, axis=-1, keepdims=True)
    return scale * weighted - values * (scale * scale * scale * inner)


def by_rows(total, work, rows=32):
    @pl.loop(0, total // rows)
    def _(index):
        work(pl.ds(pl.multiple_of(index * rows, rows), rows))


def down_rows(row, width):
    full = jnp.broadcast_to(row[...].astype(F32), (width, row.shape[1]))
    return jnp.transpose(full)


def spread_kernel(
    token, grad, w_query, w_key, w_value, w_gate, w_up, gain_one, gain_two, out_w, down,
    token_rows, units, grads, query, key, value, cosine, sine, qkv_full, gate_up_half, out_all, down_other, *scratch
):
    gather_sems = scratch[: Gather.count]
    (qs, qr, qxs, qxr, ps, pr, os, ox, orecv, local, dsem, leave, units_here, grads_here, qkv_all, qkv, gate_up) = scratch[Gather.count :]
    me = Place()
    own = [
        pltpu.make_async_copy(qkv.at[me.c], qkv_all.at[me.s, me.c], local.at[2]),
        pltpu.make_async_copy(gate_up.at[me.c], gate_up_half.at[me.c], local.at[3]),
    ]
    ready = greet_plane(me)
    over = (1 - me.s, me.c)
    rows, _, model = token.shape
    tokens = 2 * rows
    for seq in range(2):
        here = slice(seq * rows, (seq + 1) * rows)
        values = token[:, seq, :]
        token_rows[here, :] = values
        values = values.astype(F32)
        units_here[me.c, here] = (values * scale_of(values)).astype(LOW)
        grads_here[me.c, here] = grad[:, seq, :]
    ready()
    gather = Gather(me, pieces_of(units_here) + pieces_of(grads_here), [False] * 6, *gather_sems)
    down_copy = remote(down, down_other, dsem.at[0], dsem.at[1], over)

    def send_qkv(step):
        to, _ = turn(me, step)
        return remote(qkv.at[to], qkv_all.at[me.s, me.c], qs.at[step], qr.at[me.c], (me.s, to))

    def send_gate_up(step):
        to, _ = turn(me, step)
        return remote(gate_up.at[to], gate_up_half.at[me.c], ps.at[step], pr.at[me.c], (me.s, to))

    def forward(source):
        block = qkv_all.at[me.s, source]
        return remote(block, block, qxs.at[source], qxr.at[source], over)

    holder = me.at(me.z, me.y, me.s)
    out_local = pltpu.make_async_copy(out_w, out_all.at[me.k], local.at[4])
    out_near = remote(out_w, out_all.at[me.k], os.at[0], orecv.at[me.k], (me.s, me.at(me.z, me.y, 1 - me.k)))
    out_far = remote(out_w, out_all.at[me.k], ox, orecv.at[me.k], (1 - me.s, holder))

    gather.begin()
    width = query.shape[3]
    weight_rows = w_query.shape[0]
    one = down_rows(gain_one, width)
    for place in range(16):
        head = place // 2 + 8 * (place % 2)
        for index, weight in enumerate((w_query, w_key, w_value)):
            block = weight[:, head * width : (head + 1) * width].astype(F32) * one
            qkv[place, :, index * width : (index + 1) * width] = block.astype(LOW)
    own[0].start()
    for step in range(1, 16):
        send_qkv(step).start()
    units_of = gate_up.shape[2] // 4
    two = down_rows(gain_two, units_of)
    for place in range(16):
        for index, weight in enumerate((w_gate, w_up)):
            for half in range(2):
                start = (half * 16 + place) * units_of
                block = weight[:, start : start + units_of].astype(F32) * two
                start = (2 * index + half) * units_of
                gate_up[place, :, start : start + units_of] = block.astype(LOW)
    own[1].start()
    own[0].wait()
    forward(me.c).start()
    out_far.start()

    @pl.when(holder == me.c)
    def _():
        out_local.start()

    @pl.when(holder != me.c)
    def _():
        out_near.start()

    down_copy.start()
    leaving = []

    half_width = width // 2
    lane = lax.broadcasted_iota(jnp.int32, (rows, width), 1)
    row = lax.broadcasted_iota(jnp.int32, (rows, width), 0)
    freqs = jnp.exp((lane % half_width).astype(F32) * (-2.0 * math.log(rope_base) / width))
    sign = jnp.where(lane < half_width, 1.0, -1.0)

    @pl.loop(0, 16)
    def _(place):
        angles = row_place(place, row, rows // 2).astype(F32) * freqs
        cosine[place] = jnp.cos(angles)
        sine[place] = jnp.sin(angles) * sign

    def write_out(z, y):
        pair = z * 2 + y
        both = pl.ds(2 * pair, 2)
        number = len(leaving)
        for index, (here, there) in enumerate(((units_here, units), (grads_here, grads))):
            copy = pltpu.make_async_copy(here.at[both], there.at[both], leave.at[2 * number + index])
            copy.start()
            leaving.append(copy)

    def turned(values, both):
        swapped = pltpu.roll(values, width // 2, axis=1)
        place_cos = cosine[both].reshape(2 * rows, width)
        place_sin = sine[both].reshape(2 * rows, width)
        return (values * place_cos - swapped * place_sin).astype(LOW).reshape(2, rows, width)

    def project(z, y):
        both = pl.ds(2 * (z * 2 + y), 2)
        weights = qkv_all[...].reshape(model, 3 * width)
        for seq in range(2):
            block = units_here[both, seq * rows : (seq + 1) * rows].reshape(2 * rows, model)
            result = jnp.dot(block, weights, preferred_element_type=F32)
            query[both, seq] = turned(result[:, :width], both)
            key[both, seq] = turned(result[:, width : 2 * width], both)
            value[both, seq] = result[:, 2 * width :].astype(LOW).reshape(2, rows, width)

    steps = list(range(1, 16))
    waiting, ready = [(me.z, me.y)], []
    for index in range(4):
        for step in steps[4 * index : 4 * index + 4]:
            send_gate_up(step).start()
        gather.round(index)
        for z, y in waiting:
            gather.settle(z, y)
            write_out(z, y)
        ready += waiting
        waiting = [(gather.line(index), 1 - me.y)]
        if index < 3:
            waiting.append((gather.line(index + 1), me.y))
        if index == 1:
            for step in steps:
                _, source = turn(me, step)
                remote(qkv.at[0], qkv_all.at[me.s, source], qs.at[step], qr.at[source], over).wait_recv()
                forward(source).start()
        if index == 2:
            for source in range(16):
                forward(source).wait_send()
                forward(source).wait_recv()
            leave_qkv = pltpu.make_async_copy(qkv_all, qkv_full, local.at[5])
            leave_qkv.start()
        if index >= 2:
            for z, y in ready:
                project(z, y)
            ready = []
    for z, y in waiting:
        gather.settle(z, y)
        write_out(z, y)
        project(z, y)
    gather.finish()
    own[1].wait()
    leave_qkv.wait()
    for copy in leaving:
        copy.wait()
    for step in steps:
        _, source = turn(me, step)
        send_qkv(step).wait_send()
        send_gate_up(step).wait_send()
        remote(gate_up.at[0], gate_up_half.at[source], ps.at[step], pr.at[source], over).wait_recv()
    out_far.wait_send()
    down_copy.wait()

    @pl.when(holder == me.c)
    def _():
        out_local.wait()
        remote(out_w, out_all.at[1 - me.k], ox, orecv.at[1 - me.k], over).wait_recv()

    @pl.when(holder != me.c)
    def _():
        out_near.wait_send()
        for half in range(2):
            remote(out_w, out_all.at[half], ox, orecv.at[half], over).wait_recv()


def spread(token, grad, w_query, w_key, w_value, w_gate, w_up, gain_one, gain_two, out_w, down):
    def shape(lead, array):
        return jax.ShapeDtypeStruct(lead + array.shape, array.dtype)

    rows, seqs, model = token.shape
    tokens = rows * seqs
    flat = jax.ShapeDtypeStruct((16, tokens, model), LOW)
    width = model // 16
    weight_rows = w_query.shape[0]
    qkv = (weight_rows, 3 * width)
    gate_up = (weight_rows, 2 * w_gate.shape[1] // 16)
    heads = jax.ShapeDtypeStruct((16, 2, tokens // 2, width), LOW)
    table = jax.ShapeDtypeStruct((16, tokens // 2, width), F32)
    return pl.pallas_call(
        spread_kernel,
        out_shape=[
            jax.ShapeDtypeStruct((tokens, model), LOW),
            flat,
            flat,
            heads,
            heads,
            heads,
            table,
            table,
            jax.ShapeDtypeStruct((2, 16) + qkv, LOW),
            jax.ShapeDtypeStruct((16,) + gate_up, LOW),
            shape((2,), out_w),
            shape((), down),
        ],
        in_specs=[IN_VMEM] * 9 + [ANYWHERE] * 2,
        out_specs=[IN_VMEM] + [ANYWHERE] * 2 + [IN_VMEM] * 5 + [ANYWHERE] * 4,
        scratch_shapes=Gather.sems(6)
        + [DMA((16,))] * 6
        + [DMA((1,)), DMA, DMA((2,)), DMA((6,)), DMA((2,)), DMA((32,))]
        + [pltpu.VMEM((16, tokens, model), LOW)] * 2
        + [pltpu.VMEM((2, 16) + qkv, LOW), pltpu.VMEM((16,) + qkv, LOW), pltpu.VMEM((16,) + gate_up, LOW)],
        compiler_params=params(0),
    )(token, grad, w_query, w_key, w_value, w_gate, w_up, gain_one, gain_two, out_w, down)


def row_place(place, row, strip):
    return jnp.where(row < strip, place * strip + row, (31 - place) * strip + row - strip)


def key_places(strip):
    index = lax.broadcasted_iota(jnp.int32, (1, 32 * strip), 1)
    return row_place(index // (2 * strip), index % (2 * strip), strip)


def query_places(pair, strip):
    index = lax.broadcasted_iota(jnp.int32, (4 * strip, 1), 0)
    return row_place(2 * pair + index // (2 * strip), index % (2 * strip), strip)


def of_pair(block, pair, seq):
    rows, width = block.shape[2:]
    return block[pl.ds(2 * pair, 2), seq].reshape(2 * rows, width)


def forward_kernel(
    shift, valid, query, key, value, out_w, token_far, grads, gate_up, down_own, down_other,
    grad_state, branch, hidden_own_far, attended_far, hidden_far, down_far, gate_up_grad, *scratch
):
    me = Place()
    hidden_own, attended, hidden, down_full, token, grad_own, side = scratch[-15:-8]
    tokens, model = token.shape
    width = hidden.shape[2]
    gather_sems = scratch[Scatter.count : Scatter.count + Gather.count]
    units, grad_gate_up, gate_up_full, grads_here, stage, leaving, local, swap_sems = scratch[-8:]
    scatter = Scatter(me, scratch)
    brought = [
        pltpu.make_async_copy(gate_up, gate_up_full.at[me.s], local.at[0]),
        pltpu.make_async_copy(down_own, down_full.at[me.s], local.at[1]),
        pltpu.make_async_copy(down_other, down_full.at[1 - me.s], local.at[2]),
        pltpu.make_async_copy(grads, grads_here, local.at[3]),
    ]
    near = [
        pltpu.make_async_copy(token_far, token, side.at[0]),
        pltpu.make_async_copy(grads.at[me.c], grad_own, side.at[1]),
    ]
    away = [
        pltpu.make_async_copy(attended, attended_far, side.at[2]),
        pltpu.make_async_copy(hidden_own, hidden_own_far, side.at[3]),
        pltpu.make_async_copy(hidden, hidden_far, side.at[4]),
        pltpu.make_async_copy(down_full, down_far, side.at[5]),
    ]
    ready = greet(me, over_seq=True)
    swap = remote(gate_up, gate_up_full.at[me.s], swap_sems.at[0], swap_sems.at[1], (1 - me.s, me.c))
    rows, depth = query.shape[2], query.shape[3]
    strip = rows // 2
    length = rows * 16
    scale = depth ** (-0.5)

    def attention(pair):
        where = query_places(pair, strip)
        keys_at = key_places(strip)
        for seq in range(2):
            keys = key[:, seq].reshape(length, depth)
            values = value[:, seq].reshape(length, depth)
            logits = dot_right(of_pair(query, pair, seq), keys) * scale - shift
            live = (keys_at <= where) & (keys_at < valid[seq])
            weights = jnp.where(live, jax.nn.sigmoid(logits), 0.0).astype(LOW)
            attended[pl.ds(2 * pair, 2), pl.ds(seq * rows, rows)] = (
                jnp.dot(weights, values, preferred_element_type=F32).astype(LOW).reshape(2, rows, depth)
            )

    def out_terms(first, columns):
        return jnp.dot(own_last(me, attended, first), out_w[:, columns], preferred_element_type=F32)

    def met():
        ready()
        swap.start()
        for copy in near + brought:
            copy.start()

    scatter.run(attention, out_terms, write_total(hidden_own), ready=met)
    scatter.drain()
    for copy in near:
        copy.wait()

    def to_unit(at):
        values = hidden_own[at, :] + token[at, :].astype(F32)
        hidden_own[at, :] = values
        units[me.c, at] = (values * scale_of(values)).astype(LOW)

    by_rows(tokens, to_unit)
    gather = Gather(me, pieces_of(units), EARLY, *gather_sems)
    rows_of = gate_up_full.shape[1] * gate_up_full.shape[2]
    units_of = down_full.shape[1]
    first = [True]

    def consume(pair):
        if first[0]:
            for copy in brought:
                copy.wait()
            swap.wait()
            first[0] = False
        both = pl.ds(2 * pair, 2)

        def dot_rows(rows, columns):
            return jnp.dot(
                rows,
                gate_up_full[:, :, :, columns].reshape(2 * rows_of, units_of),
                preferred_element_type=F32,
            )

        @pl.loop(0, 2)
        def _(half):
            gate_at = pl.ds(pl.multiple_of(half * units_of, units_of), units_of)
            up_at = pl.ds(pl.multiple_of(width + half * units_of, units_of), units_of)
            rows = units[both].reshape(2 * tokens, model)
            gate = dot_rows(rows, gate_at)
            up = dot_rows(rows, up_at)
            grad = dot_right(grads_here[both].reshape(2 * tokens, model), down_full[half])
            sig = jax.nn.sigmoid(gate)
            silu = gate * sig

            def store(target, columns, value):
                target[both, :, columns] = value.astype(LOW).reshape(2, tokens, units_of)

            store(hidden, gate_at, silu * up)
            store(grad_gate_up, gate_at, grad * up * (sig * (1.0 + gate * (1.0 - sig))))
            store(grad_gate_up, up_at, grad * silu)

    gather.run(consume)
    for copy in away:
        copy.start()
    block_rows = gate_up_full.shape[2]

    def unit_terms(first, columns):
        start, size = columns.start, columns.size
        blocks = size // block_rows
        block = start // block_rows
        weights = gate_up_full[block // 16, pl.ds(block % 16, blocks)].reshape(size, 2 * width)
        return dot_right(own_last(me, grad_gate_up, first), weights)

    every = 16 * tokens
    part = model // 8

    def gate_up_part(number):
        def work(slot):
            left = units[:, :, number * part : (number + 1) * part].reshape(every, part)
            slot[...] = dot_left(left, grad_gate_up[...].reshape(every, 2 * width)).astype(LOW)

        return work, gate_up_grad.at[pl.ds(number * part, part)]

    fillers, end = leave(stage, [gate_up_part(n) for n in range(8)], leaving)
    scatter.run(None, unit_terms, write_total(grad_state), fillers)

    def to_state(at):
        values = hidden_own[at, :]
        back = norm_back(values, scale_of(values), grad_state[at, :])
        state = grad_own[at, :].astype(F32) + back
        grad_state[at, :] = state
        branch[at, :] = state.astype(LOW)

    by_rows(tokens, to_state)
    end()
    for copy in away:
        copy.wait()
    scatter.drain()
    gather.finish()


def forward(shift, valid, query, key, value, out_w, token, grads, gate_up, down_own, down_other):
    tokens, model = token.shape
    width = 2 * down_own.shape[0]
    full = jax.ShapeDtypeStruct((tokens, model), F32)
    return pl.pallas_call(
        functools.partial(forward_kernel, shift),
        out_shape=[
            full,
            jax.ShapeDtypeStruct((tokens, model), LOW),
            full,
            jax.ShapeDtypeStruct((16, tokens, query.shape[3]), LOW),
            jax.ShapeDtypeStruct((16, tokens, width), LOW),
            jax.ShapeDtypeStruct((2,) + down_own.shape, LOW),
            jax.ShapeDtypeStruct((model, 2 * width), LOW),
        ],
        in_specs=[IN_SMEM] + [IN_VMEM] * 4 + [ANYWHERE] * 5,
        out_specs=[IN_VMEM] * 2 + [ANYWHERE] * 5,
        scratch_shapes=Scatter.scratch(tokens, model)
        + Gather.sems(3)
        + [
            pltpu.VMEM((tokens, model), F32),
            pltpu.VMEM((16, tokens, query.shape[3]), LOW),
            pltpu.VMEM((16, tokens, width), LOW),
            pltpu.VMEM((2,) + down_own.shape, LOW),
            pltpu.VMEM((tokens, model), LOW),
            pltpu.VMEM((tokens, model), LOW),
            DMA((6,)),
        ]
        + [
            pltpu.VMEM((16, tokens, model), LOW),
            pltpu.VMEM((16, tokens, 2 * width), LOW),
            pltpu.VMEM((2,) + gate_up.shape, LOW),
            pltpu.VMEM((16, tokens, model), LOW),
            pltpu.VMEM((2, model // 8, 2 * width), LOW),
            DMA((8,)),
            DMA((4,)),
            DMA((2,)),
        ],
        compiler_params=params(1),
    )(valid, query, key, value, out_w, token, grads, gate_up, down_own, down_other)


def attend_back_kernel(
    shift, valid, branch, units, gate_up, *rest
):
    far, rest = rest[:10], rest[10:]
    in_grad, qkv_grad, out_grad, gate_up_other = rest[:4]
    key_sum, value_sum, branches, grad_qkv, units_here, total_out = rest[4:10]
    side, near, scratch = rest[10], rest[11:21], rest[21:]
    query, key, value, out_w, cosine, sine, qkv_w, attended, token, grad_state = near
    near_copies = [pltpu.make_async_copy(a, b, side.at[n]) for n, (a, b) in enumerate(zip(far, near))]
    me = Place()
    tokens, model = branch.shape
    gather = Gather(me, pieces_of(branches), EARLY, *scratch[Scatter.count : Scatter.count + Gather.count])
    sems, local = scratch[-2:]
    own = pltpu.make_async_copy(branch, branches.at[me.c], local.at[0])
    own.start()
    bring = pltpu.make_async_copy(units, units_here, local.at[1])
    ready = greet(me, over_seq=True)
    for copy in near_copies:
        copy.start()
    bring.start()
    own.wait()
    ready()
    over = (1 - me.s, me.c)
    swaps = [
        remote(gate_up.at[1 - me.s], gate_up_other, sems.at[0], sems.at[1], over),
    ]
    for copy in swaps:
        copy.start()
    rows, width = query.shape[2:]
    strip = rows // 2
    length = rows * 16
    scale = width ** (-0.5)
    key_sum[...] = jnp.zeros_like(key_sum)
    value_sum[...] = jnp.zeros_like(value_sum)

    def turn_back(values, places):
        swapped = pltpu.roll(values, width // 2, axis=1)
        turned = values * cosine[places].reshape(2 * rows, width)
        return (turned + swapped * sine[places].reshape(2 * rows, width)).astype(LOW).reshape(2, rows, width)

    first = [True]

    def consume(pair):
        if first[0]:
            for copy in near_copies[:6]:
                copy.wait()
            first[0] = False
        where = query_places(pair, strip)
        keys_at = key_places(strip)
        both = pl.ds(2 * pair, 2)
        for seq in range(2):
            here = pl.ds(seq * rows, rows)
            grad = dot_right(branches[both, here].reshape(2 * rows, -1), out_w[...]).astype(LOW)
            keys = key[:, seq].reshape(length, width)
            values = value[:, seq].reshape(length, width)
            queries = of_pair(query, pair, seq)
            logits = dot_right(queries, keys) * scale - shift
            live = (keys_at <= where) & (keys_at < valid[seq])
            sig = jnp.where(live, jax.nn.sigmoid(logits), 0.0)
            weights = sig.astype(LOW)
            grad_logits = (dot_right(grad, values) * (sig * (1.0 - sig))).astype(LOW)
            grad_query = jnp.dot(grad_logits, keys, preferred_element_type=F32) * scale
            grad_qkv[both, here, 0:width] = turn_back(grad_query, both)
            key_sum[seq] += dot_left(grad_logits, queries)
            value_sum[seq] += dot_left(weights, grad)

    gather.run(consume)

    def prepare(pair):
        both = pl.ds(2 * pair, 2)
        at = pl.ds(pl.multiple_of(pair * 2 * rows, 2 * rows), 2 * rows)
        for seq in range(2):
            here = pl.ds(seq * rows, rows)
            grad_qkv[both, here, width : 2 * width] = turn_back(key_sum[seq, at] * scale, both)
            grad_qkv[both, here, 2 * width :] = value_sum[seq, at].astype(LOW).reshape(2, rows, width)

    scatter = Scatter(me, scratch)

    def produce(first, columns):
        return dot_right(own_last(me, grad_qkv, first), qkv_w[columns, :])

    every = 16 * tokens
    for copy in near_copies[6:] + [bring]:
        copy.wait()

    def qkv_part(number, part=model // 8):
        at = slice(number * part, (number + 1) * part)
        left = units_here[:, :, at].reshape(every, part)
        qkv_grad[at, :] = dot_left(left, grad_qkv[...].reshape(every, 3 * width)).astype(LOW)

    def out_part(number, part=model // 4):
        at = slice(number * part, (number + 1) * part)
        left = attended[...].reshape(every, width)
        out_grad[:, at] = dot_left(left, branches[:, :, at].reshape(every, part)).astype(LOW)

    fillers = [functools.partial(out_part, n) for n in range(4)]
    fillers += [functools.partial(qkv_part, n) for n in range(8)]
    scatter.run(prepare, produce, write_total(total_out), fillers)

    for seq in range(2):
        for part in range(2):
            at = slice(part * rows // 2, (part + 1) * rows // 2)
            here = slice(seq * rows + at.start, seq * rows + at.stop)
            values = token[here, :].astype(F32)
            back = norm_back(values, scale_of(values), total_out[here, :])
            in_grad[at, seq, :] = grad_state[here, :] + back
    scatter.drain()
    gather.finish()
    for copy in swaps:
        copy.wait()


def attend_back(
    shift, valid, branch, units, query, key, value, out_w, qkv_w, attended, cosine, sine, gate_up, token, grad_state
):
    tokens, model = branch.shape
    rows, width = query.shape[2:]
    near = (query, key, value, out_w, cosine, sine, qkv_w, attended, token, grad_state)
    return pl.pallas_call(
        functools.partial(attend_back_kernel, shift),
        out_shape=[
            jax.ShapeDtypeStruct((rows, 2, model), F32),
            jax.ShapeDtypeStruct((model, 3 * width), LOW),
            jax.ShapeDtypeStruct((width, model), LOW),
            jax.ShapeDtypeStruct(gate_up.shape[1:], LOW),
        ],
        in_specs=[IN_SMEM] + [ANYWHERE] * 13,
        out_specs=[IN_VMEM] * 3 + [ANYWHERE],
        scratch_shapes=[pltpu.VMEM((2, 16 * rows, width), F32)] * 2
        + [
            pltpu.VMEM((16, tokens, model), LOW),
            pltpu.VMEM((16, tokens, 3 * width), LOW),
            pltpu.VMEM((16, tokens, model), LOW),
            pltpu.VMEM((tokens, model), F32),
        ]
        + [DMA((10,))]
        + [pltpu.VMEM(array.shape, array.dtype) for array in near]
        + Scatter.scratch(tokens, model)
        + Gather.sems(3)
        + [DMA((4,)), DMA((2,))],
        compiler_params=params(4),
    )(valid, branch, units, gate_up, *near)


def return_kernel(
    hidden_far, down_far, qkv_far, gate_up_far, gate_up_other, out_far, hidden_own_far, grads_far,
    total_out, qkv_back, gate_up_back, out_back, down_grad, down_other, *scratch
):
    (qx, qsum, qxs, qxr, qs, qr, psum, ps, pr, oland, os, orecv, hidden, down_w, px, sums, qkv, out_pair, hidden_own, grads, local, across) = scratch[
        Scatter.count :
    ]
    me = Place()
    ready = greet_plane(me)
    bring = [
        pltpu.make_async_copy(hidden_far, hidden, local.at[0]),
        pltpu.make_async_copy(down_far, down_w, local.at[1]),
        pltpu.make_async_copy(gate_up_far.at[me.s], psum, local.at[2]),
        pltpu.make_async_copy(gate_up_other, px, local.at[3]),
        pltpu.make_async_copy(qkv_far, qkv, local.at[4]),
        pltpu.make_async_copy(out_far, out_pair, local.at[5]),
        pltpu.make_async_copy(hidden_own_far, hidden_own, local.at[6]),
        pltpu.make_async_copy(grads_far, grads, local.at[7]),
    ]
    for copy in bring:
        copy.start()
    over = (1 - me.s, me.c)

    def cross(place):
        return remote(qkv.at[1 - me.s, place], qx.at[place], qxs.at[place], qxr.at[place], over)

    def send(sums, back, s_sem, r_sem, step):
        to, _ = turn(me, step)
        return remote(sums.at[to], back.at[me.c], s_sem.at[step], r_sem.at[me.c], (me.s, to))

    holder = me.at(me.z, me.y, me.s)

    def out_send(target_core, same):
        target = (me.s if same else 1 - me.s, me.at(me.z, me.y, target_core))
        slot = 0 if same else 1
        return remote(out_pair.at[target_core], oland.at[me.s], os.at[slot], orecv.at[me.s], target)

    inside = me.k == me.s

    def met():
        ready()
        for step in range(1, 16):
            send(psum, gate_up_back, ps, pr, step).start()
        for copy in bring[4:]:
            copy.wait()
        for step in range(1, 16):
            cross(turn(me, step)[0]).start()
        cross(me.c).start()

        @pl.when(inside)
        def _():
            out_send(1 - me.k, True).start()

        @pl.when(jnp.logical_not(inside))
        def _():
            out_send(me.k, False).start()
            remote(
                out_pair.at[1 - me.k], oland.at[me.s], os.at[0], orecv.at[me.s],
                (1 - me.s, me.at(me.z, me.y, 1 - me.k)),
            ).start()

    def between():
        for step in range(1, 16):
            to, _ = turn(me, step)
            cross(to).wait_recv()
            qsum[to] = (qkv[me.s, to].astype(F32) + qx[to].astype(F32)).astype(LOW)
            send(qsum, qkv_back, qs, qr, step).start()
        cross(me.c).wait_recv()
        qkv_back[me.c] = (qkv[me.s, me.c].astype(F32) + qx[me.c].astype(F32)).astype(LOW)

    scatter = Scatter(me, scratch)

    def produce(first, columns):
        return jnp.dot(own_last(me, hidden, first), down_w[:, columns], preferred_element_type=F32)

    for copy in bring[:4]:
        copy.wait()

    @pl.loop(0, 16)
    def _(place):
        psum[place] = (psum[place].astype(F32) + px[place].astype(F32)).astype(LOW)

    gate_up_back[me.c] = psum[me.c]
    down_swap = remote(down_grad.at[1 - me.s], down_other, across.at[0], across.at[1], over)
    parts, double, part = down_other.shape
    every = hidden.shape[0] * hidden.shape[1]

    def down_part(half, number):
        seq = 1 - me.s if half == 0 else me.s
        thin = double // 2
        start = pl.multiple_of((seq * parts + number) * thin, thin)
        left = hidden[:, :, pl.ds(start, thin)].reshape(every, thin)
        for side in range(2):
            right = grads[:, :, side * part : (side + 1) * part].reshape(every, part)
            down_grad[seq, number, pl.ds(side * thin, thin)] = dot_left(left, right).astype(LOW)
        if half == 0 and number == parts - 1:
            down_swap.start()

    fillers = [between] + [functools.partial(down_part, half, n) for half in range(2) for n in range(parts)]
    scatter.run(None, produce, write_total(sums), fillers, met)
    down_swap.wait()

    rows = total_out.shape[0]
    for seq in range(2):
        here = slice(seq * rows, (seq + 1) * rows)
        total_out[:, seq, :] = (sums[here, :] + hidden_own[here, :]).astype(LOW)
    scatter.drain()
    for step in range(1, 16):
        to, source = turn(me, step)
        for sums, back, s_sem, r_sem in ((qsum, qkv_back, qs, qr), (psum, gate_up_back, ps, pr)):
            remote(sums.at[0], back.at[source], s_sem.at[step], r_sem.at[source], over).wait_recv()
            send(sums, back, s_sem, r_sem, step).wait_send()
        cross(to).wait_send()
    cross(me.c).wait_send()

    @pl.when(inside)
    def _():
        out_send(1 - me.k, True).wait_send()
        remote(out_pair.at[0], oland.at[1 - me.s], os.at[0], orecv.at[1 - me.s], over).wait_recv()
        out_back[...] = out_pair[me.k].astype(F32) + oland[1 - me.s].astype(F32)

    @pl.when(jnp.logical_not(inside))
    def _():
        out_send(me.k, False).wait_send()
        out_send(1 - me.k, True).wait_send()
        for half in range(2):
            remote(out_pair.at[0], oland.at[half], os.at[0], orecv.at[half], over).wait_recv()
        out_back[...] = oland[0].astype(F32) + oland[1].astype(F32)


def give_back(hidden, down_w, qkv, gate_up, gate_up_other, out_pair, hidden_own, grads):
    tokens, model = hidden.shape[1], down_w.shape[1]
    down_half = (2, hidden.shape[2] // 2, model // 2)
    block = lambda array: pltpu.VMEM(array.shape[1:], LOW)
    return pl.pallas_call(
        return_kernel,
        out_shape=[
            jax.ShapeDtypeStruct((tokens // 2, 2, model), LOW),
            jax.ShapeDtypeStruct(qkv.shape[1:], LOW),
            jax.ShapeDtypeStruct(gate_up.shape[1:], LOW),
            jax.ShapeDtypeStruct(out_pair.shape[1:], F32),
            jax.ShapeDtypeStruct((2,) + down_half, LOW),
            jax.ShapeDtypeStruct(down_half, LOW),
        ],
        in_specs=[ANYWHERE] * 8,
        out_specs=[IN_VMEM] * 6,
        scratch_shapes=Scatter.scratch(tokens, model)
        + [block(qkv), block(qkv)]
        + [DMA((16,))] * 4
        + [block(gate_up)]
        + [DMA((16,))] * 2
        + [pltpu.VMEM(out_pair.shape, LOW), DMA((2,)), DMA((2,))]
        + [pltpu.VMEM(hidden.shape, LOW), pltpu.VMEM(down_w.shape, LOW), block(gate_up)]
        + [pltpu.VMEM((tokens, model), F32), pltpu.VMEM(qkv.shape, LOW), pltpu.VMEM(out_pair.shape, LOW)]
        + [pltpu.VMEM((tokens, model), F32), pltpu.VMEM(grads.shape, LOW), DMA((8,)), DMA((2,))],
        compiler_params=params(5),
    )(hidden, down_w, qkv, gate_up, gate_up_other, out_pair, hidden_own, grads)


def assemble_kernel(
    gain_one, gain_two, qkv_far, w_query_far, w_key_far, w_value_far, gate_up_far, w_gate_far, w_up_far,
    down_far, down_other_far,
    query_grad, key_grad, value_grad, gate_grad, up_grad, down_grad, gain_one_grad, gain_two_grad, *near
):
    qkv_back, w_query, w_key, w_value, gate_up_back, w_gate, w_up, down_own, down_other, sems = near
    far = (qkv_far, w_query_far, w_key_far, w_value_far, gate_up_far, w_gate_far, w_up_far)
    far += (down_far.at[lax.axis_index("seq")], down_other_far)
    copies = [pltpu.make_async_copy(a, b, sems.at[n]) for n, (a, b) in enumerate(zip(far, near))]
    for copy in copies:
        copy.start()

    def lanes(total):
        return jnp.sum(jnp.transpose(total), axis=0, keepdims=True)

    width = qkv_back.shape[2] // 3
    rows = qkv_back.shape[1]
    one = down_rows(gain_one, width)
    total = jnp.zeros((rows, width), F32)
    for copy in copies[:4]:
        copy.wait()
    for place in range(16):
        at = slice((place // 2 + 8 * (place % 2)) * width, (place // 2 + 8 * (place % 2) + 1) * width)
        for index, (weight, target) in enumerate(
            ((w_query, query_grad), (w_key, key_grad), (w_value, value_grad))
        ):
            block = qkv_back[place, :, index * width : (index + 1) * width].astype(F32)
            target[:, at] = block * one
            total += block * weight[:, at].astype(F32)
    gain_one_grad[...] = lanes(total)
    width = gate_up_back.shape[2] // 4
    two = down_rows(gain_two, width)
    total = jnp.zeros((rows, width), F32)
    for copy in copies[4:7]:
        copy.wait()
    for place in range(16):
        for half in range(2):
            at = slice((half * 16 + place) * width, (half * 16 + place + 1) * width)
            for index, (weight, target) in enumerate(((w_gate, gate_grad), (w_up, up_grad))):
                start = (2 * index + half) * width
                block = gate_up_back[place, :, start : start + width].astype(F32)
                target[:, at] = block * two
                total += block * weight[:, at].astype(F32)
    gain_two_grad[...] = lanes(total)
    for copy in copies[7:]:
        copy.wait()
    parts, double, part = down_own.shape
    depth = double // 2
    for number in range(parts):
        for half in range(2):
            at = slice(half * depth, (half + 1) * depth)
            down_grad[number * depth : (number + 1) * depth, half * part : (half + 1) * part] = (
                down_own[number, at].astype(F32) + down_other[number, at].astype(F32)
            )


def assemble(gain_one, gain_two, qkv_back, w_query, w_key, w_value, gate_up_back, w_gate, w_up, down, down_other):
    rows, model = w_query.shape
    narrow = jax.ShapeDtypeStruct((rows, model), F32)
    wide = jax.ShapeDtypeStruct(w_gate.shape, F32)
    gain = jax.ShapeDtypeStruct((1, rows), F32)
    parts, double, part = down_other.shape
    near = (qkv_back, w_query, w_key, w_value, gate_up_back, w_gate, w_up, down_other, down_other)
    return pl.pallas_call(
        assemble_kernel,
        out_shape=[narrow] * 3
        + [wide] * 2
        + [jax.ShapeDtypeStruct((parts * double // 2, 2 * part), F32)]
        + [gain] * 2,
        in_specs=[IN_VMEM] * 2 + [ANYWHERE] * 9,
        out_specs=[IN_VMEM] * 8,
        scratch_shapes=[pltpu.VMEM(array.shape, LOW) for array in near] + [DMA((9,))],
        compiler_params=pltpu.CompilerParams(vmem_limit_bytes=60 << 20),
    )(gain_one, gain_two, qkv_back, w_query, w_key, w_value, gate_up_back, w_gate, w_up, down, down_other)


def move_tokens_step(
    layer_in,
    valid_len,
    norm1_gain,
    w_query,
    w_key,
    w_value,
    w_out,
    norm2_gain,
    w_gate,
    w_up,
    w_down,
    cotangent,
):
    local_rows, _, model = layer_in.shape
    width = model // HEADS
    cp_devices = 16
    shift = math.log(cp_devices * local_rows)
    weight_rows = w_gate.shape[0]
    gain_one, gain_two = norm1_gain[None], norm2_gain[None]

    token_rows, units, grads, query, key, value, cosine, back_sine, qkv_w, gate_up_own, head_out, down_other = spread(
        layer_in, cotangent, w_query, w_key, w_value, w_gate, w_up,
        gain_one, gain_two, w_out, w_down,
    )
    qkv_w = qkv_w.reshape(model, 3 * width)
    head_out = head_out.reshape(width, model)
    grad_state, branch, hidden_state, attended, hidden, down_full, gate_up_grad = forward(
        shift, valid_len, query, key, value, head_out, token_rows, grads, gate_up_own, w_down, down_other
    )
    gate_up_grad = gate_up_grad.reshape(2, cp_devices, weight_rows, -1)
    in_grad, qkv_grad, out_grad, gate_up_grad_other = attend_back(
        shift, valid_len, branch, units, query, key, value, head_out, qkv_w, attended,
        cosine, back_sine, gate_up_grad, token_rows, grad_state,
    )
    layer_out, qkv_back, gate_up_back, out_back, down_grad, down_grad_other = give_back(
        hidden,
        down_full.reshape(-1, model),
        qkv_grad.reshape(2, cp_devices, weight_rows, -1),
        gate_up_grad,
        gate_up_grad_other,
        out_grad.reshape(2, width // 2, model),
        hidden_state,
        grads,
    )
    query_grad, key_grad, value_grad, gate_grad, up_grad, down_back, gain_one_grad, gain_two_grad = assemble(
        gain_one, gain_two, qkv_back, w_query, w_key, w_value, gate_up_back, w_gate, w_up, down_grad, down_grad_other
    )
    return (
        layer_out,
        in_grad,
        gain_one_grad[0],
        query_grad,
        key_grad,
        value_grad,
        out_back,
        gain_two_grad[0],
        gate_grad,
        up_grad,
        down_back,
    )


def solution(mesh):
    fits = mesh.shape["cp"] == HEADS and mesh.shape["seq"] == 2
    on_device = move_tokens_step if fits else gather_weights_step
    placed = (
        P("cp", "seq", None),
        P("seq"),
        P(("seq", "cp")),
        P(("seq", "cp"), None),
        P(("seq", "cp"), None),
        P(("seq", "cp"), None),
        P(("seq", "cp"), None),
        P(("seq", "cp")),
        P(("seq", "cp"), None),
        P(("seq", "cp"), None),
        P(("seq", "cp"), None),
        P("cp", "seq", None),
    )
    return jax.shard_map(
        on_device,
        mesh=mesh,
        in_specs=placed,
        out_specs=(
            P("cp", "seq", None),
            P("cp", "seq", None),
            P(("seq", "cp")),
            P(("seq", "cp"), None),
            P(("seq", "cp"), None),
            P(("seq", "cp"), None),
            P(("seq", "cp"), None),
            P(("seq", "cp")),
            P(("seq", "cp"), None),
            P(("seq", "cp"), None),
            P(("seq", "cp"), None),
        ),
        check_vma=False,
    )
```

```python
import functools
import math

import jax
import jax.numpy as jnp
from jax import lax
from jax.experimental import pallas as pl
from jax.experimental.pallas import tpu as pltpu
from jax.sharding import PartitionSpec as P

HEADS = 16


norm_eps = 1e-05
rope_base = 10000.0


def row_positions(indices, strip_rows, devices):
    owner_index = indices // (2 * strip_rows)
    within = indices % (2 * strip_rows)
    return jnp.where(
        within < strip_rows,
        owner_index * strip_rows + within,
        (2 * devices - 1 - owner_index) * strip_rows + within - strip_rows,
    )


def rotate(values, positions, num_heads):
    count_rows, model_width = values.shape
    head_width = model_width // num_heads
    half_width = head_width // 2
    freqs_table = rope_base ** (-2.0 * jnp.arange(half_width, dtype=jnp.float32) / head_width)
    angles = positions.astype(jnp.float32)[:, None] * freqs_table[None, :]
    cosine = jnp.cos(angles)[:, None, :]
    sine_table = jnp.sin(angles)[:, None, :]
    split_heads = values.reshape(count_rows, num_heads, head_width)
    former = split_heads[:, :, :half_width]
    latter = split_heads[:, :, half_width:]
    turned = jnp.concatenate(
        [former * cosine - latter * sine_table, latter * cosine + former * sine_table], axis=2
    )
    return turned.reshape(count_rows, model_width)


def norm_scale(values):
    return values * lax.rsqrt(jnp.mean(values * values, axis=-1, keepdims=True) + norm_eps)


def normed(values, gain_vector):
    return norm_scale(values) * gain_vector


def swiglu(gate_rows, up_rows):
    return jax.nn.silu(gate_rows) * up_rows


def dot_right(left, right):
    return lax.dot_general(
        left, right, (((1,), (1,)), ((), ())), preferred_element_type=jnp.float32
    )


def dot_left(left, right):
    return lax.dot_general(
        left, right, (((0,), (0,)), ((), ())), preferred_element_type=jnp.float32
    )


def split_blocks(array, block_rows):
    return array.reshape((array.shape[0] // block_rows, block_rows) + array.shape[1:])


def key_mask(query_pos, key_pos, valid_count):
    causal = key_pos[None, :] <= query_pos[:, None]
    live_keys = key_pos[None, :] < valid_count[:, None]
    return (causal[None, None, :, :] & live_keys[:, None, None, :]).astype(jnp.float32)


def scores_of(queries, key_rows, query_pos, key_pos, valid_count, score_shift):
    head_width = queries.shape[3]
    raw_scores = jnp.einsum(
        "qshd,kshd->shqk", queries, key_rows, preferred_element_type=jnp.float32
    )
    return (
        raw_scores * head_width ** (-0.5) - score_shift,
        key_mask(query_pos, key_pos, valid_count),
    )


def block_grads(queries, grad_rows, key_rows, values, query_pos, key_pos, valid_count, score_shift):
    logits, mask_table = scores_of(queries, key_rows, query_pos, key_pos, valid_count, score_shift)
    sigmoid_table = jax.nn.sigmoid(logits)
    weights_low = (sigmoid_table * mask_table).astype(jnp.bfloat16)
    grad_weights = jnp.einsum(
        "qshd,kshd->shqk", grad_rows, values, preferred_element_type=jnp.float32
    )
    grad_logits = (grad_weights * mask_table * (sigmoid_table * (1.0 - sigmoid_table))).astype(
        jnp.bfloat16
    )
    return (weights_low, grad_logits)


def make_norm_fold(normalized, pieces):
    gain_part = pieces[0].astype(jnp.float32)
    scaled = (normalized * gain_part).astype(jnp.bfloat16)
    totals = tuple(
        (
            jnp.dot(scaled, weight_piece, preferred_element_type=jnp.float32)
            for weight_piece in pieces[1:]
        )
    )
    return (gain_part,) + totals


def make_row_fold(left_rows, weight_piece):
    return jnp.dot(left_rows, weight_piece, preferred_element_type=jnp.float32)


def gather_weights_step(
    layer_in,
    valid_len,
    norm1_gain,
    w_query,
    w_key,
    w_value,
    w_out,
    norm2_gain,
    w_gate,
    w_up,
    w_down,
    cotangent,
):
    local_rows, local_seqs, model_width = layer_in.shape
    num_heads = HEADS
    head_width = model_width // num_heads
    strip_rows = local_rows // 2
    cp_devices = lax.axis_size("cp")
    cp_place = lax.axis_index("cp")
    seq_length = local_rows * cp_devices
    score_shift = math.log(seq_length)
    score_scale = head_width ** (-0.5)
    token_count = local_rows * local_seqs
    local_pos = row_positions(
        cp_place * local_rows + jnp.arange(local_rows, dtype=jnp.int32), strip_rows, cp_devices
    )
    token_pos = jnp.broadcast_to(local_pos[:, None], (local_rows, local_seqs)).reshape(token_count)
    every_pos = row_positions(jnp.arange(seq_length, dtype=jnp.int32), strip_rows, cp_devices)
    block_rows = math.gcd(seq_length, 512)
    head_shape = (local_rows, local_seqs, num_heads, head_width)
    row_shape = (local_rows, local_seqs, model_width)
    zero_heads = jnp.zeros(head_shape, jnp.float32)
    inputs = layer_in.reshape(token_count, model_width).astype(jnp.float32)
    input_norm = norm_scale(inputs)
    gain_one, query, key_proj, value = make_norm_fold(
        input_norm,
        (
            lax.all_gather(norm1_gain, ("seq", "cp"), axis=0, tiled=True),
            lax.all_gather(w_query, ("seq", "cp"), axis=0, tiled=True),
            lax.all_gather(w_key, ("seq", "cp"), axis=0, tiled=True),
            lax.all_gather(w_value, ("seq", "cp"), axis=0, tiled=True),
        ),
    )
    normed_one = (input_norm * gain_one).astype(jnp.bfloat16)
    query_low = rotate(query, token_pos, num_heads).astype(jnp.bfloat16)
    key_low = rotate(key_proj, token_pos, num_heads).astype(jnp.bfloat16)
    value_low = value.astype(jnp.bfloat16)
    query_heads = query_low.reshape(head_shape)
    key_local = key_low.reshape(row_shape)
    value_local = value_low.reshape(row_shape)
    key_piece = lax.all_gather(key_local, "cp", axis=0, tiled=True)
    value_piece = lax.all_gather(value_local, "cp", axis=0, tiled=True)
    piece_rows = key_piece.shape[0]
    piece_block = math.gcd(piece_rows, 512)
    piece_pos = row_positions(jnp.arange(piece_rows, dtype=jnp.int32), strip_rows, cp_devices)

    def scan_step(partial_sum, block_items):
        key_block, value_block, block_pos = block_items
        logits, mask_table = scores_of(
            query_heads,
            key_block.reshape(piece_block, local_seqs, num_heads, head_width),
            local_pos,
            block_pos,
            valid_len,
            score_shift,
        )
        weights_low = (jax.nn.sigmoid(logits) * mask_table).astype(jnp.bfloat16)
        added = jnp.einsum(
            "shqk,kshd->qshd",
            weights_low,
            value_block.reshape(piece_block, local_seqs, num_heads, head_width),
            preferred_element_type=jnp.float32,
        )
        return (partial_sum + added, None)

    result, _ = lax.scan(
        scan_step,
        zero_heads,
        (
            split_blocks(key_piece, piece_block),
            split_blocks(value_piece, piece_block),
            split_blocks(piece_pos, piece_block),
        ),
    )
    attended_low = result.reshape(token_count, model_width).astype(jnp.bfloat16)
    attn_branch = make_row_fold(
        attended_low, lax.all_gather(w_out, ("seq", "cp"), axis=0, tiled=True)
    )
    hidden_state = inputs + attn_branch
    hidden_norm = norm_scale(hidden_state)
    gain_two, gate_rows, up_rows = make_norm_fold(
        hidden_norm,
        (
            lax.all_gather(norm2_gain, ("seq", "cp"), axis=0, tiled=True),
            lax.all_gather(w_gate, ("seq", "cp"), axis=0, tiled=True),
            lax.all_gather(w_up, ("seq", "cp"), axis=0, tiled=True),
        ),
    )
    normed_two = (hidden_norm * gain_two).astype(jnp.bfloat16)
    hidden_units = swiglu(gate_rows, up_rows).astype(jnp.bfloat16)
    ff_branch = make_row_fold(
        hidden_units, lax.all_gather(w_down, ("seq", "cp"), axis=0, tiled=True)
    )
    layer_out = (hidden_state + ff_branch).astype(jnp.bfloat16).reshape(row_shape)
    grad_out = cotangent.reshape(token_count, model_width)
    gate_all, up_all, down_all = (
        lax.all_gather(w_gate, ("seq", "cp"), axis=0, tiled=True),
        lax.all_gather(w_up, ("seq", "cp"), axis=0, tiled=True),
        lax.all_gather(w_down, ("seq", "cp"), axis=0, tiled=True),
    )
    grad_hidden = dot_right(grad_out, down_all)
    _, pull_swiglu = jax.vjp(swiglu, gate_rows, up_rows)
    grad_gate, grad_up = pull_swiglu(grad_hidden)
    grad_gate_low = grad_gate.astype(jnp.bfloat16)
    grad_up_low = grad_up.astype(jnp.bfloat16)
    grad_norm_two = dot_right(grad_gate_low, gate_all) + dot_right(grad_up_low, up_all)
    _, pull_two = jax.vjp(normed, hidden_state, gain_two)
    grad_from_two, gain_two_term = pull_two(grad_norm_two)
    ff_grads = (
        lax.psum_scatter(gain_two_term, ("seq", "cp"), scatter_dimension=0, tiled=True),
        lax.psum_scatter(
            dot_left(normed_two, grad_gate_low), ("seq", "cp"), scatter_dimension=0, tiled=True
        ),
        lax.psum_scatter(
            dot_left(normed_two, grad_up_low), ("seq", "cp"), scatter_dimension=0, tiled=True
        ),
        lax.psum_scatter(
            dot_left(hidden_units, grad_out), ("seq", "cp"), scatter_dimension=0, tiled=True
        ),
    )
    grad_state = grad_out.astype(jnp.float32) + grad_from_two
    query_all, key_all, value_all, out_all = (
        lax.all_gather(w_query, ("seq", "cp"), axis=0, tiled=True),
        lax.all_gather(w_key, ("seq", "cp"), axis=0, tiled=True),
        lax.all_gather(w_value, ("seq", "cp"), axis=0, tiled=True),
        lax.all_gather(w_out, ("seq", "cp"), axis=0, tiled=True),
    )
    grad_branch_low = grad_state.astype(jnp.bfloat16)
    grad_attended_low = dot_right(grad_branch_low, out_all).astype(jnp.bfloat16)
    grad_heads = grad_attended_low.reshape(head_shape)
    key_heads_local = key_local.reshape(head_shape)
    value_heads_local = value_local.reshape(head_shape)
    keys_every, values_every, queries_every, grads_every = (
        lax.all_gather(key_local, "cp", axis=0, tiled=True),
        lax.all_gather(value_local, "cp", axis=0, tiled=True),
        lax.all_gather(query_low.reshape(row_shape), "cp", axis=0, tiled=True),
        lax.all_gather(grad_attended_low.reshape(row_shape), "cp", axis=0, tiled=True),
    )

    def key_step(partial_sums, block_items):
        query_block, grad_block_rows, block_pos = block_items
        query_part = query_block.reshape(block_rows, local_seqs, num_heads, head_width)
        grad_part = grad_block_rows.reshape(block_rows, local_seqs, num_heads, head_width)
        weights_low, grad_logits = block_grads(
            query_part,
            grad_part,
            key_heads_local,
            value_heads_local,
            block_pos,
            local_pos,
            valid_len,
            score_shift,
        )
        key_added = jnp.einsum(
            "shqk,qshd->kshd", grad_logits, query_part, preferred_element_type=jnp.float32
        )
        value_added = jnp.einsum(
            "shqk,qshd->kshd", weights_low, grad_part, preferred_element_type=jnp.float32
        )
        return ((partial_sums[0] + key_added, partial_sums[1] + value_added), None)

    (key_sum, value_sum), _ = lax.scan(
        key_step,
        (zero_heads, zero_heads),
        (
            split_blocks(queries_every, block_rows),
            split_blocks(grads_every, block_rows),
            split_blocks(every_pos, block_rows),
        ),
    )
    grad_key_rot = key_sum.reshape(token_count, model_width) * score_scale
    grad_value_sum = value_sum.reshape(token_count, model_width)

    def query_step(partial_sum, block_items):
        key_block, value_block, block_pos = block_items
        key_heads = key_block.reshape(block_rows, local_seqs, num_heads, head_width)
        _, grad_logits = block_grads(
            query_heads,
            grad_heads,
            key_heads,
            value_block.reshape(block_rows, local_seqs, num_heads, head_width),
            local_pos,
            block_pos,
            valid_len,
            score_shift,
        )
        added = jnp.einsum(
            "shqk,kshd->qshd", grad_logits, key_heads, preferred_element_type=jnp.float32
        )
        return (partial_sum + added, None)

    query_sum, _ = lax.scan(
        query_step,
        zero_heads,
        (
            split_blocks(keys_every, block_rows),
            split_blocks(values_every, block_rows),
            split_blocks(every_pos, block_rows),
        ),
    )
    grad_query_rot = query_sum.reshape(token_count, model_width) * score_scale
    grad_query_low = rotate(grad_query_rot, -token_pos, num_heads).astype(jnp.bfloat16)
    grad_key_low = rotate(grad_key_rot, -token_pos, num_heads).astype(jnp.bfloat16)
    grad_value_low = grad_value_sum.astype(jnp.bfloat16)
    grad_norm_one = (
        dot_right(grad_query_low, query_all)
        + dot_right(grad_key_low, key_all)
        + dot_right(grad_value_low, value_all)
    )
    _, pull_one = jax.vjp(normed, inputs, gain_one)
    grad_from_one, gain_one_term = pull_one(grad_norm_one)
    in_grad = (grad_state + grad_from_one).reshape(row_shape)
    attn_grads = (
        lax.psum_scatter(gain_one_term, ("seq", "cp"), scatter_dimension=0, tiled=True),
        lax.psum_scatter(
            dot_left(normed_one, grad_query_low), ("seq", "cp"), scatter_dimension=0, tiled=True
        ),
        lax.psum_scatter(
            dot_left(normed_one, grad_key_low), ("seq", "cp"), scatter_dimension=0, tiled=True
        ),
        lax.psum_scatter(
            dot_left(normed_one, grad_value_low), ("seq", "cp"), scatter_dimension=0, tiled=True
        ),
        lax.psum_scatter(
            dot_left(attended_low, grad_branch_low), ("seq", "cp"), scatter_dimension=0, tiled=True
        ),
    )
    return (
        layer_out,
        in_grad,
        attn_grads[0],
        attn_grads[1],
        attn_grads[2],
        attn_grads[3],
        attn_grads[4],
        ff_grads[0],
        ff_grads[1],
        ff_grads[2],
        ff_grads[3],
    )


MESH = pl.DeviceIdType.MESH
DMA = pltpu.SemaphoreType.DMA
LOW = jnp.bfloat16
F32 = jnp.float32
ANYWHERE = pl.BlockSpec(memory_space=pl.ANY)
IN_VMEM = pl.BlockSpec(memory_space=pltpu.VMEM)
IN_SMEM = pl.BlockSpec(memory_space=pltpu.SMEM)


class Place:
    def __init__(self):
        self.s = lax.axis_index("seq")
        self.c = lax.axis_index("cp")
        self.z = self.c // 4
        self.y = (self.c // 2) % 2
        self.k = self.c % 2

    def at(self, z, y, k):
        return z * 4 + y * 2 + k

    def device(self, place):
        return (self.s, place)


def pick(z, table):
    value = jnp.int32(table[0])
    for index in range(1, 4):
        value = jnp.where(z == index, jnp.int32(table[index]), value)
    return value


NEAREST = ((1, 0, 1, 2), (2, 2, 3, 1), (3, 3, 0, 0))
FARTHEST = ((3, 3, 0, 0), (2, 2, 3, 1), (1, 0, 1, 2))


def remote(source, target, send, recv, device):
    return pltpu.make_async_remote_copy(
        src_ref=source,
        dst_ref=target,
        send_sem=send,
        recv_sem=recv,
        device_id=device,
        device_id_type=MESH,
    )


def hail(device):
    pl.semaphore_signal(
        pltpu.get_barrier_semaphore(), inc=1, device_id=device, device_id_type=MESH
    )


def greet(me, over_seq=False):
    hail((me.s, me.at(me.z, 1 - me.y, me.k)))
    hail((me.s, me.at(me.z, me.y, 1 - me.k)))

    @pl.when(me.z < 3)
    def _():
        hail((me.s, me.at(me.z + 1, me.y, me.k)))

    @pl.when(me.z > 0)
    def _():
        hail((me.s, me.at(me.z - 1, me.y, me.k)))

    ends = (me.z == 0).astype(jnp.int32) + (me.z == 3).astype(jnp.int32)
    if over_seq:
        hail((1 - me.s, me.c))
    return lambda: pl.semaphore_wait(
        pltpu.get_barrier_semaphore(), 4 - ends + (1 if over_seq else 0)
    )


def greet_plane(me):
    for step in range(1, 16):
        hail((me.s, (me.c + step) % 16))
    hail((1 - me.s, me.c))
    hail((1 - me.s, me.at(me.z, me.y, 1 - me.k)))
    return lambda: pl.semaphore_wait(pltpu.get_barrier_semaphore(), 17)


class Gather:
    def __init__(self, me, views, early, z_sem, far_sem, y_sem, k_sem, recv):
        self.me, self.views, self.early = me, views, early
        self.z_sem, self.far_sem, self.y_sem, self.k_sem, self.recv = z_sem, far_sem, y_sem, k_sem, recv

    count = 5

    @staticmethod
    def sems(pieces):
        return [DMA((pieces * n,)) for n in (5, 5, 4, 8, 16)]

    def copy(self, piece, place, sem, device):
        block = self.views[piece](place)
        return remote(block, block, sem, self.recv.at[piece * 16 + place], device)

    def arrived(self, piece, place):
        self.copy(piece, place, self.k_sem.at[0], self.me.device(self.me.c)).wait_recv()

    def line(self, index):
        return self.me.z if index == 0 else pick(self.me.z, NEAREST[index - 1])

    def along(self, piece, place, index, up, sems):
        me = self.me
        target = jnp.minimum(me.c + 4, 12 + me.c % 4) if up else jnp.maximum(me.c - 4, me.c % 4)
        return self.copy(piece, place, sems.at[piece * 5 + index], me.device(target))

    def across(self, piece, place, index):
        me = self.me
        target = me.at(me.z, 1 - me.y, me.k)
        return self.copy(piece, place, self.y_sem.at[piece * 4 + index], me.device(target))

    def partner(self, piece, place, index):
        me = self.me
        target = me.at(me.z, me.y, 1 - me.k)
        return self.copy(piece, place, self.k_sem.at[piece * 8 + index], me.device(target))

    def spread_along(self, piece, place, index, sems, go):
        me, z = self.me, self.line(index)
        if index == 0:

            @pl.when(me.z < 3)
            def _():
                go(self.along(piece, place, 0, True, sems))

            @pl.when(me.z > 0)
            def _():
                go(self.along(piece, place, 4, False, sems))
        else:

            @pl.when((z < me.z) & (me.z < 3))
            def _():
                go(self.along(piece, place, index, True, sems))

            @pl.when((z > me.z) & (me.z > 0))
            def _():
                go(self.along(piece, place, index, False, sems))

    def send_near(self, piece, index, go=lambda copy: copy.start()):
        me = self.me
        place = me.at(self.line(index), me.y, me.k)
        if index == 0 or not self.early[piece]:
            go(self.across(piece, place, index))
        self.spread_along(piece, place, index, self.z_sem, go)
        go(self.partner(piece, place, index))

    def send_far(self, piece, index, go=lambda copy: copy.start()):
        me = self.me
        place = me.at(self.line(index), 1 - me.y, me.k)
        if self.early[piece]:
            self.spread_along(piece, place, index, self.far_sem, go)
        go(self.partner(piece, place, 4 + index))

    def begin(self):
        for piece in range(len(self.views)):
            self.send_near(piece, 0)

    def round(self, index):
        me = self.me
        for piece in range(len(self.views)):
            if index < 3:
                self.arrived(piece, me.at(self.line(index + 1), me.y, me.k))
                self.send_near(piece, index + 1)
            self.arrived(piece, me.at(self.line(index), 1 - me.y, me.k))
            self.send_far(piece, index)

    def settle(self, z, y):
        for piece in range(len(self.views)):
            self.arrived(piece, self.me.at(z, y, 1 - self.me.k))

    def run(self, consume):
        me = self.me
        self.begin()
        waiting = [(me.z, me.y)]
        for index in range(4):
            self.round(index)
            ready, waiting = waiting, []
            if index < 3:
                waiting.append((self.line(index + 1), me.y))
            waiting.append((self.line(index), 1 - me.y))
            for z, y in ready:
                self.settle(z, y)
                consume(z * 2 + y)
        for z, y in waiting:
            self.settle(z, y)
            consume(z * 2 + y)

    def finish(self):
        for piece in range(len(self.views)):
            for index in range(4):
                self.send_near(piece, index, lambda copy: copy.wait_send())
                self.send_far(piece, index, lambda copy: copy.wait_send())


class Scatter:
    pieces = 2

    def __init__(self, me, scratch):
        self.me = me
        (self.k_out, self.k_in, self.y_out, self.y_in, self.z_out, self.z_in, self.mine, self.kept) = scratch[:8]
        (self.ks, self.kr, self.ys, self.yr, self.zs, self.zl, self.zr) = scratch[8:15]

    count = 15

    @classmethod
    def scratch(cls, rows, width):
        n = cls.pieces
        part = width // n
        low = [pltpu.VMEM((n * count, rows, part), LOW) for count in (8, 8, 4, 4, 3, 5)]
        full = [pltpu.VMEM((n * count, rows, part), F32) for count in (1, 4)]
        return low + full + [DMA((n * count,)) for count in (8, 8, 4, 4, 3, 4, 4)]

    def partner(self, slot):
        me = self.me
        target = me.device(me.at(me.z, me.y, 1 - me.k))
        return remote(self.k_out.at[slot], self.k_in.at[slot], self.ks.at[slot], self.kr.at[slot], target)

    def across(self, z, index, piece):
        me, n = self.me, self.pieces
        out, land = index * n + piece, z * n + piece
        target = me.device(me.at(me.z, 1 - me.y, me.k))
        return remote(self.y_out.at[out], self.y_in.at[land], self.ys.at[out], self.yr.at[land], target)

    def along(self, z, index, piece, up):
        me, n = self.me, self.pieces
        out, land = index * n + piece, z * n + piece
        target = jnp.minimum(me.c + 4, 12 + me.c % 4) if up else jnp.maximum(me.c - 4, me.c % 4)
        into = self.z_in.at[land if up else jnp.where(z == me.z - 1, 4, z) * n + piece]
        sem = (self.zl if up else self.zr).at[land]
        return remote(self.z_out.at[out], into, self.zs.at[out], sem, me.device(target))

    def line(self, index):
        return self.me.z if index == 3 else pick(self.me.z, FARTHEST[index])

    def emit(self, produce, z, y, piece, slot, keep):
        part = 512
        rows, width = keep.shape

        @pl.loop(0, width // part)
        def _(index):
            here = pl.ds(pl.multiple_of(index * part, part), part)
            start = pl.multiple_of(piece * width + index * part, part)
            value = produce(self.me.at(z, y, 0), pl.ds(start, part))
            self.k_out[slot, :, here] = value[:rows].astype(LOW)
            keep[:, here] = value[rows:]

    def add(self, target, base, *blocks):
        part = 512

        @pl.loop(0, target.shape[-1] // part)
        def _(index):
            here = pl.ds(pl.multiple_of(index * part, part), part)
            value = base[:, here]
            for block in blocks:
                value = value + block[:, here].astype(F32)
            target[:, here] = value.astype(target.dtype)

    def run(self, prepare, produce, finish, fillers=(), ready=lambda: None, after=lambda: None):
        me, n = self.me, self.pieces
        fillers = list(fillers)
        steps = [(index, piece) for index in range(4) for piece in range(n)]
        for number in range(len(steps) + 1):
            if number < len(steps):
                index, piece = steps[number]
                z = self.line(index)
                if prepare is not None and piece == 0:
                    prepare(z * 2 + 1 - me.y)
                self.emit(produce, z, 1 - me.y, piece, number, self.mine.at[number % 2])
                if number == 0:
                    ready()
                self.partner(number).start()
            if number > 0:
                index, piece = steps[number - 1]
                self.partner(number - 1).wait_recv()
                self.add(self.y_out.at[number - 1], self.mine.at[(number - 1) % 2], self.k_in.at[number - 1])
                self.across(self.line(index), index, piece).start()

        after()

        def own(number):
            index, piece = steps[number]
            z = self.line(index)
            if prepare is not None and piece == 0:
                prepare(z * 2 + me.y)
            self.emit(produce, z, me.y, piece, 4 * n + number, self.kept.at[number])
            self.partner(4 * n + number).start()

        ahead = n
        for number in range(ahead):
            own(number)
        for number in range(len(steps)):
            if number + ahead < len(steps):
                own(number + ahead)
            if prepare is None or number + ahead >= len(steps) - n:
                for _ in range(-(-len(fillers) // (len(steps) - number))):
                    fillers.pop(0)()
            self.collect(number, *steps[number], finish)

    def collect(self, number, index, piece, finish):
        me, n = self.me, self.pieces
        z = self.line(index)
        slot, land = 4 * n + number, z * n + piece
        kept = self.kept.at[number]
        self.partner(slot).wait_recv()
        self.across(z, index, piece).wait_recv()
        self.add(kept, kept, self.k_in.at[slot], self.y_in.at[land])
        if index < 3:
            from_below, from_above = (z > me.z) & (me.z > 0), (z < me.z) & (me.z < 3)
        else:
            from_below, from_above = me.z > 0, me.z < 3

        @pl.when(from_below)
        def _():
            self.along(z, 0, piece, True).wait_recv()
            self.add(kept, kept, self.z_in.at[land])

        @pl.when(from_above)
        def _():
            self.along(z, 0, piece, False).wait_recv()
            self.add(kept, kept, self.z_in.at[4 * n + piece if index == 3 else land])

        if index < 3:
            self.add(self.z_out.at[number], kept)

            @pl.when(z > me.z)
            def _():
                self.along(z, index, piece, True).start()

            @pl.when(z < me.z)
            def _():
                self.along(z, index, piece, False).start()
        else:
            finish(piece, kept)

    def drain(self):
        me, n = self.me, self.pieces
        for slot in range(8 * n):
            self.partner(slot).wait_send()
        for index in range(4):
            z = self.line(index)
            for piece in range(n):
                self.across(z, index, piece).wait_send()
                if index < 3:

                    @pl.when(z > me.z)
                    def _():
                        self.along(z, index, piece, True).wait_send()

                    @pl.when(z < me.z)
                    def _():
                        self.along(z, index, piece, False).wait_send()


def write_total(total_out):
    def finish(piece, kept):
        width = kept.shape[-1]
        total_out[:, piece * width : (piece + 1) * width] = kept[...]

    return finish


def leave(stage, parts, sems):
    copies = []

    def run(number, work, place):
        if number >= 2:
            copies[number - 2].wait()
        slot = stage.at[number % 2]
        work(slot)
        copies.append(pltpu.make_async_copy(slot, place, sems.at[number]))
        copies[number].start()

    def end():
        for copy in copies[-2:]:
            copy.wait()

    return [functools.partial(run, number, *part) for number, part in enumerate(parts)], end


def own_last(me, block, first):
    return jnp.concatenate([block[first + 1 - me.k], block[first + me.k]], axis=0)


def params(collective_id):
    return pltpu.CompilerParams(
        collective_id=collective_id, has_side_effects=True, vmem_limit_bytes=60 << 20
    )


def turn(me, step):
    dz, dy, dk = step // 4, (step // 2) % 2, step % 2
    to = me.at((me.z + dz) % 4, (me.y + dy) % 2, (me.k + dk) % 2)
    source = me.at((me.z + 4 - dz) % 4, (me.y + dy) % 2, (me.k + dk) % 2)
    return to, source


def cuts(rows):
    return ((0, rows // 2), (rows // 2, rows * 7 // 8 - rows // 2), (rows * 7 // 8, rows // 8))


EARLY = [False, False, True]


def pieces_of(array):
    return [
        lambda place, start=start, size=size: array.at[place, pl.ds(start, size)]
        for start, size in cuts(array.shape[1])
    ]


def scale_of(values):
    return lax.rsqrt(jnp.mean(values * values, axis=-1, keepdims=True) + norm_eps)


def norm_back(values, scale, weighted):
    inner = jnp.mean(values * weighted, axis=-1, keepdims=True)
    return scale * weighted - values * (scale * scale * scale * inner)


def by_rows(total, work, rows=32):
    @pl.loop(0, total // rows)
    def _(index):
        work(pl.ds(pl.multiple_of(index * rows, rows), rows))


def down_rows(row, width):
    full = jnp.broadcast_to(row[...].astype(F32), (width, row.shape[1]))
    return jnp.transpose(full)


def spread_kernel(
    token, grad, w_query, w_key, w_value, w_gate, w_up, gain_one, gain_two, out_w, down,
    token_rows, units, grads, query, key, value, cosine, sine, qkv_full, gate_up_half, out_all, down_other, *scratch
):
    gather_sems = scratch[: Gather.count]
    (qs, qr, qxs, qxr, ps, pr, os, ox, orecv, local, dsem, leave, units_here, grads_here, qkv_all, qkv, gate_up) = scratch[Gather.count :]
    me = Place()
    own = [
        pltpu.make_async_copy(qkv.at[me.c], qkv_all.at[me.s, me.c], local.at[2]),
        pltpu.make_async_copy(gate_up.at[me.c], gate_up_half.at[me.c], local.at[3]),
    ]
    ready = greet_plane(me)
    over = (1 - me.s, me.c)
    rows, _, model = token.shape
    tokens = 2 * rows
    for seq in range(2):
        here = slice(seq * rows, (seq + 1) * rows)
        values = token[:, seq, :]
        token_rows[here, :] = values
        values = values.astype(F32)
        units_here[me.c, here] = (values * scale_of(values)).astype(LOW)
        grads_here[me.c, here] = grad[:, seq, :]
    ready()
    gather = Gather(me, pieces_of(units_here) + pieces_of(grads_here), [False] * 3 + EARLY, *gather_sems)
    down_copy = remote(down, down_other, dsem.at[0], dsem.at[1], over)

    def send_qkv(step):
        to, _ = turn(me, step)
        return remote(qkv.at[to], qkv_all.at[me.s, me.c], qs.at[step], qr.at[me.c], (me.s, to))

    def send_gate_up(step):
        to, _ = turn(me, step)
        return remote(gate_up.at[to], gate_up_half.at[me.c], ps.at[step], pr.at[me.c], (me.s, to))

    def forward(source):
        block = qkv_all.at[me.s, source]
        return remote(block, block, qxs.at[source], qxr.at[source], over)

    holder = me.at(me.z, me.y, me.s)
    out_local = pltpu.make_async_copy(out_w, out_all.at[me.k], local.at[4])
    out_near = remote(out_w, out_all.at[me.k], os.at[0], orecv.at[me.k], (me.s, me.at(me.z, me.y, 1 - me.k)))
    out_far = remote(out_w, out_all.at[me.k], ox, orecv.at[me.k], (1 - me.s, holder))

    gather.begin()
    width = query.shape[3]
    weight_rows = w_query.shape[0]
    one = down_rows(gain_one, width)
    for place in range(16):
        head = place // 2 + 8 * (place % 2)
        for index, weight in enumerate((w_query, w_key, w_value)):
            block = weight[:, head * width : (head + 1) * width].astype(F32) * one
            qkv[place, :, index * width : (index + 1) * width] = block.astype(LOW)
    own[0].start()
    for step in range(1, 16):
        send_qkv(step).start()
    units_of = gate_up.shape[2] // 4
    two = down_rows(gain_two, units_of)
    for place in range(16):
        for index, weight in enumerate((w_gate, w_up)):
            for half in range(2):
                start = (half * 16 + place) * units_of
                block = weight[:, start : start + units_of].astype(F32) * two
                start = (2 * index + half) * units_of
                gate_up[place, :, start : start + units_of] = block.astype(LOW)
    own[1].start()
    own[0].wait()
    forward(me.c).start()
    out_far.start()

    @pl.when(holder == me.c)
    def _():
        out_local.start()

    @pl.when(holder != me.c)
    def _():
        out_near.start()

    down_copy.start()
    leaving = []

    half_width = width // 2
    lane = lax.broadcasted_iota(jnp.int32, (rows, width), 1)
    row = lax.broadcasted_iota(jnp.int32, (rows, width), 0)
    freqs = jnp.exp((lane % half_width).astype(F32) * (-2.0 * math.log(rope_base) / width))
    sign = jnp.where(lane < half_width, 1.0, -1.0)

    @pl.loop(0, 16)
    def _(place):
        angles = row_place(place, row, rows // 2).astype(F32) * freqs
        cosine[place] = jnp.cos(angles)
        sine[place] = jnp.sin(angles) * sign

    def write_out(z, y):
        pair = z * 2 + y
        both = pl.ds(2 * pair, 2)
        number = len(leaving)
        for index, (here, there) in enumerate(((units_here, units), (grads_here, grads))):
            copy = pltpu.make_async_copy(here.at[both], there.at[both], leave.at[2 * number + index])
            copy.start()
            leaving.append(copy)

    def turned(values, both):
        swapped = pltpu.roll(values, width // 2, axis=1)
        place_cos = cosine[both].reshape(2 * rows, width)
        place_sin = sine[both].reshape(2 * rows, width)
        return (values * place_cos - swapped * place_sin).astype(LOW).reshape(2, rows, width)

    def project(z, y):
        both = pl.ds(2 * (z * 2 + y), 2)
        weights = qkv_all[...].reshape(model, 3 * width)
        for seq in range(2):
            block = units_here[both, seq * rows : (seq + 1) * rows].reshape(2 * rows, model)
            result = jnp.dot(block, weights, preferred_element_type=F32)
            query[both, seq] = turned(result[:, :width], both)
            key[both, seq] = turned(result[:, width : 2 * width], both)
            value[both, seq] = result[:, 2 * width :].astype(LOW).reshape(2, rows, width)

    steps = list(range(1, 16))
    waiting, ready = [(me.z, me.y)], []
    for index in range(4):
        for step in steps[4 * index : 4 * index + 4]:
            send_gate_up(step).start()
        gather.round(index)
        for z, y in waiting:
            gather.settle(z, y)
            write_out(z, y)
        ready += waiting
        waiting = [(gather.line(index), 1 - me.y)]
        if index < 3:
            waiting.append((gather.line(index + 1), me.y))
        if index == 1:
            for step in steps:
                _, source = turn(me, step)
                remote(qkv.at[0], qkv_all.at[me.s, source], qs.at[step], qr.at[source], over).wait_recv()
                forward(source).start()
        if index == 2:
            for source in range(16):
                forward(source).wait_send()
                forward(source).wait_recv()
            leave_qkv = pltpu.make_async_copy(qkv_all, qkv_full, local.at[5])
            leave_qkv.start()
        if index >= 2:
            for z, y in ready:
                project(z, y)
            ready = []
    for z, y in waiting:
        gather.settle(z, y)
        write_out(z, y)
        project(z, y)
    gather.finish()
    own[1].wait()
    leave_qkv.wait()
    for copy in leaving:
        copy.wait()
    for step in steps:
        _, source = turn(me, step)
        send_qkv(step).wait_send()
        send_gate_up(step).wait_send()
        remote(gate_up.at[0], gate_up_half.at[source], ps.at[step], pr.at[source], over).wait_recv()
    out_far.wait_send()
    down_copy.wait()

    @pl.when(holder == me.c)
    def _():
        out_local.wait()
        remote(out_w, out_all.at[1 - me.k], ox, orecv.at[1 - me.k], over).wait_recv()

    @pl.when(holder != me.c)
    def _():
        out_near.wait_send()
        for half in range(2):
            remote(out_w, out_all.at[half], ox, orecv.at[half], over).wait_recv()


def spread(token, grad, w_query, w_key, w_value, w_gate, w_up, gain_one, gain_two, out_w, down):
    def shape(lead, array):
        return jax.ShapeDtypeStruct(lead + array.shape, array.dtype)

    rows, seqs, model = token.shape
    tokens = rows * seqs
    flat = jax.ShapeDtypeStruct((16, tokens, model), LOW)
    width = model // 16
    weight_rows = w_query.shape[0]
    qkv = (weight_rows, 3 * width)
    gate_up = (weight_rows, 2 * w_gate.shape[1] // 16)
    heads = jax.ShapeDtypeStruct((16, 2, tokens // 2, width), LOW)
    table = jax.ShapeDtypeStruct((16, tokens // 2, width), F32)
    return pl.pallas_call(
        spread_kernel,
        out_shape=[
            jax.ShapeDtypeStruct((tokens, model), LOW),
            flat,
            flat,
            heads,
            heads,
            heads,
            table,
            table,
            jax.ShapeDtypeStruct((2, 16) + qkv, LOW),
            jax.ShapeDtypeStruct((16,) + gate_up, LOW),
            shape((2,), out_w),
            shape((), down),
        ],
        in_specs=[IN_VMEM] * 9 + [ANYWHERE] * 2,
        out_specs=[IN_VMEM] + [ANYWHERE] * 2 + [IN_VMEM] * 5 + [ANYWHERE] * 4,
        scratch_shapes=Gather.sems(6)
        + [DMA((16,))] * 6
        + [DMA((1,)), DMA, DMA((2,)), DMA((6,)), DMA((2,)), DMA((32,))]
        + [pltpu.VMEM((16, tokens, model), LOW)] * 2
        + [pltpu.VMEM((2, 16) + qkv, LOW), pltpu.VMEM((16,) + qkv, LOW), pltpu.VMEM((16,) + gate_up, LOW)],
        compiler_params=params(0),
    )(token, grad, w_query, w_key, w_value, w_gate, w_up, gain_one, gain_two, out_w, down)


def row_place(place, row, strip):
    return jnp.where(row < strip, place * strip + row, (31 - place) * strip + row - strip)


def key_places(strip):
    index = lax.broadcasted_iota(jnp.int32, (1, 32 * strip), 1)
    return row_place(index // (2 * strip), index % (2 * strip), strip)


def query_places(pair, strip):
    index = lax.broadcasted_iota(jnp.int32, (4 * strip, 1), 0)
    return row_place(2 * pair + index // (2 * strip), index % (2 * strip), strip)


def of_pair(block, pair, seq):
    rows, width = block.shape[2:]
    return block[pl.ds(2 * pair, 2), seq].reshape(2 * rows, width)


def forward_kernel(
    shift, valid, query, key, value, out_w, token_far, grads, gate_up, down_own, down_other,
    grad_state, branch, hidden_own_far, attended_far, hidden_far, down_far, gate_up_grad, *scratch
):
    me = Place()
    hidden_own, attended, hidden, down_full, token, grad_own, side = scratch[-15:-8]
    tokens, model = token.shape
    width = hidden.shape[2]
    gather_sems = scratch[Scatter.count : Scatter.count + Gather.count]
    units, grad_gate_up, gate_up_full, grads_here, stage, leaving, local, swap_sems = scratch[-8:]
    scatter = Scatter(me, scratch)
    brought = [
        pltpu.make_async_copy(gate_up, gate_up_full.at[me.s], local.at[0]),
        pltpu.make_async_copy(down_own, down_full.at[me.s], local.at[1]),
        pltpu.make_async_copy(down_other, down_full.at[1 - me.s], local.at[2]),
        pltpu.make_async_copy(grads, grads_here, local.at[3]),
    ]
    near = [
        pltpu.make_async_copy(token_far, token, side.at[0]),
        pltpu.make_async_copy(grads.at[me.c], grad_own, side.at[1]),
    ]
    away = [
        pltpu.make_async_copy(attended, attended_far, side.at[2]),
        pltpu.make_async_copy(hidden_own, hidden_own_far, side.at[3]),
        pltpu.make_async_copy(hidden, hidden_far, side.at[4]),
        pltpu.make_async_copy(down_full, down_far, side.at[5]),
    ]
    ready = greet(me, over_seq=True)
    swap = remote(gate_up, gate_up_full.at[me.s], swap_sems.at[0], swap_sems.at[1], (1 - me.s, me.c))
    rows, depth = query.shape[2], query.shape[3]
    strip = rows // 2
    length = rows * 16
    scale = depth ** (-0.5)

    def attention(pair):
        where = query_places(pair, strip)
        keys_at = key_places(strip)
        for seq in range(2):
            keys = key[:, seq].reshape(length, depth)
            values = value[:, seq].reshape(length, depth)
            logits = dot_right(of_pair(query, pair, seq), keys) * scale - shift
            live = (keys_at <= where) & (keys_at < valid[seq])
            weights = jnp.where(live, jax.nn.sigmoid(logits), 0.0).astype(LOW)
            attended[pl.ds(2 * pair, 2), pl.ds(seq * rows, rows)] = (
                jnp.dot(weights, values, preferred_element_type=F32).astype(LOW).reshape(2, rows, depth)
            )

    def out_terms(first, columns):
        return jnp.dot(own_last(me, attended, first), out_w[:, columns], preferred_element_type=F32)

    def met():
        ready()
        swap.start()
        for copy in near + brought:
            copy.start()

    scatter.run(attention, out_terms, write_total(hidden_own), ready=met)
    scatter.drain()
    for copy in near:
        copy.wait()

    def to_unit(at):
        values = hidden_own[at, :] + token[at, :].astype(F32)
        hidden_own[at, :] = values
        units[me.c, at] = (values * scale_of(values)).astype(LOW)

    by_rows(tokens, to_unit)
    gather = Gather(me, pieces_of(units), EARLY, *gather_sems)
    rows_of = gate_up_full.shape[1] * gate_up_full.shape[2]
    units_of = down_full.shape[1]
    first = [True]

    def consume(pair):
        if first[0]:
            for copy in brought:
                copy.wait()
            swap.wait()
            first[0] = False
        both = pl.ds(2 * pair, 2)

        def dot_rows(rows, columns):
            return jnp.dot(
                rows,
                gate_up_full[:, :, :, columns].reshape(2 * rows_of, units_of),
                preferred_element_type=F32,
            )

        @pl.loop(0, 2)
        def _(half):
            gate_at = pl.ds(pl.multiple_of(half * units_of, units_of), units_of)
            up_at = pl.ds(pl.multiple_of(width + half * units_of, units_of), units_of)
            rows = units[both].reshape(2 * tokens, model)
            gate = dot_rows(rows, gate_at)
            up = dot_rows(rows, up_at)
            grad = dot_right(grads_here[both].reshape(2 * tokens, model), down_full[half])
            sig = jax.nn.sigmoid(gate)
            silu = gate * sig

            def store(target, columns, value):
                target[both, :, columns] = value.astype(LOW).reshape(2, tokens, units_of)

            store(hidden, gate_at, silu * up)
            store(grad_gate_up, gate_at, grad * up * (sig * (1.0 + gate * (1.0 - sig))))
            store(grad_gate_up, up_at, grad * silu)

    gather.run(consume)
    for copy in away:
        copy.start()
    block_rows = gate_up_full.shape[2]

    def unit_terms(first, columns):
        start, size = columns.start, columns.size
        blocks = size // block_rows
        block = start // block_rows
        weights = gate_up_full[block // 16, pl.ds(block % 16, blocks)].reshape(size, 2 * width)
        return dot_right(own_last(me, grad_gate_up, first), weights)

    every = 16 * tokens
    part = model // 8

    def gate_up_part(number):
        def work(slot):
            left = units[:, :, number * part : (number + 1) * part].reshape(every, part)
            slot[...] = dot_left(left, grad_gate_up[...].reshape(every, 2 * width)).astype(LOW)

        return work, gate_up_grad.at[pl.ds(number * part, part)]

    fillers, end = leave(stage, [gate_up_part(n) for n in range(8)], leaving)
    scatter.run(None, unit_terms, write_total(grad_state), fillers)

    def to_state(at):
        values = hidden_own[at, :]
        back = norm_back(values, scale_of(values), grad_state[at, :])
        state = grad_own[at, :].astype(F32) + back
        grad_state[at, :] = state
        branch[at, :] = state.astype(LOW)

    by_rows(tokens, to_state)
    end()
    for copy in away:
        copy.wait()
    scatter.drain()
    gather.finish()


def forward(shift, valid, query, key, value, out_w, token, grads, gate_up, down_own, down_other):
    tokens, model = token.shape
    width = 2 * down_own.shape[0]
    full = jax.ShapeDtypeStruct((tokens, model), F32)
    return pl.pallas_call(
        functools.partial(forward_kernel, shift),
        out_shape=[
            full,
            jax.ShapeDtypeStruct((tokens, model), LOW),
            full,
            jax.ShapeDtypeStruct((16, tokens, query.shape[3]), LOW),
            jax.ShapeDtypeStruct((16, tokens, width), LOW),
            jax.ShapeDtypeStruct((2,) + down_own.shape, LOW),
            jax.ShapeDtypeStruct((model, 2 * width), LOW),
        ],
        in_specs=[IN_SMEM] + [IN_VMEM] * 4 + [ANYWHERE] * 5,
        out_specs=[IN_VMEM] * 2 + [ANYWHERE] * 5,
        scratch_shapes=Scatter.scratch(tokens, model)
        + Gather.sems(3)
        + [
            pltpu.VMEM((tokens, model), F32),
            pltpu.VMEM((16, tokens, query.shape[3]), LOW),
            pltpu.VMEM((16, tokens, width), LOW),
            pltpu.VMEM((2,) + down_own.shape, LOW),
            pltpu.VMEM((tokens, model), LOW),
            pltpu.VMEM((tokens, model), LOW),
            DMA((6,)),
        ]
        + [
            pltpu.VMEM((16, tokens, model), LOW),
            pltpu.VMEM((16, tokens, 2 * width), LOW),
            pltpu.VMEM((2,) + gate_up.shape, LOW),
            pltpu.VMEM((16, tokens, model), LOW),
            pltpu.VMEM((2, model // 8, 2 * width), LOW),
            DMA((8,)),
            DMA((4,)),
            DMA((2,)),
        ],
        compiler_params=params(1),
    )(valid, query, key, value, out_w, token, grads, gate_up, down_own, down_other)


def attend_back_kernel(
    shift, valid, branch, units, gate_up, *rest
):
    far, rest = rest[:10], rest[10:]
    in_grad, qkv_grad, out_grad, gate_up_other = rest[:4]
    key_sum, value_sum, branches, grad_qkv, units_here, total_out = rest[4:10]
    side, near, scratch = rest[10], rest[11:21], rest[21:]
    query, key, value, out_w, cosine, sine, qkv_w, attended, token, grad_state = near
    near_copies = [pltpu.make_async_copy(a, b, side.at[n]) for n, (a, b) in enumerate(zip(far, near))]
    me = Place()
    tokens, model = branch.shape
    gather = Gather(me, pieces_of(branches), EARLY, *scratch[Scatter.count : Scatter.count + Gather.count])
    sems, local = scratch[-2:]
    own = pltpu.make_async_copy(branch, branches.at[me.c], local.at[0])
    own.start()
    bring = pltpu.make_async_copy(units, units_here, local.at[1])
    ready = greet(me, over_seq=True)
    for copy in near_copies:
        copy.start()
    bring.start()
    own.wait()
    ready()
    over = (1 - me.s, me.c)
    swaps = [
        remote(gate_up.at[1 - me.s], gate_up_other, sems.at[0], sems.at[1], over),
    ]
    for copy in swaps:
        copy.start()
    rows, width = query.shape[2:]
    strip = rows // 2
    length = rows * 16
    scale = width ** (-0.5)
    key_sum[...] = jnp.zeros_like(key_sum)
    value_sum[...] = jnp.zeros_like(value_sum)

    def turn_back(values, places):
        swapped = pltpu.roll(values, width // 2, axis=1)
        turned = values * cosine[places].reshape(2 * rows, width)
        return (turned + swapped * sine[places].reshape(2 * rows, width)).astype(LOW).reshape(2, rows, width)

    first = [True]

    def consume(pair):
        if first[0]:
            for copy in near_copies[:6]:
                copy.wait()
            first[0] = False
        where = query_places(pair, strip)
        keys_at = key_places(strip)
        both = pl.ds(2 * pair, 2)
        for seq in range(2):
            here = pl.ds(seq * rows, rows)
            grad = dot_right(branches[both, here].reshape(2 * rows, -1), out_w[...]).astype(LOW)
            keys = key[:, seq].reshape(length, width)
            values = value[:, seq].reshape(length, width)
            queries = of_pair(query, pair, seq)
            logits = dot_right(queries, keys) * scale - shift
            live = (keys_at <= where) & (keys_at < valid[seq])
            sig = jnp.where(live, jax.nn.sigmoid(logits), 0.0)
            weights = sig.astype(LOW)
            grad_logits = (dot_right(grad, values) * (sig * (1.0 - sig))).astype(LOW)
            grad_query = jnp.dot(grad_logits, keys, preferred_element_type=F32) * scale
            grad_qkv[both, here, 0:width] = turn_back(grad_query, both)
            key_sum[seq] += dot_left(grad_logits, queries)
            value_sum[seq] += dot_left(weights, grad)

    gather.run(consume)

    def prepare(pair):
        both = pl.ds(2 * pair, 2)
        at = pl.ds(pl.multiple_of(pair * 2 * rows, 2 * rows), 2 * rows)
        for seq in range(2):
            here = pl.ds(seq * rows, rows)
            grad_qkv[both, here, width : 2 * width] = turn_back(key_sum[seq, at] * scale, both)
            grad_qkv[both, here, 2 * width :] = value_sum[seq, at].astype(LOW).reshape(2, rows, width)

    scatter = Scatter(me, scratch)

    def produce(first, columns):
        return dot_right(own_last(me, grad_qkv, first), qkv_w[columns, :])

    every = 16 * tokens
    for copy in near_copies[6:] + [bring]:
        copy.wait()

    def qkv_part(number, part=model // 8):
        at = slice(number * part, (number + 1) * part)
        left = units_here[:, :, at].reshape(every, part)
        qkv_grad[at, :] = dot_left(left, grad_qkv[...].reshape(every, 3 * width)).astype(LOW)

    def out_part(number, part=model // 4):
        at = slice(number * part, (number + 1) * part)
        left = attended[...].reshape(every, width)
        out_grad[:, at] = dot_left(left, branches[:, :, at].reshape(every, part)).astype(LOW)

    fillers = [functools.partial(out_part, n) for n in range(4)]
    fillers += [functools.partial(qkv_part, n) for n in range(8)]
    scatter.run(prepare, produce, write_total(total_out), fillers)

    for seq in range(2):
        for part in range(2):
            at = slice(part * rows // 2, (part + 1) * rows // 2)
            here = slice(seq * rows + at.start, seq * rows + at.stop)
            values = token[here, :].astype(F32)
            back = norm_back(values, scale_of(values), total_out[here, :])
            in_grad[at, seq, :] = grad_state[here, :] + back
    scatter.drain()
    gather.finish()
    for copy in swaps:
        copy.wait()


def attend_back(
    shift, valid, branch, units, query, key, value, out_w, qkv_w, attended, cosine, sine, gate_up, token, grad_state
):
    tokens, model = branch.shape
    rows, width = query.shape[2:]
    near = (query, key, value, out_w, cosine, sine, qkv_w, attended, token, grad_state)
    return pl.pallas_call(
        functools.partial(attend_back_kernel, shift),
        out_shape=[
            jax.ShapeDtypeStruct((rows, 2, model), F32),
            jax.ShapeDtypeStruct((model, 3 * width), LOW),
            jax.ShapeDtypeStruct((width, model), LOW),
            jax.ShapeDtypeStruct(gate_up.shape[1:], LOW),
        ],
        in_specs=[IN_SMEM] + [ANYWHERE] * 13,
        out_specs=[IN_VMEM] * 3 + [ANYWHERE],
        scratch_shapes=[pltpu.VMEM((2, 16 * rows, width), F32)] * 2
        + [
            pltpu.VMEM((16, tokens, model), LOW),
            pltpu.VMEM((16, tokens, 3 * width), LOW),
            pltpu.VMEM((16, tokens, model), LOW),
            pltpu.VMEM((tokens, model), F32),
        ]
        + [DMA((10,))]
        + [pltpu.VMEM(array.shape, array.dtype) for array in near]
        + Scatter.scratch(tokens, model)
        + Gather.sems(3)
        + [DMA((4,)), DMA((2,))],
        compiler_params=params(4),
    )(valid, branch, units, gate_up, *near)


def return_kernel(
    hidden_far, down_far, qkv_far, gate_up_far, gate_up_other, out_far, hidden_own_far, grads_far,
    total_out, qkv_back, gate_up_back, out_back, down_grad, down_other, *scratch
):
    (qx, qsum, qxs, qxr, qs, qr, psum, ps, pr, oland, os, orecv, hidden, down_w, px, sums, qkv, out_pair, hidden_own, grads, local, across) = scratch[
        Scatter.count :
    ]
    me = Place()
    ready = greet_plane(me)
    bring = [
        pltpu.make_async_copy(hidden_far, hidden, local.at[0]),
        pltpu.make_async_copy(down_far, down_w, local.at[1]),
        pltpu.make_async_copy(gate_up_far.at[me.s], psum, local.at[2]),
        pltpu.make_async_copy(gate_up_other, px, local.at[3]),
        pltpu.make_async_copy(qkv_far, qkv, local.at[4]),
        pltpu.make_async_copy(out_far, out_pair, local.at[5]),
        pltpu.make_async_copy(hidden_own_far, hidden_own, local.at[6]),
        pltpu.make_async_copy(grads_far, grads, local.at[7]),
    ]
    for copy in bring:
        copy.start()
    over = (1 - me.s, me.c)

    def cross(place):
        return remote(qkv.at[1 - me.s, place], qx.at[place], qxs.at[place], qxr.at[place], over)

    def send(sums, back, s_sem, r_sem, step):
        to, _ = turn(me, step)
        return remote(sums.at[to], back.at[me.c], s_sem.at[step], r_sem.at[me.c], (me.s, to))

    holder = me.at(me.z, me.y, me.s)

    def out_send(target_core, same):
        target = (me.s if same else 1 - me.s, me.at(me.z, me.y, target_core))
        slot = 0 if same else 1
        return remote(out_pair.at[target_core], oland.at[me.s], os.at[slot], orecv.at[me.s], target)

    inside = me.k == me.s

    def met():
        ready()
        for step in range(1, 16):
            send(psum, gate_up_back, ps, pr, step).start()
        for copy in bring[4:]:
            copy.wait()
        for step in range(1, 16):
            cross(turn(me, step)[0]).start()
        cross(me.c).start()

        @pl.when(inside)
        def _():
            out_send(1 - me.k, True).start()

        @pl.when(jnp.logical_not(inside))
        def _():
            out_send(me.k, False).start()
            remote(
                out_pair.at[1 - me.k], oland.at[me.s], os.at[0], orecv.at[me.s],
                (1 - me.s, me.at(me.z, me.y, 1 - me.k)),
            ).start()

    def between():
        for step in range(1, 16):
            to, _ = turn(me, step)
            cross(to).wait_recv()
            qsum[to] = (qkv[me.s, to].astype(F32) + qx[to].astype(F32)).astype(LOW)
            send(qsum, qkv_back, qs, qr, step).start()
        cross(me.c).wait_recv()
        qkv_back[me.c] = (qkv[me.s, me.c].astype(F32) + qx[me.c].astype(F32)).astype(LOW)

    scatter = Scatter(me, scratch)

    def produce(first, columns):
        return jnp.dot(own_last(me, hidden, first), down_w[:, columns], preferred_element_type=F32)

    for copy in bring[:4]:
        copy.wait()

    @pl.loop(0, 16)
    def _(place):
        psum[place] = (psum[place].astype(F32) + px[place].astype(F32)).astype(LOW)

    gate_up_back[me.c] = psum[me.c]
    down_swap = remote(down_grad.at[1 - me.s], down_other, across.at[0], across.at[1], over)
    parts, double, part = down_other.shape
    every = hidden.shape[0] * hidden.shape[1]

    def down_part(half, number):
        seq = 1 - me.s if half == 0 else me.s
        thin = double // 2
        start = pl.multiple_of((seq * parts + number) * thin, thin)
        left = hidden[:, :, pl.ds(start, thin)].reshape(every, thin)
        for side in range(2):
            right = grads[:, :, side * part : (side + 1) * part].reshape(every, part)
            down_grad[seq, number, pl.ds(side * thin, thin)] = dot_left(left, right).astype(LOW)
        if half == 0 and number == parts - 1:
            down_swap.start()

    fillers = [between] + [functools.partial(down_part, half, n) for half in range(2) for n in range(parts)]
    scatter.run(None, produce, write_total(sums), fillers, met)
    down_swap.wait()

    rows = total_out.shape[0]
    for seq in range(2):
        here = slice(seq * rows, (seq + 1) * rows)
        total_out[:, seq, :] = (sums[here, :] + hidden_own[here, :]).astype(LOW)
    scatter.drain()
    for step in range(1, 16):
        to, source = turn(me, step)
        for sums, back, s_sem, r_sem in ((qsum, qkv_back, qs, qr), (psum, gate_up_back, ps, pr)):
            remote(sums.at[0], back.at[source], s_sem.at[step], r_sem.at[source], over).wait_recv()
            send(sums, back, s_sem, r_sem, step).wait_send()
        cross(to).wait_send()
    cross(me.c).wait_send()

    @pl.when(inside)
    def _():
        out_send(1 - me.k, True).wait_send()
        remote(out_pair.at[0], oland.at[1 - me.s], os.at[0], orecv.at[1 - me.s], over).wait_recv()
        out_back[...] = out_pair[me.k].astype(F32) + oland[1 - me.s].astype(F32)

    @pl.when(jnp.logical_not(inside))
    def _():
        out_send(me.k, False).wait_send()
        out_send(1 - me.k, True).wait_send()
        for half in range(2):
            remote(out_pair.at[0], oland.at[half], os.at[0], orecv.at[half], over).wait_recv()
        out_back[...] = oland[0].astype(F32) + oland[1].astype(F32)


def give_back(hidden, down_w, qkv, gate_up, gate_up_other, out_pair, hidden_own, grads):
    tokens, model = hidden.shape[1], down_w.shape[1]
    down_half = (2, hidden.shape[2] // 2, model // 2)
    block = lambda array: pltpu.VMEM(array.shape[1:], LOW)
    return pl.pallas_call(
        return_kernel,
        out_shape=[
            jax.ShapeDtypeStruct((tokens // 2, 2, model), LOW),
            jax.ShapeDtypeStruct(qkv.shape[1:], LOW),
            jax.ShapeDtypeStruct(gate_up.shape[1:], LOW),
            jax.ShapeDtypeStruct(out_pair.shape[1:], F32),
            jax.ShapeDtypeStruct((2,) + down_half, LOW),
            jax.ShapeDtypeStruct(down_half, LOW),
        ],
        in_specs=[ANYWHERE] * 8,
        out_specs=[IN_VMEM] * 6,
        scratch_shapes=Scatter.scratch(tokens, model)
        + [block(qkv), block(qkv)]
        + [DMA((16,))] * 4
        + [block(gate_up)]
        + [DMA((16,))] * 2
        + [pltpu.VMEM(out_pair.shape, LOW), DMA((2,)), DMA((2,))]
        + [pltpu.VMEM(hidden.shape, LOW), pltpu.VMEM(down_w.shape, LOW), block(gate_up)]
        + [pltpu.VMEM((tokens, model), F32), pltpu.VMEM(qkv.shape, LOW), pltpu.VMEM(out_pair.shape, LOW)]
        + [pltpu.VMEM((tokens, model), F32), pltpu.VMEM(grads.shape, LOW), DMA((8,)), DMA((2,))],
        compiler_params=params(5),
    )(hidden, down_w, qkv, gate_up, gate_up_other, out_pair, hidden_own, grads)


def assemble_kernel(
    gain_one, gain_two, qkv_far, w_query_far, w_key_far, w_value_far, gate_up_far, w_gate_far, w_up_far,
    down_far, down_other_far,
    query_grad, key_grad, value_grad, gate_grad, up_grad, down_grad, gain_one_grad, gain_two_grad, *near
):
    qkv_back, w_query, w_key, w_value, gate_up_back, w_gate, w_up, down_own, down_other, sems = near
    far = (qkv_far, w_query_far, w_key_far, w_value_far, gate_up_far, w_gate_far, w_up_far)
    far += (down_far.at[lax.axis_index("seq")], down_other_far)
    copies = [pltpu.make_async_copy(a, b, sems.at[n]) for n, (a, b) in enumerate(zip(far, near))]
    for copy in copies:
        copy.start()

    def lanes(total):
        return jnp.sum(jnp.transpose(total), axis=0, keepdims=True)

    width = qkv_back.shape[2] // 3
    rows = qkv_back.shape[1]
    one = down_rows(gain_one, width)
    total = jnp.zeros((rows, width), F32)
    for copy in copies[:4]:
        copy.wait()
    for place in range(16):
        at = slice((place // 2 + 8 * (place % 2)) * width, (place // 2 + 8 * (place % 2) + 1) * width)
        for index, (weight, target) in enumerate(
            ((w_query, query_grad), (w_key, key_grad), (w_value, value_grad))
        ):
            block = qkv_back[place, :, index * width : (index + 1) * width].astype(F32)
            target[:, at] = block * one
            total += block * weight[:, at].astype(F32)
    gain_one_grad[...] = lanes(total)
    width = gate_up_back.shape[2] // 4
    two = down_rows(gain_two, width)
    total = jnp.zeros((rows, width), F32)
    for copy in copies[4:7]:
        copy.wait()
    for place in range(16):
        for half in range(2):
            at = slice((half * 16 + place) * width, (half * 16 + place + 1) * width)
            for index, (weight, target) in enumerate(((w_gate, gate_grad), (w_up, up_grad))):
                start = (2 * index + half) * width
                block = gate_up_back[place, :, start : start + width].astype(F32)
                target[:, at] = block * two
                total += block * weight[:, at].astype(F32)
    gain_two_grad[...] = lanes(total)
    for copy in copies[7:]:
        copy.wait()
    parts, double, part = down_own.shape
    depth = double // 2
    for number in range(parts):
        for half in range(2):
            at = slice(half * depth, (half + 1) * depth)
            down_grad[number * depth : (number + 1) * depth, half * part : (half + 1) * part] = (
                down_own[number, at].astype(F32) + down_other[number, at].astype(F32)
            )


def assemble(gain_one, gain_two, qkv_back, w_query, w_key, w_value, gate_up_back, w_gate, w_up, down, down_other):
    rows, model = w_query.shape
    narrow = jax.ShapeDtypeStruct((rows, model), F32)
    wide = jax.ShapeDtypeStruct(w_gate.shape, F32)
    gain = jax.ShapeDtypeStruct((1, rows), F32)
    parts, double, part = down_other.shape
    near = (qkv_back, w_query, w_key, w_value, gate_up_back, w_gate, w_up, down_other, down_other)
    return pl.pallas_call(
        assemble_kernel,
        out_shape=[narrow] * 3
        + [wide] * 2
        + [jax.ShapeDtypeStruct((parts * double // 2, 2 * part), F32)]
        + [gain] * 2,
        in_specs=[IN_VMEM] * 2 + [ANYWHERE] * 9,
        out_specs=[IN_VMEM] * 8,
        scratch_shapes=[pltpu.VMEM(array.shape, LOW) for array in near] + [DMA((9,))],
        compiler_params=pltpu.CompilerParams(vmem_limit_bytes=60 << 20),
    )(gain_one, gain_two, qkv_back, w_query, w_key, w_value, gate_up_back, w_gate, w_up, down, down_other)


def move_tokens_step(
    layer_in,
    valid_len,
    norm1_gain,
    w_query,
    w_key,
    w_value,
    w_out,
    norm2_gain,
    w_gate,
    w_up,
    w_down,
    cotangent,
):
    local_rows, _, model = layer_in.shape
    width = model // HEADS
    cp_devices = 16
    shift = math.log(cp_devices * local_rows)
    weight_rows = w_gate.shape[0]
    gain_one, gain_two = norm1_gain[None], norm2_gain[None]

    token_rows, units, grads, query, key, value, cosine, back_sine, qkv_w, gate_up_own, head_out, down_other = spread(
        layer_in, cotangent, w_query, w_key, w_value, w_gate, w_up,
        gain_one, gain_two, w_out, w_down,
    )
    qkv_w = qkv_w.reshape(model, 3 * width)
    head_out = head_out.reshape(width, model)
    grad_state, branch, hidden_state, attended, hidden, down_full, gate_up_grad = forward(
        shift, valid_len, query, key, value, head_out, token_rows, grads, gate_up_own, w_down, down_other
    )
    gate_up_grad = gate_up_grad.reshape(2, cp_devices, weight_rows, -1)
    in_grad, qkv_grad, out_grad, gate_up_grad_other = attend_back(
        shift, valid_len, branch, units, query, key, value, head_out, qkv_w, attended,
        cosine, back_sine, gate_up_grad, token_rows, grad_state,
    )
    layer_out, qkv_back, gate_up_back, out_back, down_grad, down_grad_other = give_back(
        hidden,
        down_full.reshape(-1, model),
        qkv_grad.reshape(2, cp_devices, weight_rows, -1),
        gate_up_grad,
        gate_up_grad_other,
        out_grad.reshape(2, width // 2, model),
        hidden_state,
        grads,
    )
    query_grad, key_grad, value_grad, gate_grad, up_grad, down_back, gain_one_grad, gain_two_grad = assemble(
        gain_one, gain_two, qkv_back, w_query, w_key, w_value, gate_up_back, w_gate, w_up, down_grad, down_grad_other
    )
    return (
        layer_out,
        in_grad,
        gain_one_grad[0],
        query_grad,
        key_grad,
        value_grad,
        out_back,
        gain_two_grad[0],
        gate_grad,
        up_grad,
        down_back,
    )


def solution(mesh):
    fits = mesh.shape["cp"] == HEADS and mesh.shape["seq"] == 2
    on_device = move_tokens_step if fits else gather_weights_step
    placed = (
        P("cp", "seq", None),
        P("seq"),
        P(("seq", "cp")),
        P(("seq", "cp"), None),
        P(("seq", "cp"), None),
        P(("seq", "cp"), None),
        P(("seq", "cp"), None),
        P(("seq", "cp")),
        P(("seq", "cp"), None),
        P(("seq", "cp"), None),
        P(("seq", "cp"), None),
        P("cp", "seq", None),
    )
    return jax.shard_map(
        on_device,
        mesh=mesh,
        in_specs=placed,
        out_specs=(
            P("cp", "seq", None),
            P("cp", "seq", None),
            P(("seq", "cp")),
            P(("seq", "cp"), None),
            P(("seq", "cp"), None),
            P(("seq", "cp"), None),
            P(("seq", "cp"), None),
            P(("seq", "cp")),
            P(("seq", "cp"), None),
            P(("seq", "cp"), None),
            P(("seq", "cp"), None),
        ),
        check_vma=False,
    )
```

```python
import functools
import math

import jax
import jax.numpy as jnp
from jax import lax
from jax.experimental import pallas as pl
from jax.experimental.pallas import tpu as pltpu
from jax.sharding import PartitionSpec as P

HEADS = 16


norm_eps = 1e-05
rope_base = 10000.0


def row_positions(indices, strip_rows, devices):
    owner_index = indices // (2 * strip_rows)
    within = indices % (2 * strip_rows)
    return jnp.where(
        within < strip_rows,
        owner_index * strip_rows + within,
        (2 * devices - 1 - owner_index) * strip_rows + within - strip_rows,
    )


def rotate(values, positions, num_heads):
    count_rows, model_width = values.shape
    head_width = model_width // num_heads
    half_width = head_width // 2
    freqs_table = rope_base ** (-2.0 * jnp.arange(half_width, dtype=jnp.float32) / head_width)
    angles = positions.astype(jnp.float32)[:, None] * freqs_table[None, :]
    cosine = jnp.cos(angles)[:, None, :]
    sine_table = jnp.sin(angles)[:, None, :]
    split_heads = values.reshape(count_rows, num_heads, head_width)
    former = split_heads[:, :, :half_width]
    latter = split_heads[:, :, half_width:]
    turned = jnp.concatenate(
        [former * cosine - latter * sine_table, latter * cosine + former * sine_table], axis=2
    )
    return turned.reshape(count_rows, model_width)


def norm_scale(values):
    return values * lax.rsqrt(jnp.mean(values * values, axis=-1, keepdims=True) + norm_eps)


def normed(values, gain_vector):
    return norm_scale(values) * gain_vector


def swiglu(gate_rows, up_rows):
    return jax.nn.silu(gate_rows) * up_rows


def dot_right(left, right):
    return lax.dot_general(
        left, right, (((1,), (1,)), ((), ())), preferred_element_type=jnp.float32
    )


def dot_left(left, right):
    return lax.dot_general(
        left, right, (((0,), (0,)), ((), ())), preferred_element_type=jnp.float32
    )


def split_blocks(array, block_rows):
    return array.reshape((array.shape[0] // block_rows, block_rows) + array.shape[1:])


def key_mask(query_pos, key_pos, valid_count):
    causal = key_pos[None, :] <= query_pos[:, None]
    live_keys = key_pos[None, :] < valid_count[:, None]
    return (causal[None, None, :, :] & live_keys[:, None, None, :]).astype(jnp.float32)


def scores_of(queries, key_rows, query_pos, key_pos, valid_count, score_shift):
    head_width = queries.shape[3]
    raw_scores = jnp.einsum(
        "qshd,kshd->shqk", queries, key_rows, preferred_element_type=jnp.float32
    )
    return (
        raw_scores * head_width ** (-0.5) - score_shift,
        key_mask(query_pos, key_pos, valid_count),
    )


def block_grads(queries, grad_rows, key_rows, values, query_pos, key_pos, valid_count, score_shift):
    logits, mask_table = scores_of(queries, key_rows, query_pos, key_pos, valid_count, score_shift)
    sigmoid_table = jax.nn.sigmoid(logits)
    weights_low = (sigmoid_table * mask_table).astype(jnp.bfloat16)
    grad_weights = jnp.einsum(
        "qshd,kshd->shqk", grad_rows, values, preferred_element_type=jnp.float32
    )
    grad_logits = (grad_weights * mask_table * (sigmoid_table * (1.0 - sigmoid_table))).astype(
        jnp.bfloat16
    )
    return (weights_low, grad_logits)


def make_norm_fold(normalized, pieces):
    gain_part = pieces[0].astype(jnp.float32)
    scaled = (normalized * gain_part).astype(jnp.bfloat16)
    totals = tuple(
        (
            jnp.dot(scaled, weight_piece, preferred_element_type=jnp.float32)
            for weight_piece in pieces[1:]
        )
    )
    return (gain_part,) + totals


def make_row_fold(left_rows, weight_piece):
    return jnp.dot(left_rows, weight_piece, preferred_element_type=jnp.float32)


def gather_weights_step(
    layer_in,
    valid_len,
    norm1_gain,
    w_query,
    w_key,
    w_value,
    w_out,
    norm2_gain,
    w_gate,
    w_up,
    w_down,
    cotangent,
):
    local_rows, local_seqs, model_width = layer_in.shape
    num_heads = HEADS
    head_width = model_width // num_heads
    strip_rows = local_rows // 2
    cp_devices = lax.axis_size("cp")
    cp_place = lax.axis_index("cp")
    seq_length = local_rows * cp_devices
    score_shift = math.log(seq_length)
    score_scale = head_width ** (-0.5)
    token_count = local_rows * local_seqs
    local_pos = row_positions(
        cp_place * local_rows + jnp.arange(local_rows, dtype=jnp.int32), strip_rows, cp_devices
    )
    token_pos = jnp.broadcast_to(local_pos[:, None], (local_rows, local_seqs)).reshape(token_count)
    every_pos = row_positions(jnp.arange(seq_length, dtype=jnp.int32), strip_rows, cp_devices)
    block_rows = math.gcd(seq_length, 512)
    head_shape = (local_rows, local_seqs, num_heads, head_width)
    row_shape = (local_rows, local_seqs, model_width)
    zero_heads = jnp.zeros(head_shape, jnp.float32)
    inputs = layer_in.reshape(token_count, model_width).astype(jnp.float32)
    input_norm = norm_scale(inputs)
    gain_one, query, key_proj, value = make_norm_fold(
        input_norm,
        (
            lax.all_gather(norm1_gain, ("seq", "cp"), axis=0, tiled=True),
            lax.all_gather(w_query, ("seq", "cp"), axis=0, tiled=True),
            lax.all_gather(w_key, ("seq", "cp"), axis=0, tiled=True),
            lax.all_gather(w_value, ("seq", "cp"), axis=0, tiled=True),
        ),
    )
    normed_one = (input_norm * gain_one).astype(jnp.bfloat16)
    query_low = rotate(query, token_pos, num_heads).astype(jnp.bfloat16)
    key_low = rotate(key_proj, token_pos, num_heads).astype(jnp.bfloat16)
    value_low = value.astype(jnp.bfloat16)
    query_heads = query_low.reshape(head_shape)
    key_local = key_low.reshape(row_shape)
    value_local = value_low.reshape(row_shape)
    key_piece = lax.all_gather(key_local, "cp", axis=0, tiled=True)
    value_piece = lax.all_gather(value_local, "cp", axis=0, tiled=True)
    piece_rows = key_piece.shape[0]
    piece_block = math.gcd(piece_rows, 512)
    piece_pos = row_positions(jnp.arange(piece_rows, dtype=jnp.int32), strip_rows, cp_devices)

    def scan_step(partial_sum, block_items):
        key_block, value_block, block_pos = block_items
        logits, mask_table = scores_of(
            query_heads,
            key_block.reshape(piece_block, local_seqs, num_heads, head_width),
            local_pos,
            block_pos,
            valid_len,
            score_shift,
        )
        weights_low = (jax.nn.sigmoid(logits) * mask_table).astype(jnp.bfloat16)
        added = jnp.einsum(
            "shqk,kshd->qshd",
            weights_low,
            value_block.reshape(piece_block, local_seqs, num_heads, head_width),
            preferred_element_type=jnp.float32,
        )
        return (partial_sum + added, None)

    result, _ = lax.scan(
        scan_step,
        zero_heads,
        (
            split_blocks(key_piece, piece_block),
            split_blocks(value_piece, piece_block),
            split_blocks(piece_pos, piece_block),
        ),
    )
    attended_low = result.reshape(token_count, model_width).astype(jnp.bfloat16)
    attn_branch = make_row_fold(
        attended_low, lax.all_gather(w_out, ("seq", "cp"), axis=0, tiled=True)
    )
    hidden_state = inputs + attn_branch
    hidden_norm = norm_scale(hidden_state)
    gain_two, gate_rows, up_rows = make_norm_fold(
        hidden_norm,
        (
            lax.all_gather(norm2_gain, ("seq", "cp"), axis=0, tiled=True),
            lax.all_gather(w_gate, ("seq", "cp"), axis=0, tiled=True),
            lax.all_gather(w_up, ("seq", "cp"), axis=0, tiled=True),
        ),
    )
    normed_two = (hidden_norm * gain_two).astype(jnp.bfloat16)
    hidden_units = swiglu(gate_rows, up_rows).astype(jnp.bfloat16)
    ff_branch = make_row_fold(
        hidden_units, lax.all_gather(w_down, ("seq", "cp"), axis=0, tiled=True)
    )
    layer_out = (hidden_state + ff_branch).astype(jnp.bfloat16).reshape(row_shape)
    grad_out = cotangent.reshape(token_count, model_width)
    gate_all, up_all, down_all = (
        lax.all_gather(w_gate, ("seq", "cp"), axis=0, tiled=True),
        lax.all_gather(w_up, ("seq", "cp"), axis=0, tiled=True),
        lax.all_gather(w_down, ("seq", "cp"), axis=0, tiled=True),
    )
    grad_hidden = dot_right(grad_out, down_all)
    _, pull_swiglu = jax.vjp(swiglu, gate_rows, up_rows)
    grad_gate, grad_up = pull_swiglu(grad_hidden)
    grad_gate_low = grad_gate.astype(jnp.bfloat16)
    grad_up_low = grad_up.astype(jnp.bfloat16)
    grad_norm_two = dot_right(grad_gate_low, gate_all) + dot_right(grad_up_low, up_all)
    _, pull_two = jax.vjp(normed, hidden_state, gain_two)
    grad_from_two, gain_two_term = pull_two(grad_norm_two)
    ff_grads = (
        lax.psum_scatter(gain_two_term, ("seq", "cp"), scatter_dimension=0, tiled=True),
        lax.psum_scatter(
            dot_left(normed_two, grad_gate_low), ("seq", "cp"), scatter_dimension=0, tiled=True
        ),
        lax.psum_scatter(
            dot_left(normed_two, grad_up_low), ("seq", "cp"), scatter_dimension=0, tiled=True
        ),
        lax.psum_scatter(
            dot_left(hidden_units, grad_out), ("seq", "cp"), scatter_dimension=0, tiled=True
        ),
    )
    grad_state = grad_out.astype(jnp.float32) + grad_from_two
    query_all, key_all, value_all, out_all = (
        lax.all_gather(w_query, ("seq", "cp"), axis=0, tiled=True),
        lax.all_gather(w_key, ("seq", "cp"), axis=0, tiled=True),
        lax.all_gather(w_value, ("seq", "cp"), axis=0, tiled=True),
        lax.all_gather(w_out, ("seq", "cp"), axis=0, tiled=True),
    )
    grad_branch_low = grad_state.astype(jnp.bfloat16)
    grad_attended_low = dot_right(grad_branch_low, out_all).astype(jnp.bfloat16)
    grad_heads = grad_attended_low.reshape(head_shape)
    key_heads_local = key_local.reshape(head_shape)
    value_heads_local = value_local.reshape(head_shape)
    keys_every, values_every, queries_every, grads_every = (
        lax.all_gather(key_local, "cp", axis=0, tiled=True),
        lax.all_gather(value_local, "cp", axis=0, tiled=True),
        lax.all_gather(query_low.reshape(row_shape), "cp", axis=0, tiled=True),
        lax.all_gather(grad_attended_low.reshape(row_shape), "cp", axis=0, tiled=True),
    )

    def key_step(partial_sums, block_items):
        query_block, grad_block_rows, block_pos = block_items
        query_part = query_block.reshape(block_rows, local_seqs, num_heads, head_width)
        grad_part = grad_block_rows.reshape(block_rows, local_seqs, num_heads, head_width)
        weights_low, grad_logits = block_grads(
            query_part,
            grad_part,
            key_heads_local,
            value_heads_local,
            block_pos,
            local_pos,
            valid_len,
            score_shift,
        )
        key_added = jnp.einsum(
            "shqk,qshd->kshd", grad_logits, query_part, preferred_element_type=jnp.float32
        )
        value_added = jnp.einsum(
            "shqk,qshd->kshd", weights_low, grad_part, preferred_element_type=jnp.float32
        )
        return ((partial_sums[0] + key_added, partial_sums[1] + value_added), None)

    (key_sum, value_sum), _ = lax.scan(
        key_step,
        (zero_heads, zero_heads),
        (
            split_blocks(queries_every, block_rows),
            split_blocks(grads_every, block_rows),
            split_blocks(every_pos, block_rows),
        ),
    )
    grad_key_rot = key_sum.reshape(token_count, model_width) * score_scale
    grad_value_sum = value_sum.reshape(token_count, model_width)

    def query_step(partial_sum, block_items):
        key_block, value_block, block_pos = block_items
        key_heads = key_block.reshape(block_rows, local_seqs, num_heads, head_width)
        _, grad_logits = block_grads(
            query_heads,
            grad_heads,
            key_heads,
            value_block.reshape(block_rows, local_seqs, num_heads, head_width),
            local_pos,
            block_pos,
            valid_len,
            score_shift,
        )
        added = jnp.einsum(
            "shqk,kshd->qshd", grad_logits, key_heads, preferred_element_type=jnp.float32
        )
        return (partial_sum + added, None)

    query_sum, _ = lax.scan(
        query_step,
        zero_heads,
        (
            split_blocks(keys_every, block_rows),
            split_blocks(values_every, block_rows),
            split_blocks(every_pos, block_rows),
        ),
    )
    grad_query_rot = query_sum.reshape(token_count, model_width) * score_scale
    grad_query_low = rotate(grad_query_rot, -token_pos, num_heads).astype(jnp.bfloat16)
    grad_key_low = rotate(grad_key_rot, -token_pos, num_heads).astype(jnp.bfloat16)
    grad_value_low = grad_value_sum.astype(jnp.bfloat16)
    grad_norm_one = (
        dot_right(grad_query_low, query_all)
        + dot_right(grad_key_low, key_all)
        + dot_right(grad_value_low, value_all)
    )
    _, pull_one = jax.vjp(normed, inputs, gain_one)
    grad_from_one, gain_one_term = pull_one(grad_norm_one)
    in_grad = (grad_state + grad_from_one).reshape(row_shape)
    attn_grads = (
        lax.psum_scatter(gain_one_term, ("seq", "cp"), scatter_dimension=0, tiled=True),
        lax.psum_scatter(
            dot_left(normed_one, grad_query_low), ("seq", "cp"), scatter_dimension=0, tiled=True
        ),
        lax.psum_scatter(
            dot_left(normed_one, grad_key_low), ("seq", "cp"), scatter_dimension=0, tiled=True
        ),
        lax.psum_scatter(
            dot_left(normed_one, grad_value_low), ("seq", "cp"), scatter_dimension=0, tiled=True
        ),
        lax.psum_scatter(
            dot_left(attended_low, grad_branch_low), ("seq", "cp"), scatter_dimension=0, tiled=True
        ),
    )
    return (
        layer_out,
        in_grad,
        attn_grads[0],
        attn_grads[1],
        attn_grads[2],
        attn_grads[3],
        attn_grads[4],
        ff_grads[0],
        ff_grads[1],
        ff_grads[2],
        ff_grads[3],
    )


MESH = pl.DeviceIdType.MESH
DMA = pltpu.SemaphoreType.DMA
LOW = jnp.bfloat16
F32 = jnp.float32
ANYWHERE = pl.BlockSpec(memory_space=pl.ANY)
IN_VMEM = pl.BlockSpec(memory_space=pltpu.VMEM)
IN_SMEM = pl.BlockSpec(memory_space=pltpu.SMEM)


class Place:
    def __init__(self):
        self.s = lax.axis_index("seq")
        self.c = lax.axis_index("cp")
        self.z = self.c // 4
        self.y = (self.c // 2) % 2
        self.k = self.c % 2

    def at(self, z, y, k):
        return z * 4 + y * 2 + k

    def device(self, place):
        return (self.s, place)


def pick(z, table):
    value = jnp.int32(table[0])
    for index in range(1, 4):
        value = jnp.where(z == index, jnp.int32(table[index]), value)
    return value


NEAREST = ((1, 0, 1, 2), (2, 2, 3, 1), (3, 3, 0, 0))
FARTHEST = ((3, 3, 0, 0), (2, 2, 3, 1), (1, 0, 1, 2))


def remote(source, target, send, recv, device):
    return pltpu.make_async_remote_copy(
        src_ref=source,
        dst_ref=target,
        send_sem=send,
        recv_sem=recv,
        device_id=device,
        device_id_type=MESH,
    )


def hail(device):
    pl.semaphore_signal(
        pltpu.get_barrier_semaphore(), inc=1, device_id=device, device_id_type=MESH
    )


def greet(me, over_seq=False):
    hail((me.s, me.at(me.z, 1 - me.y, me.k)))
    hail((me.s, me.at(me.z, me.y, 1 - me.k)))

    @pl.when(me.z < 3)
    def _():
        hail((me.s, me.at(me.z + 1, me.y, me.k)))

    @pl.when(me.z > 0)
    def _():
        hail((me.s, me.at(me.z - 1, me.y, me.k)))

    ends = (me.z == 0).astype(jnp.int32) + (me.z == 3).astype(jnp.int32)
    if over_seq:
        hail((1 - me.s, me.c))
    return lambda: pl.semaphore_wait(
        pltpu.get_barrier_semaphore(), 4 - ends + (1 if over_seq else 0)
    )


def greet_plane(me):
    for step in range(1, 16):
        hail((me.s, (me.c + step) % 16))
    hail((1 - me.s, me.c))
    hail((1 - me.s, me.at(me.z, me.y, 1 - me.k)))
    return lambda: pl.semaphore_wait(pltpu.get_barrier_semaphore(), 17)


class Gather:
    def __init__(self, me, views, early, z_sem, far_sem, y_sem, k_sem, recv):
        self.me, self.views, self.early = me, views, early
        self.z_sem, self.far_sem, self.y_sem, self.k_sem, self.recv = z_sem, far_sem, y_sem, k_sem, recv

    count = 5

    @staticmethod
    def sems(pieces):
        return [DMA((pieces * n,)) for n in (5, 5, 4, 8, 16)]

    def copy(self, piece, place, sem, device):
        block = self.views[piece](place)
        return remote(block, block, sem, self.recv.at[piece * 16 + place], device)

    def arrived(self, piece, place):
        self.copy(piece, place, self.k_sem.at[0], self.me.device(self.me.c)).wait_recv()

    def line(self, index):
        return self.me.z if index == 0 else pick(self.me.z, NEAREST[index - 1])

    def along(self, piece, place, index, up, sems):
        me = self.me
        target = jnp.minimum(me.c + 4, 12 + me.c % 4) if up else jnp.maximum(me.c - 4, me.c % 4)
        return self.copy(piece, place, sems.at[piece * 5 + index], me.device(target))

    def across(self, piece, place, index):
        me = self.me
        target = me.at(me.z, 1 - me.y, me.k)
        return self.copy(piece, place, self.y_sem.at[piece * 4 + index], me.device(target))

    def partner(self, piece, place, index):
        me = self.me
        target = me.at(me.z, me.y, 1 - me.k)
        return self.copy(piece, place, self.k_sem.at[piece * 8 + index], me.device(target))

    def spread_along(self, piece, place, index, sems, go):
        me, z = self.me, self.line(index)
        if index == 0:

            @pl.when(me.z < 3)
            def _():
                go(self.along(piece, place, 0, True, sems))

            @pl.when(me.z > 0)
            def _():
                go(self.along(piece, place, 4, False, sems))
        else:

            @pl.when((z < me.z) & (me.z < 3))
            def _():
                go(self.along(piece, place, index, True, sems))

            @pl.when((z > me.z) & (me.z > 0))
            def _():
                go(self.along(piece, place, index, False, sems))

    def send_near(self, piece, index, go=lambda copy: copy.start()):
        me = self.me
        place = me.at(self.line(index), me.y, me.k)
        if index == 0 or not self.early[piece]:
            go(self.across(piece, place, index))
        self.spread_along(piece, place, index, self.z_sem, go)
        go(self.partner(piece, place, index))

    def send_far(self, piece, index, go=lambda copy: copy.start()):
        me = self.me
        place = me.at(self.line(index), 1 - me.y, me.k)
        if self.early[piece]:
            self.spread_along(piece, place, index, self.far_sem, go)
        go(self.partner(piece, place, 4 + index))

    def begin(self):
        for piece in range(len(self.views)):
            self.send_near(piece, 0)

    def round(self, index):
        me = self.me
        for piece in range(len(self.views)):
            if index < 3:
                self.arrived(piece, me.at(self.line(index + 1), me.y, me.k))
                self.send_near(piece, index + 1)
            self.arrived(piece, me.at(self.line(index), 1 - me.y, me.k))
            self.send_far(piece, index)

    def settle(self, z, y):
        for piece in range(len(self.views)):
            self.arrived(piece, self.me.at(z, y, 1 - self.me.k))

    def run(self, consume):
        me = self.me
        self.begin()
        waiting = [(me.z, me.y)]
        for index in range(4):
            self.round(index)
            ready, waiting = waiting, []
            if index < 3:
                waiting.append((self.line(index + 1), me.y))
            waiting.append((self.line(index), 1 - me.y))
            for z, y in ready:
                self.settle(z, y)
                consume(z * 2 + y)
        for z, y in waiting:
            self.settle(z, y)
            consume(z * 2 + y)

    def finish(self):
        for piece in range(len(self.views)):
            for index in range(4):
                self.send_near(piece, index, lambda copy: copy.wait_send())
                self.send_far(piece, index, lambda copy: copy.wait_send())


class Scatter:
    pieces = 2

    def __init__(self, me, scratch):
        self.me = me
        (self.k_out, self.k_in, self.y_out, self.y_in, self.z_out, self.z_in, self.mine, self.kept) = scratch[:8]
        (self.ks, self.kr, self.ys, self.yr, self.zs, self.zl, self.zr) = scratch[8:15]

    count = 15

    @classmethod
    def scratch(cls, rows, width):
        n = cls.pieces
        part = width // n
        low = [pltpu.VMEM((n * count, rows, part), LOW) for count in (8, 8, 4, 4, 3, 5)]
        full = [pltpu.VMEM((n * count, rows, part), F32) for count in (1, 4)]
        return low + full + [DMA((n * count,)) for count in (8, 8, 4, 4, 3, 4, 4)]

    def partner(self, slot):
        me = self.me
        target = me.device(me.at(me.z, me.y, 1 - me.k))
        return remote(self.k_out.at[slot], self.k_in.at[slot], self.ks.at[slot], self.kr.at[slot], target)

    def across(self, z, index, piece):
        me, n = self.me, self.pieces
        out, land = index * n + piece, z * n + piece
        target = me.device(me.at(me.z, 1 - me.y, me.k))
        return remote(self.y_out.at[out], self.y_in.at[land], self.ys.at[out], self.yr.at[land], target)

    def along(self, z, index, piece, up):
        me, n = self.me, self.pieces
        out, land = index * n + piece, z * n + piece
        target = jnp.minimum(me.c + 4, 12 + me.c % 4) if up else jnp.maximum(me.c - 4, me.c % 4)
        into = self.z_in.at[land if up else jnp.where(z == me.z - 1, 4, z) * n + piece]
        sem = (self.zl if up else self.zr).at[land]
        return remote(self.z_out.at[out], into, self.zs.at[out], sem, me.device(target))

    def line(self, index):
        return self.me.z if index == 3 else pick(self.me.z, FARTHEST[index])

    def emit(self, produce, z, y, piece, slot, keep):
        part = 512
        rows, width = keep.shape

        @pl.loop(0, width // part)
        def _(index):
            here = pl.ds(pl.multiple_of(index * part, part), part)
            start = pl.multiple_of(piece * width + index * part, part)
            value = produce(self.me.at(z, y, 0), pl.ds(start, part))
            self.k_out[slot, :, here] = value[:rows].astype(LOW)
            keep[:, here] = value[rows:]

    def add(self, target, base, *blocks):
        part = 512

        @pl.loop(0, target.shape[-1] // part)
        def _(index):
            here = pl.ds(pl.multiple_of(index * part, part), part)
            value = base[:, here]
            for block in blocks:
                value = value + block[:, here].astype(F32)
            target[:, here] = value.astype(target.dtype)

    def run(self, prepare, produce, finish, fillers=(), ready=lambda: None, after=lambda: None):
        me, n = self.me, self.pieces
        fillers = list(fillers)
        steps = [(index, piece) for index in range(4) for piece in range(n)]
        for number in range(len(steps) + 1):
            if number < len(steps):
                index, piece = steps[number]
                z = self.line(index)
                if prepare is not None and piece == 0:
                    prepare(z * 2 + 1 - me.y)
                self.emit(produce, z, 1 - me.y, piece, number, self.mine.at[number % 2])
                if number == 0:
                    ready()
                self.partner(number).start()
            if number > 0:
                index, piece = steps[number - 1]
                self.partner(number - 1).wait_recv()
                self.add(self.y_out.at[number - 1], self.mine.at[(number - 1) % 2], self.k_in.at[number - 1])
                self.across(self.line(index), index, piece).start()

        after()

        def own(number):
            index, piece = steps[number]
            z = self.line(index)
            if prepare is not None and piece == 0:
                prepare(z * 2 + me.y)
            self.emit(produce, z, me.y, piece, 4 * n + number, self.kept.at[number])
            self.partner(4 * n + number).start()

        ahead = n
        for number in range(ahead):
            own(number)
        for number in range(len(steps)):
            if number + ahead < len(steps):
                own(number + ahead)
            if prepare is None or number + ahead >= len(steps) - n:
                for _ in range(-(-len(fillers) // (len(steps) - number))):
                    fillers.pop(0)()
            self.collect(number, *steps[number], finish)

    def collect(self, number, index, piece, finish):
        me, n = self.me, self.pieces
        z = self.line(index)
        slot, land = 4 * n + number, z * n + piece
        kept = self.kept.at[number]
        self.partner(slot).wait_recv()
        self.across(z, index, piece).wait_recv()
        self.add(kept, kept, self.k_in.at[slot], self.y_in.at[land])
        if index < 3:
            from_below, from_above = (z > me.z) & (me.z > 0), (z < me.z) & (me.z < 3)
        else:
            from_below, from_above = me.z > 0, me.z < 3

        @pl.when(from_below)
        def _():
            self.along(z, 0, piece, True).wait_recv()
            self.add(kept, kept, self.z_in.at[land])

        @pl.when(from_above)
        def _():
            self.along(z, 0, piece, False).wait_recv()
            self.add(kept, kept, self.z_in.at[4 * n + piece if index == 3 else land])

        if index < 3:
            self.add(self.z_out.at[number], kept)

            @pl.when(z > me.z)
            def _():
                self.along(z, index, piece, True).start()

            @pl.when(z < me.z)
            def _():
                self.along(z, index, piece, False).start()
        else:
            finish(piece, kept)

    def drain(self):
        me, n = self.me, self.pieces
        for slot in range(8 * n):
            self.partner(slot).wait_send()
        for index in range(4):
            z = self.line(index)
            for piece in range(n):
                self.across(z, index, piece).wait_send()
                if index < 3:

                    @pl.when(z > me.z)
                    def _():
                        self.along(z, index, piece, True).wait_send()

                    @pl.when(z < me.z)
                    def _():
                        self.along(z, index, piece, False).wait_send()


def write_total(total_out):
    def finish(piece, kept):
        width = kept.shape[-1]
        total_out[:, piece * width : (piece + 1) * width] = kept[...]

    return finish


def leave(stage, parts, sems):
    copies = []

    def run(number, work, place):
        if number >= 2:
            copies[number - 2].wait()
        slot = stage.at[number % 2]
        work(slot)
        copies.append(pltpu.make_async_copy(slot, place, sems.at[number]))
        copies[number].start()

    def end():
        for copy in copies[-2:]:
            copy.wait()

    return [functools.partial(run, number, *part) for number, part in enumerate(parts)], end


def own_last(me, block, first):
    return jnp.concatenate([block[first + 1 - me.k], block[first + me.k]], axis=0)


def params(collective_id):
    return pltpu.CompilerParams(
        collective_id=collective_id, has_side_effects=True, vmem_limit_bytes=60 << 20
    )


def turn(me, step):
    dz, dy, dk = step // 4, (step // 2) % 2, step % 2
    to = me.at((me.z + dz) % 4, (me.y + dy) % 2, (me.k + dk) % 2)
    source = me.at((me.z + 4 - dz) % 4, (me.y + dy) % 2, (me.k + dk) % 2)
    return to, source


def cuts(rows):
    return ((0, rows // 2), (rows // 2, rows * 7 // 8 - rows // 2), (rows * 7 // 8, rows // 8))


EARLY = [False, False, True]


def pieces_of(array):
    return [
        lambda place, start=start, size=size: array.at[place, pl.ds(start, size)]
        for start, size in cuts(array.shape[1])
    ]


def scale_of(values):
    return lax.rsqrt(jnp.mean(values * values, axis=-1, keepdims=True) + norm_eps)


def norm_back(values, scale, weighted):
    inner = jnp.mean(values * weighted, axis=-1, keepdims=True)
    return scale * weighted - values * (scale * scale * scale * inner)


def by_rows(total, work, rows=32):
    @pl.loop(0, total // rows)
    def _(index):
        work(pl.ds(pl.multiple_of(index * rows, rows), rows))


def down_rows(row, width):
    full = jnp.broadcast_to(row[...].astype(F32), (width, row.shape[1]))
    return jnp.transpose(full)


def spread_kernel(
    token, grad, w_query, w_key, w_value, w_gate, w_up, gain_one, gain_two, out_w, down,
    token_rows, units, grads, query, key, value, cosine, sine, qkv_full, gate_up_half, out_all, down_other, *scratch
):
    gather_sems = scratch[: Gather.count]
    (qs, qr, qxs, qxr, ps, pr, os, ox, orecv, local, dsem, leave, units_here, grads_here, qkv_all, qkv, gate_up) = scratch[Gather.count :]
    me = Place()
    own = [
        pltpu.make_async_copy(qkv.at[me.c], qkv_all.at[me.s, me.c], local.at[2]),
        pltpu.make_async_copy(gate_up.at[me.c], gate_up_half.at[me.c], local.at[3]),
    ]
    ready = greet_plane(me)
    over = (1 - me.s, me.c)
    rows, _, model = token.shape
    tokens = 2 * rows
    for seq in range(2):
        here = slice(seq * rows, (seq + 1) * rows)
        values = token[:, seq, :]
        token_rows[here, :] = values
        values = values.astype(F32)
        units_here[me.c, here] = (values * scale_of(values)).astype(LOW)
        grads_here[me.c, here] = grad[:, seq, :]
    ready()
    gather = Gather(me, pieces_of(units_here) + pieces_of(grads_here), [False] * 3 + EARLY, *gather_sems)
    down_copy = remote(down, down_other, dsem.at[0], dsem.at[1], over)

    def send_qkv(step):
        to, _ = turn(me, step)
        return remote(qkv.at[to], qkv_all.at[me.s, me.c], qs.at[step], qr.at[me.c], (me.s, to))

    def send_gate_up(step):
        to, _ = turn(me, step)
        return remote(gate_up.at[to], gate_up_half.at[me.c], ps.at[step], pr.at[me.c], (me.s, to))

    def forward(source):
        block = qkv_all.at[me.s, source]
        return remote(block, block, qxs.at[source], qxr.at[source], over)

    holder = me.at(me.z, me.y, me.s)
    out_local = pltpu.make_async_copy(out_w, out_all.at[me.k], local.at[4])
    out_near = remote(out_w, out_all.at[me.k], os.at[0], orecv.at[me.k], (me.s, me.at(me.z, me.y, 1 - me.k)))
    out_far = remote(out_w, out_all.at[me.k], ox, orecv.at[me.k], (1 - me.s, holder))

    gather.begin()
    width = query.shape[3]
    weight_rows = w_query.shape[0]
    one = down_rows(gain_one, width)
    for place in range(16):
        head = place // 2 + 8 * (place % 2)
        for index, weight in enumerate((w_query, w_key, w_value)):
            block = weight[:, head * width : (head + 1) * width].astype(F32) * one
            qkv[place, :, index * width : (index + 1) * width] = block.astype(LOW)
    own[0].start()
    for step in range(1, 16):
        send_qkv(step).start()
    units_of = gate_up.shape[2] // 4
    two = down_rows(gain_two, units_of)
    for place in range(16):
        for index, weight in enumerate((w_gate, w_up)):
            for half in range(2):
                start = (half * 16 + place) * units_of
                block = weight[:, start : start + units_of].astype(F32) * two
                start = (2 * index + half) * units_of
                gate_up[place, :, start : start + units_of] = block.astype(LOW)
    own[1].start()
    own[0].wait()
    forward(me.c).start()
    out_far.start()

    @pl.when(holder == me.c)
    def _():
        out_local.start()

    @pl.when(holder != me.c)
    def _():
        out_near.start()

    down_copy.start()
    leaving = []

    half_width = width // 2
    lane = lax.broadcasted_iota(jnp.int32, (rows, width), 1)
    row = lax.broadcasted_iota(jnp.int32, (rows, width), 0)
    freqs = jnp.exp((lane % half_width).astype(F32) * (-2.0 * math.log(rope_base) / width))
    sign = jnp.where(lane < half_width, 1.0, -1.0)

    @pl.loop(0, 16)
    def _(place):
        angles = row_place(place, row, rows // 2).astype(F32) * freqs
        cosine[place] = jnp.cos(angles)
        sine[place] = jnp.sin(angles) * sign

    def write_out(z, y):
        pair = z * 2 + y
        both = pl.ds(2 * pair, 2)
        number = len(leaving)
        for index, (here, there) in enumerate(((units_here, units), (grads_here, grads))):
            copy = pltpu.make_async_copy(here.at[both], there.at[both], leave.at[2 * number + index])
            copy.start()
            leaving.append(copy)

    def turned(values, both):
        swapped = pltpu.roll(values, width // 2, axis=1)
        place_cos = cosine[both].reshape(2 * rows, width)
        place_sin = sine[both].reshape(2 * rows, width)
        return (values * place_cos - swapped * place_sin).astype(LOW).reshape(2, rows, width)

    def project(z, y):
        both = pl.ds(2 * (z * 2 + y), 2)
        weights = qkv_all[...].reshape(model, 3 * width)
        for seq in range(2):
            block = units_here[both, seq * rows : (seq + 1) * rows].reshape(2 * rows, model)
            result = jnp.dot(block, weights, preferred_element_type=F32)
            query[both, seq] = turned(result[:, :width], both)
            key[both, seq] = turned(result[:, width : 2 * width], both)
            value[both, seq] = result[:, 2 * width :].astype(LOW).reshape(2, rows, width)

    steps = list(range(1, 16))
    waiting, ready = [(me.z, me.y)], []
    for index in range(4):
        for step in steps[4 * index : 4 * index + 4]:
            send_gate_up(step).start()
        gather.round(index)
        for z, y in waiting:
            gather.settle(z, y)
            write_out(z, y)
        ready += waiting
        waiting = [(gather.line(index), 1 - me.y)]
        if index < 3:
            waiting.append((gather.line(index + 1), me.y))
        if index == 1:
            for step in steps:
                _, source = turn(me, step)
                remote(qkv.at[0], qkv_all.at[me.s, source], qs.at[step], qr.at[source], over).wait_recv()
                forward(source).start()
        if index == 2:
            for source in range(16):
                forward(source).wait_send()
                forward(source).wait_recv()
            leave_qkv = pltpu.make_async_copy(qkv_all, qkv_full, local.at[5])
            leave_qkv.start()
        if index >= 2:
            for z, y in ready:
                project(z, y)
            ready = []
    for z, y in waiting:
        gather.settle(z, y)
        write_out(z, y)
        project(z, y)
    gather.finish()
    own[1].wait()
    leave_qkv.wait()
    for copy in leaving:
        copy.wait()
    for step in steps:
        _, source = turn(me, step)
        send_qkv(step).wait_send()
        send_gate_up(step).wait_send()
        remote(gate_up.at[0], gate_up_half.at[source], ps.at[step], pr.at[source], over).wait_recv()
    out_far.wait_send()
    down_copy.wait()

    @pl.when(holder == me.c)
    def _():
        out_local.wait()
        remote(out_w, out_all.at[1 - me.k], ox, orecv.at[1 - me.k], over).wait_recv()

    @pl.when(holder != me.c)
    def _():
        out_near.wait_send()
        for half in range(2):
            remote(out_w, out_all.at[half], ox, orecv.at[half], over).wait_recv()


def spread(token, grad, w_query, w_key, w_value, w_gate, w_up, gain_one, gain_two, out_w, down):
    def shape(lead, array):
        return jax.ShapeDtypeStruct(lead + array.shape, array.dtype)

    rows, seqs, model = token.shape
    tokens = rows * seqs
    flat = jax.ShapeDtypeStruct((16, tokens, model), LOW)
    width = model // 16
    weight_rows = w_query.shape[0]
    qkv = (weight_rows, 3 * width)
    gate_up = (weight_rows, 2 * w_gate.shape[1] // 16)
    heads = jax.ShapeDtypeStruct((16, 2, tokens // 2, width), LOW)
    table = jax.ShapeDtypeStruct((16, tokens // 2, width), F32)
    return pl.pallas_call(
        spread_kernel,
        out_shape=[
            jax.ShapeDtypeStruct((tokens, model), LOW),
            flat,
            flat,
            heads,
            heads,
            heads,
            table,
            table,
            jax.ShapeDtypeStruct((2, 16) + qkv, LOW),
            jax.ShapeDtypeStruct((16,) + gate_up, LOW),
            shape((2,), out_w),
            shape((), down),
        ],
        in_specs=[IN_VMEM] * 9 + [ANYWHERE] * 2,
        out_specs=[IN_VMEM] + [ANYWHERE] * 2 + [IN_VMEM] * 5 + [ANYWHERE] * 4,
        scratch_shapes=Gather.sems(6)
        + [DMA((16,))] * 6
        + [DMA((1,)), DMA, DMA((2,)), DMA((6,)), DMA((2,)), DMA((32,))]
        + [pltpu.VMEM((16, tokens, model), LOW)] * 2
        + [pltpu.VMEM((2, 16) + qkv, LOW), pltpu.VMEM((16,) + qkv, LOW), pltpu.VMEM((16,) + gate_up, LOW)],
        compiler_params=params(0),
    )(token, grad, w_query, w_key, w_value, w_gate, w_up, gain_one, gain_two, out_w, down)


def row_place(place, row, strip):
    return jnp.where(row < strip, place * strip + row, (31 - place) * strip + row - strip)


def key_places(strip):
    index = lax.broadcasted_iota(jnp.int32, (1, 32 * strip), 1)
    return row_place(index // (2 * strip), index % (2 * strip), strip)


def query_places(pair, strip):
    index = lax.broadcasted_iota(jnp.int32, (4 * strip, 1), 0)
    return row_place(2 * pair + index // (2 * strip), index % (2 * strip), strip)


def of_pair(block, pair, seq):
    rows, width = block.shape[2:]
    return block[pl.ds(2 * pair, 2), seq].reshape(2 * rows, width)


def forward_kernel(
    shift, valid, query, key, value, out_w, token_far, grads, gate_up, down_own, down_other,
    grad_state, branch, hidden_own_far, attended_far, hidden_far, down_far, gate_up_grad, *scratch
):
    me = Place()
    hidden_own, attended, hidden, down_full, token, grad_own, side = scratch[-15:-8]
    tokens, model = token.shape
    width = hidden.shape[2]
    gather_sems = scratch[Scatter.count : Scatter.count + Gather.count]
    units, grad_gate_up, gate_up_full, grads_here, stage, leaving, local, swap_sems = scratch[-8:]
    scatter = Scatter(me, scratch)
    brought = [
        pltpu.make_async_copy(gate_up, gate_up_full.at[me.s], local.at[0]),
        pltpu.make_async_copy(down_own, down_full.at[me.s], local.at[1]),
        pltpu.make_async_copy(down_other, down_full.at[1 - me.s], local.at[2]),
        pltpu.make_async_copy(grads, grads_here, local.at[3]),
    ]
    near = [
        pltpu.make_async_copy(token_far, token, side.at[0]),
        pltpu.make_async_copy(grads.at[me.c], grad_own, side.at[1]),
    ]
    away = [
        pltpu.make_async_copy(attended, attended_far, side.at[2]),
        pltpu.make_async_copy(hidden_own, hidden_own_far, side.at[3]),
        pltpu.make_async_copy(hidden, hidden_far, side.at[4]),
        pltpu.make_async_copy(down_full, down_far, side.at[5]),
    ]
    ready = greet(me, over_seq=True)
    swap = remote(gate_up, gate_up_full.at[me.s], swap_sems.at[0], swap_sems.at[1], (1 - me.s, me.c))
    rows, depth = query.shape[2], query.shape[3]
    strip = rows // 2
    length = rows * 16
    scale = depth ** (-0.5)

    def attention(pair):
        where = query_places(pair, strip)
        keys_at = key_places(strip)
        for seq in range(2):
            keys = key[:, seq].reshape(length, depth)
            values = value[:, seq].reshape(length, depth)
            logits = dot_right(of_pair(query, pair, seq), keys) * scale - shift
            live = (keys_at <= where) & (keys_at < valid[seq])
            weights = jnp.where(live, jax.nn.sigmoid(logits), 0.0).astype(LOW)
            attended[pl.ds(2 * pair, 2), pl.ds(seq * rows, rows)] = (
                jnp.dot(weights, values, preferred_element_type=F32).astype(LOW).reshape(2, rows, depth)
            )

    def out_terms(first, columns):
        return jnp.dot(own_last(me, attended, first), out_w[:, columns], preferred_element_type=F32)

    def met():
        ready()
        swap.start()
        for copy in near + brought:
            copy.start()

    scatter.run(attention, out_terms, write_total(hidden_own), ready=met)
    scatter.drain()
    for copy in near:
        copy.wait()

    def to_unit(at):
        values = hidden_own[at, :] + token[at, :].astype(F32)
        hidden_own[at, :] = values
        units[me.c, at] = (values * scale_of(values)).astype(LOW)

    by_rows(tokens, to_unit)
    gather = Gather(me, pieces_of(units), EARLY, *gather_sems)
    rows_of = gate_up_full.shape[1] * gate_up_full.shape[2]
    units_of = down_full.shape[1]
    first = [True]

    def consume(pair):
        if first[0]:
            for copy in brought:
                copy.wait()
            swap.wait()
            first[0] = False
        both = pl.ds(2 * pair, 2)

        def dot_rows(rows, columns):
            return jnp.dot(
                rows,
                gate_up_full[:, :, :, columns].reshape(2 * rows_of, units_of),
                preferred_element_type=F32,
            )

        @pl.loop(0, 2)
        def _(half):
            gate_at = pl.ds(pl.multiple_of(half * units_of, units_of), units_of)
            up_at = pl.ds(pl.multiple_of(width + half * units_of, units_of), units_of)
            rows = units[both].reshape(2 * tokens, model)
            gate = dot_rows(rows, gate_at)
            up = dot_rows(rows, up_at)
            grad = dot_right(grads_here[both].reshape(2 * tokens, model), down_full[half])
            sig = jax.nn.sigmoid(gate)
            silu = gate * sig

            def store(target, columns, value):
                target[both, :, columns] = value.astype(LOW).reshape(2, tokens, units_of)

            store(hidden, gate_at, silu * up)
            store(grad_gate_up, gate_at, grad * up * (sig * (1.0 + gate * (1.0 - sig))))
            store(grad_gate_up, up_at, grad * silu)

    gather.run(consume)
    for copy in away:
        copy.start()
    block_rows = gate_up_full.shape[2]

    def unit_terms(first, columns):
        start, size = columns.start, columns.size
        blocks = size // block_rows
        block = start // block_rows
        weights = gate_up_full[block // 16, pl.ds(block % 16, blocks)].reshape(size, 2 * width)
        return dot_right(own_last(me, grad_gate_up, first), weights)

    every = 16 * tokens
    part = model // 8

    def gate_up_part(number):
        def work(slot):
            left = units[:, :, number * part : (number + 1) * part].reshape(every, part)
            slot[...] = dot_left(left, grad_gate_up[...].reshape(every, 2 * width)).astype(LOW)

        return work, gate_up_grad.at[pl.ds(number * part, part)]

    fillers, end = leave(stage, [gate_up_part(n) for n in range(8)], leaving)
    scatter.run(None, unit_terms, write_total(grad_state), fillers)

    def to_state(at):
        values = hidden_own[at, :]
        back = norm_back(values, scale_of(values), grad_state[at, :])
        state = grad_own[at, :].astype(F32) + back
        grad_state[at, :] = state
        branch[at, :] = state.astype(LOW)

    by_rows(tokens, to_state)
    end()
    for copy in away:
        copy.wait()
    scatter.drain()
    gather.finish()


def forward(shift, valid, query, key, value, out_w, token, grads, gate_up, down_own, down_other):
    tokens, model = token.shape
    width = 2 * down_own.shape[0]
    full = jax.ShapeDtypeStruct((tokens, model), F32)
    return pl.pallas_call(
        functools.partial(forward_kernel, shift),
        out_shape=[
            full,
            jax.ShapeDtypeStruct((tokens, model), LOW),
            full,
            jax.ShapeDtypeStruct((16, tokens, query.shape[3]), LOW),
            jax.ShapeDtypeStruct((16, tokens, width), LOW),
            jax.ShapeDtypeStruct((2,) + down_own.shape, LOW),
            jax.ShapeDtypeStruct((model, 2 * width), LOW),
        ],
        in_specs=[IN_SMEM] + [IN_VMEM] * 4 + [ANYWHERE] * 5,
        out_specs=[IN_VMEM] * 2 + [ANYWHERE] * 5,
        scratch_shapes=Scatter.scratch(tokens, model)
        + Gather.sems(3)
        + [
            pltpu.VMEM((tokens, model), F32),
            pltpu.VMEM((16, tokens, query.shape[3]), LOW),
            pltpu.VMEM((16, tokens, width), LOW),
            pltpu.VMEM((2,) + down_own.shape, LOW),
            pltpu.VMEM((tokens, model), LOW),
            pltpu.VMEM((tokens, model), LOW),
            DMA((6,)),
        ]
        + [
            pltpu.VMEM((16, tokens, model), LOW),
            pltpu.VMEM((16, tokens, 2 * width), LOW),
            pltpu.VMEM((2,) + gate_up.shape, LOW),
            pltpu.VMEM((16, tokens, model), LOW),
            pltpu.VMEM((2, model // 8, 2 * width), LOW),
            DMA((8,)),
            DMA((4,)),
            DMA((2,)),
        ],
        compiler_params=params(1),
    )(valid, query, key, value, out_w, token, grads, gate_up, down_own, down_other)


def attend_back_kernel(
    shift, valid, branch, units, gate_up, *rest
):
    far, rest = rest[:10], rest[10:]
    in_grad, qkv_grad, out_grad, gate_up_other = rest[:4]
    key_sum, value_sum, branches, grad_qkv, units_here, total_out = rest[4:10]
    side, near, scratch = rest[10], rest[11:21], rest[21:]
    query, key, value, out_w, cosine, sine, qkv_w, attended, token, grad_state = near
    near_copies = [pltpu.make_async_copy(a, b, side.at[n]) for n, (a, b) in enumerate(zip(far, near))]
    me = Place()
    tokens, model = branch.shape
    gather = Gather(me, pieces_of(branches), EARLY, *scratch[Scatter.count : Scatter.count + Gather.count])
    sems, local = scratch[-2:]
    own = pltpu.make_async_copy(branch, branches.at[me.c], local.at[0])
    own.start()
    bring = pltpu.make_async_copy(units, units_here, local.at[1])
    ready = greet(me, over_seq=True)
    for copy in near_copies:
        copy.start()
    bring.start()
    own.wait()
    ready()
    over = (1 - me.s, me.c)
    swaps = [
        remote(gate_up.at[1 - me.s], gate_up_other, sems.at[0], sems.at[1], over),
    ]
    for copy in swaps:
        copy.start()
    rows, width = query.shape[2:]
    strip = rows // 2
    length = rows * 16
    scale = width ** (-0.5)
    key_sum[...] = jnp.zeros_like(key_sum)
    value_sum[...] = jnp.zeros_like(value_sum)

    def turn_back(values, places):
        swapped = pltpu.roll(values, width // 2, axis=1)
        turned = values * cosine[places].reshape(2 * rows, width)
        return (turned + swapped * sine[places].reshape(2 * rows, width)).astype(LOW).reshape(2, rows, width)

    first = [True]

    def consume(pair):
        if first[0]:
            for copy in near_copies[:6]:
                copy.wait()
            first[0] = False
        where = query_places(pair, strip)
        keys_at = key_places(strip)
        both = pl.ds(2 * pair, 2)
        for seq in range(2):
            here = pl.ds(seq * rows, rows)
            grad = dot_right(branches[both, here].reshape(2 * rows, -1), out_w[...]).astype(LOW)
            keys = key[:, seq].reshape(length, width)
            values = value[:, seq].reshape(length, width)
            queries = of_pair(query, pair, seq)
            logits = dot_right(queries, keys) * scale - shift
            live = (keys_at <= where) & (keys_at < valid[seq])
            sig = jnp.where(live, jax.nn.sigmoid(logits), 0.0)
            weights = sig.astype(LOW)
            grad_logits = (dot_right(grad, values) * (sig * (1.0 - sig))).astype(LOW)
            grad_query = jnp.dot(grad_logits, keys, preferred_element_type=F32) * scale
            grad_qkv[both, here, 0:width] = turn_back(grad_query, both)
            key_sum[seq] += dot_left(grad_logits, queries)
            value_sum[seq] += dot_left(weights, grad)

    gather.run(consume)

    def prepare(pair):
        both = pl.ds(2 * pair, 2)
        at = pl.ds(pl.multiple_of(pair * 2 * rows, 2 * rows), 2 * rows)
        for seq in range(2):
            here = pl.ds(seq * rows, rows)
            grad_qkv[both, here, width : 2 * width] = turn_back(key_sum[seq, at] * scale, both)
            grad_qkv[both, here, 2 * width :] = value_sum[seq, at].astype(LOW).reshape(2, rows, width)

    scatter = Scatter(me, scratch)

    def produce(first, columns):
        return dot_right(own_last(me, grad_qkv, first), qkv_w[columns, :])

    every = 16 * tokens
    for copy in near_copies[6:] + [bring]:
        copy.wait()

    def qkv_part(number, part=model // 8):
        at = slice(number * part, (number + 1) * part)
        left = units_here[:, :, at].reshape(every, part)
        qkv_grad[at, :] = dot_left(left, grad_qkv[...].reshape(every, 3 * width)).astype(LOW)

    def out_part(number, part=model // 4):
        at = slice(number * part, (number + 1) * part)
        left = attended[...].reshape(every, width)
        out_grad[:, at] = dot_left(left, branches[:, :, at].reshape(every, part)).astype(LOW)

    fillers = [functools.partial(out_part, n) for n in range(4)]
    fillers += [functools.partial(qkv_part, n) for n in range(8)]
    scatter.run(prepare, produce, write_total(total_out), fillers)

    for seq in range(2):
        for part in range(2):
            at = slice(part * rows // 2, (part + 1) * rows // 2)
            here = slice(seq * rows + at.start, seq * rows + at.stop)
            values = token[here, :].astype(F32)
            back = norm_back(values, scale_of(values), total_out[here, :])
            in_grad[at, seq, :] = grad_state[here, :] + back
    scatter.drain()
    gather.finish()
    for copy in swaps:
        copy.wait()


def attend_back(
    shift, valid, branch, units, query, key, value, out_w, qkv_w, attended, cosine, sine, gate_up, token, grad_state
):
    tokens, model = branch.shape
    rows, width = query.shape[2:]
    near = (query, key, value, out_w, cosine, sine, qkv_w, attended, token, grad_state)
    return pl.pallas_call(
        functools.partial(attend_back_kernel, shift),
        out_shape=[
            jax.ShapeDtypeStruct((rows, 2, model), F32),
            jax.ShapeDtypeStruct((model, 3 * width), LOW),
            jax.ShapeDtypeStruct((width, model), LOW),
            jax.ShapeDtypeStruct(gate_up.shape[1:], LOW),
        ],
        in_specs=[IN_SMEM] + [ANYWHERE] * 13,
        out_specs=[IN_VMEM] * 3 + [ANYWHERE],
        scratch_shapes=[pltpu.VMEM((2, 16 * rows, width), F32)] * 2
        + [
            pltpu.VMEM((16, tokens, model), LOW),
            pltpu.VMEM((16, tokens, 3 * width), LOW),
            pltpu.VMEM((16, tokens, model), LOW),
            pltpu.VMEM((tokens, model), F32),
        ]
        + [DMA((10,))]
        + [pltpu.VMEM(array.shape, array.dtype) for array in near]
        + Scatter.scratch(tokens, model)
        + Gather.sems(3)
        + [DMA((4,)), DMA((2,))],
        compiler_params=params(4),
    )(valid, branch, units, gate_up, *near)


def return_kernel(
    hidden_far, down_far, qkv_far, gate_up_far, gate_up_other, out_far, hidden_own_far, grads_far,
    total_out, qkv_back, gate_up_back, out_back, down_grad, down_other, *scratch
):
    (qx, qsum, qxs, qxr, qs, qr, psum, ps, pr, oland, os, orecv, hidden, down_w, px, sums, qkv, out_pair, hidden_own, grads, local, across) = scratch[
        Scatter.count :
    ]
    me = Place()
    ready = greet_plane(me)
    bring = [
        pltpu.make_async_copy(hidden_far, hidden, local.at[0]),
        pltpu.make_async_copy(down_far, down_w, local.at[1]),
        pltpu.make_async_copy(gate_up_far.at[me.s], psum, local.at[2]),
        pltpu.make_async_copy(gate_up_other, px, local.at[3]),
        pltpu.make_async_copy(qkv_far, qkv, local.at[4]),
        pltpu.make_async_copy(out_far, out_pair, local.at[5]),
        pltpu.make_async_copy(hidden_own_far, hidden_own, local.at[6]),
        pltpu.make_async_copy(grads_far, grads, local.at[7]),
    ]
    for copy in bring:
        copy.start()
    over = (1 - me.s, me.c)

    def cross(place):
        return remote(qkv.at[1 - me.s, place], qx.at[place], qxs.at[place], qxr.at[place], over)

    def send(sums, back, s_sem, r_sem, step):
        to, _ = turn(me, step)
        return remote(sums.at[to], back.at[me.c], s_sem.at[step], r_sem.at[me.c], (me.s, to))

    holder = me.at(me.z, me.y, me.s)

    def out_send(target_core, same):
        target = (me.s if same else 1 - me.s, me.at(me.z, me.y, target_core))
        slot = 0 if same else 1
        return remote(out_pair.at[target_core], oland.at[me.s], os.at[slot], orecv.at[me.s], target)

    inside = me.k == me.s

    def met():
        ready()
        for step in range(1, 16):
            send(psum, gate_up_back, ps, pr, step).start()
        for copy in bring[4:]:
            copy.wait()
        for step in range(1, 16):
            cross(turn(me, step)[0]).start()
        cross(me.c).start()

        @pl.when(inside)
        def _():
            out_send(1 - me.k, True).start()

        @pl.when(jnp.logical_not(inside))
        def _():
            out_send(me.k, False).start()
            remote(
                out_pair.at[1 - me.k], oland.at[me.s], os.at[0], orecv.at[me.s],
                (1 - me.s, me.at(me.z, me.y, 1 - me.k)),
            ).start()

    def between():
        for step in range(1, 16):
            to, _ = turn(me, step)
            cross(to).wait_recv()
            qsum[to] = (qkv[me.s, to].astype(F32) + qx[to].astype(F32)).astype(LOW)
            send(qsum, qkv_back, qs, qr, step).start()
        cross(me.c).wait_recv()
        qkv_back[me.c] = (qkv[me.s, me.c].astype(F32) + qx[me.c].astype(F32)).astype(LOW)

    scatter = Scatter(me, scratch)

    def produce(first, columns):
        return jnp.dot(own_last(me, hidden, first), down_w[:, columns], preferred_element_type=F32)

    for copy in bring[:4]:
        copy.wait()

    @pl.loop(0, 16)
    def _(place):
        psum[place] = (psum[place].astype(F32) + px[place].astype(F32)).astype(LOW)

    gate_up_back[me.c] = psum[me.c]
    down_swap = remote(down_grad.at[1 - me.s], down_other, across.at[0], across.at[1], over)
    parts, double, part = down_other.shape
    every = hidden.shape[0] * hidden.shape[1]

    def down_part(half, number):
        seq = 1 - me.s if half == 0 else me.s
        thin = double // 2
        start = pl.multiple_of((seq * parts + number) * thin, thin)
        left = hidden[:, :, pl.ds(start, thin)].reshape(every, thin)
        for side in range(2):
            right = grads[:, :, side * part : (side + 1) * part].reshape(every, part)
            down_grad[seq, number, pl.ds(side * thin, thin)] = dot_left(left, right).astype(LOW)
        if half == 0 and number == parts - 1:
            down_swap.start()

    fillers = [between] + [functools.partial(down_part, half, n) for half in range(2) for n in range(parts)]
    scatter.run(None, produce, write_total(sums), fillers, met)
    down_swap.wait()

    rows = total_out.shape[0]
    for seq in range(2):
        here = slice(seq * rows, (seq + 1) * rows)
        total_out[:, seq, :] = (sums[here, :] + hidden_own[here, :]).astype(LOW)
    scatter.drain()
    for step in range(1, 16):
        to, source = turn(me, step)
        for sums, back, s_sem, r_sem in ((qsum, qkv_back, qs, qr), (psum, gate_up_back, ps, pr)):
            remote(sums.at[0], back.at[source], s_sem.at[step], r_sem.at[source], over).wait_recv()
            send(sums, back, s_sem, r_sem, step).wait_send()
        cross(to).wait_send()
    cross(me.c).wait_send()

    @pl.when(inside)
    def _():
        out_send(1 - me.k, True).wait_send()
        remote(out_pair.at[0], oland.at[1 - me.s], os.at[0], orecv.at[1 - me.s], over).wait_recv()
        out_back[...] = out_pair[me.k].astype(F32) + oland[1 - me.s].astype(F32)

    @pl.when(jnp.logical_not(inside))
    def _():
        out_send(me.k, False).wait_send()
        out_send(1 - me.k, True).wait_send()
        for half in range(2):
            remote(out_pair.at[0], oland.at[half], os.at[0], orecv.at[half], over).wait_recv()
        out_back[...] = oland[0].astype(F32) + oland[1].astype(F32)


def give_back(hidden, down_w, qkv, gate_up, gate_up_other, out_pair, hidden_own, grads):
    tokens, model = hidden.shape[1], down_w.shape[1]
    down_half = (2, hidden.shape[2] // 2, model // 2)
    block = lambda array: pltpu.VMEM(array.shape[1:], LOW)
    return pl.pallas_call(
        return_kernel,
        out_shape=[
            jax.ShapeDtypeStruct((tokens // 2, 2, model), LOW),
            jax.ShapeDtypeStruct(qkv.shape[1:], LOW),
            jax.ShapeDtypeStruct(gate_up.shape[1:], LOW),
            jax.ShapeDtypeStruct(out_pair.shape[1:], F32),
            jax.ShapeDtypeStruct((2,) + down_half, LOW),
            jax.ShapeDtypeStruct(down_half, LOW),
        ],
        in_specs=[ANYWHERE] * 8,
        out_specs=[IN_VMEM] * 6,
        scratch_shapes=Scatter.scratch(tokens, model)
        + [block(qkv), block(qkv)]
        + [DMA((16,))] * 4
        + [block(gate_up)]
        + [DMA((16,))] * 2
        + [pltpu.VMEM(out_pair.shape, LOW), DMA((2,)), DMA((2,))]
        + [pltpu.VMEM(hidden.shape, LOW), pltpu.VMEM(down_w.shape, LOW), block(gate_up)]
        + [pltpu.VMEM((tokens, model), F32), pltpu.VMEM(qkv.shape, LOW), pltpu.VMEM(out_pair.shape, LOW)]
        + [pltpu.VMEM((tokens, model), F32), pltpu.VMEM(grads.shape, LOW), DMA((8,)), DMA((2,))],
        compiler_params=params(5),
    )(hidden, down_w, qkv, gate_up, gate_up_other, out_pair, hidden_own, grads)


def assemble_kernel(
    gain_one, gain_two, qkv_far, w_query_far, w_key_far, w_value_far, gate_up_far, w_gate_far, w_up_far,
    down_far, down_other_far, layer_out_far, in_grad_far, out_grad_far,
    query_grad, key_grad, value_grad, gate_grad, up_grad, down_grad, gain_one_grad, gain_two_grad,
    layer_out, in_grad, out_grad, *near
):
    qkv_back, w_query, w_key, w_value, gate_up_back, w_gate, w_up, down_own, down_other, *held, sems, pass_sems = near
    far = (qkv_far, w_query_far, w_key_far, w_value_far, gate_up_far, w_gate_far, w_up_far)
    far += (down_far.at[lax.axis_index("seq")], down_other_far)
    copies = [pltpu.make_async_copy(a, b, sems.at[n]) for n, (a, b) in enumerate(zip(far, near))]
    for copy in copies:
        copy.start()
    sources, targets = (layer_out_far, in_grad_far, out_grad_far), (layer_out, in_grad, out_grad)
    passed = [pltpu.make_async_copy(sources[n], held[n], pass_sems.at[n]) for n in range(3)]
    onward = [pltpu.make_async_copy(held[n], targets[n], pass_sems.at[3 + n]) for n in range(3)]
    for copy in passed:
        copy.start()

    def lanes(total):
        return jnp.sum(jnp.transpose(total), axis=0, keepdims=True)

    width = qkv_back.shape[2] // 3
    rows = qkv_back.shape[1]
    one = down_rows(gain_one, width)
    total = jnp.zeros((rows, width), F32)
    for copy in copies[:4]:
        copy.wait()
    for place in range(16):
        at = slice((place // 2 + 8 * (place % 2)) * width, (place // 2 + 8 * (place % 2) + 1) * width)
        for index, (weight, target) in enumerate(
            ((w_query, query_grad), (w_key, key_grad), (w_value, value_grad))
        ):
            block = qkv_back[place, :, index * width : (index + 1) * width].astype(F32)
            target[:, at] = block * one
            total += block * weight[:, at].astype(F32)
    gain_one_grad[...] = lanes(total)
    for n in range(3):
        passed[n].wait()
        onward[n].start()
    width = gate_up_back.shape[2] // 4
    two = down_rows(gain_two, width)
    total = jnp.zeros((rows, width), F32)
    for copy in copies[4:7]:
        copy.wait()
    for place in range(16):
        for half in range(2):
            at = slice((half * 16 + place) * width, (half * 16 + place + 1) * width)
            for index, (weight, target) in enumerate(((w_gate, gate_grad), (w_up, up_grad))):
                start = (2 * index + half) * width
                block = gate_up_back[place, :, start : start + width].astype(F32)
                target[:, at] = block * two
                total += block * weight[:, at].astype(F32)
    gain_two_grad[...] = lanes(total)
    for copy in copies[7:]:
        copy.wait()
    parts, double, part = down_own.shape
    depth = double // 2
    for number in range(parts):
        for half in range(2):
            at = slice(half * depth, (half + 1) * depth)
            down_grad[number * depth : (number + 1) * depth, half * part : (half + 1) * part] = (
                down_own[number, at].astype(F32) + down_other[number, at].astype(F32)
            )
    for copy in onward:
        copy.wait()


def assemble(
    gain_one, gain_two, qkv_back, w_query, w_key, w_value, gate_up_back, w_gate, w_up, down, down_other, *passed
):
    rows, model = w_query.shape
    narrow = jax.ShapeDtypeStruct((rows, model), F32)
    wide = jax.ShapeDtypeStruct(w_gate.shape, F32)
    gain = jax.ShapeDtypeStruct((1, rows), F32)
    parts, double, part = down_other.shape
    near = (qkv_back, w_query, w_key, w_value, gate_up_back, w_gate, w_up, down_other, down_other)
    return pl.pallas_call(
        assemble_kernel,
        out_shape=[narrow] * 3
        + [wide] * 2
        + [jax.ShapeDtypeStruct((parts * double // 2, 2 * part), F32)]
        + [gain] * 2
        + [jax.ShapeDtypeStruct(array.shape, array.dtype) for array in passed],
        in_specs=[IN_VMEM] * 2 + [ANYWHERE] * 12,
        out_specs=[IN_VMEM] * 8 + [ANYWHERE] * 3,
        scratch_shapes=[pltpu.VMEM(array.shape, LOW) for array in near]
        + [pltpu.VMEM(array.shape, array.dtype) for array in passed]
        + [DMA((9,)), DMA((6,))],
        compiler_params=pltpu.CompilerParams(vmem_limit_bytes=60 << 20),
    )(gain_one, gain_two, qkv_back, w_query, w_key, w_value, gate_up_back, w_gate, w_up, down, down_other, *passed)


def move_tokens_step(
    layer_in,
    valid_len,
    norm1_gain,
    w_query,
    w_key,
    w_value,
    w_out,
    norm2_gain,
    w_gate,
    w_up,
    w_down,
    cotangent,
):
    local_rows, _, model = layer_in.shape
    width = model // HEADS
    cp_devices = 16
    shift = math.log(cp_devices * local_rows)
    weight_rows = w_gate.shape[0]
    gain_one, gain_two = norm1_gain[None], norm2_gain[None]

    token_rows, units, grads, query, key, value, cosine, back_sine, qkv_w, gate_up_own, head_out, down_other = spread(
        layer_in, cotangent, w_query, w_key, w_value, w_gate, w_up,
        gain_one, gain_two, w_out, w_down,
    )
    qkv_w = qkv_w.reshape(model, 3 * width)
    head_out = head_out.reshape(width, model)
    grad_state, branch, hidden_state, attended, hidden, down_full, gate_up_grad = forward(
        shift, valid_len, query, key, value, head_out, token_rows, grads, gate_up_own, w_down, down_other
    )
    gate_up_grad = gate_up_grad.reshape(2, cp_devices, weight_rows, -1)
    in_grad, qkv_grad, out_grad, gate_up_grad_other = attend_back(
        shift, valid_len, branch, units, query, key, value, head_out, qkv_w, attended,
        cosine, back_sine, gate_up_grad, token_rows, grad_state,
    )
    layer_out, qkv_back, gate_up_back, out_back, down_grad, down_grad_other = give_back(
        hidden,
        down_full.reshape(-1, model),
        qkv_grad.reshape(2, cp_devices, weight_rows, -1),
        gate_up_grad,
        gate_up_grad_other,
        out_grad.reshape(2, width // 2, model),
        hidden_state,
        grads,
    )
    (query_grad, key_grad, value_grad, gate_grad, up_grad, down_back, gain_one_grad, gain_two_grad,
     layer_out, in_grad, out_back) = assemble(
        gain_one, gain_two, qkv_back, w_query, w_key, w_value, gate_up_back, w_gate, w_up, down_grad, down_grad_other,
        layer_out, in_grad, out_back,
    )
    return (
        layer_out,
        in_grad,
        gain_one_grad[0],
        query_grad,
        key_grad,
        value_grad,
        out_back,
        gain_two_grad[0],
        gate_grad,
        up_grad,
        down_back,
    )


def solution(mesh):
    fits = mesh.shape["cp"] == HEADS and mesh.shape["seq"] == 2
    on_device = move_tokens_step if fits else gather_weights_step
    placed = (
        P("cp", "seq", None),
        P("seq"),
        P(("seq", "cp")),
        P(("seq", "cp"), None),
        P(("seq", "cp"), None),
        P(("seq", "cp"), None),
        P(("seq", "cp"), None),
        P(("seq", "cp")),
        P(("seq", "cp"), None),
        P(("seq", "cp"), None),
        P(("seq", "cp"), None),
        P("cp", "seq", None),
    )
    return jax.shard_map(
        on_device,
        mesh=mesh,
        in_specs=placed,
        out_specs=(
            P("cp", "seq", None),
            P("cp", "seq", None),
            P(("seq", "cp")),
            P(("seq", "cp"), None),
            P(("seq", "cp"), None),
            P(("seq", "cp"), None),
            P(("seq", "cp"), None),
            P(("seq", "cp")),
            P(("seq", "cp"), None),
            P(("seq", "cp"), None),
            P(("seq", "cp"), None),
        ),
        check_vma=False,
    )
```
